32 devices in a mesh: section: 4 (over y, x), dp: 8 (over z, core).
Axes of the slice: x: 2, y: 2, z: 4, core: 2. Of those that a mesh axis runs over, the one named last changes fastest.
Arguments:
- latents: float32 [32, 256, 16], P('dp'), may hold values from -6 to 6
- noise: float32 [32, 256, 16], P('dp'), may hold values from -6 to 6
- timesteps: int32 [32], P('dp'), may hold values from 0 to 999
- labels: int32 [32], P('dp'), may hold values from 0 to 999
- patch_mask: int32 [32, 256], P('dp'), may hold values from 0 to 1, as said below
- w_in: float32 [4, 1152, 16128], P('section', 'dp'), may hold values from -0.1875 to 0.1875
- w_down: float32 [4, 4608, 1152], P('section', 'dp'), may hold values from -0.09375 to 0.09375
- b_blk: float32 [4, 16128], P('section', 'dp'), may hold values from -1.25 to 1.25
- small_mats: float32 [1152, 4744], P('dp', 'section')
- small_bias: float32 [5776], P('section'), may hold values from -1.25 to 1.25
- m_in: float32 [4, 1152, 16128], P('section', 'dp'), may hold values from -5.9604645e-07 to 5.9604645e-07
- m_down: float32 [4, 4608, 1152], P('section', 'dp'), may hold values from -5.722046e-06 to 5.722046e-06
- m_bias: float32 [4, 16128], P('section', 'dp'), may hold values from -1.9073486e-06 to 1.9073486e-06
- m_small: float32 [1152, 4744], P('dp', 'section'), may hold values from -5.722046e-06 to 5.722046e-06
- m_sbias: float32 [5776], P('section'), may hold values from -2.2888184e-05 to 2.2888184e-05
- v_in: float32 [4, 1152, 16128], P('section', 'dp'), may hold values from 4.946241e-18 to 7.9139857e-17
- v_down: float32 [4, 4608, 1152], P('section', 'dp'), may hold values from 4.946241e-18 to 7.9139857e-17
- v_bias: float32 [4, 16128], P('section', 'dp'), may hold values from 7.9139857e-17 to 1.2662377e-15
- v_small: float32 [1152, 4744], P('dp', 'section'), may hold values from 4.946241e-18 to 8.6805556e-15
- v_sbias: float32 [5776], P('section'), may hold values from 7.9139857e-17 to 1.2662377e-15
Outputs:
- loss: float32 [], replicated
- grad_norm: float32 [], replicated
- w_in_new: float32 [4, 1152, 16128], P('section', 'dp')
- m_in_new: float32 [4, 1152, 16128], P('section', 'dp')
- v_in_new: float32 [4, 1152, 16128], P('section', 'dp')
- w_down_new: float32 [4, 4608, 1152], P('section', 'dp')
- m_down_new: float32 [4, 4608, 1152], P('section', 'dp')
- v_down_new: float32 [4, 4608, 1152], P('section', 'dp')
- b_blk_new: float32 [4, 16128], P('section', 'dp')
- m_bias_new: float32 [4, 16128], P('section', 'dp')
- v_bias_new: float32 [4, 16128], P('section', 'dp')
- small_mats_new: float32 [1152, 4744], P('dp', 'section')
- m_small_new: float32 [1152, 4744], P('dp', 'section')
- v_small_new: float32 [1152, 4744], P('dp', 'section')
- small_bias_new: float32 [5776], P('section')
- m_sbias_new: float32 [5776], P('section')
- v_sbias_new: float32 [5776], P('section')
The draws below stay inside these ranges and needn't reach their ends.
Inputs may be any that keep to these rules, and one draw needn't show every extreme that they name: `patch_mask`: the first patch of every image counts.
All inputs are finite; a program needn't handle non-finite values.
Results may differ from the reference program's by a relative error of at most 0.0022.
Values may be sent and summed in bfloat16 or wider, within the bound.
A program may use at most 640 MiB of HBM per device.

```python
import math
import jax
import jax.numpy as jnp
from jax import lax

D = 1152
HEADS = 16
HEAD_DIM = 72
FF = 4608
CLASSES = 1000
FREQ = 256
PATCH_IN = 16
GRID = 16
IMG_DEV = 4
PATCHES = 256
LAYERS = 4
IMAGES = 32
WIDE = 16128
SMALLC = 4744
SB = 5776
PARAMS = 101086864


def draw_patch_mask(key, part):
    rolls = jax.random.randint(key, (IMAGES, PATCHES), 0, 1000)
    index = jnp.arange(IMAGES, dtype=jnp.int32)
    limit = 250 + 650 * index // max(IMAGES - 1, 1)
    chosen = (rolls < limit[:, None]).astype(jnp.int32)
    return chosen.at[:, 0].set(1)


def draw_small_mats(key, part):
    column = jnp.arange(SMALLC, dtype=jnp.int32)
    time_start = PATCH_IN
    label_start = PATCH_IN + FREQ
    second_start = label_start + CLASSES
    spread = jnp.where(column < time_start, PATCH_IN ** (-0.5), jnp.where(column < label_start, FREQ ** (-0.5), jnp.where(column < second_start, 0.5, D ** (-0.5)))).astype(jnp.float32)
    base = jax.random.normal(key, (D, SMALLC), jnp.float32)
    return base * spread[None, :]


def draw_v_small(key, part):
    lower = 5e-10 / PARAMS
    upper = 8e-09 / PARAMS
    spot = jax.random.uniform(key, (D, SMALLC), jnp.float32)
    return jnp.exp(math.log(lower) + spot * math.log(upper / lower)).astype(jnp.float32)


def place_ends(array, rng, smallest, high):
    longest = array.shape.index(max(array.shape))
    spots = []
    for shift in (0, 1):
        where = [jax.random.randint(jax.random.fold_in(rng, axis), (), 0, length) for axis, length in enumerate(array.shape)]
        where[longest] = (where[longest] + shift) % array.shape[longest]
        spots.append(tuple(where))
    return array.at[spots[0]].set(smallest).at[spots[1]].set(high)


def level_of(own_key, dims, cuts, low, largest):
    loudness, own = 1.0, jax.random.fold_in(own_key, 6)
    for position, shards_of in cuts:
        steps = jnp.exp(jax.random.uniform(jax.random.fold_in(own, position), (shards_of,), jnp.float32, low / len(cuts), largest / len(cuts)))
        loudness = loudness * jnp.repeat(steps, dims[position] // shards_of).reshape([-1 if axis == position else 1 for axis in range(len(dims))])
    return loudness


def centred(stream_key, extent, deviation, most, shards=(), kind=jnp.bfloat16):
    level = level_of(stream_key, extent, shards, -0.22, 0.18) if shards else 1.0
    drawn = jax.random.normal(stream_key, extent, jnp.float32) * deviation * level
    return jnp.minimum(jnp.maximum(drawn, -most), most).astype(kind)


def setup_inputs(seed: int = 0) -> dict:
    splits = jax.random.split(jax.random.key(seed), 21)
    latents = centred(splits[0], (IMAGES, PATCHES, PATCH_IN), 1.0, 6.0, ((0, 8),), jnp.float32)
    noise = centred(splits[1], (IMAGES, PATCHES, PATCH_IN), 1.0, 6.0, ((0, 8),), jnp.float32)
    timesteps = place_ends(jax.random.randint(splits[2], (IMAGES,), 0, 1000), jax.random.fold_in(splits[2], 1), 0, 999).astype(jnp.int32)
    labels = place_ends(jax.random.randint(splits[3], (IMAGES,), 0, CLASSES), jax.random.fold_in(splits[3], 1), 0, CLASSES - 1).astype(jnp.int32)
    patch_mask = draw_patch_mask(jax.random.fold_in(splits[20], 71), 0)
    w_in = centred(splits[5], (LAYERS, D, WIDE), D ** -0.5, 0.1875, ((0, 4), (1, 8)), jnp.float32)
    w_down = centred(splits[6], (LAYERS, FF, D), FF ** -0.5, 0.09375, ((0, 4), (1, 8)), jnp.float32)
    b_blk = centred(splits[7], (LAYERS, WIDE), 0.2, 1.25, ((0, 4), (1, 8)), jnp.float32)
    small_mats = draw_small_mats(jax.random.fold_in(splits[20], 71), 0)
    small_bias = centred(splits[9], (SB,), 0.2, 1.25, ((0, 4),), jnp.float32)
    m_in = centred(splits[10], (LAYERS, D, WIDE), (0.001 * PARAMS ** -0.5), 5.960464477539062e-07, ((0, 4), (1, 8)), jnp.float32)
    m_down = centred(splits[11], (LAYERS, FF, D), (0.009 * PARAMS ** -0.5), 5.7220458984375e-06, ((0, 4), (1, 8)), jnp.float32)
    m_bias = centred(splits[12], (LAYERS, WIDE), (0.003 * PARAMS ** -0.5), 1.9073486328125e-06, ((0, 4), (1, 8)), jnp.float32)
    m_small = centred(splits[13], (D, SMALLC), (0.009 * PARAMS ** -0.5), 5.7220458984375e-06, ((0, 8), (1, 4)), jnp.float32)
    m_sbias = centred(splits[14], (SB,), (0.036 * PARAMS ** -0.5), 2.288818359375e-05, ((0, 4),), jnp.float32)
    v_in = jnp.clip(jnp.exp(math.log(7.913985659641068e-17) - 2.7725887 * jax.random.uniform(splits[15], (LAYERS, D, WIDE), jnp.float32) ** level_of(splits[15], (LAYERS, D, WIDE), ((0, 4), (1, 8)), -0.2, 0.2)), 4.9462410372756676e-18, 7.913985659641068e-17)
    v_down = jnp.clip(jnp.exp(math.log(7.913985659641068e-17) - 2.7725887 * jax.random.uniform(splits[16], (LAYERS, FF, D), jnp.float32) ** level_of(splits[16], (LAYERS, FF, D), ((0, 4), (1, 8)), -0.2, 0.2)), 4.9462410372756676e-18, 7.913985659641068e-17)
    v_bias = jnp.clip(jnp.exp(math.log(1.2662377055425709e-15) - 2.7725887 * jax.random.uniform(splits[17], (LAYERS, WIDE), jnp.float32) ** level_of(splits[17], (LAYERS, WIDE), ((0, 4), (1, 8)), -0.2, 0.2)), 7.913985659641068e-17, 1.2662377055425709e-15)
    v_small = draw_v_small(jax.random.fold_in(splits[20], 71), 0)
    v_sbias = jnp.clip(jnp.exp(math.log(1.2662377055425709e-15) - 2.7725887 * jax.random.uniform(splits[19], (SB,), jnp.float32) ** level_of(splits[19], (SB,), ((0, 4),), -0.2, 0.2)), 7.913985659641068e-17, 1.2662377055425709e-15)
    return dict(latents=latents, noise=noise, timesteps=timesteps, labels=labels, patch_mask=patch_mask, w_in=w_in, w_down=w_down, b_blk=b_blk, small_mats=small_mats, small_bias=small_bias, m_in=m_in, m_down=m_down, m_bias=m_bias, m_small=m_small, m_sbias=m_sbias, v_in=v_in, v_down=v_down, v_bias=v_bias, v_small=v_small, v_sbias=v_sbias)


@jax.custom_vjp
def low(v):
    return lax.optimization_barrier(v.astype(jnp.bfloat16)).astype(jnp.float32)

@jax.custom_vjp
def low_back(v):
    return v

def low_keep(v):
    return (low(v), None)

def low_pass(kept, grad):
    return (grad,)

def back_keep(v):
    return (v, None)

def back_low(kept, grad):
    return (low(grad),)
low.defvjp(low_keep, low_pass)
low_back.defvjp(back_keep, back_low)
HIGH = lax.Precision.HIGHEST
EPS_NORM = 1e-06
CLIP = 0.001
RATE = 0.005
BETA_ONE = 0.9
BETA_TWO = 0.999
ADAM_EPS = 1e-08
DECAY = 0.01
STEP_POWER = 10.0

def product(left_side, right_side):
    return jnp.dot(left_side, right_side, precision=HIGH, preferred_element_type=jnp.float32)

def normalize(values):
    center = values - lax.optimization_barrier(jnp.mean(values, axis=-1, keepdims=True))
    return center * lax.rsqrt(lax.optimization_barrier(jnp.mean(center * center, axis=-1, keepdims=True)) + EPS_NORM)

def modulate(values, shifting, scaling):
    return normalize(values) * (1.0 + scaling[:, None, :]) + shifting[:, None, :]

def gelu_tanh(values):
    return 0.5 * values * (1.0 + jnp.tanh(0.7978845608028654 * (values + 0.044715 * values * values * values)))

def positions():
    quarter = D // 4
    omega = jnp.exp(-math.log(10000.0) * jnp.arange(quarter, dtype=jnp.float32) / quarter)
    spot = jnp.arange(PATCHES, dtype=jnp.int32)
    row_angle = (spot // GRID).astype(jnp.float32)[:, None] * omega[None, :]
    col_angle = (spot % GRID).astype(jnp.float32)[:, None] * omega[None, :]
    return jnp.concatenate([jnp.sin(row_angle), jnp.cos(row_angle), jnp.sin(col_angle), jnp.cos(col_angle)], axis=1)

def time_features(time_steps):
    half = FREQ // 2
    freqs = jnp.exp(-math.log(10000.0) * jnp.arange(half, dtype=jnp.float32) / half)
    angles = time_steps.astype(jnp.float32)[:, None] * freqs[None, :]
    return jnp.concatenate([jnp.cos(angles), jnp.sin(angles)], axis=1)

def alpha_bar(time_steps):
    return jnp.cos((time_steps.astype(jnp.float32) / 1000.0 + 0.008) / 1.008 * (math.pi / 2)) ** 2

def block(residual, condition, w_full, w_second, bias_full):
    groups = residual.shape[0]
    ada_at = 4 * D + FF
    act_cond = low(jax.nn.silu(condition))
    modulation = jnp.split(low_back(product(act_cond, w_full[:, ada_at:]) + bias_full[ada_at:]), 6, axis=1)
    mixed_one = low(modulate(residual, modulation[0], modulation[1]))
    projected = product(mixed_one, w_full[:, :3 * D])
    head_shape = (groups, PATCHES, HEADS, HEAD_DIM)
    queries = low(low_back(projected[..., :D] + bias_full[:D])).reshape(head_shape)
    key_heads = low(low_back(projected[..., D:2 * D])).reshape(head_shape)
    value_heads = low(low_back(projected[..., 2 * D:] + bias_full[D:2 * D])).reshape(head_shape)
    scores = low_back(jnp.einsum('gqhe,gkhe->ghqk', queries, key_heads, precision=HIGH) * HEAD_DIM ** (-0.5))
    attention = low(jax.nn.softmax(scores, axis=-1))
    attended = jnp.einsum('ghqk,gkhe->gqhe', attention, value_heads, precision=HIGH).reshape(groups, PATCHES, D)
    attended = low(low_back(attended))
    branch = low_back(product(attended, w_full[:, 3 * D:4 * D]) + bias_full[2 * D:3 * D])
    middle = residual + modulation[2][:, None, :] * branch
    mixed_two = low(modulate(middle, modulation[3], modulation[4]))
    pre_act = low_back(product(mixed_two, w_full[:, 4 * D:ada_at]) + bias_full[3 * D:3 * D + FF])
    second = low_back(product(low(gelu_tanh(pre_act)), w_second) + bias_full[3 * D + FF:ada_at])
    return middle + modulation[5][:, None, :] * second

def group_loss(params_low, latents, noise, timesteps, labels, patch_mask):
    w_in, w_down, b_blk, small_mats, small_bias = params_low
    o_label = PATCH_IN + FREQ
    o_second = o_label + CLASSES
    o_film = o_second + D
    o_out = o_film + 2 * D
    fade = alpha_bar(timesteps)[:, None, None]
    noisy = low(jnp.sqrt(fade) * latents + jnp.sqrt(1.0 - fade) * noise)
    residual = low_back(jnp.einsum('gpi,di->gpd', noisy, small_mats[:, :PATCH_IN], precision=HIGH) + small_bias[:D]) + positions()[None]
    time_low = low(time_features(timesteps))
    time_hidden = jnp.einsum('gf,df->gd', time_low, small_mats[:, PATCH_IN:o_label], precision=HIGH) + small_bias[D:2 * D]
    time_act = low(jax.nn.silu(low_back(time_hidden)))
    label_rows = jnp.take(small_mats[:, o_label:o_second], labels, axis=1).T
    condition = low_back(product(time_act, small_mats[:, o_second:o_film]) + small_bias[2 * D:3 * D] + label_rows)
    for layer in range(LAYERS):
        if layer > 0:
            residual = low(low_back(residual))
            condition = low(low_back(condition))
        residual = block(residual, condition, w_in[layer], w_down[layer], b_blk[layer])
    act_final = low(jax.nn.silu(condition))
    film_out = low_back(product(act_final, small_mats[:, o_film:o_out]) + small_bias[3 * D:5 * D])
    mixed = low(modulate(residual, film_out[:, :D], film_out[:, D:]))
    output = low_back(jnp.einsum('gpd,dj->gpj', mixed, small_mats[:, o_out:], precision=HIGH) + small_bias[5 * D:])
    mismatch = output - noise
    return jnp.sum(patch_mask.astype(jnp.float32)[..., None] * mismatch * mismatch)

def adam_update(weight, gradient, first_moment, second_moment, scaling):
    gradient = gradient * scaling
    first_new = BETA_ONE * first_moment + (1.0 - BETA_ONE) * gradient
    second_new = BETA_TWO * second_moment + (1.0 - BETA_TWO) * gradient * gradient
    ratio = first_new / (1.0 - BETA_ONE ** STEP_POWER) / (jnp.sqrt(second_new / (1.0 - BETA_TWO ** STEP_POWER)) + ADAM_EPS)
    return (weight - RATE * (ratio + DECAY * weight), first_new, second_new)

def reference(latents, noise, timesteps, labels, patch_mask, w_in, w_down, b_blk, small_mats, small_bias, m_in, m_down, m_bias, m_small, m_sbias, v_in, v_down, v_bias, v_small, v_sbias):
    count = jnp.sum(patch_mask.astype(jnp.float32)) * PATCH_IN
    groups = IMAGES // IMG_DEV
    batches = (latents.reshape(groups, IMG_DEV, PATCHES, PATCH_IN), noise.reshape(groups, IMG_DEV, PATCHES, PATCH_IN), timesteps.reshape(groups, IMG_DEV), labels.reshape(groups, IMG_DEV), patch_mask.reshape(groups, IMG_DEV, PATCHES))

    def total(params):
        params_low = tuple((low(item) for item in params))

        def group_step(carry, batch):
            return (carry + jax.checkpoint(group_loss)(params_low, *batch), None)
        summed, unused = lax.scan(group_step, jnp.zeros((), jnp.float32), batches)
        return summed / count
    params = (w_in, w_down, b_blk, small_mats, small_bias)
    loss, pull = jax.vjp(total, params)
    grads = pull(jnp.ones((), jnp.float32))[0]
    squares = sum((jnp.sum(item * item) for item in grads))
    grad_norm = jnp.sqrt(squares)
    scaling = jnp.minimum(1.0, CLIP / grad_norm)
    firsts = (m_in, m_down, m_bias, m_small, m_sbias)
    seconds = (v_in, v_down, v_bias, v_small, v_sbias)
    results = [adam_update(params[index], grads[index], firsts[index], seconds[index], scaling) for index in range(5)]
    return (loss, grad_norm, results[0][0], results[0][1], results[0][2], results[1][0], results[1][1], results[1][2], results[2][0], results[2][1], results[2][2], results[3][0], results[3][1], results[3][2], results[4][0], results[4][1], results[4][2])
```

```python
import functools
import math

import jax
import jax.numpy as jnp
from jax import lax
from jax.experimental import pallas as pl
from jax.experimental.pallas import tpu as pltpu
from jax.sharding import PartitionSpec as P

D = 1152
HEADS = 16
HEAD_DIM = 72
FF = 4608
CLASSES = 1000
FREQ = 256
PATCH_IN = 16
GRID = 16


EPS_NORM = 1e-06
CLIP = 0.001
RATE = 0.005
BETA_ONE = 0.9
BETA_TWO = 0.999
ADAM_EPS = 1e-08
DECAY = 0.01
STEP_POWER = 10.0


def passed_along(value, axis, steps):
    count = lax.axis_size(axis)
    first, last = (max(0, -steps), min(count, count - steps))
    return lax.ppermute(value, axis, [(source, source + steps) for source in range(first, last)])


def matmul(left_side, right_side):
    return jnp.dot(left_side, right_side, preferred_element_type=jnp.float32)


def matmul_tn(left_side, right_side):
    return lax.dot_general(
        left_side, right_side, (((0,), (0,)), ((), ())), preferred_element_type=jnp.float32
    )


def matmul_nt(left_side, right_side):
    return lax.dot_general(
        left_side, right_side, (((1,), (1,)), ((), ())), preferred_element_type=jnp.float32
    )


def column_sum(values):
    return jnp.sum(values.astype(jnp.float32), axis=0)


def normalize(values):
    center = values - jnp.mean(values, axis=-1, keepdims=True)
    invstd = lax.rsqrt(jnp.mean(center * center, axis=-1, keepdims=True) + EPS_NORM)
    return (center * invstd, invstd)


def norm_back(grad_normed, normed, invstd):
    return invstd * (
        grad_normed
        - jnp.mean(grad_normed, axis=-1, keepdims=True)
        - normed * jnp.mean(grad_normed * normed, axis=-1, keepdims=True)
    )


def gelu_tanh(values):
    return (
        0.5
        * values
        * (1.0 + jnp.tanh(0.7978845608028654 * (values + 0.044715 * values * values * values)))
    )


def gelu_grad(values):
    inner = jnp.tanh(0.7978845608028654 * (values + 0.044715 * values * values * values))
    return 0.5 * (1.0 + inner) + 0.5 * values * (1.0 - inner * inner) * 0.7978845608028654 * (
        1.0 + 0.134145 * values * values
    )


def silu_grad(values):
    sigma = jax.nn.sigmoid(values)
    return sigma * (1.0 + values * (1.0 - sigma))


def positions(patches):
    quarter = D // 4
    omega = jnp.exp(-math.log(10000.0) * jnp.arange(quarter, dtype=jnp.float32) / quarter)
    spot = jnp.arange(patches, dtype=jnp.int32)
    row_angle = (spot // GRID).astype(jnp.float32)[:, None] * omega[None, :]
    col_angle = (spot % GRID).astype(jnp.float32)[:, None] * omega[None, :]
    return jnp.concatenate(
        [jnp.sin(row_angle), jnp.cos(row_angle), jnp.sin(col_angle), jnp.cos(col_angle)], axis=1
    )


def time_features(time_steps):
    half = FREQ // 2
    freqs = jnp.exp(-math.log(10000.0) * jnp.arange(half, dtype=jnp.float32) / half)
    angles = time_steps.astype(jnp.float32)[:, None] * freqs[None, :]
    return jnp.concatenate([jnp.cos(angles), jnp.sin(angles)], axis=1)


def alpha_bar(time_steps):
    return jnp.cos((time_steps.astype(jnp.float32) / 1000.0 + 0.008) / 1.008 * (math.pi / 2)) ** 2


def label_table(label_part):
    return (label_part[:, None] == jnp.arange(CLASSES, dtype=jnp.int32)[None, :]).astype(
        jnp.bfloat16
    )


MESH = pl.DeviceIdType.MESH
DIRECT = 8


def rounded(values):
    return lax.reduce_precision(values, 8, 7)


def meet(axis, count, here):
    barrier = pltpu.get_barrier_semaphore()
    for step in range(1, count):
        pl.semaphore_signal(
            barrier, inc=1, device_id={axis: lax.rem(here + step, count)}, device_id_type=MESH
        )
    pl.semaphore_wait(barrier, count - 1)


def share_kernel(axis, count, personal, in_ref, out_ref, send_sem, recv_sem):
    here = lax.axis_index(axis)
    meet(axis, count, here)
    copies = []
    for step in range(1, count):
        target = lax.rem(here + step, count)
        copy = pltpu.make_async_remote_copy(
            src_ref=in_ref.at[target] if personal else in_ref,
            dst_ref=out_ref.at[here],
            send_sem=send_sem.at[step - 1],
            recv_sem=recv_sem.at[step - 1],
            device_id={axis: target},
            device_id_type=MESH,
        )
        copy.start()
        copies.append(copy)
    out_ref[here] = in_ref[here] if personal else in_ref[...]
    for copy in copies:
        copy.wait()


def share(value, axis, personal, ident):
    count = lax.axis_size(axis)
    shape = value.shape if personal else (count,) + value.shape
    return pl.pallas_call(
        functools.partial(share_kernel, axis, count, personal),
        out_shape=jax.ShapeDtypeStruct(shape, value.dtype),
        in_specs=[pl.BlockSpec(memory_space=pltpu.VMEM)],
        out_specs=pl.BlockSpec(memory_space=pltpu.VMEM),
        scratch_shapes=[
            pltpu.SemaphoreType.DMA((count - 1,)),
            pltpu.SemaphoreType.DMA((count - 1,)),
        ],
        compiler_params=pltpu.CompilerParams(collective_id=ident, has_side_effects=True),
        name="share",
    )(value)


def spread(value, axis, ident):
    if lax.axis_size(axis) > DIRECT:
        return lax.all_gather(value, axis)
    return share(value, axis, False, ident)


def exchange(value, axis, ident):
    if lax.axis_size(axis) > DIRECT:
        return lax.all_to_all(value, axis, 0, 0)
    return share(value, axis, True, ident)


def row_sums(left_side, right_side):
    product = matmul_tn(left_side, right_side)
    count = lax.axis_size("dp")
    if count != DIRECT:
        return lax.psum_scatter(product, "dp", scatter_dimension=0, tiled=True)
    here = lax.axis_index("dp")
    core, chip, chips = (here % 2, here // 2, count // 2)
    parted = product.reshape(chips, 2, product.shape[0] // count, product.shape[1])
    other = lax.dynamic_index_in_dim(parted, 1 - core, 1, keepdims=False)
    same = lax.dynamic_index_in_dim(parted, core, 1, keepdims=False)
    both = same + lax.ppermute(other, "dp", [(i, i ^ 1) for i in range(count)])
    total = lax.dynamic_index_in_dim(both, chip, 0, keepdims=False)
    for step in range(1, chips):
        block = lax.dynamic_index_in_dim(both, (chip + step) % chips, 0, keepdims=False)
        arrived = lax.ppermute(
            block.astype(jnp.bfloat16),
            "dp",
            [(i, (i + 2 * step) % count) for i in range(count)],
        )
        total = total + arrived.astype(jnp.float32)
    return total


def attend_kernel(qkv_ref, out_ref):
    for head in range(HEADS):
        at = head * HEAD_DIM
        query = qkv_ref[:, at : at + HEAD_DIM]
        key = qkv_ref[:, D + at : D + at + HEAD_DIM]
        value = qkv_ref[:, 2 * D + at : 2 * D + at + HEAD_DIM]
        scores = matmul_nt(query, key) * HEAD_DIM ** (-0.5)
        attention = jnp.exp(scores - jnp.max(scores, axis=-1, keepdims=True))
        attention = attention * (1.0 / jnp.sum(attention, axis=-1, keepdims=True))
        out_ref[:, at : at + HEAD_DIM] = matmul(attention.astype(jnp.bfloat16), value).astype(
            jnp.bfloat16
        )


def attend(qkv_low):
    patches = qkv_low.shape[0]
    return pl.pallas_call(
        attend_kernel,
        out_shape=jax.ShapeDtypeStruct((patches, D), jnp.bfloat16),
        cost_estimate=pl.CostEstimate(
            flops=4 * patches * patches * D,
            bytes_accessed=8 * patches * D,
            transcendentals=HEADS * patches * patches,
        ),
        name="attend",
    )(qkv_low)


def attend_back_kernel(qkv_ref, grad_ref, out_ref):
    scaling = HEAD_DIM ** (-0.5)
    for head in range(HEADS):
        at = head * HEAD_DIM
        query = qkv_ref[:, at : at + HEAD_DIM]
        key = qkv_ref[:, D + at : D + at + HEAD_DIM]
        value = qkv_ref[:, 2 * D + at : 2 * D + at + HEAD_DIM]
        grad = grad_ref[:, at : at + HEAD_DIM]
        scores = matmul_nt(query, key) * scaling
        attention = jnp.exp(scores - jnp.max(scores, axis=-1, keepdims=True))
        attention = attention * (1.0 / jnp.sum(attention, axis=-1, keepdims=True))
        d_probs = matmul_nt(grad, value)
        d_scores = (
            attention * (d_probs - jnp.sum(attention * d_probs, axis=-1, keepdims=True))
        ).astype(jnp.bfloat16)
        attention_low = attention.astype(jnp.bfloat16)
        out_ref[:, at : at + HEAD_DIM] = (matmul(d_scores, key) * scaling).astype(jnp.bfloat16)
        out_ref[:, D + at : D + at + HEAD_DIM] = (matmul_tn(d_scores, query) * scaling).astype(
            jnp.bfloat16
        )
        out_ref[:, 2 * D + at : 2 * D + at + HEAD_DIM] = matmul_tn(attention_low, grad).astype(
            jnp.bfloat16
        )


def attend_back(qkv_low, grad):
    patches = qkv_low.shape[0]
    return pl.pallas_call(
        attend_back_kernel,
        out_shape=jax.ShapeDtypeStruct((patches, 3 * D), jnp.bfloat16),
        cost_estimate=pl.CostEstimate(
            flops=10 * patches * patches * D,
            bytes_accessed=14 * patches * D,
            transcendentals=HEADS * patches * patches,
        ),
        name="attend_back",
    )(qkv_low, grad)


def image_forward(residual, modulation, weights):
    w_qkv, w_proj, w_hidden, w_second, bias = weights
    normed_one, unused = normalize(residual)
    mixed_one = (normed_one * (1.0 + modulation[1]) + modulation[0]).astype(jnp.bfloat16)
    qkv_bias = jnp.concatenate([bias[:D], jnp.zeros((D,), jnp.float32), bias[D : 2 * D]])
    qkv_low = (matmul(mixed_one, w_qkv) + qkv_bias).astype(jnp.bfloat16)
    att_low = attend(qkv_low)
    branch = matmul(att_low, w_proj) + bias[2 * D : 3 * D]
    middle = residual + modulation[2] * branch
    normed_two, unused = normalize(middle)
    mixed_two = (normed_two * (1.0 + modulation[4]) + modulation[3]).astype(jnp.bfloat16)
    pre_act = matmul(mixed_two, w_hidden) + bias[3 * D : 3 * D + FF]
    act_low = gelu_tanh(pre_act).astype(jnp.bfloat16)
    second = matmul(act_low, w_second) + bias[3 * D + FF : 4 * D + FF]
    output = middle + modulation[5] * second
    return (
        output,
        (
            residual,
            mixed_one,
            qkv_low,
            att_low,
            branch,
            middle,
            mixed_two,
            pre_act,
            act_low,
            second,
        ),
    )


def image_backward(grad_out, kept, modulation, weights):
    w_qkv, w_proj, w_hidden, w_second, unused = weights
    residual, qkv_low, branch, middle, pre_act, second = kept
    d_second = (grad_out * modulation[5]).astype(jnp.bfloat16)
    d_gate_two = jnp.sum(grad_out * second, axis=0)
    d_pre = (matmul_nt(d_second, w_second) * gelu_grad(pre_act)).astype(jnp.bfloat16)
    d_mixed_two = matmul_nt(d_pre, w_hidden)
    normed_two, invstd_two = normalize(middle)
    d_shift_two = jnp.sum(d_mixed_two, axis=0)
    d_scale_two = jnp.sum(d_mixed_two * normed_two, axis=0)
    d_middle = grad_out + norm_back(d_mixed_two * (1.0 + modulation[4]), normed_two, invstd_two)
    d_gate_one = jnp.sum(d_middle * branch, axis=0)
    d_branch = (d_middle * modulation[2]).astype(jnp.bfloat16)
    d_att = matmul_nt(d_branch, w_proj).astype(jnp.bfloat16)
    d_qkv = attend_back(qkv_low, d_att)
    d_mixed_one = matmul_nt(d_qkv, w_qkv)
    normed_one, invstd_one = normalize(residual)
    d_shift_one = jnp.sum(d_mixed_one, axis=0)
    d_scale_one = jnp.sum(d_mixed_one * normed_one, axis=0)
    d_residual = d_middle + norm_back(
        d_mixed_one * (1.0 + modulation[1]), normed_one, invstd_one
    )
    d_ada = jnp.concatenate(
        [d_shift_one, d_scale_one, d_gate_one, d_shift_two, d_scale_two, d_gate_two]
    ).astype(jnp.bfloat16)
    return (d_residual, (d_second, d_pre, d_branch, d_qkv, d_ada))


def head_step(residual, film, noise_part, mask_part, inv_count, w_out, b_out):
    shifting, scaling = (film[:, :D], film[:, D:])
    normed, invstd = normalize(residual)
    mixed = (normed * (1.0 + scaling[:, None]) + shifting[:, None]).astype(jnp.bfloat16)
    output = (
        jnp.einsum("bpd,dj->bpj", mixed, w_out, preferred_element_type=jnp.float32) + b_out
    )
    mismatch = output - noise_part
    mask_float = mask_part.astype(jnp.float32)[:, :, None]
    squared = jnp.sum(mask_float * mismatch * mismatch)
    d_output = (2.0 * inv_count * mask_float * mismatch).astype(jnp.bfloat16)
    g_output = jnp.einsum("bpd,bpj->dj", mixed, d_output, preferred_element_type=jnp.float32)
    d_mixed = jnp.einsum("bpj,dj->bpd", d_output, w_out, preferred_element_type=jnp.float32)
    d_film = jnp.concatenate(
        [jnp.sum(d_mixed, axis=1), jnp.sum(d_mixed * normed, axis=1)], axis=1
    ).astype(jnp.bfloat16)
    d_residual = norm_back(d_mixed * (1.0 + scaling[:, None]), normed, invstd)
    g_bias = jnp.sum(d_output.astype(jnp.float32), axis=(0, 1))
    return (squared, d_residual, d_film, g_output, g_bias)


def adam_update(weight, gradient, first_moment, second_moment, scaling):
    gradient = gradient * scaling
    first_new = BETA_ONE * first_moment + (1.0 - BETA_ONE) * gradient
    second_new = BETA_TWO * second_moment + (1.0 - BETA_TWO) * gradient * gradient
    ratio = (
        first_new
        / (1.0 - BETA_ONE**STEP_POWER)
        / (jnp.sqrt(second_new / (1.0 - BETA_TWO**STEP_POWER)) + ADAM_EPS)
    )
    return (weight - RATE * (ratio + DECAY * weight), first_new, second_new)


def body(
    latents,
    noise,
    timesteps,
    labels,
    patch_mask,
    w_in,
    w_down,
    b_blk,
    small_mats,
    small_bias,
    m_in,
    m_down,
    m_bias,
    m_small,
    m_sbias,
    v_in,
    v_down,
    v_bias,
    v_small,
    v_sbias,
):
    section_index = lax.axis_index("section")
    dp_index = lax.axis_index("dp")
    sections = lax.axis_size("section")
    is_first = section_index == 0
    is_last = section_index == sections - 1
    low = jnp.bfloat16
    images, patches = patch_mask.shape
    rows = w_in.shape[1]
    row_at = dp_index * rows
    ada_at = 4 * D + FF
    o_label = PATCH_IN + FREQ
    o_second = o_label + CLASSES
    o_film = o_second + D
    o_out = o_film + 2 * D

    def gathered(value, axis="dp", dim=0):
        return lax.all_gather(value, axis, axis=dim, tiled=True)

    in_low = w_in[0].astype(low)
    w_ada = in_low[:, ada_at:]
    w_qkv = gathered(in_low[:, : 3 * D])
    w_proj = gathered(in_low[:, 3 * D : 4 * D])
    w_hidden = gathered(in_low[:, 4 * D : ada_at])
    w_second = gathered(w_down[0].astype(low))

    small_low = small_mats.astype(low)
    edge_own = jnp.where(is_first, small_mats[:, :PATCH_IN], small_mats[:, -PATCH_IN:])
    bias_width = b_blk.shape[1]
    pieces = [
        b_blk[0],
        edge_own.reshape(-1),
        timesteps.astype(jnp.float32),
        labels.astype(jnp.float32),
        jnp.sum(patch_mask).astype(jnp.float32)[None],
    ]
    block = jnp.concatenate(pieces)[None]
    blocks = spread(block, "dp", 1)[:, 0]
    ends = [0]
    for piece in pieces:
        ends.append(ends[-1] + piece.shape[0])
    bias_full = rounded(blocks[:, : ends[1]].reshape(-1))
    w_edge = blocks[:, ends[1] : ends[2]].reshape(D, PATCH_IN).astype(low)
    times_all = blocks[:, ends[2] : ends[3]].reshape(-1).astype(jnp.int32)
    labels_all = blocks[:, ends[3] : ends[4]].reshape(-1).astype(jnp.int32)
    valid_total = jnp.sum(blocks[:, ends[4]])
    inv_count = 1.0 / (valid_total * PATCH_IN)
    weights = (w_qkv, w_proj, w_hidden, w_second, bias_full)

    small_width = small_mats.shape[1]
    sbias_width = small_bias.shape[0]
    extra = -(-sbias_width // small_width)
    sbias_rows = jnp.pad(small_bias, (0, extra * small_width - sbias_width)).astype(low)
    small_block = jnp.concatenate([small_low, sbias_rows.reshape(extra, small_width)], axis=0)
    small_blocks = spread(small_block, "section", 2)
    small_rows = jnp.concatenate([small_blocks[i, :rows] for i in range(sections)], axis=1)
    small_used = (
        small_blocks[:, rows:].reshape(sections, -1)[:, :sbias_width].reshape(-1)
    ).astype(jnp.float32)

    shards = lax.axis_size("dp")
    time_low = time_features(times_all).astype(low)
    one_hot = label_table(labels_all)
    time_hidden = matmul_nt(time_low, small_rows[:, PATCH_IN:o_label]) + lax.dynamic_slice_in_dim(
        small_used, D + row_at, rows, 0
    )
    time_act = jax.nn.silu(time_hidden).astype(low)
    cond_part = matmul(time_act, small_rows[:, o_second:o_film])
    label_part = matmul_nt(one_hot, small_rows[:, o_label:o_second])
    cond_part = jnp.concatenate([cond_part, label_part], axis=1).reshape(shards, images, D + rows)
    cond_got = exchange(cond_part, "dp", 3)
    cond_own = (
        jnp.sum(cond_got[:, :, :D], axis=0)
        + small_used[2 * D : 3 * D]
        + jnp.swapaxes(cond_got[:, :, D:], 0, 1).reshape(images, D)
    )
    cond_cols = exchange(jnp.swapaxes(cond_own.reshape(images, shards, rows), 0, 1), "dp", 4)
    cond_first = cond_cols.reshape(shards * images, rows)
    cond_later = rounded(cond_first)
    cond_here = jnp.where(is_first, cond_first, cond_later)
    act_here = jax.nn.silu(cond_here).astype(low)
    act_later = jax.nn.silu(cond_later).astype(low)
    ada_part = jnp.concatenate(
        [matmul(act_here, w_ada), matmul(act_later, small_rows[:, o_film:o_out])], axis=1
    )
    ada_got = exchange(ada_part.reshape(shards, images * 8 * D // 128, 128), "dp", 5)
    ada_own = jnp.sum(ada_got, axis=0).reshape(images, 8 * D)
    film = ada_own[:, 6 * D :] + small_used[3 * D : 5 * D]
    ada = (ada_own[:, : 6 * D] + bias_full[ada_at:]).reshape(images, 6, D)

    fade = alpha_bar(timesteps)[:, None, None]
    noisy_low = (jnp.sqrt(fade) * latents + jnp.sqrt(1.0 - fade) * noise).astype(low)
    tokens = jnp.einsum(
        "bpi,di->bpd", noisy_low, w_edge, preferred_element_type=jnp.float32
    )
    tokens = tokens + small_used[:D] + positions(patches)[None]

    def slot_of(raw):
        return (jnp.where((raw >= 0) & (raw < images), raw, images), jnp.clip(raw, 0, images - 1))

    def put(whole, piece, slot):
        return lax.dynamic_update_index_in_dim(whole, piece, slot, 0)

    def buffers(widths):
        return [jnp.zeros((images + 1, patches) + (width,), kind) for width, kind in widths]

    ticks = images + sections - 1
    wide = jnp.float32
    kept_all = buffers(
        [
            (D, wide),
            (D, low),
            (3 * D, low),
            (D, low),
            (D, wide),
            (D, wide),
            (D, low),
            (FF, wide),
            (FF, low),
            (D, wide),
            (D, wide),
        ]
    )
    arrived = jnp.zeros((patches, D), low)
    for tick in range(ticks):
        store_at, read_at = slot_of(tick - section_index)
        residual = jnp.where(is_first, tokens[min(tick, images - 1)], arrived.astype(wide))
        modulation = lax.dynamic_index_in_dim(ada, read_at, 0, keepdims=False)
        output, kept = image_forward(residual, modulation, weights)
        if tick < ticks - 1:
            arrived = passed_along(output.astype(low), "section", 1)
        kept_all = [put(whole, piece, store_at) for whole, piece in zip(kept_all, kept + (output,))]

    (
        residual_all,
        mixed_one_all,
        qkv_all,
        att_all,
        branch_all,
        middle_all,
        mixed_two_all,
        pre_all,
        act_all,
        second_all,
        output_all,
    ) = kept_all

    squared, head_grad, d_film, g_output, g_out_bias = head_step(
        output_all[:images],
        film,
        noise,
        patch_mask,
        inv_count,
        w_edge,
        small_used[5 * D :],
    )
    loss_part = jnp.where(is_last, squared * inv_count, 0.0)
    film_all = spread(d_film, "dp", 6).reshape(shards * images, 2 * D)
    film_all = spread(film_all, "section", 7)[sections - 1]

    grads_all = buffers([(D, low), (FF, low), (D, low), (3 * D, low)])
    ada_grads = jnp.zeros((images + 1, 6 * D), low)
    token_grads = jnp.zeros((images + 1, patches, D), low)
    arrived = jnp.zeros((patches, D), low)
    for tick in range(ticks):
        store_at, read_at = slot_of(tick - (sections - 1 - section_index))
        grad_out = jnp.where(
            is_last, head_grad[min(tick, images - 1)], arrived.astype(jnp.float32)
        )
        kept = [
            lax.dynamic_index_in_dim(whole, read_at, 0, keepdims=False)
            for whole in (residual_all, qkv_all, branch_all, middle_all, pre_all, second_all)
        ]
        modulation = lax.dynamic_index_in_dim(ada, read_at, 0, keepdims=False)
        d_residual, pieces = image_backward(grad_out, kept, modulation, weights)
        d_low = d_residual.astype(low)
        if tick < ticks - 1:
            arrived = passed_along(d_low, "section", -1)
        grads_all = [put(whole, piece, store_at) for whole, piece in zip(grads_all, pieces[:4])]
        ada_grads = put(ada_grads, pieces[4], store_at)
        token_grads = put(token_grads, d_low, store_at)

    def flat(whole):
        return whole[:images].reshape(images * patches, whole.shape[2])

    d_second, d_pre, d_branch, d_qkv = [flat(whole) for whole in grads_all]
    d_tokens = flat(token_grads)
    d_ada = ada_grads[:images]

    shard_proj = row_sums(flat(att_all), d_branch)
    shard_down = row_sums(flat(act_all), d_second)
    shard_hidden = row_sums(flat(mixed_two_all), d_pre)
    shard_qkv = row_sums(flat(mixed_one_all), d_qkv)
    d_ada_all = spread(d_ada, "dp", 8).reshape(shards * images, 6 * D)
    shard_ada = matmul_tn(act_here, d_ada_all)
    shard_in = jnp.concatenate([shard_qkv, shard_proj, shard_hidden, shard_ada], axis=1)

    cond_piece = matmul_nt(d_ada_all, w_ada) * silu_grad(cond_here)
    cond_pieces = spread(cond_piece, "section", 9)
    d_cond = matmul_nt(film_all, small_rows[:, o_film:o_out]) * silu_grad(cond_later)
    for layer in reversed(range(sections)):
        d_cond = rounded(d_cond + cond_pieces[layer])
    d_cond_rows = d_cond.astype(low)
    d_cond_all = jnp.swapaxes(spread(d_cond_rows, "dp", 10), 0, 1).reshape(shards * images, D)
    d_time = (
        matmul_nt(d_cond_all, small_rows[:, o_second:o_film]) * silu_grad(time_hidden)
    ).astype(low)
    g_edge = jnp.where(
        is_first,
        matmul_tn(d_tokens, noisy_low.reshape(images * patches, PATCH_IN)),
        g_output,
    )
    qkv_sums = column_sum(d_qkv)
    bias_sums = jnp.concatenate(
        [
            qkv_sums[:D],
            qkv_sums[2 * D :],
            column_sum(d_branch),
            column_sum(d_pre),
            column_sum(d_second),
            column_sum(d_ada),
        ]
    )
    sums = jnp.concatenate(
        [
            bias_sums.reshape(shards, -1),
            g_edge.reshape(shards, -1),
            jnp.broadcast_to(column_sum(d_tokens), (shards, D)),
            jnp.broadcast_to(g_out_bias, (shards, PATCH_IN)),
            jnp.broadcast_to(column_sum(d_time), (shards, rows)),
        ],
        axis=1,
    )
    sums = exchange(sums[:, None], "dp", 11)[:, 0]
    edge_end = bias_width + rows * PATCH_IN
    shard_bias = jnp.sum(sums[:, :bias_width], axis=0)
    edge_rows = jnp.sum(sums[:, bias_width:edge_end], axis=0).reshape(rows, PATCH_IN)
    token_sums = jnp.sum(sums[:, edge_end : edge_end + D], axis=0)
    out_sums = jnp.sum(sums[:, edge_end + D : edge_end + D + PATCH_IN], axis=0)
    time_sums = sums[:, edge_end + D + PATCH_IN :].reshape(-1)
    small_grad = jnp.concatenate(
        [
            edge_rows,
            matmul_tn(d_time, time_low),
            matmul_tn(d_cond_rows, one_hot),
            matmul_tn(time_act, d_cond_all),
            matmul_tn(act_later, film_all),
            edge_rows,
        ],
        axis=1,
    )
    small_shard = lax.dynamic_slice_in_dim(small_grad, section_index * small_width, small_width, 1)
    sbias_grad = jnp.concatenate(
        [token_sums, time_sums, column_sum(d_cond_all), column_sum(film_all), out_sums]
    )
    sbias_shard = lax.dynamic_slice_in_dim(
        sbias_grad, section_index * sbias_width, sbias_width, 0
    )

    dp_zero = (dp_index == 0).astype(jnp.float32)
    squares = (
        jnp.sum(shard_in * shard_in)
        + jnp.sum(shard_down * shard_down)
        + jnp.sum(shard_bias * shard_bias)
        + jnp.sum(small_shard * small_shard)
        + dp_zero * jnp.sum(sbias_shard * sbias_shard)
    )
    norm_square, loss = lax.psum((squares, loss_part), ("section", "dp"))
    grad_norm = jnp.sqrt(norm_square)
    scaling = jnp.minimum(1.0, CLIP / grad_norm)
    new_in, first_in, second_in = adam_update(w_in, shard_in[None], m_in, v_in, scaling)
    new_down, first_down, second_down = adam_update(
        w_down, shard_down[None], m_down, v_down, scaling
    )
    new_bias, first_bias, second_bias = adam_update(
        b_blk, shard_bias[None], m_bias, v_bias, scaling
    )
    new_small, first_small, second_small = adam_update(
        small_mats, small_shard, m_small, v_small, scaling
    )
    new_sbias, first_sbias, second_sbias = adam_update(
        small_bias, sbias_shard, m_sbias, v_sbias, scaling
    )
    return (
        loss,
        grad_norm,
        new_in,
        first_in,
        second_in,
        new_down,
        first_down,
        second_down,
        new_bias,
        first_bias,
        second_bias,
        new_small,
        first_small,
        second_small,
        new_sbias,
        first_sbias,
        second_sbias,
    )


def solution(mesh):
    in_specs = (
        P("dp", None, None),
        P("dp", None, None),
        P("dp"),
        P("dp"),
        P("dp", None),
        P("section", "dp", None),
        P("section", "dp", None),
        P("section", "dp"),
        P("dp", "section"),
        P("section"),
        P("section", "dp", None),
        P("section", "dp", None),
        P("section", "dp"),
        P("dp", "section"),
        P("section"),
        P("section", "dp", None),
        P("section", "dp", None),
        P("section", "dp"),
        P("dp", "section"),
        P("section"),
    )
    out_specs = (
        P(),
        P(),
        P("section", "dp", None),
        P("section", "dp", None),
        P("section", "dp", None),
        P("section", "dp", None),
        P("section", "dp", None),
        P("section", "dp", None),
        P("section", "dp"),
        P("section", "dp"),
        P("section", "dp"),
        P("dp", "section"),
        P("dp", "section"),
        P("dp", "section"),
        P("section"),
        P("section"),
        P("section"),
    )
    return jax.shard_map(body, mesh=mesh, in_specs=in_specs, out_specs=out_specs, check_vma=False)
```

```python
import functools
import math

import jax
import jax.numpy as jnp
from jax import lax
from jax.experimental import pallas as pl
from jax.experimental.pallas import tpu as pltpu
from jax.sharding import PartitionSpec as P

D = 1152
HEADS = 16
HEAD_DIM = 72
FF = 4608
CLASSES = 1000
FREQ = 256
PATCH_IN = 16
GRID = 16


EPS_NORM = 1e-06
CLIP = 0.001
RATE = 0.005
BETA_ONE = 0.9
BETA_TWO = 0.999
ADAM_EPS = 1e-08
DECAY = 0.01
STEP_POWER = 10.0


def passed_along(value, axis, steps):
    count = lax.axis_size(axis)
    first, last = (max(0, -steps), min(count, count - steps))
    return lax.ppermute(value, axis, [(source, source + steps) for source in range(first, last)])


def matmul(left_side, right_side):
    return jnp.dot(left_side, right_side, preferred_element_type=jnp.float32)


def matmul_tn(left_side, right_side):
    return lax.dot_general(
        left_side, right_side, (((0,), (0,)), ((), ())), preferred_element_type=jnp.float32
    )


def matmul_nt(left_side, right_side):
    return lax.dot_general(
        left_side, right_side, (((1,), (1,)), ((), ())), preferred_element_type=jnp.float32
    )


def column_sum(values):
    return jnp.sum(values.astype(jnp.float32), axis=0)


def normalize(values):
    center = values - jnp.mean(values, axis=-1, keepdims=True)
    invstd = lax.rsqrt(jnp.mean(center * center, axis=-1, keepdims=True) + EPS_NORM)
    return (center * invstd, invstd)


def norm_back(grad_normed, normed, invstd):
    return invstd * (
        grad_normed
        - jnp.mean(grad_normed, axis=-1, keepdims=True)
        - normed * jnp.mean(grad_normed * normed, axis=-1, keepdims=True)
    )


def gelu_tanh(values):
    return (
        0.5
        * values
        * (1.0 + jnp.tanh(0.7978845608028654 * (values + 0.044715 * values * values * values)))
    )


def gelu_grad(values):
    inner = jnp.tanh(0.7978845608028654 * (values + 0.044715 * values * values * values))
    return 0.5 * (1.0 + inner) + 0.5 * values * (1.0 - inner * inner) * 0.7978845608028654 * (
        1.0 + 0.134145 * values * values
    )


def silu_grad(values):
    sigma = jax.nn.sigmoid(values)
    return sigma * (1.0 + values * (1.0 - sigma))


def positions(patches):
    quarter = D // 4
    omega = jnp.exp(-math.log(10000.0) * jnp.arange(quarter, dtype=jnp.float32) / quarter)
    spot = jnp.arange(patches, dtype=jnp.int32)
    row_angle = (spot // GRID).astype(jnp.float32)[:, None] * omega[None, :]
    col_angle = (spot % GRID).astype(jnp.float32)[:, None] * omega[None, :]
    return jnp.concatenate(
        [jnp.sin(row_angle), jnp.cos(row_angle), jnp.sin(col_angle), jnp.cos(col_angle)], axis=1
    )


def time_features(time_steps):
    half = FREQ // 2
    freqs = jnp.exp(-math.log(10000.0) * jnp.arange(half, dtype=jnp.float32) / half)
    angles = time_steps.astype(jnp.float32)[:, None] * freqs[None, :]
    return jnp.concatenate([jnp.cos(angles), jnp.sin(angles)], axis=1)


def alpha_bar(time_steps):
    return jnp.cos((time_steps.astype(jnp.float32) / 1000.0 + 0.008) / 1.008 * (math.pi / 2)) ** 2


def label_table(label_part):
    return (label_part[:, None] == jnp.arange(CLASSES, dtype=jnp.int32)[None, :]).astype(
        jnp.bfloat16
    )


MESH = pl.DeviceIdType.MESH
DIRECT = 8


def rounded(values):
    return lax.reduce_precision(values, 8, 7)


def meet(axis, count, here):
    barrier = pltpu.get_barrier_semaphore()
    for step in range(1, count):
        pl.semaphore_signal(
            barrier, inc=1, device_id={axis: lax.rem(here + step, count)}, device_id_type=MESH
        )
    pl.semaphore_wait(barrier, count - 1)


def share_kernel(axis, count, personal, in_ref, out_ref, send_sem, recv_sem):
    here = lax.axis_index(axis)
    meet(axis, count, here)
    copies = []
    for step in range(1, count):
        target = lax.rem(here + step, count)
        copy = pltpu.make_async_remote_copy(
            src_ref=in_ref.at[target] if personal else in_ref,
            dst_ref=out_ref.at[here],
            send_sem=send_sem.at[step - 1],
            recv_sem=recv_sem.at[step - 1],
            device_id={axis: target},
            device_id_type=MESH,
        )
        copy.start()
        copies.append(copy)
    out_ref[here] = in_ref[here] if personal else in_ref[...]
    for copy in copies:
        copy.wait()


def share(value, axis, personal, ident):
    count = lax.axis_size(axis)
    shape = value.shape if personal else (count,) + value.shape
    return pl.pallas_call(
        functools.partial(share_kernel, axis, count, personal),
        out_shape=jax.ShapeDtypeStruct(shape, value.dtype),
        in_specs=[pl.BlockSpec(memory_space=pltpu.VMEM)],
        out_specs=pl.BlockSpec(memory_space=pltpu.VMEM),
        scratch_shapes=[
            pltpu.SemaphoreType.DMA((count - 1,)),
            pltpu.SemaphoreType.DMA((count - 1,)),
        ],
        compiler_params=pltpu.CompilerParams(collective_id=ident, has_side_effects=True),
        name="share",
    )(value)


def spread(value, axis, ident):
    if lax.axis_size(axis) > DIRECT:
        return lax.all_gather(value, axis)
    return share(value, axis, False, ident)


def exchange(value, axis, ident):
    if lax.axis_size(axis) > DIRECT:
        return lax.all_to_all(value, axis, 0, 0)
    return share(value, axis, True, ident)


def row_sums(pairs):
    count = lax.axis_size("dp")
    if count != DIRECT:
        products = [matmul_tn(left_side, right_side) for left_side, right_side in pairs]
        return (
            [lax.psum_scatter(one, "dp", scatter_dimension=0, tiled=True) for one in products],
            products[-1],
        )
    here = lax.axis_index("dp")
    core, chip, chips = (here % 2, here // 2, count // 2)
    totals, blocks = ([], [])
    for index, pair in enumerate(pairs):
        if index >= 2:
            pair = lax.optimization_barrier((pair, blocks[index - 2]))[0]
        product = matmul_tn(*pair)
        parted = product.reshape(chips, 2, product.shape[0] // count, product.shape[1])
        other = lax.dynamic_index_in_dim(parted, 1 - core, 1, keepdims=False)
        same = lax.dynamic_index_in_dim(parted, core, 1, keepdims=False)
        both = same + lax.ppermute(other, "dp", [(i, i ^ 1) for i in range(count)])
        total = lax.dynamic_index_in_dim(both, chip, 0, keepdims=False)
        blocks.append(
            [
                lax.dynamic_index_in_dim(both, (chip + step) % chips, 0, keepdims=False).astype(
                    jnp.bfloat16
                )
                for step in range(1, chips)
            ]
        )
        for step in range(1, chips):
            arrived = lax.ppermute(
                blocks[-1][step - 1], "dp", [(i, (i + 2 * step) % count) for i in range(count)]
            )
            total = total + arrived.astype(jnp.float32)
        totals.append(total)
    return (totals, blocks[-1])


def attend_kernel(qkv_ref, out_ref):
    for head in range(HEADS):
        at = head * HEAD_DIM
        query = qkv_ref[:, at : at + HEAD_DIM]
        key = qkv_ref[:, D + at : D + at + HEAD_DIM]
        value = qkv_ref[:, 2 * D + at : 2 * D + at + HEAD_DIM]
        scores = matmul_nt(query, key) * HEAD_DIM ** (-0.5)
        attention = jnp.exp(scores - jnp.max(scores, axis=-1, keepdims=True))
        attention = attention * (1.0 / jnp.sum(attention, axis=-1, keepdims=True))
        out_ref[:, at : at + HEAD_DIM] = matmul(attention.astype(jnp.bfloat16), value).astype(
            jnp.bfloat16
        )


def attend_back_kernel(qkv_ref, grad_ref, out_ref):
    scaling = HEAD_DIM ** (-0.5)
    for head in range(HEADS):
        at = head * HEAD_DIM
        query = qkv_ref[:, at : at + HEAD_DIM]
        key = qkv_ref[:, D + at : D + at + HEAD_DIM]
        value = qkv_ref[:, 2 * D + at : 2 * D + at + HEAD_DIM]
        grad = grad_ref[:, at : at + HEAD_DIM]
        scores = matmul_nt(query, key) * scaling
        attention = jnp.exp(scores - jnp.max(scores, axis=-1, keepdims=True))
        attention = attention * (1.0 / jnp.sum(attention, axis=-1, keepdims=True))
        d_probs = matmul_nt(grad, value)
        d_scores = (
            attention * (d_probs - jnp.sum(attention * d_probs, axis=-1, keepdims=True))
        ).astype(jnp.bfloat16)
        attention_low = attention.astype(jnp.bfloat16)
        out_ref[:, at : at + HEAD_DIM] = (matmul(d_scores, key) * scaling).astype(jnp.bfloat16)
        out_ref[:, D + at : D + at + HEAD_DIM] = (matmul_tn(d_scores, query) * scaling).astype(
            jnp.bfloat16
        )
        out_ref[:, 2 * D + at : 2 * D + at + HEAD_DIM] = matmul_tn(attention_low, grad).astype(
            jnp.bfloat16
        )


ROW_BLOCK = 64
KEPT = (
    ("residual", D, jnp.float32),
    ("mixed_one", D, jnp.bfloat16),
    ("qkv", 3 * D, jnp.bfloat16),
    ("att", D, jnp.bfloat16),
    ("branch", D, jnp.float32),
    ("middle", D, jnp.float32),
    ("mixed_two", D, jnp.bfloat16),
    ("pre", FF, jnp.float32),
    ("act", FF, jnp.bfloat16),
    ("second", D, jnp.float32),
    ("output", D, jnp.float32),
)
READ = ("residual", "qkv", "branch", "middle", "pre", "second")
MADE = (
    ("d_second", D, jnp.bfloat16),
    ("d_pre", FF, jnp.bfloat16),
    ("d_branch", D, jnp.bfloat16),
    ("d_qkv", 3 * D, jnp.bfloat16),
    ("d_residual", D, jnp.bfloat16),
)
WEIGHTS = ((D, 3 * D), (D, D), (D, FF), (FF, D))


def by_rows(patches, step):
    @pl.loop(0, patches // ROW_BLOCK)
    def run(index):
        step(pl.ds(pl.multiple_of(index * ROW_BLOCK, ROW_BLOCK), ROW_BLOCK))


def started(source, target, sem):
    copy = pltpu.make_async_copy(source, target, sem)
    copy.start()
    return copy


def forward_kernel(patches, given, meta, arrived, bias, ada, tokens, wq, wp, wh, ws, *refs):
    count = len(KEPT)
    send, outs = (refs[given], refs[given + 1 : given + 1 + count])
    scratch = refs[given + 1 + count :]
    kept = {name: scratch[i] for i, (name, unused, kind) in enumerate(KEPT)}
    wq_v, wp_v, wh_v, ws_v, w_sem, x_sem, out_sem = scratch[count:]
    loads = [started(wq.at[:, pl.ds(i * D, D)], wq_v.at[:, pl.ds(i * D, D)], w_sem.at[i]) for i in range(3)]
    loads.append(started(wp, wp_v, w_sem.at[3]))
    loads += [
        started(wh.at[:, pl.ds(i * D, D)], wh_v.at[:, pl.ds(i * D, D)], w_sem.at[4 + i])
        for i in range(FF // D)
    ]
    third = D // 3
    loads += [
        started(ws.at[:, pl.ds(i * third, third)], ws_v.at[:, pl.ds(i * third, third)], w_sem.at[8 + i])
        for i in range(3)
    ]
    saves = []

    def start_if_valid(copy):
        @pl.when(meta[3] == 1)
        def start():
            copy.start()

    def save(name):
        index = [item[0] for item in KEPT].index(name)
        saves.append(pltpu.make_async_copy(kept[name], outs[index].at[meta[0]], out_sem.at[index]))
        start_if_valid(saves[-1])

    residual = kept["residual"]

    @pl.when(meta[2] == 1)
    def take_tokens():
        started(tokens.at[meta[1]], residual, x_sem).wait()

    @pl.when(meta[2] == 0)
    def take_arrived():
        residual[...] = arrived[...].astype(jnp.float32)

    save("residual")
    modulation = ada[meta[0]]

    def mix_one(at):
        normed, unused = normalize(residual[at])
        kept["mixed_one"][at] = (normed * (1.0 + modulation[1:2]) + modulation[0:1]).astype(
            jnp.bfloat16
        )

    by_rows(patches, mix_one)
    save("mixed_one")
    for part in range(3):
        loads[part].wait()
        cols = slice(part * D, part * D + D)
        kept["qkv"][:, cols] = (
            matmul(kept["mixed_one"][...], wq_v[:, cols]) + bias[:, cols]
        ).astype(jnp.bfloat16)
    save("qkv")
    attend_kernel(kept["qkv"], kept["att"])
    save("att")
    loads[3].wait()
    kept["branch"][...] = matmul(kept["att"][...], wp_v[...]) + bias[:, 3 * D : 4 * D]
    save("branch")

    def mix_two(at):
        middle = residual[at] + modulation[2:3] * kept["branch"][at]
        kept["middle"][at] = middle
        normed, unused = normalize(middle)
        kept["mixed_two"][at] = (normed * (1.0 + modulation[4:5]) + modulation[3:4]).astype(
            jnp.bfloat16
        )

    by_rows(patches, mix_two)
    save("middle")
    save("mixed_two")
    for part in range(FF // D):
        loads[4 + part].wait()
        cols = slice(part * D, part * D + D)
        pre = (
            matmul(kept["mixed_two"][...], wh_v[:, cols])
            + bias[:, 4 * D + part * D : 5 * D + part * D]
        )
        kept["pre"][:, cols] = pre
        kept["act"][:, cols] = gelu_tanh(pre).astype(jnp.bfloat16)
    save("pre")
    save("act")
    for part in range(3):
        loads[8 + part].wait()
        cols = slice(part * third, part * third + third)
        second = (
            matmul(kept["act"][...], ws_v[:, cols])
            + bias[:, 4 * D + FF + part * third : 4 * D + FF + part * third + third]
        )
        kept["second"][:, cols] = second
        output = kept["middle"][:, cols] + modulation[5:6, cols] * second
        kept["output"][:, cols] = output
        send[:, cols] = output.astype(jnp.bfloat16)
    save("second")
    save("output")

    @pl.when(meta[3] == 1)
    def finish():
        for copy in saves:
            copy.wait()


def backward_kernel(patches, given, meta, arrived, ada, head_grad, wq, wp, wh, ws, *refs):
    reads, made = (len(READ), len(MADE))
    sources, refs = (refs[:reads], refs[reads + given :])
    send, outs, ada_out = (refs[0], refs[1 : made + 1], refs[made + 1])
    scratch = refs[made + 2 :]
    kept = {name: scratch[i] for i, name in enumerate(READ)}
    grads = {name: scratch[reads + i] for i, (name, unused, kind) in enumerate(MADE)}
    (
        flow,
        mixed,
        att_grad,
        sums,
        wq_v,
        wp_v,
        wh_v,
        ws_v,
        w_sem,
        in_sem,
        x_sem,
        out_sem,
    ) = scratch[reads + made :]

    def fetch(name):
        index = READ.index(name)
        return started(sources[index].at[meta[0]], kept[name], in_sem.at[index])

    fetched = {"second": fetch("second")}
    loads = [started(ws.at[pl.ds(i * D, D)], ws_v.at[pl.ds(i * D, D)], w_sem.at[i]) for i in range(FF // D)]
    for name in ("pre", "middle", "branch", "qkv", "residual"):
        fetched[name] = fetch(name)
    third = D // 3
    loads += [
        started(wh.at[pl.ds(i * third, third)], wh_v.at[pl.ds(i * third, third)], w_sem.at[4 + i])
        for i in range(3)
    ]
    loads.append(started(wp, wp_v, w_sem.at[7]))
    loads += [
        started(wq.at[pl.ds(i * third, third)], wq_v.at[pl.ds(i * third, third)], w_sem.at[8 + i])
        for i in range(3)
    ]
    saves = []

    def start_if_valid(copy):
        @pl.when(meta[3] == 1)
        def start():
            copy.start()

    def save(name):
        index = [item[0] for item in MADE].index(name)
        saves.append(pltpu.make_async_copy(grads[name], outs[index].at[meta[0]], out_sem.at[index]))
        start_if_valid(saves[-1])

    @pl.when(meta[2] == 1)
    def take_head():
        started(head_grad.at[meta[1]], flow, x_sem).wait()

    @pl.when(meta[2] == 0)
    def take_arrived():
        flow[...] = arrived[...].astype(jnp.float32)

    modulation = ada[meta[0]]
    sums[...] = jnp.zeros_like(sums)

    def add_sum(row, values):
        sums[row : row + 1] += jnp.sum(values, axis=0, keepdims=True)

    fetched["second"].wait()

    def open_second(at):
        grad = flow[at]
        grads["d_second"][at] = (grad * modulation[5:6]).astype(jnp.bfloat16)
        add_sum(5, grad * kept["second"][at])

    by_rows(patches, open_second)
    save("d_second")
    fetched["pre"].wait()
    for part in range(FF // D):
        loads[part].wait()
        cols = slice(part * D, part * D + D)
        grads["d_pre"][:, cols] = (
            matmul_nt(grads["d_second"][...], ws_v[cols]) * gelu_grad(kept["pre"][:, cols])
        ).astype(jnp.bfloat16)
    save("d_pre")
    for part in range(3):
        loads[4 + part].wait()
        cols = slice(part * third, part * third + third)
        mixed[:, cols] = matmul_nt(grads["d_pre"][...], wh_v[cols])
    fetched["middle"].wait()
    fetched["branch"].wait()

    def through_two(at):
        normed, invstd = normalize(kept["middle"][at])
        grad = mixed[at]
        add_sum(3, grad)
        add_sum(4, grad * normed)
        total = flow[at] + norm_back(grad * (1.0 + modulation[4:5]), normed, invstd)
        flow[at] = total
        add_sum(2, total * kept["branch"][at])
        grads["d_branch"][at] = (total * modulation[2:3]).astype(jnp.bfloat16)

    by_rows(patches, through_two)
    save("d_branch")
    loads[7].wait()
    att_grad[...] = matmul_nt(grads["d_branch"][...], wp_v[...]).astype(jnp.bfloat16)
    fetched["qkv"].wait()
    attend_back_kernel(kept["qkv"], att_grad, grads["d_qkv"])
    save("d_qkv")
    for part in range(3):
        loads[8 + part].wait()
        cols = slice(part * third, part * third + third)
        mixed[:, cols] = matmul_nt(grads["d_qkv"][...], wq_v[cols])
    fetched["residual"].wait()

    def through_one(at):
        normed, invstd = normalize(kept["residual"][at])
        grad = mixed[at]
        add_sum(0, grad)
        add_sum(1, grad * normed)
        total = flow[at] + norm_back(grad * (1.0 + modulation[1:2]), normed, invstd)
        low = total.astype(jnp.bfloat16)
        grads["d_residual"][at] = low
        send[at] = low

    by_rows(patches, through_one)
    save("d_residual")
    saves.append(pltpu.make_async_copy(sums, ada_out.at[meta[0]], x_sem))
    start_if_valid(saves[-1])

    @pl.when(meta[3] == 1)
    def finish():
        for copy in saves:
            copy.wait()


def specs(*spaces):
    return [
        pl.BlockSpec(memory_space={"s": pltpu.SMEM, "v": pltpu.VMEM, "h": pl.ANY}[space])
        for space in "".join(spaces)
    ]


def weight_scratch():
    return [pltpu.VMEM(shape, jnp.bfloat16) for shape in WEIGHTS] + [
        pltpu.SemaphoreType.DMA((11,))
    ]


def block_cost(patches, factor):
    area = sum(rows * columns for rows, columns in WEIGHTS)
    return pl.CostEstimate(
        flops=2 * patches * area + factor * patches * patches * D,
        bytes_accessed=2 * area + 64 * patches * D,
        transcendentals=patches * (FF + HEADS * patches),
    )


def image_forward(meta, arrived, bias, ada, tokens, weights, buffers):
    patches, given, count = (arrived.shape[0], len(buffers), len(KEPT))
    images = ada.shape[0]
    outs = pl.pallas_call(
        functools.partial(forward_kernel, patches, given),
        out_shape=[jax.ShapeDtypeStruct((patches, D), jnp.bfloat16)]
        + [jax.ShapeDtypeStruct((images, patches, width), kind) for unused, width, kind in KEPT],
        in_specs=specs("svvv", "h" * (5 + given)),
        out_specs=specs("v", "h" * count),
        scratch_shapes=[pltpu.VMEM((patches, width), kind) for unused, width, kind in KEPT]
        + weight_scratch()
        + [pltpu.SemaphoreType.DMA, pltpu.SemaphoreType.DMA((count,))],
        input_output_aliases={9 + i: 1 + i for i in range(given)},
        compiler_params=pltpu.CompilerParams(vmem_limit_bytes=60 << 20),
        cost_estimate=block_cost(patches, 4),
        name="image_forward",
    )(meta, arrived, bias, ada, tokens, *weights, *buffers)
    return (outs[0], outs[1:])


def image_backward(meta, arrived, ada, head_grad, weights, sources, buffers):
    patches, given, images = (arrived.shape[0], len(buffers), ada.shape[0])
    reads, made = (len(READ), len(MADE))
    kinds = {name: (width, kind) for name, width, kind in KEPT}
    outs = pl.pallas_call(
        functools.partial(backward_kernel, patches, given),
        out_shape=[jax.ShapeDtypeStruct((patches, D), jnp.bfloat16)]
        + [jax.ShapeDtypeStruct((images, patches, width), kind) for unused, width, kind in MADE]
        + [jax.ShapeDtypeStruct((images, 8, D), jnp.float32)],
        in_specs=specs("svv", "h" * (5 + reads + given)),
        out_specs=specs("v", "h" * (made + 1)),
        scratch_shapes=[pltpu.VMEM((patches, kinds[name][0]), kinds[name][1]) for name in READ]
        + [pltpu.VMEM((patches, width), kind) for unused, width, kind in MADE]
        + [
            pltpu.VMEM((patches, D), jnp.float32),
            pltpu.VMEM((patches, D), jnp.float32),
            pltpu.VMEM((patches, D), jnp.bfloat16),
            pltpu.VMEM((8, D), jnp.float32),
        ]
        + weight_scratch()
        + [
            pltpu.SemaphoreType.DMA((reads,)),
            pltpu.SemaphoreType.DMA,
            pltpu.SemaphoreType.DMA((made,)),
        ],
        input_output_aliases={8 + reads + i: 1 + i for i in range(given)},
        compiler_params=pltpu.CompilerParams(vmem_limit_bytes=60 << 20),
        cost_estimate=block_cost(patches, 10),
        name="image_backward",
    )(meta, arrived, ada, head_grad, *weights, *sources, *buffers)
    return (outs[0], outs[1:])


def head_step(residual, film, noise_part, mask_part, inv_count, w_out, b_out):
    shifting, scaling = (film[:, :D], film[:, D:])
    normed, invstd = normalize(residual)
    mixed = (normed * (1.0 + scaling[:, None]) + shifting[:, None]).astype(jnp.bfloat16)
    output = (
        jnp.einsum("bpd,dj->bpj", mixed, w_out, preferred_element_type=jnp.float32) + b_out
    )
    mismatch = output - noise_part
    mask_float = mask_part.astype(jnp.float32)[:, :, None]
    squared = jnp.sum(mask_float * mismatch * mismatch)
    d_output = (2.0 * inv_count * mask_float * mismatch).astype(jnp.bfloat16)
    g_output = jnp.einsum("bpd,bpj->dj", mixed, d_output, preferred_element_type=jnp.float32)
    d_mixed = jnp.einsum("bpj,dj->bpd", d_output, w_out, preferred_element_type=jnp.float32)
    d_film = jnp.concatenate(
        [jnp.sum(d_mixed, axis=1), jnp.sum(d_mixed * normed, axis=1)], axis=1
    ).astype(jnp.bfloat16)
    d_residual = norm_back(d_mixed * (1.0 + scaling[:, None]), normed, invstd)
    g_bias = jnp.sum(d_output.astype(jnp.float32), axis=(0, 1))
    return (squared, d_residual, d_film, g_output, g_bias)


def adam_update(weight, gradient, first_moment, second_moment, scaling):
    gradient = gradient * scaling
    first_new = BETA_ONE * first_moment + (1.0 - BETA_ONE) * gradient
    second_new = BETA_TWO * second_moment + (1.0 - BETA_TWO) * gradient * gradient
    ratio = (
        first_new
        / (1.0 - BETA_ONE**STEP_POWER)
        / (jnp.sqrt(second_new / (1.0 - BETA_TWO**STEP_POWER)) + ADAM_EPS)
    )
    return (weight - RATE * (ratio + DECAY * weight), first_new, second_new)


def body(
    latents,
    noise,
    timesteps,
    labels,
    patch_mask,
    w_in,
    w_down,
    b_blk,
    small_mats,
    small_bias,
    m_in,
    m_down,
    m_bias,
    m_small,
    m_sbias,
    v_in,
    v_down,
    v_bias,
    v_small,
    v_sbias,
):
    section_index = lax.axis_index("section")
    dp_index = lax.axis_index("dp")
    sections = lax.axis_size("section")
    is_first = section_index == 0
    is_last = section_index == sections - 1
    low = jnp.bfloat16
    images, patches = patch_mask.shape
    rows = w_in.shape[1]
    row_at = dp_index * rows
    ada_at = 4 * D + FF
    o_label = PATCH_IN + FREQ
    o_second = o_label + CLASSES
    o_film = o_second + D
    o_out = o_film + 2 * D

    def gathered(value, axis="dp", dim=0):
        return lax.all_gather(value, axis, axis=dim, tiled=True)

    in_low = w_in[0].astype(low)
    w_ada = in_low[:, ada_at:]
    w_qkv = gathered(in_low[:, : 3 * D])
    w_proj = gathered(in_low[:, 3 * D : 4 * D])
    w_hidden = gathered(in_low[:, 4 * D : ada_at])
    w_second = gathered(w_down[0].astype(low))

    small_low = small_mats.astype(low)
    edge_own = jnp.where(is_first, small_mats[:, :PATCH_IN], small_mats[:, -PATCH_IN:])
    bias_width = b_blk.shape[1]
    pieces = [
        b_blk[0],
        edge_own.reshape(-1),
        timesteps.astype(jnp.float32),
        labels.astype(jnp.float32),
        jnp.sum(patch_mask).astype(jnp.float32)[None],
    ]
    block = jnp.concatenate(pieces)[None]
    blocks = spread(block, "dp", 1)[:, 0]
    ends = [0]
    for piece in pieces:
        ends.append(ends[-1] + piece.shape[0])
    bias_full = rounded(blocks[:, : ends[1]].reshape(-1))
    w_edge = blocks[:, ends[1] : ends[2]].reshape(D, PATCH_IN).astype(low)
    times_all = blocks[:, ends[2] : ends[3]].reshape(-1).astype(jnp.int32)
    labels_all = blocks[:, ends[3] : ends[4]].reshape(-1).astype(jnp.int32)
    valid_total = jnp.sum(blocks[:, ends[4]])
    inv_count = 1.0 / (valid_total * PATCH_IN)
    weights = (w_qkv, w_proj, w_hidden, w_second)

    small_width = small_mats.shape[1]
    sbias_width = small_bias.shape[0]
    extra = -(-sbias_width // small_width)
    sbias_rows = jnp.pad(small_bias, (0, extra * small_width - sbias_width)).astype(low)
    small_block = jnp.concatenate([small_low, sbias_rows.reshape(extra, small_width)], axis=0)
    small_blocks = spread(small_block, "section", 2)
    small_rows = jnp.concatenate([small_blocks[i, :rows] for i in range(sections)], axis=1)
    small_used = (
        small_blocks[:, rows:].reshape(sections, -1)[:, :sbias_width].reshape(-1)
    ).astype(jnp.float32)

    shards = lax.axis_size("dp")
    time_low = time_features(times_all).astype(low)
    one_hot = label_table(labels_all)
    time_hidden = matmul_nt(time_low, small_rows[:, PATCH_IN:o_label]) + lax.dynamic_slice_in_dim(
        small_used, D + row_at, rows, 0
    )
    time_act = jax.nn.silu(time_hidden).astype(low)
    cond_part = matmul(time_act, small_rows[:, o_second:o_film])
    label_part = matmul_nt(one_hot, small_rows[:, o_label:o_second])
    cond_part = jnp.concatenate([cond_part, label_part], axis=1).reshape(shards, images, D + rows)
    cond_got = exchange(cond_part, "dp", 3)
    cond_own = (
        jnp.sum(cond_got[:, :, :D], axis=0)
        + small_used[2 * D : 3 * D]
        + jnp.swapaxes(cond_got[:, :, D:], 0, 1).reshape(images, D)
    )
    cond_cols = exchange(jnp.swapaxes(cond_own.reshape(images, shards, rows), 0, 1), "dp", 4)
    cond_first = cond_cols.reshape(shards * images, rows)
    cond_later = rounded(cond_first)
    cond_here = jnp.where(is_first, cond_first, cond_later)
    act_here = jax.nn.silu(cond_here).astype(low)
    act_later = jax.nn.silu(cond_later).astype(low)
    ada_part = jnp.concatenate(
        [matmul(act_here, w_ada), matmul(act_later, small_rows[:, o_film:o_out])], axis=1
    )
    ada_got = exchange(ada_part.reshape(shards, images * 8 * D // 128, 128), "dp", 5)
    ada_own = jnp.sum(ada_got, axis=0).reshape(images, 8 * D)
    film = ada_own[:, 6 * D :] + small_used[3 * D : 5 * D]
    ada = (ada_own[:, : 6 * D] + bias_full[ada_at:]).reshape(images, 6, D)
    bias_row = jnp.concatenate(
        [bias_full[:D], jnp.zeros((D,), jnp.float32), bias_full[D:ada_at]]
    )[None]

    fade = alpha_bar(timesteps)[:, None, None]
    noisy_low = (jnp.sqrt(fade) * latents + jnp.sqrt(1.0 - fade) * noise).astype(low)
    tokens = jnp.einsum(
        "bpi,di->bpd", noisy_low, w_edge, preferred_element_type=jnp.float32
    )
    tokens = tokens + small_used[:D] + positions(patches)[None]

    def meta_of(raw, edge, tick):
        inside = (raw >= 0) & (raw < images)
        items = [jnp.clip(raw, 0, images - 1), min(tick, images - 1), edge, inside]
        return jnp.stack([jnp.asarray(item, jnp.int32) for item in items])

    ticks = images + sections - 1
    kept_all = []
    arrived = jnp.zeros((patches, D), low)
    for tick in range(ticks):
        meta = meta_of(tick - section_index, is_first, tick)
        output, kept_all = image_forward(meta, arrived, bias_row, ada, tokens, weights, kept_all)
        if tick < ticks - 1:
            arrived = passed_along(output, "section", 1)
    kept_of = {item[0]: whole for item, whole in zip(KEPT, kept_all)}

    squared, head_grad, d_film, g_output, g_out_bias = head_step(
        kept_of["output"],
        film,
        noise,
        patch_mask,
        inv_count,
        w_edge,
        small_used[5 * D :],
    )
    loss_part = jnp.where(is_last, squared * inv_count, 0.0)
    made_all = []
    arrived = jnp.zeros((patches, D), low)
    for tick in range(ticks):
        meta = meta_of(tick - (sections - 1 - section_index), is_last, tick)
        d_low, made_all = image_backward(
            meta, arrived, ada, head_grad, weights, [kept_of[name] for name in READ], made_all
        )
        if tick < ticks - 1:
            arrived = passed_along(d_low, "section", -1)

    def flat(whole):
        return whole.reshape(images * patches, whole.shape[2])

    d_second, d_pre, d_branch, d_qkv, d_tokens = [flat(whole) for whole in made_all[:5]]
    d_ada = made_all[5][:, :6].astype(low).reshape(images, 6 * D)

    (shard_proj, shard_down, shard_hidden, shard_qkv), late = row_sums(
        [
            (flat(kept_of["att"]), d_branch),
            (flat(kept_of["act"]), d_second),
            (flat(kept_of["mixed_two"]), d_pre),
            (flat(kept_of["mixed_one"]), d_qkv),
        ]
    )
    d_ada, d_film, unused = lax.optimization_barrier((d_ada, d_film, late))
    film_all = spread(d_film, "dp", 6).reshape(shards * images, 2 * D)
    film_all = spread(film_all, "section", 7)[sections - 1]
    d_ada_all = spread(d_ada, "dp", 8).reshape(shards * images, 6 * D)
    shard_ada = matmul_tn(act_here, d_ada_all)
    shard_in = jnp.concatenate([shard_qkv, shard_proj, shard_hidden, shard_ada], axis=1)

    cond_piece = matmul_nt(d_ada_all, w_ada) * silu_grad(cond_here)
    cond_pieces = spread(cond_piece, "section", 9)
    d_cond = matmul_nt(film_all, small_rows[:, o_film:o_out]) * silu_grad(cond_later)
    for layer in reversed(range(sections)):
        d_cond = rounded(d_cond + cond_pieces[layer])
    d_cond_rows = d_cond.astype(low)
    d_cond_all = jnp.swapaxes(spread(d_cond_rows, "dp", 10), 0, 1).reshape(shards * images, D)
    d_time = (
        matmul_nt(d_cond_all, small_rows[:, o_second:o_film]) * silu_grad(time_hidden)
    ).astype(low)
    g_edge = jnp.where(
        is_first,
        matmul_tn(d_tokens, noisy_low.reshape(images * patches, PATCH_IN)),
        g_output,
    )
    qkv_sums = column_sum(d_qkv)
    bias_sums = jnp.concatenate(
        [
            qkv_sums[:D],
            qkv_sums[2 * D :],
            column_sum(d_branch),
            column_sum(d_pre),
            column_sum(d_second),
            column_sum(d_ada),
        ]
    )
    sums = jnp.concatenate(
        [
            bias_sums.reshape(shards, -1),
            g_edge.reshape(shards, -1),
            jnp.broadcast_to(column_sum(d_tokens), (shards, D)),
            jnp.broadcast_to(g_out_bias, (shards, PATCH_IN)),
            jnp.broadcast_to(column_sum(d_time), (shards, rows)),
        ],
        axis=1,
    )
    sums = exchange(sums[:, None], "dp", 11)[:, 0]
    edge_end = bias_width + rows * PATCH_IN
    shard_bias = jnp.sum(sums[:, :bias_width], axis=0)
    edge_rows = jnp.sum(sums[:, bias_width:edge_end], axis=0).reshape(rows, PATCH_IN)
    token_sums = jnp.sum(sums[:, edge_end : edge_end + D], axis=0)
    out_sums = jnp.sum(sums[:, edge_end + D : edge_end + D + PATCH_IN], axis=0)
    time_sums = sums[:, edge_end + D + PATCH_IN :].reshape(-1)
    small_grad = jnp.concatenate(
        [
            edge_rows,
            matmul_tn(d_time, time_low),
            matmul_tn(d_cond_rows, one_hot),
            matmul_tn(time_act, d_cond_all),
            matmul_tn(act_later, film_all),
            edge_rows,
        ],
        axis=1,
    )
    small_shard = lax.dynamic_slice_in_dim(small_grad, section_index * small_width, small_width, 1)
    sbias_grad = jnp.concatenate(
        [token_sums, time_sums, column_sum(d_cond_all), column_sum(film_all), out_sums]
    )
    sbias_shard = lax.dynamic_slice_in_dim(
        sbias_grad, section_index * sbias_width, sbias_width, 0
    )

    dp_zero = (dp_index == 0).astype(jnp.float32)
    squares = (
        jnp.sum(shard_in * shard_in)
        + jnp.sum(shard_down * shard_down)
        + jnp.sum(shard_bias * shard_bias)
        + jnp.sum(small_shard * small_shard)
        + dp_zero * jnp.sum(sbias_shard * sbias_shard)
    )
    norm_square, loss = lax.psum((squares, loss_part), ("section", "dp"))
    grad_norm = jnp.sqrt(norm_square)
    scaling = jnp.minimum(1.0, CLIP / grad_norm)
    new_in, first_in, second_in = adam_update(w_in, shard_in[None], m_in, v_in, scaling)
    new_down, first_down, second_down = adam_update(
        w_down, shard_down[None], m_down, v_down, scaling
    )
    new_bias, first_bias, second_bias = adam_update(
        b_blk, shard_bias[None], m_bias, v_bias, scaling
    )
    new_small, first_small, second_small = adam_update(
        small_mats, small_shard, m_small, v_small, scaling
    )
    new_sbias, first_sbias, second_sbias = adam_update(
        small_bias, sbias_shard, m_sbias, v_sbias, scaling
    )
    return (
        loss,
        grad_norm,
        new_in,
        first_in,
        second_in,
        new_down,
        first_down,
        second_down,
        new_bias,
        first_bias,
        second_bias,
        new_small,
        first_small,
        second_small,
        new_sbias,
        first_sbias,
        second_sbias,
    )


def solution(mesh):
    in_specs = (
        P("dp", None, None),
        P("dp", None, None),
        P("dp"),
        P("dp"),
        P("dp", None),
        P("section", "dp", None),
        P("section", "dp", None),
        P("section", "dp"),
        P("dp", "section"),
        P("section"),
        P("section", "dp", None),
        P("section", "dp", None),
        P("section", "dp"),
        P("dp", "section"),
        P("section"),
        P("section", "dp", None),
        P("section", "dp", None),
        P("section", "dp"),
        P("dp", "section"),
        P("section"),
    )
    out_specs = (
        P(),
        P(),
        P("section", "dp", None),
        P("section", "dp", None),
        P("section", "dp", None),
        P("section", "dp", None),
        P("section", "dp", None),
        P("section", "dp", None),
        P("section", "dp"),
        P("section", "dp"),
        P("section", "dp"),
        P("dp", "section"),
        P("dp", "section"),
        P("dp", "section"),
        P("section"),
        P("section"),
        P("section"),
    )
    return jax.shard_map(body, mesh=mesh, in_specs=in_specs, out_specs=out_specs, check_vma=False)
```

```python
import functools
import math

import jax
import jax.numpy as jnp
from jax import lax
from jax.experimental import pallas as pl
from jax.experimental.pallas import tpu as pltpu
from jax.sharding import PartitionSpec as P

D = 1152
HEADS = 16
HEAD_DIM = 72
FF = 4608
CLASSES = 1000
FREQ = 256
PATCH_IN = 16
GRID = 16


EPS_NORM = 1e-06
CLIP = 0.001
RATE = 0.005
BETA_ONE = 0.9
BETA_TWO = 0.999
ADAM_EPS = 1e-08
DECAY = 0.01
STEP_POWER = 10.0


def passed_along(value, axis, steps):
    count = lax.axis_size(axis)
    first, last = (max(0, -steps), min(count, count - steps))
    return lax.ppermute(value, axis, [(source, source + steps) for source in range(first, last)])


def matmul(left_side, right_side):
    return jnp.dot(left_side, right_side, preferred_element_type=jnp.float32)


def matmul_tn(left_side, right_side):
    return lax.dot_general(
        left_side, right_side, (((0,), (0,)), ((), ())), preferred_element_type=jnp.float32
    )


def matmul_nt(left_side, right_side):
    return lax.dot_general(
        left_side, right_side, (((1,), (1,)), ((), ())), preferred_element_type=jnp.float32
    )


def column_sum(values):
    return jnp.sum(values.astype(jnp.float32), axis=0)


def normalize(values):
    center = values - jnp.mean(values, axis=-1, keepdims=True)
    invstd = lax.rsqrt(jnp.mean(center * center, axis=-1, keepdims=True) + EPS_NORM)
    return (center * invstd, invstd)


def norm_back(grad_normed, normed, invstd):
    return invstd * (
        grad_normed
        - jnp.mean(grad_normed, axis=-1, keepdims=True)
        - normed * jnp.mean(grad_normed * normed, axis=-1, keepdims=True)
    )


def gelu_tanh(values):
    return (
        0.5
        * values
        * (1.0 + jnp.tanh(0.7978845608028654 * (values + 0.044715 * values * values * values)))
    )


def gelu_grad(values):
    inner = jnp.tanh(0.7978845608028654 * (values + 0.044715 * values * values * values))
    return 0.5 * (1.0 + inner) + 0.5 * values * (1.0 - inner * inner) * 0.7978845608028654 * (
        1.0 + 0.134145 * values * values
    )


def silu_grad(values):
    sigma = jax.nn.sigmoid(values)
    return sigma * (1.0 + values * (1.0 - sigma))


def positions(patches):
    quarter = D // 4
    omega = jnp.exp(-math.log(10000.0) * jnp.arange(quarter, dtype=jnp.float32) / quarter)
    spot = jnp.arange(patches, dtype=jnp.int32)
    row_angle = (spot // GRID).astype(jnp.float32)[:, None] * omega[None, :]
    col_angle = (spot % GRID).astype(jnp.float32)[:, None] * omega[None, :]
    return jnp.concatenate(
        [jnp.sin(row_angle), jnp.cos(row_angle), jnp.sin(col_angle), jnp.cos(col_angle)], axis=1
    )


def time_features(time_steps):
    half = FREQ // 2
    freqs = jnp.exp(-math.log(10000.0) * jnp.arange(half, dtype=jnp.float32) / half)
    angles = time_steps.astype(jnp.float32)[:, None] * freqs[None, :]
    return jnp.concatenate([jnp.cos(angles), jnp.sin(angles)], axis=1)


def alpha_bar(time_steps):
    return jnp.cos((time_steps.astype(jnp.float32) / 1000.0 + 0.008) / 1.008 * (math.pi / 2)) ** 2


def label_table(label_part):
    return (label_part[:, None] == jnp.arange(CLASSES, dtype=jnp.int32)[None, :]).astype(
        jnp.bfloat16
    )


MESH = pl.DeviceIdType.MESH
DIRECT = 8


def rounded(values):
    return lax.reduce_precision(values, 8, 7)


def meet(axis, count, here):
    barrier = pltpu.get_barrier_semaphore()
    for step in range(1, count):
        pl.semaphore_signal(
            barrier, inc=1, device_id={axis: lax.rem(here + step, count)}, device_id_type=MESH
        )
    pl.semaphore_wait(barrier, count - 1)


def share_kernel(axis, count, personal, in_ref, out_ref, send_sem, recv_sem):
    here = lax.axis_index(axis)
    meet(axis, count, here)
    copies = []
    for step in range(1, count):
        target = lax.rem(here + step, count)
        copy = pltpu.make_async_remote_copy(
            src_ref=in_ref.at[target] if personal else in_ref,
            dst_ref=out_ref.at[here],
            send_sem=send_sem.at[step - 1],
            recv_sem=recv_sem.at[step - 1],
            device_id={axis: target},
            device_id_type=MESH,
        )
        copy.start()
        copies.append(copy)
    out_ref[here] = in_ref[here] if personal else in_ref[...]
    for copy in copies:
        copy.wait()


def share(value, axis, personal, ident):
    count = lax.axis_size(axis)
    shape = value.shape if personal else (count,) + value.shape
    return pl.pallas_call(
        functools.partial(share_kernel, axis, count, personal),
        out_shape=jax.ShapeDtypeStruct(shape, value.dtype),
        in_specs=[pl.BlockSpec(memory_space=pltpu.VMEM)],
        out_specs=pl.BlockSpec(memory_space=pltpu.VMEM),
        scratch_shapes=[
            pltpu.SemaphoreType.DMA((count - 1,)),
            pltpu.SemaphoreType.DMA((count - 1,)),
        ],
        compiler_params=pltpu.CompilerParams(collective_id=ident, has_side_effects=True),
        name="share",
    )(value)


def spread(value, axis, ident):
    if lax.axis_size(axis) > DIRECT:
        return lax.all_gather(value, axis)
    return share(value, axis, False, ident)


def exchange(value, axis, ident):
    if lax.axis_size(axis) > DIRECT:
        return lax.all_to_all(value, axis, 0, 0)
    return share(value, axis, True, ident)


def products_kernel(units, rows, *refs):
    lefts, rights = (refs[:4], refs[4:8])
    own_out, block_outs, bias_out = (refs[8], refs[9:12], refs[12])
    (
        left_v,
        right_v,
        product,
        got,
        own_v,
        low_v,
        left_sem,
        right_sem,
        send_sem,
        recv_sem,
        own_sem,
        low_sem,
    ) = refs[13:]
    here = lax.axis_index("dp")
    core, chip = (lax.rem(here, 2), here // 2)
    chips = 4
    partner = {"dp": here + 1 - 2 * core}
    barrier = pltpu.get_barrier_semaphore()
    pl.semaphore_signal(barrier, inc=1, device_id=partner, device_id_type=MESH)
    pl.semaphore_wait(barrier, 1)
    tall = chips * rows
    plan, last = ([], [None, None])
    slots = [1, 1]
    for left, left_at, right, right_at, gathers in units:
        fresh = []
        for side, key in enumerate(((left, left_at), (right, right_at))):
            fresh.append(last[side] != key)
            if fresh[-1]:
                slots[side] = 1 - slots[side]
                last[side] = key
        plan.append((tuple(slots), tuple(fresh)))

    def loads_of(index):
        left, left_at, right, right_at, gathers = units[index]
        (left_slot, right_slot), (left_fresh, right_fresh) = plan[index]
        copies = []
        if left_fresh:
            copies.append(
                pltpu.make_async_copy(
                    lefts[left].at[:, pl.ds(left_at, D)], left_v.at[left_slot], left_sem.at[left_slot]
                )
            )
        if right_fresh:
            copies.append(
                pltpu.make_async_copy(
                    rights[right].at[:, pl.ds(right_at, D)],
                    right_v.at[right_slot],
                    right_sem.at[right_slot],
                )
            )
        return copies

    def to_partner(source, target, sems):
        copy = pltpu.make_async_remote_copy(
            src_ref=source,
            dst_ref=target,
            send_sem=send_sem.at[sems],
            recv_sem=recv_sem.at[sems],
            device_id=partner,
            device_id_type=MESH,
        )
        copy.start()
        return copy

    pending, crossing, leaving = ({}, {}, {})

    def load(index):
        pending[index] = loads_of(index)
        for copy in pending[index]:
            copy.start()

    def multiply(index):
        gathers = units[index][4]
        left_slot, right_slot = plan[index][0]
        for copy in pending[index]:
            copy.wait()
        if index + 1 < len(units):
            load(index + 1)
        if index >= 2:
            for copy in crossing[index - 2]:
                copy.wait_send()
        slot, place = (index % 2, index % 4)
        product[slot] = lax.dot_general(
            left_v[left_slot],
            right_v[right_slot],
            (((0,), (0,)), ((), ())),
            preferred_element_type=jnp.float32,
        )
        if plan[index][1][1]:
            ones = jnp.ones((8, right_v.shape[1]), jnp.bfloat16)
            bias_out[index] = matmul(ones, right_v[right_slot])
        if gathers is None:
            crossing[index] = [
                to_partner(
                    product.at[slot, pl.ds(pl.multiple_of((2 * i + 1 - core) * rows, 8), rows)],
                    got.at[place, pl.ds(i * rows, rows)],
                    place * chips + i,
                )
                for i in range(chips)
            ]
        else:
            crossing[index] = [
                to_partner(
                    product.at[slot, pl.ds(pl.multiple_of((1 - core) * tall, 8), tall)],
                    got.at[place],
                    place * chips,
                )
            ]

    def combine(index):
        gathers = units[index][4]
        slot, place, side = (index % 2, index % 4, index % 2)
        for copy in crossing[index]:
            copy.wait_recv()
        if index >= 2:
            finish(index - 2)
        at_slot = slot_of[index]
        if gathers is None:
            for step in range(chips):
                other = lax.rem(chip + step, chips)
                value = (
                    product[slot, pl.ds(pl.multiple_of((2 * other + core) * rows, 8), rows)]
                    + got[place, pl.ds(pl.multiple_of(other * rows, 8), rows)]
                )
                if step == 0:
                    own_v[side, 0:rows] = value
                else:
                    low_v[side, (step - 1) * rows : step * rows] = value.astype(jnp.bfloat16)
            copies = [
                pltpu.make_async_copy(
                    own_v.at[side, pl.ds(0, rows)], own_out.at[at_slot], own_sem.at[side]
                )
            ]
            for step in range(1, chips):
                copies.append(
                    pltpu.make_async_copy(
                        low_v.at[side, pl.ds((step - 1) * rows, rows)],
                        block_outs[step - 1].at[at_slot],
                        low_sem.at[side, step - 1],
                    )
                )
            for copy in copies:
                copy.start()
            leaving[index] = [(None, copies)]
        else:
            step_here = lax.rem(gathers + chips - chip, chips)
            cases = []
            for step in range(chips):
                held = own_v if step == 0 else low_v
                out = own_out if step == 0 else block_outs[step - 1]
                sem = own_sem.at[side] if step == 0 else low_sem.at[side, step - 1]
                copies = [
                    pltpu.make_async_copy(
                        held.at[side, pl.ds(i * rows, rows)],
                        out.at[at_slot + i],
                        sem if i == 0 else more_sem(step, side, i),
                    )
                    for i in range(chips)
                ]
                cases.append((step_here == step, copies))

                @pl.when(step_here == step)
                def put(held=held, copies=copies):
                    value = product[slot, pl.ds(pl.multiple_of(core * tall, 8), tall)] + got[place]
                    held[side] = value.astype(held.dtype)
                    for copy in copies:
                        copy.start()

            leaving[index] = cases

    def more_sem(step, side, i):
        return own_sem.at[2 + side * 3 + i - 1] if step == 0 else low_sem.at[side, 3 * i + step - 1]

    def finish(index):
        for condition, copies in leaving[index]:
            if condition is None:
                for copy in copies:
                    copy.wait()
            else:

                @pl.when(condition)
                def settle(copies=copies):
                    for copy in copies:
                        copy.wait()

    slot_of, used = ({}, 0)
    for index, unit in enumerate(units):
        slot_of[index] = used
        if unit[4] is None:
            used += 1
    load(0)
    multiply(0)
    for index in range(len(units)):
        if index + 1 < len(units):
            multiply(index + 1)
        combine(index)
    for index in range(max(0, len(units) - 2), len(units)):
        finish(index)
        for copy in crossing[index]:
            copy.wait_send()


def chip_products(units, lefts, rights, rows, ident):
    tokens = lefts[0].shape[0]
    places = sum(unit[4] is None for unit in units) + 4 * any(unit[4] is not None for unit in units)
    outs = pl.pallas_call(
        functools.partial(products_kernel, units, rows),
        out_shape=[jax.ShapeDtypeStruct((places, rows, D), jnp.float32)]
        + [jax.ShapeDtypeStruct((places, rows, D), jnp.bfloat16) for unused in range(3)]
        + [jax.ShapeDtypeStruct((len(units), 8, D), jnp.float32)],
        in_specs=specs("h" * 8),
        out_specs=specs("h" * 4, "v"),
        scratch_shapes=[
            pltpu.VMEM((2, tokens, D), jnp.bfloat16),
            pltpu.VMEM((2, tokens, D), jnp.bfloat16),
            pltpu.VMEM((2, 8 * rows, D), jnp.float32),
            pltpu.VMEM((4, 4 * rows, D), jnp.float32),
            pltpu.VMEM((2, 4 * rows, D), jnp.float32),
            pltpu.VMEM((2, 4 * rows, D), jnp.bfloat16),
            pltpu.SemaphoreType.DMA((2,)),
            pltpu.SemaphoreType.DMA((2,)),
            pltpu.SemaphoreType.DMA((16,)),
            pltpu.SemaphoreType.DMA((16,)),
            pltpu.SemaphoreType.DMA((8,)),
            pltpu.SemaphoreType.DMA((2, 12)),
        ],
        compiler_params=pltpu.CompilerParams(
            collective_id=ident, has_side_effects=True, vmem_limit_bytes=60 << 20
        ),
        cost_estimate=pl.CostEstimate(
            flops=2 * tokens * D * D * len(units),
            bytes_accessed=len(units) * tokens * D * 4,
            transcendentals=0,
        ),
        name="chip_products",
    )(*lefts, *rights)
    return (outs[0], outs[1:4], outs[4][:, 0])


def row_sums(lefts, rights, early):
    count = lax.axis_size("dp")
    if count != DIRECT:
        products = [matmul_tn(one, other) for one, other in zip(lefts, rights)]
        sums = [lax.psum_scatter(one, "dp", scatter_dimension=0, tiled=True) for one in products]
        wide = jnp.concatenate([sums[0], sums[1], sums[2]], axis=1)
        return (wide, sums[3], [column_sum(one) for one in rights], products[3], early)
    rows = D // count
    chips = count // 2
    parts = FF // D
    first = [(0, 0, 0, i * D, None) for i in range(3)] + [(1, 0, 1, 0, None)]
    rest = [(2, 0, 2, i * D, None) for i in range(parts)] + [
        (3, i * D, 3, 0, i) for i in range(parts)
    ]
    totals, biases, tied = ([], [], None)
    for ident, units in ((12, first), (13, rest)):
        if tied is not None:
            lefts, rights, tied, early = lax.optimization_barrier((lefts, rights, tied, early))
        total, blocks, bias = chip_products(tuple(units), lefts, rights, rows, ident)
        for step in range(1, chips):
            arrived = lax.ppermute(
                blocks[step - 1], "dp", [(i, (i + 2 * step) % count) for i in range(count)]
            )
            total = total + arrived.astype(jnp.float32)
        tied = blocks
        totals.append(total)
        biases.append(bias)
    wide = [totals[0][i] for i in range(4)] + [totals[1][i] for i in range(parts)]
    sums = [biases[0][:3].reshape(-1), biases[0][3], biases[1][:parts].reshape(-1), biases[1][parts]]
    late = (tied, totals[0])
    return (jnp.concatenate(wide, axis=1), totals[1][parts:].reshape(-1, D), sums, late, early)


def attend_kernel(qkv_ref, out_ref):
    for head in range(HEADS):
        at = head * HEAD_DIM
        query = qkv_ref[:, at : at + HEAD_DIM]
        key = qkv_ref[:, D + at : D + at + HEAD_DIM]
        value = qkv_ref[:, 2 * D + at : 2 * D + at + HEAD_DIM]
        scores = matmul_nt(query, key) * HEAD_DIM ** (-0.5)
        attention = jnp.exp(scores - jnp.max(scores, axis=-1, keepdims=True))
        attention = attention * (1.0 / jnp.sum(attention, axis=-1, keepdims=True))
        out_ref[:, at : at + HEAD_DIM] = matmul(attention.astype(jnp.bfloat16), value).astype(
            jnp.bfloat16
        )


def attend_back_kernel(qkv_ref, grad_ref, out_ref):
    scaling = HEAD_DIM ** (-0.5)
    for head in range(HEADS):
        at = head * HEAD_DIM
        query = qkv_ref[:, at : at + HEAD_DIM]
        key = qkv_ref[:, D + at : D + at + HEAD_DIM]
        value = qkv_ref[:, 2 * D + at : 2 * D + at + HEAD_DIM]
        grad = grad_ref[:, at : at + HEAD_DIM]
        scores = matmul_nt(query, key) * scaling
        attention = jnp.exp(scores - jnp.max(scores, axis=-1, keepdims=True))
        attention = attention * (1.0 / jnp.sum(attention, axis=-1, keepdims=True))
        d_probs = matmul_nt(grad, value)
        d_scores = (
            attention * (d_probs - jnp.sum(attention * d_probs, axis=-1, keepdims=True))
        ).astype(jnp.bfloat16)
        attention_low = attention.astype(jnp.bfloat16)
        out_ref[:, at : at + HEAD_DIM] = (matmul(d_scores, key) * scaling).astype(jnp.bfloat16)
        out_ref[:, D + at : D + at + HEAD_DIM] = (matmul_tn(d_scores, query) * scaling).astype(
            jnp.bfloat16
        )
        out_ref[:, 2 * D + at : 2 * D + at + HEAD_DIM] = matmul_tn(attention_low, grad).astype(
            jnp.bfloat16
        )


ROW_BLOCK = 64
KEPT = (
    ("residual", D, jnp.float32),
    ("mixed_one", D, jnp.bfloat16),
    ("qkv", 3 * D, jnp.bfloat16),
    ("att", D, jnp.bfloat16),
    ("branch", D, jnp.float32),
    ("middle", D, jnp.float32),
    ("mixed_two", D, jnp.bfloat16),
    ("pre", FF, jnp.float32),
    ("act", FF, jnp.bfloat16),
    ("second", D, jnp.float32),
    ("output", D, jnp.float32),
)
READ = ("residual", "qkv", "branch", "middle", "pre", "second")
MADE = (
    ("d_second", D, jnp.bfloat16),
    ("d_pre", FF, jnp.bfloat16),
    ("d_branch", D, jnp.bfloat16),
    ("d_qkv", 3 * D, jnp.bfloat16),
    ("d_residual", D, jnp.bfloat16),
)
WEIGHTS = ((D, 3 * D), (D, D), (D, FF), (FF, D))


def by_rows(patches, step):
    @pl.loop(0, patches // ROW_BLOCK)
    def run(index):
        step(pl.ds(pl.multiple_of(index * ROW_BLOCK, ROW_BLOCK), ROW_BLOCK))


def started(source, target, sem):
    copy = pltpu.make_async_copy(source, target, sem)
    copy.start()
    return copy


def forward_kernel(patches, given, meta, arrived, bias, ada, tokens, wq, wp, wh, ws, *refs):
    count = len(KEPT)
    send, outs = (refs[given], refs[given + 1 : given + 1 + count])
    scratch = refs[given + 1 + count :]
    kept = {name: scratch[i] for i, (name, unused, kind) in enumerate(KEPT)}
    wq_v, wp_v, wh_v, ws_v, w_sem, x_sem, out_sem = scratch[count:]
    loads = [started(wq.at[:, pl.ds(i * D, D)], wq_v.at[:, pl.ds(i * D, D)], w_sem.at[i]) for i in range(3)]
    loads.append(started(wp, wp_v, w_sem.at[3]))
    loads += [
        started(wh.at[:, pl.ds(i * D, D)], wh_v.at[:, pl.ds(i * D, D)], w_sem.at[4 + i])
        for i in range(FF // D)
    ]
    third = D // 3
    loads += [
        started(ws.at[:, pl.ds(i * third, third)], ws_v.at[:, pl.ds(i * third, third)], w_sem.at[8 + i])
        for i in range(3)
    ]
    saves = []

    def start_if_valid(copy):
        @pl.when(meta[3] == 1)
        def start():
            copy.start()

    def save(name):
        index = [item[0] for item in KEPT].index(name)
        saves.append(pltpu.make_async_copy(kept[name], outs[index].at[meta[0]], out_sem.at[index]))
        start_if_valid(saves[-1])

    residual = kept["residual"]

    @pl.when(meta[2] == 1)
    def take_tokens():
        started(tokens.at[meta[1]], residual, x_sem).wait()

    @pl.when(meta[2] == 0)
    def take_arrived():
        residual[...] = arrived[...].astype(jnp.float32)

    save("residual")
    modulation = ada[meta[0]]

    def mix_one(at):
        normed, unused = normalize(residual[at])
        kept["mixed_one"][at] = (normed * (1.0 + modulation[1:2]) + modulation[0:1]).astype(
            jnp.bfloat16
        )

    by_rows(patches, mix_one)
    save("mixed_one")
    for part in range(3):
        loads[part].wait()
        cols = slice(part * D, part * D + D)
        kept["qkv"][:, cols] = (
            matmul(kept["mixed_one"][...], wq_v[:, cols]) + bias[:, cols]
        ).astype(jnp.bfloat16)
    save("qkv")
    attend_kernel(kept["qkv"], kept["att"])
    save("att")
    loads[3].wait()
    kept["branch"][...] = matmul(kept["att"][...], wp_v[...]) + bias[:, 3 * D : 4 * D]
    save("branch")

    def mix_two(at):
        middle = residual[at] + modulation[2:3] * kept["branch"][at]
        kept["middle"][at] = middle
        normed, unused = normalize(middle)
        kept["mixed_two"][at] = (normed * (1.0 + modulation[4:5]) + modulation[3:4]).astype(
            jnp.bfloat16
        )

    by_rows(patches, mix_two)
    save("middle")
    save("mixed_two")
    for part in range(FF // D):
        loads[4 + part].wait()
        cols = slice(part * D, part * D + D)
        pre = (
            matmul(kept["mixed_two"][...], wh_v[:, cols])
            + bias[:, 4 * D + part * D : 5 * D + part * D]
        )
        kept["pre"][:, cols] = pre
        kept["act"][:, cols] = gelu_tanh(pre).astype(jnp.bfloat16)
    save("pre")
    save("act")
    for part in range(3):
        loads[8 + part].wait()
        cols = slice(part * third, part * third + third)
        second = (
            matmul(kept["act"][...], ws_v[:, cols])
            + bias[:, 4 * D + FF + part * third : 4 * D + FF + part * third + third]
        )
        kept["second"][:, cols] = second
        output = kept["middle"][:, cols] + modulation[5:6, cols] * second
        kept["output"][:, cols] = output
        send[:, cols] = output.astype(jnp.bfloat16)
    save("second")
    save("output")

    @pl.when(meta[3] == 1)
    def finish():
        for copy in saves:
            copy.wait()


def backward_kernel(patches, given, meta, arrived, ada, head_grad, wq, wp, wh, ws, *refs):
    reads, made = (len(READ), len(MADE))
    sources, refs = (refs[:reads], refs[reads + given :])
    send, outs, ada_out = (refs[0], refs[1 : made + 1], refs[made + 1])
    scratch = refs[made + 2 :]
    kept = {name: scratch[i] for i, name in enumerate(READ)}
    grads = {name: scratch[reads + i] for i, (name, unused, kind) in enumerate(MADE)}
    (
        flow,
        mixed,
        att_grad,
        sums,
        wq_v,
        wp_v,
        wh_v,
        ws_v,
        w_sem,
        in_sem,
        x_sem,
        out_sem,
    ) = scratch[reads + made :]

    def fetch(name):
        index = READ.index(name)
        return started(sources[index].at[meta[0]], kept[name], in_sem.at[index])

    fetched = {"second": fetch("second")}
    loads = [started(ws.at[pl.ds(i * D, D)], ws_v.at[pl.ds(i * D, D)], w_sem.at[i]) for i in range(FF // D)]
    for name in ("pre", "middle", "branch", "qkv", "residual"):
        fetched[name] = fetch(name)
    third = D // 3
    loads += [
        started(wh.at[pl.ds(i * third, third)], wh_v.at[pl.ds(i * third, third)], w_sem.at[4 + i])
        for i in range(3)
    ]
    loads.append(started(wp, wp_v, w_sem.at[7]))
    loads += [
        started(wq.at[pl.ds(i * third, third)], wq_v.at[pl.ds(i * third, third)], w_sem.at[8 + i])
        for i in range(3)
    ]
    saves = []

    def start_if_valid(copy):
        @pl.when(meta[3] == 1)
        def start():
            copy.start()

    def save(name):
        index = [item[0] for item in MADE].index(name)
        saves.append(pltpu.make_async_copy(grads[name], outs[index].at[meta[0]], out_sem.at[index]))
        start_if_valid(saves[-1])

    @pl.when(meta[2] == 1)
    def take_head():
        started(head_grad.at[meta[1]], flow, x_sem).wait()

    @pl.when(meta[2] == 0)
    def take_arrived():
        flow[...] = arrived[...].astype(jnp.float32)

    modulation = ada[meta[0]]
    sums[...] = jnp.zeros_like(sums)

    def add_sum(row, values):
        sums[row : row + 1] += jnp.sum(values, axis=0, keepdims=True)

    fetched["second"].wait()

    def open_second(at):
        grad = flow[at]
        grads["d_second"][at] = (grad * modulation[5:6]).astype(jnp.bfloat16)
        add_sum(5, grad * kept["second"][at])

    by_rows(patches, open_second)
    save("d_second")
    fetched["pre"].wait()
    for part in range(FF // D):
        loads[part].wait()
        cols = slice(part * D, part * D + D)
        grads["d_pre"][:, cols] = (
            matmul_nt(grads["d_second"][...], ws_v[cols]) * gelu_grad(kept["pre"][:, cols])
        ).astype(jnp.bfloat16)
    save("d_pre")
    for part in range(3):
        loads[4 + part].wait()
        cols = slice(part * third, part * third + third)
        mixed[:, cols] = matmul_nt(grads["d_pre"][...], wh_v[cols])
    fetched["middle"].wait()
    fetched["branch"].wait()

    def through_two(at):
        normed, invstd = normalize(kept["middle"][at])
        grad = mixed[at]
        add_sum(3, grad)
        add_sum(4, grad * normed)
        total = flow[at] + norm_back(grad * (1.0 + modulation[4:5]), normed, invstd)
        flow[at] = total
        add_sum(2, total * kept["branch"][at])
        grads["d_branch"][at] = (total * modulation[2:3]).astype(jnp.bfloat16)

    by_rows(patches, through_two)
    save("d_branch")
    loads[7].wait()
    att_grad[...] = matmul_nt(grads["d_branch"][...], wp_v[...]).astype(jnp.bfloat16)
    fetched["qkv"].wait()
    attend_back_kernel(kept["qkv"], att_grad, grads["d_qkv"])
    save("d_qkv")
    for part in range(3):
        loads[8 + part].wait()
        cols = slice(part * third, part * third + third)
        mixed[:, cols] = matmul_nt(grads["d_qkv"][...], wq_v[cols])
    fetched["residual"].wait()

    def through_one(at):
        normed, invstd = normalize(kept["residual"][at])
        grad = mixed[at]
        add_sum(0, grad)
        add_sum(1, grad * normed)
        total = flow[at] + norm_back(grad * (1.0 + modulation[1:2]), normed, invstd)
        low = total.astype(jnp.bfloat16)
        grads["d_residual"][at] = low
        send[at] = low

    by_rows(patches, through_one)
    save("d_residual")
    saves.append(pltpu.make_async_copy(sums, ada_out.at[meta[0]], x_sem))
    start_if_valid(saves[-1])

    @pl.when(meta[3] == 1)
    def finish():
        for copy in saves:
            copy.wait()


def specs(*spaces):
    return [
        pl.BlockSpec(memory_space={"s": pltpu.SMEM, "v": pltpu.VMEM, "h": pl.ANY}[space])
        for space in "".join(spaces)
    ]


def weight_scratch():
    return [pltpu.VMEM(shape, jnp.bfloat16) for shape in WEIGHTS] + [
        pltpu.SemaphoreType.DMA((11,))
    ]


def block_cost(patches, factor):
    area = sum(rows * columns for rows, columns in WEIGHTS)
    return pl.CostEstimate(
        flops=2 * patches * area + factor * patches * patches * D,
        bytes_accessed=2 * area + 64 * patches * D,
        transcendentals=patches * (FF + HEADS * patches),
    )


def image_forward(meta, arrived, bias, ada, tokens, weights, buffers):
    patches, given, count = (arrived.shape[0], len(buffers), len(KEPT))
    images = ada.shape[0]
    outs = pl.pallas_call(
        functools.partial(forward_kernel, patches, given),
        out_shape=[jax.ShapeDtypeStruct((patches, D), jnp.bfloat16)]
        + [jax.ShapeDtypeStruct((images, patches, width), kind) for unused, width, kind in KEPT],
        in_specs=specs("svvv", "h" * (5 + given)),
        out_specs=specs("v", "h" * count),
        scratch_shapes=[pltpu.VMEM((patches, width), kind) for unused, width, kind in KEPT]
        + weight_scratch()
        + [pltpu.SemaphoreType.DMA, pltpu.SemaphoreType.DMA((count,))],
        input_output_aliases={9 + i: 1 + i for i in range(given)},
        compiler_params=pltpu.CompilerParams(vmem_limit_bytes=60 << 20),
        cost_estimate=block_cost(patches, 4),
        name="image_forward",
    )(meta, arrived, bias, ada, tokens, *weights, *buffers)
    return (outs[0], outs[1:])


def image_backward(meta, arrived, ada, head_grad, weights, sources, buffers):
    patches, given, images = (arrived.shape[0], len(buffers), ada.shape[0])
    reads, made = (len(READ), len(MADE))
    kinds = {name: (width, kind) for name, width, kind in KEPT}
    outs = pl.pallas_call(
        functools.partial(backward_kernel, patches, given),
        out_shape=[jax.ShapeDtypeStruct((patches, D), jnp.bfloat16)]
        + [jax.ShapeDtypeStruct((images, patches, width), kind) for unused, width, kind in MADE]
        + [jax.ShapeDtypeStruct((images, 8, D), jnp.float32)],
        in_specs=specs("svv", "h" * (5 + reads + given)),
        out_specs=specs("v", "h" * (made + 1)),
        scratch_shapes=[pltpu.VMEM((patches, kinds[name][0]), kinds[name][1]) for name in READ]
        + [pltpu.VMEM((patches, width), kind) for unused, width, kind in MADE]
        + [
            pltpu.VMEM((patches, D), jnp.float32),
            pltpu.VMEM((patches, D), jnp.float32),
            pltpu.VMEM((patches, D), jnp.bfloat16),
            pltpu.VMEM((8, D), jnp.float32),
        ]
        + weight_scratch()
        + [
            pltpu.SemaphoreType.DMA((reads,)),
            pltpu.SemaphoreType.DMA,
            pltpu.SemaphoreType.DMA((made,)),
        ],
        input_output_aliases={8 + reads + i: 1 + i for i in range(given)},
        compiler_params=pltpu.CompilerParams(vmem_limit_bytes=60 << 20),
        cost_estimate=block_cost(patches, 10),
        name="image_backward",
    )(meta, arrived, ada, head_grad, *weights, *sources, *buffers)
    return (outs[0], outs[1:])


def head_step(residual, film, noise_part, mask_part, inv_count, w_out, b_out):
    shifting, scaling = (film[:, :D], film[:, D:])
    normed, invstd = normalize(residual)
    mixed = (normed * (1.0 + scaling[:, None]) + shifting[:, None]).astype(jnp.bfloat16)
    output = (
        jnp.einsum("bpd,dj->bpj", mixed, w_out, preferred_element_type=jnp.float32) + b_out
    )
    mismatch = output - noise_part
    mask_float = mask_part.astype(jnp.float32)[:, :, None]
    squared = jnp.sum(mask_float * mismatch * mismatch)
    d_output = (2.0 * inv_count * mask_float * mismatch).astype(jnp.bfloat16)
    g_output = jnp.einsum("bpd,bpj->dj", mixed, d_output, preferred_element_type=jnp.float32)
    d_mixed = jnp.einsum("bpj,dj->bpd", d_output, w_out, preferred_element_type=jnp.float32)
    d_film = jnp.concatenate(
        [jnp.sum(d_mixed, axis=1), jnp.sum(d_mixed * normed, axis=1)], axis=1
    ).astype(jnp.bfloat16)
    d_residual = norm_back(d_mixed * (1.0 + scaling[:, None]), normed, invstd)
    g_bias = jnp.sum(d_output.astype(jnp.float32), axis=(0, 1))
    return (squared, d_residual, d_film, g_output, g_bias)


def adam_update(weight, gradient, first_moment, second_moment, scaling):
    gradient = gradient * scaling
    first_new = BETA_ONE * first_moment + (1.0 - BETA_ONE) * gradient
    second_new = BETA_TWO * second_moment + (1.0 - BETA_TWO) * gradient * gradient
    ratio = (
        first_new
        / (1.0 - BETA_ONE**STEP_POWER)
        / (jnp.sqrt(second_new / (1.0 - BETA_TWO**STEP_POWER)) + ADAM_EPS)
    )
    return (weight - RATE * (ratio + DECAY * weight), first_new, second_new)


def body(
    latents,
    noise,
    timesteps,
    labels,
    patch_mask,
    w_in,
    w_down,
    b_blk,
    small_mats,
    small_bias,
    m_in,
    m_down,
    m_bias,
    m_small,
    m_sbias,
    v_in,
    v_down,
    v_bias,
    v_small,
    v_sbias,
):
    section_index = lax.axis_index("section")
    dp_index = lax.axis_index("dp")
    sections = lax.axis_size("section")
    is_first = section_index == 0
    is_last = section_index == sections - 1
    low = jnp.bfloat16
    images, patches = patch_mask.shape
    rows = w_in.shape[1]
    row_at = dp_index * rows
    ada_at = 4 * D + FF
    o_label = PATCH_IN + FREQ
    o_second = o_label + CLASSES
    o_film = o_second + D
    o_out = o_film + 2 * D

    def gathered(value, axis="dp", dim=0):
        return lax.all_gather(value, axis, axis=dim, tiled=True)

    in_low = w_in[0].astype(low)
    w_ada = in_low[:, ada_at:]
    w_qkv = gathered(in_low[:, : 3 * D])
    w_proj = gathered(in_low[:, 3 * D : 4 * D])
    w_hidden = gathered(in_low[:, 4 * D : ada_at])
    w_second = gathered(w_down[0].astype(low))

    small_low = small_mats.astype(low)
    edge_own = jnp.where(is_first, small_mats[:, :PATCH_IN], small_mats[:, -PATCH_IN:])
    bias_width = b_blk.shape[1]
    pieces = [
        b_blk[0],
        edge_own.reshape(-1),
        timesteps.astype(jnp.float32),
        labels.astype(jnp.float32),
        jnp.sum(patch_mask).astype(jnp.float32)[None],
    ]
    block = jnp.concatenate(pieces)[None]
    blocks = spread(block, "dp", 1)[:, 0]
    ends = [0]
    for piece in pieces:
        ends.append(ends[-1] + piece.shape[0])
    bias_full = rounded(blocks[:, : ends[1]].reshape(-1))
    w_edge = blocks[:, ends[1] : ends[2]].reshape(D, PATCH_IN).astype(low)
    times_all = blocks[:, ends[2] : ends[3]].reshape(-1).astype(jnp.int32)
    labels_all = blocks[:, ends[3] : ends[4]].reshape(-1).astype(jnp.int32)
    valid_total = jnp.sum(blocks[:, ends[4]])
    inv_count = 1.0 / (valid_total * PATCH_IN)
    weights = (w_qkv, w_proj, w_hidden, w_second)

    small_width = small_mats.shape[1]
    sbias_width = small_bias.shape[0]
    extra = -(-sbias_width // small_width)
    sbias_rows = jnp.pad(small_bias, (0, extra * small_width - sbias_width)).astype(low)
    small_block = jnp.concatenate([small_low, sbias_rows.reshape(extra, small_width)], axis=0)
    small_blocks = spread(small_block, "section", 2)
    small_rows = jnp.concatenate([small_blocks[i, :rows] for i in range(sections)], axis=1)
    small_used = (
        small_blocks[:, rows:].reshape(sections, -1)[:, :sbias_width].reshape(-1)
    ).astype(jnp.float32)

    shards = lax.axis_size("dp")
    time_low = time_features(times_all).astype(low)
    one_hot = label_table(labels_all)
    time_hidden = matmul_nt(time_low, small_rows[:, PATCH_IN:o_label]) + lax.dynamic_slice_in_dim(
        small_used, D + row_at, rows, 0
    )
    time_act = jax.nn.silu(time_hidden).astype(low)
    cond_part = matmul(time_act, small_rows[:, o_second:o_film])
    label_part = matmul_nt(one_hot, small_rows[:, o_label:o_second])
    cond_part = jnp.concatenate([cond_part, label_part], axis=1).reshape(shards, images, D + rows)
    cond_got = exchange(cond_part, "dp", 3)
    cond_own = (
        jnp.sum(cond_got[:, :, :D], axis=0)
        + small_used[2 * D : 3 * D]
        + jnp.swapaxes(cond_got[:, :, D:], 0, 1).reshape(images, D)
    )
    cond_cols = exchange(jnp.swapaxes(cond_own.reshape(images, shards, rows), 0, 1), "dp", 4)
    cond_first = cond_cols.reshape(shards * images, rows)
    cond_later = rounded(cond_first)
    cond_here = jnp.where(is_first, cond_first, cond_later)
    act_here = jax.nn.silu(cond_here).astype(low)
    act_later = jax.nn.silu(cond_later).astype(low)
    ada_part = jnp.concatenate(
        [matmul(act_here, w_ada), matmul(act_later, small_rows[:, o_film:o_out])], axis=1
    )
    ada_got = exchange(ada_part.reshape(shards, images * 8 * D // 128, 128), "dp", 5)
    ada_own = jnp.sum(ada_got, axis=0).reshape(images, 8 * D)
    film = ada_own[:, 6 * D :] + small_used[3 * D : 5 * D]
    ada = (ada_own[:, : 6 * D] + bias_full[ada_at:]).reshape(images, 6, D)
    bias_row = jnp.concatenate(
        [bias_full[:D], jnp.zeros((D,), jnp.float32), bias_full[D:ada_at]]
    )[None]

    fade = alpha_bar(timesteps)[:, None, None]
    noisy_low = (jnp.sqrt(fade) * latents + jnp.sqrt(1.0 - fade) * noise).astype(low)
    tokens = jnp.einsum(
        "bpi,di->bpd", noisy_low, w_edge, preferred_element_type=jnp.float32
    )
    tokens = tokens + small_used[:D] + positions(patches)[None]

    def meta_of(raw, edge, tick):
        inside = (raw >= 0) & (raw < images)
        items = [jnp.clip(raw, 0, images - 1), min(tick, images - 1), edge, inside]
        return jnp.stack([jnp.asarray(item, jnp.int32) for item in items])

    ticks = images + sections - 1
    kept_all = []
    arrived = jnp.zeros((patches, D), low)
    for tick in range(ticks):
        meta = meta_of(tick - section_index, is_first, tick)
        output, kept_all = image_forward(meta, arrived, bias_row, ada, tokens, weights, kept_all)
        if tick < ticks - 1:
            arrived = passed_along(output, "section", 1)
    kept_of = {item[0]: whole for item, whole in zip(KEPT, kept_all)}

    squared, head_grad, d_film, g_output, g_out_bias = head_step(
        kept_of["output"],
        film,
        noise,
        patch_mask,
        inv_count,
        w_edge,
        small_used[5 * D :],
    )
    loss_part = jnp.where(is_last, squared * inv_count, 0.0)
    made_all = []
    arrived = jnp.zeros((patches, D), low)
    for tick in range(ticks):
        meta = meta_of(tick - (sections - 1 - section_index), is_last, tick)
        d_low, made_all = image_backward(
            meta, arrived, ada, head_grad, weights, [kept_of[name] for name in READ], made_all
        )
        if tick < ticks - 1:
            arrived = passed_along(d_low, "section", -1)

    def flat(whole):
        return whole.reshape(images * patches, whole.shape[2])

    d_second, d_pre, d_branch, d_qkv, d_tokens = [flat(whole) for whole in made_all[:5]]
    d_ada = made_all[5][:, :6].astype(low).reshape(images, 6 * D)

    token_sums = column_sum(d_tokens)
    g_edge = jnp.where(
        is_first,
        matmul_tn(d_tokens, noisy_low.reshape(images * patches, PATCH_IN)),
        g_output,
    )
    shard_wide, shard_down, right_sums, late, (token_sums, g_edge) = row_sums(
        [flat(kept_of[name]) for name in ("mixed_one", "att", "mixed_two", "act")],
        [d_qkv, d_branch, d_pre, d_second],
        (token_sums, g_edge),
    )
    d_ada, d_film, unused = lax.optimization_barrier((d_ada, d_film, late))
    film_all = spread(d_film, "dp", 6).reshape(shards * images, 2 * D)
    film_all = spread(film_all, "section", 7)[sections - 1]
    d_ada_all = spread(d_ada, "dp", 8).reshape(shards * images, 6 * D)

    cond_piece = matmul_nt(d_ada_all, w_ada) * silu_grad(cond_here)
    cond_pieces = spread(cond_piece, "section", 9)
    d_cond = matmul_nt(film_all, small_rows[:, o_film:o_out]) * silu_grad(cond_later)
    for layer in reversed(range(sections)):
        d_cond = rounded(d_cond + cond_pieces[layer])
    d_cond_rows = d_cond.astype(low)
    d_cond_all = jnp.swapaxes(spread(d_cond_rows, "dp", 10), 0, 1).reshape(shards * images, D)
    d_time = (
        matmul_nt(d_cond_all, small_rows[:, o_second:o_film]) * silu_grad(time_hidden)
    ).astype(low)
    bias_sums = jnp.concatenate(
        [
            right_sums[0][:D],
            right_sums[0][2 * D :],
            right_sums[1],
            right_sums[2],
            right_sums[3],
            column_sum(d_ada),
        ]
    )
    sums = jnp.concatenate(
        [
            bias_sums.reshape(shards, -1),
            g_edge.reshape(shards, -1),
            jnp.broadcast_to(token_sums, (shards, D)),
            jnp.broadcast_to(g_out_bias, (shards, PATCH_IN)),
            jnp.broadcast_to(column_sum(d_time), (shards, rows)),
        ],
        axis=1,
    )
    sums = exchange(sums[:, None], "dp", 11)[:, 0]
    (
        sums,
        d_ada_all,
        d_cond_all,
        d_cond_rows,
        d_time,
        film_all,
        shard_wide,
        shard_down,
    ) = lax.optimization_barrier(
        (sums, d_ada_all, d_cond_all, d_cond_rows, d_time, film_all, shard_wide, shard_down)
    )
    shard_ada = matmul_tn(act_here, d_ada_all)
    shard_in = jnp.concatenate([shard_wide, shard_ada], axis=1)
    edge_end = bias_width + rows * PATCH_IN
    shard_bias = jnp.sum(sums[:, :bias_width], axis=0)
    edge_rows = jnp.sum(sums[:, bias_width:edge_end], axis=0).reshape(rows, PATCH_IN)
    token_sums = jnp.sum(sums[:, edge_end : edge_end + D], axis=0)
    out_sums = jnp.sum(sums[:, edge_end + D : edge_end + D + PATCH_IN], axis=0)
    time_sums = sums[:, edge_end + D + PATCH_IN :].reshape(-1)
    small_grad = jnp.concatenate(
        [
            edge_rows,
            matmul_tn(d_time, time_low),
            matmul_tn(d_cond_rows, one_hot),
            matmul_tn(time_act, d_cond_all),
            matmul_tn(act_later, film_all),
            edge_rows,
        ],
        axis=1,
    )
    small_shard = lax.dynamic_slice_in_dim(small_grad, section_index * small_width, small_width, 1)
    sbias_grad = jnp.concatenate(
        [token_sums, time_sums, column_sum(d_cond_all), column_sum(film_all), out_sums]
    )
    sbias_shard = lax.dynamic_slice_in_dim(
        sbias_grad, section_index * sbias_width, sbias_width, 0
    )

    dp_zero = (dp_index == 0).astype(jnp.float32)
    squares = (
        jnp.sum(shard_in * shard_in)
        + jnp.sum(shard_down * shard_down)
        + jnp.sum(shard_bias * shard_bias)
        + jnp.sum(small_shard * small_shard)
        + dp_zero * jnp.sum(sbias_shard * sbias_shard)
    )
    pair = jnp.broadcast_to(jnp.stack([squares, loss_part])[:, None], (2, 128))
    pair = jnp.sum(spread(pair, "dp", 14), axis=0)
    pair = jnp.sum(spread(pair, "section", 15), axis=0)
    norm_square, loss = (pair[0, 0], pair[1, 0])
    grad_norm = jnp.sqrt(norm_square)
    scaling = jnp.minimum(1.0, CLIP / grad_norm)
    new_in, first_in, second_in = adam_update(w_in, shard_in[None], m_in, v_in, scaling)
    new_down, first_down, second_down = adam_update(
        w_down, shard_down[None], m_down, v_down, scaling
    )
    new_bias, first_bias, second_bias = adam_update(
        b_blk, shard_bias[None], m_bias, v_bias, scaling
    )
    new_small, first_small, second_small = adam_update(
        small_mats, small_shard, m_small, v_small, scaling
    )
    new_sbias, first_sbias, second_sbias = adam_update(
        small_bias, sbias_shard, m_sbias, v_sbias, scaling
    )
    return (
        loss,
        grad_norm,
        new_in,
        first_in,
        second_in,
        new_down,
        first_down,
        second_down,
        new_bias,
        first_bias,
        second_bias,
        new_small,
        first_small,
        second_small,
        new_sbias,
        first_sbias,
        second_sbias,
    )


def solution(mesh):
    in_specs = (
        P("dp", None, None),
        P("dp", None, None),
        P("dp"),
        P("dp"),
        P("dp", None),
        P("section", "dp", None),
        P("section", "dp", None),
        P("section", "dp"),
        P("dp", "section"),
        P("section"),
        P("section", "dp", None),
        P("section", "dp", None),
        P("section", "dp"),
        P("dp", "section"),
        P("section"),
        P("section", "dp", None),
        P("section", "dp", None),
        P("section", "dp"),
        P("dp", "section"),
        P("section"),
    )
    out_specs = (
        P(),
        P(),
        P("section", "dp", None),
        P("section", "dp", None),
        P("section", "dp", None),
        P("section", "dp", None),
        P("section", "dp", None),
        P("section", "dp", None),
        P("section", "dp"),
        P("section", "dp"),
        P("section", "dp"),
        P("dp", "section"),
        P("dp", "section"),
        P("dp", "section"),
        P("section"),
        P("section"),
        P("section"),
    )
    return jax.shard_map(body, mesh=mesh, in_specs=in_specs, out_specs=out_specs, check_vma=False)
```

```python
import functools
import math

import jax
import jax.numpy as jnp
from jax import lax
from jax.experimental import pallas as pl
from jax.experimental.pallas import tpu as pltpu
from jax.sharding import PartitionSpec as P

D = 1152
HEADS = 16
HEAD_DIM = 72
FF = 4608
CLASSES = 1000
FREQ = 256
PATCH_IN = 16
GRID = 16


EPS_NORM = 1e-06
CLIP = 0.001
RATE = 0.005
BETA_ONE = 0.9
BETA_TWO = 0.999
ADAM_EPS = 1e-08
DECAY = 0.01
STEP_POWER = 10.0


def passed_along(value, axis, steps):
    count = lax.axis_size(axis)
    first, last = (max(0, -steps), min(count, count - steps))
    return lax.ppermute(value, axis, [(source, source + steps) for source in range(first, last)])


def matmul(left_side, right_side):
    return jnp.dot(left_side, right_side, preferred_element_type=jnp.float32)


def matmul_tn(left_side, right_side):
    return lax.dot_general(
        left_side, right_side, (((0,), (0,)), ((), ())), preferred_element_type=jnp.float32
    )


def matmul_nt(left_side, right_side):
    return lax.dot_general(
        left_side, right_side, (((1,), (1,)), ((), ())), preferred_element_type=jnp.float32
    )


def column_sum(values):
    return jnp.sum(values.astype(jnp.float32), axis=0)


def normalize(values):
    center = values - jnp.mean(values, axis=-1, keepdims=True)
    invstd = lax.rsqrt(jnp.mean(center * center, axis=-1, keepdims=True) + EPS_NORM)
    return (center * invstd, invstd)


def norm_back(grad_normed, normed, invstd):
    return invstd * (
        grad_normed
        - jnp.mean(grad_normed, axis=-1, keepdims=True)
        - normed * jnp.mean(grad_normed * normed, axis=-1, keepdims=True)
    )


def gelu_tanh(values):
    return (
        0.5
        * values
        * (1.0 + jnp.tanh(0.7978845608028654 * (values + 0.044715 * values * values * values)))
    )


def gelu_grad(values):
    inner = jnp.tanh(0.7978845608028654 * (values + 0.044715 * values * values * values))
    return 0.5 * (1.0 + inner) + 0.5 * values * (1.0 - inner * inner) * 0.7978845608028654 * (
        1.0 + 0.134145 * values * values
    )


def silu_grad(values):
    sigma = jax.nn.sigmoid(values)
    return sigma * (1.0 + values * (1.0 - sigma))


def positions(patches):
    quarter = D // 4
    omega = jnp.exp(-math.log(10000.0) * jnp.arange(quarter, dtype=jnp.float32) / quarter)
    spot = jnp.arange(patches, dtype=jnp.int32)
    row_angle = (spot // GRID).astype(jnp.float32)[:, None] * omega[None, :]
    col_angle = (spot % GRID).astype(jnp.float32)[:, None] * omega[None, :]
    return jnp.concatenate(
        [jnp.sin(row_angle), jnp.cos(row_angle), jnp.sin(col_angle), jnp.cos(col_angle)], axis=1
    )


def time_features(time_steps):
    half = FREQ // 2
    freqs = jnp.exp(-math.log(10000.0) * jnp.arange(half, dtype=jnp.float32) / half)
    angles = time_steps.astype(jnp.float32)[:, None] * freqs[None, :]
    return jnp.concatenate([jnp.cos(angles), jnp.sin(angles)], axis=1)


def alpha_bar(time_steps):
    return jnp.cos((time_steps.astype(jnp.float32) / 1000.0 + 0.008) / 1.008 * (math.pi / 2)) ** 2


def label_table(label_part):
    return (label_part[:, None] == jnp.arange(CLASSES, dtype=jnp.int32)[None, :]).astype(
        jnp.bfloat16
    )


MESH = pl.DeviceIdType.MESH
DIRECT = 8


def rounded(values):
    return lax.reduce_precision(values, 8, 7)


def meet(axis, count, here):
    barrier = pltpu.get_barrier_semaphore()
    for step in range(1, count):
        pl.semaphore_signal(
            barrier, inc=1, device_id={axis: lax.rem(here + step, count)}, device_id_type=MESH
        )
    pl.semaphore_wait(barrier, count - 1)


def share_kernel(axis, count, personal, in_ref, out_ref, send_sem, recv_sem):
    here = lax.axis_index(axis)
    meet(axis, count, here)
    copies = []
    for step in range(1, count):
        target = lax.rem(here + step, count)
        copy = pltpu.make_async_remote_copy(
            src_ref=in_ref.at[target] if personal else in_ref,
            dst_ref=out_ref.at[here],
            send_sem=send_sem.at[step - 1],
            recv_sem=recv_sem.at[step - 1],
            device_id={axis: target},
            device_id_type=MESH,
        )
        copy.start()
        copies.append(copy)
    out_ref[here] = in_ref[here] if personal else in_ref[...]
    for copy in copies:
        copy.wait()


def share(value, axis, personal, ident):
    count = lax.axis_size(axis)
    shape = value.shape if personal else (count,) + value.shape
    return pl.pallas_call(
        functools.partial(share_kernel, axis, count, personal),
        out_shape=jax.ShapeDtypeStruct(shape, value.dtype),
        in_specs=[pl.BlockSpec(memory_space=pltpu.VMEM)],
        out_specs=pl.BlockSpec(memory_space=pltpu.VMEM),
        scratch_shapes=[
            pltpu.SemaphoreType.DMA((count - 1,)),
            pltpu.SemaphoreType.DMA((count - 1,)),
        ],
        compiler_params=pltpu.CompilerParams(collective_id=ident, has_side_effects=True),
        name="share",
    )(value)


def spread(value, axis, ident):
    if lax.axis_size(axis) > DIRECT:
        return lax.all_gather(value, axis)
    return share(value, axis, False, ident)


def exchange(value, axis, ident):
    if lax.axis_size(axis) > DIRECT:
        return lax.all_to_all(value, axis, 0, 0)
    return share(value, axis, True, ident)


def products_kernel(units, rows, extra, *refs):
    lefts, rights, given = (refs[:4], refs[4:8], refs[8 : 8 + extra])
    refs = refs[8 + extra :]
    own_out, block_outs, bias_out, spread_out = (refs[0], refs[1:4], refs[4], refs[5 : 5 + extra])
    refs = refs[5 + extra :]
    (
        left_v,
        right_v,
        product,
        got,
        own_v,
        low_v,
        left_sem,
        right_sem,
        send_sem,
        recv_sem,
        own_sem,
        low_sem,
    ) = refs[:12]
    here = lax.axis_index("dp")
    core, chip = (lax.rem(here, 2), here // 2)
    chips = 4
    partner = {"dp": here + 1 - 2 * core}
    spreading = []
    if extra:
        count = 2 * chips
        meet("dp", count, here)
        for step in range(1, count):
            copy = pltpu.make_async_remote_copy(
                src_ref=given[0],
                dst_ref=spread_out[0].at[here],
                send_sem=refs[12].at[step - 1],
                recv_sem=refs[13].at[step - 1],
                device_id={"dp": lax.rem(here + step, count)},
                device_id_type=MESH,
            )
            copy.start()
            spreading.append(copy)
        spread_out[0][here] = given[0][...]
    else:
        barrier = pltpu.get_barrier_semaphore()
        pl.semaphore_signal(barrier, inc=1, device_id=partner, device_id_type=MESH)
        pl.semaphore_wait(barrier, 1)
    tall = chips * rows
    plan, last = ([], [None, None])
    slots = [1, 1]
    for left, left_at, right, right_at, gathers in units:
        fresh = []
        for side, key in enumerate(((left, left_at), (right, right_at))):
            fresh.append(last[side] != key)
            if fresh[-1]:
                slots[side] = 1 - slots[side]
                last[side] = key
        plan.append((tuple(slots), tuple(fresh)))

    def loads_of(index):
        left, left_at, right, right_at, gathers = units[index]
        (left_slot, right_slot), (left_fresh, right_fresh) = plan[index]
        copies = []
        if left_fresh:
            copies.append(
                pltpu.make_async_copy(
                    lefts[left].at[:, pl.ds(left_at, D)], left_v.at[left_slot], left_sem.at[left_slot]
                )
            )
        if right_fresh:
            copies.append(
                pltpu.make_async_copy(
                    rights[right].at[:, pl.ds(right_at, D)],
                    right_v.at[right_slot],
                    right_sem.at[right_slot],
                )
            )
        return copies

    def to_partner(source, target, sems):
        copy = pltpu.make_async_remote_copy(
            src_ref=source,
            dst_ref=target,
            send_sem=send_sem.at[sems],
            recv_sem=recv_sem.at[sems],
            device_id=partner,
            device_id_type=MESH,
        )
        copy.start()
        return copy

    pending, crossing, leaving = ({}, {}, {})

    def load(index):
        pending[index] = loads_of(index)
        for copy in pending[index]:
            copy.start()

    def multiply(index):
        gathers = units[index][4]
        left_slot, right_slot = plan[index][0]
        for copy in pending[index]:
            copy.wait()
        if index + 1 < len(units):
            load(index + 1)
        if index >= 2:
            for copy in crossing[index - 2]:
                copy.wait_send()
        slot, place = (index % 2, index % 4)
        product[slot] = lax.dot_general(
            left_v[left_slot],
            right_v[right_slot],
            (((0,), (0,)), ((), ())),
            preferred_element_type=jnp.float32,
        )
        if plan[index][1][1]:
            ones = jnp.ones((8, right_v.shape[1]), jnp.bfloat16)
            bias_out[index] = matmul(ones, right_v[right_slot])
        if gathers is None:
            crossing[index] = [
                to_partner(
                    product.at[slot, pl.ds(pl.multiple_of((2 * i + 1 - core) * rows, 8), rows)],
                    got.at[place, pl.ds(i * rows, rows)],
                    place * chips + i,
                )
                for i in range(chips)
            ]
        else:
            crossing[index] = [
                to_partner(
                    product.at[slot, pl.ds(pl.multiple_of((1 - core) * tall, 8), tall)],
                    got.at[place],
                    place * chips,
                )
            ]

    def combine(index):
        gathers = units[index][4]
        slot, place, side = (index % 2, index % 4, index % 2)
        for copy in crossing[index]:
            copy.wait_recv()
        if index >= 2:
            finish(index - 2)
        at_slot = slot_of[index]
        if gathers is None:
            for step in range(chips):
                other = lax.rem(chip + step, chips)
                value = (
                    product[slot, pl.ds(pl.multiple_of((2 * other + core) * rows, 8), rows)]
                    + got[place, pl.ds(pl.multiple_of(other * rows, 8), rows)]
                )
                if step == 0:
                    own_v[side, 0:rows] = value
                else:
                    low_v[side, (step - 1) * rows : step * rows] = value.astype(jnp.bfloat16)
            copies = [
                pltpu.make_async_copy(
                    own_v.at[side, pl.ds(0, rows)], own_out.at[at_slot], own_sem.at[side]
                )
            ]
            for step in range(1, chips):
                copies.append(
                    pltpu.make_async_copy(
                        low_v.at[side, pl.ds((step - 1) * rows, rows)],
                        block_outs[step - 1].at[at_slot],
                        low_sem.at[side, step - 1],
                    )
                )
            for copy in copies:
                copy.start()
            leaving[index] = [(None, copies)]
        else:
            step_here = lax.rem(gathers + chips - chip, chips)
            cases = []
            for step in range(chips):
                held = own_v if step == 0 else low_v
                out = own_out if step == 0 else block_outs[step - 1]
                sem = own_sem.at[side] if step == 0 else low_sem.at[side, step - 1]
                copies = [
                    pltpu.make_async_copy(
                        held.at[side, pl.ds(i * rows, rows)],
                        out.at[at_slot + i],
                        sem if i == 0 else more_sem(step, side, i),
                    )
                    for i in range(chips)
                ]
                cases.append((step_here == step, copies))

                @pl.when(step_here == step)
                def put(held=held, copies=copies):
                    value = product[slot, pl.ds(pl.multiple_of(core * tall, 8), tall)] + got[place]
                    held[side] = value.astype(held.dtype)
                    for copy in copies:
                        copy.start()

            leaving[index] = cases

    def more_sem(step, side, i):
        return own_sem.at[2 + side * 3 + i - 1] if step == 0 else low_sem.at[side, 3 * i + step - 1]

    def finish(index):
        for condition, copies in leaving[index]:
            if condition is None:
                for copy in copies:
                    copy.wait()
            else:

                @pl.when(condition)
                def settle(copies=copies):
                    for copy in copies:
                        copy.wait()

    slot_of, used = ({}, 0)
    for index, unit in enumerate(units):
        slot_of[index] = used
        if unit[4] is None:
            used += 1
    load(0)
    multiply(0)
    for index in range(len(units)):
        if index + 1 < len(units):
            multiply(index + 1)
        combine(index)
    for index in range(max(0, len(units) - 2), len(units)):
        finish(index)
        for copy in crossing[index]:
            copy.wait_send()
    for copy in spreading:
        copy.wait()


def chip_products(units, lefts, rights, rows, ident, given=()):
    tokens = lefts[0].shape[0]
    places = sum(unit[4] is None for unit in units) + 4 * any(unit[4] is not None for unit in units)
    outs = pl.pallas_call(
        functools.partial(products_kernel, units, rows, len(given)),
        out_shape=[jax.ShapeDtypeStruct((places, rows, D), jnp.float32)]
        + [jax.ShapeDtypeStruct((places, rows, D), jnp.bfloat16) for unused in range(3)]
        + [jax.ShapeDtypeStruct((len(units), 8, D), jnp.float32)]
        + [jax.ShapeDtypeStruct((DIRECT,) + one.shape, one.dtype) for one in given],
        in_specs=specs("h" * 8, "v" * len(given)),
        out_specs=specs("h" * 4, "v", "v" * len(given)),
        scratch_shapes=[
            pltpu.VMEM((2, tokens, D), jnp.bfloat16),
            pltpu.VMEM((2, tokens, D), jnp.bfloat16),
            pltpu.VMEM((2, 8 * rows, D), jnp.float32),
            pltpu.VMEM((4, 4 * rows, D), jnp.float32),
            pltpu.VMEM((2, 4 * rows, D), jnp.float32),
            pltpu.VMEM((2, 4 * rows, D), jnp.bfloat16),
            pltpu.SemaphoreType.DMA((2,)),
            pltpu.SemaphoreType.DMA((2,)),
            pltpu.SemaphoreType.DMA((16,)),
            pltpu.SemaphoreType.DMA((16,)),
            pltpu.SemaphoreType.DMA((8,)),
            pltpu.SemaphoreType.DMA((2, 12)),
        ]
        + [pltpu.SemaphoreType.DMA((DIRECT - 1,))] * (2 * len(given)),
        compiler_params=pltpu.CompilerParams(
            collective_id=ident, has_side_effects=True, vmem_limit_bytes=60 << 20
        ),
        cost_estimate=pl.CostEstimate(
            flops=2 * tokens * D * D * len(units),
            bytes_accessed=len(units) * tokens * D * 4,
            transcendentals=0,
        ),
        name="chip_products",
    )(*lefts, *rights, *given)
    return (outs[0], outs[1:4], outs[4][:, 0], outs[5:])


def row_sums(lefts, rights, early, given):
    count = lax.axis_size("dp")
    if count != DIRECT:
        products = [matmul_tn(one, other) for one, other in zip(lefts, rights)]
        sums = [lax.psum_scatter(one, "dp", scatter_dimension=0, tiled=True) for one in products]
        wide = jnp.concatenate([sums[0], sums[1], sums[2]], axis=1)
        given = lax.all_gather(given, "dp")
        biases = [column_sum(one) for one in rights]
        return (wide, sums[3], biases, products[3], early, given)
    rows = D // count
    chips = count // 2
    parts = FF // D
    first = [(0, 0, 0, i * D, None) for i in range(3)] + [(1, 0, 1, 0, None)]
    rest = [(2, 0, 2, i * D, None) for i in range(parts)] + [
        (3, i * D, 3, 0, i) for i in range(parts)
    ]
    totals, biases, tied, given_all = ([], [], None, None)
    for ident, units in ((12, first), (13, rest)):
        if tied is not None:
            lefts, rights, tied, early = lax.optimization_barrier((lefts, rights, tied, early))
        total, blocks, bias, shared = chip_products(
            tuple(units), lefts, rights, rows, ident, (given,) if tied is None else ()
        )
        given_all = shared[0] if tied is None else given_all
        for step in range(1, chips):
            arrived = lax.ppermute(
                blocks[step - 1], "dp", [(i, (i + 2 * step) % count) for i in range(count)]
            )
            total = total + arrived.astype(jnp.float32)
        tied = blocks
        totals.append(total)
        biases.append(bias)
    wide = [totals[0][i] for i in range(4)] + [totals[1][i] for i in range(parts)]
    sums = [biases[0][:3].reshape(-1), biases[0][3], biases[1][:parts].reshape(-1), biases[1][parts]]
    late = (tied, totals[0])
    down = totals[1][parts:].reshape(-1, D)
    return (jnp.concatenate(wide, axis=1), down, sums, late, early, given_all)


GROUP = 4


def contract(left_side, right_side, left_axis, right_axis):
    return lax.dot_general(
        left_side,
        right_side,
        (((left_axis,), (right_axis,)), ((), ())),
        preferred_element_type=jnp.float32,
    )


def heads_of(ref, at, group):
    return [
        ref[at + head * HEAD_DIM : at + (head + 1) * HEAD_DIM] for head in group
    ]


def softmax_down(scores):
    weights = jnp.exp(scores - jnp.max(scores, axis=0, keepdims=True))
    return weights * (1.0 / jnp.sum(weights, axis=0, keepdims=True))


def stacked(values):
    return jnp.concatenate([value.astype(jnp.bfloat16) for value in values], axis=0)


def attend_kernel(qkv_ref, out_ref):
    scaling = HEAD_DIM ** (-0.5)
    for first in range(0, HEADS, GROUP):
        group = range(first, first + GROUP)
        rows = slice(first * HEAD_DIM, (first + GROUP) * HEAD_DIM)
        queries, keys = (heads_of(qkv_ref, 0, group), heads_of(qkv_ref, D, group))
        values = heads_of(qkv_ref, 2 * D, group)
        scores = [contract(key, query, 0, 0) * scaling for key, query in zip(keys, queries)]
        probs = [softmax_down(score).astype(jnp.bfloat16) for score in scores]
        out_ref[rows] = stacked([contract(v, p, 1, 0) for v, p in zip(values, probs)])


def attend_back_kernel(qkv_ref, grad_ref, out_ref):
    scaling = HEAD_DIM ** (-0.5)
    for first in range(0, HEADS, GROUP):
        group = range(first, first + GROUP)
        at, to = (first * HEAD_DIM, (first + GROUP) * HEAD_DIM)
        queries, keys = (heads_of(qkv_ref, 0, group), heads_of(qkv_ref, D, group))
        values, grads = (heads_of(qkv_ref, 2 * D, group), heads_of(grad_ref, 0, group))
        scores = [contract(key, query, 0, 0) * scaling for key, query in zip(keys, queries)]
        d_probs = [contract(value, grad, 0, 0) for value, grad in zip(values, grads)]
        probs = [softmax_down(score) for score in scores]
        d_scores = [
            (p * (d - jnp.sum(p * d, axis=0, keepdims=True))).astype(jnp.bfloat16)
            for p, d in zip(probs, d_probs)
        ]
        lows = [p.astype(jnp.bfloat16) for p in probs]
        out_ref[at:to] = stacked([contract(k, d, 1, 0) * scaling for k, d in zip(keys, d_scores)])
        out_ref[D + at : D + to] = stacked(
            [contract(q, d, 1, 1) * scaling for q, d in zip(queries, d_scores)]
        )
        out_ref[2 * D + at : 2 * D + to] = stacked(
            [contract(g, p, 1, 1) for g, p in zip(grads, lows)]
        )


ROW_BLOCK = 64
KEPT = (
    ("residual", D, jnp.float32),
    ("mixed_one", D, jnp.bfloat16),
    ("qkv", 3 * D, jnp.bfloat16),
    ("att", D, jnp.bfloat16),
    ("branch", D, jnp.float32),
    ("middle", D, jnp.float32),
    ("mixed_two", D, jnp.bfloat16),
    ("pre", FF, jnp.float32),
    ("act", FF, jnp.bfloat16),
    ("second", D, jnp.float32),
    ("output", D, jnp.float32),
)
READ = ("residual", "qkv", "branch", "middle", "pre", "second")
MADE = (
    ("d_second", D, jnp.bfloat16),
    ("d_pre", FF, jnp.bfloat16),
    ("d_branch", D, jnp.bfloat16),
    ("d_qkv", 3 * D, jnp.bfloat16),
    ("d_residual", D, jnp.bfloat16),
)
WEIGHTS = ((D, 3 * D), (D, D), (D, FF), (FF, D))


def kept_shape(name, width, kind, patches):
    return (width, patches) if name == "qkv" else (patches, width)


def by_rows(patches, step):
    @pl.loop(0, patches // ROW_BLOCK)
    def run(index):
        step(pl.ds(pl.multiple_of(index * ROW_BLOCK, ROW_BLOCK), ROW_BLOCK))


def started(source, target, sem):
    copy = pltpu.make_async_copy(source, target, sem)
    copy.start()
    return copy


def forward_kernel(
    patches, given, meta, arrived, bias, qkv_bias, ada, tokens, wq, wp, wh, ws, *refs
):
    count = len(KEPT)
    send, outs = (refs[given], refs[given + 1 : given + 1 + count])
    scratch = refs[given + 1 + count :]
    kept = {name: scratch[i] for i, (name, unused, kind) in enumerate(KEPT)}
    att_down, wq_v, wp_v, wh_v, ws_v, w_sem, x_sem, out_sem = scratch[count:]
    loads = [started(wq.at[:, pl.ds(i * D, D)], wq_v.at[:, pl.ds(i * D, D)], w_sem.at[i]) for i in range(3)]
    loads.append(started(wp, wp_v, w_sem.at[3]))
    loads += [
        started(wh.at[:, pl.ds(i * D, D)], wh_v.at[:, pl.ds(i * D, D)], w_sem.at[4 + i])
        for i in range(FF // D)
    ]
    third = D // 3
    loads += [
        started(ws.at[:, pl.ds(i * third, third)], ws_v.at[:, pl.ds(i * third, third)], w_sem.at[8 + i])
        for i in range(3)
    ]
    saves = []

    def start_if_valid(copy):
        @pl.when(meta[3] == 1)
        def start():
            copy.start()

    def save(name):
        index = [item[0] for item in KEPT].index(name)
        saves.append(pltpu.make_async_copy(kept[name], outs[index].at[meta[0]], out_sem.at[index]))
        start_if_valid(saves[-1])

    residual = kept["residual"]

    @pl.when(meta[2] == 1)
    def take_tokens():
        started(tokens.at[meta[1]], residual, x_sem).wait()

    @pl.when(meta[2] == 0)
    def take_arrived():
        residual[...] = arrived[...].astype(jnp.float32)

    save("residual")
    modulation = ada[meta[0]]

    def mix_one(at):
        normed, unused = normalize(residual[at])
        kept["mixed_one"][at] = (normed * (1.0 + modulation[1:2]) + modulation[0:1]).astype(
            jnp.bfloat16
        )

    by_rows(patches, mix_one)
    save("mixed_one")
    for part in range(3):
        loads[part].wait()
        cols = slice(part * D, part * D + D)
        kept["qkv"][cols] = (
            contract(wq_v[:, cols], kept["mixed_one"][...], 0, 1) + qkv_bias[cols]
        ).astype(jnp.bfloat16)
    save("qkv")
    attend_kernel(kept["qkv"], att_down)
    loads[3].wait()
    kept["branch"][...] = contract(att_down[...], wp_v[...], 0, 0) + bias[:, :D]
    kept["att"][...] = att_down[...].T
    save("branch")
    save("att")
    for load in loads[4:]:
        load.wait()

    def mix_two(at):
        middle = residual[at] + modulation[2:3] * kept["branch"][at]
        kept["middle"][at] = middle
        normed, unused = normalize(middle)
        kept["mixed_two"][at] = (normed * (1.0 + modulation[4:5]) + modulation[3:4]).astype(
            jnp.bfloat16
        )

    by_rows(patches, mix_two)
    save("middle")
    save("mixed_two")
    for part in range(FF // D):
        cols = slice(part * D, part * D + D)
        pre = (
            matmul(kept["mixed_two"][...], wh_v[:, cols])
            + bias[:, D + part * D : 2 * D + part * D]
        )
        kept["pre"][:, cols] = pre
        kept["act"][:, cols] = gelu_tanh(pre).astype(jnp.bfloat16)
    save("pre")
    save("act")
    for part in range(3):
        cols = slice(part * third, part * third + third)
        second = (
            matmul(kept["act"][...], ws_v[:, cols])
            + bias[:, D + FF + part * third : D + FF + part * third + third]
        )
        kept["second"][:, cols] = second
        output = kept["middle"][:, cols] + modulation[5:6, cols] * second
        kept["output"][:, cols] = output
        send[:, cols] = output.astype(jnp.bfloat16)
    save("second")
    save("output")

    @pl.when(meta[3] == 1)
    def finish():
        for copy in saves:
            copy.wait()


def backward_kernel(patches, given, meta, arrived, ada, head_grad, wq, wp, wh, ws, *refs):
    reads, made = (len(READ), len(MADE))
    sources, refs = (refs[:reads], refs[reads + given :])
    send, outs, ada_out = (refs[0], refs[1 : made + 1], refs[made + 1])
    scratch = refs[made + 2 :]
    kept = {name: scratch[i] for i, name in enumerate(READ)}
    grads = {name: scratch[reads + i] for i, (name, unused, kind) in enumerate(MADE)}
    (
        flow,
        mixed,
        att_grad,
        qkv_grad,
        sums,
        wq_v,
        wp_v,
        wh_v,
        ws_v,
        w_sem,
        in_sem,
        x_sem,
        out_sem,
    ) = scratch[reads + made :]

    def fetch(name):
        index = READ.index(name)
        return started(sources[index].at[meta[0]], kept[name], in_sem.at[index])

    fetched = {"second": fetch("second")}
    loads = [started(ws.at[pl.ds(i * D, D)], ws_v.at[pl.ds(i * D, D)], w_sem.at[i]) for i in range(FF // D)]
    for name in ("pre", "middle", "branch", "qkv", "residual"):
        fetched[name] = fetch(name)
    third = D // 3
    loads += [
        started(wh.at[pl.ds(i * third, third)], wh_v.at[pl.ds(i * third, third)], w_sem.at[4 + i])
        for i in range(3)
    ]
    loads.append(started(wp, wp_v, w_sem.at[7]))
    loads += [
        started(wq.at[pl.ds(i * third, third)], wq_v.at[pl.ds(i * third, third)], w_sem.at[8 + i])
        for i in range(3)
    ]
    saves = []

    def start_if_valid(copy):
        @pl.when(meta[3] == 1)
        def start():
            copy.start()

    def save(name):
        index = [item[0] for item in MADE].index(name)
        saves.append(pltpu.make_async_copy(grads[name], outs[index].at[meta[0]], out_sem.at[index]))
        start_if_valid(saves[-1])

    @pl.when(meta[2] == 1)
    def take_head():
        started(head_grad.at[meta[1]], flow, x_sem).wait()

    @pl.when(meta[2] == 0)
    def take_arrived():
        flow[...] = arrived[...].astype(jnp.float32)

    modulation = ada[meta[0]]
    sums[...] = jnp.zeros_like(sums)

    def add_sum(row, values):
        sums[row : row + 1] += jnp.sum(values, axis=0, keepdims=True)

    fetched["second"].wait()

    def open_second(at):
        grad = flow[at]
        grads["d_second"][at] = (grad * modulation[5:6]).astype(jnp.bfloat16)
        add_sum(5, grad * kept["second"][at])

    by_rows(patches, open_second)
    save("d_second")
    fetched["pre"].wait()
    for load in loads[:4]:
        load.wait()
    for part in range(FF // D):
        cols = slice(part * D, part * D + D)
        grads["d_pre"][:, cols] = (
            matmul_nt(grads["d_second"][...], ws_v[cols]) * gelu_grad(kept["pre"][:, cols])
        ).astype(jnp.bfloat16)
    save("d_pre")
    for load in loads[4:7]:
        load.wait()
    for part in range(3):
        cols = slice(part * third, part * third + third)
        mixed[:, cols] = matmul_nt(grads["d_pre"][...], wh_v[cols])
    fetched["middle"].wait()
    fetched["branch"].wait()

    def through_two(at):
        normed, invstd = normalize(kept["middle"][at])
        grad = mixed[at]
        add_sum(3, grad)
        add_sum(4, grad * normed)
        total = flow[at] + norm_back(grad * (1.0 + modulation[4:5]), normed, invstd)
        flow[at] = total
        add_sum(2, total * kept["branch"][at])
        grads["d_branch"][at] = (total * modulation[2:3]).astype(jnp.bfloat16)

    by_rows(patches, through_two)
    save("d_branch")
    loads[7].wait()
    att_grad[...] = contract(wp_v[...], grads["d_branch"][...], 1, 1).astype(jnp.bfloat16)
    fetched["qkv"].wait()
    attend_back_kernel(kept["qkv"], att_grad, qkv_grad)
    for load in loads[8:]:
        load.wait()
    for part in range(3):
        cols = slice(part * third, part * third + third)
        mixed[:, cols] = contract(qkv_grad[...], wq_v[cols], 0, 1)
    grads["d_qkv"][...] = qkv_grad[...].T
    save("d_qkv")
    fetched["residual"].wait()

    def through_one(at):
        normed, invstd = normalize(kept["residual"][at])
        grad = mixed[at]
        add_sum(0, grad)
        add_sum(1, grad * normed)
        total = flow[at] + norm_back(grad * (1.0 + modulation[1:2]), normed, invstd)
        low = total.astype(jnp.bfloat16)
        grads["d_residual"][at] = low
        send[at] = low

    by_rows(patches, through_one)
    save("d_residual")
    saves.append(pltpu.make_async_copy(sums, ada_out.at[meta[0]], x_sem))
    start_if_valid(saves[-1])

    @pl.when(meta[3] == 1)
    def finish():
        for copy in saves:
            copy.wait()


def specs(*spaces):
    return [
        pl.BlockSpec(memory_space={"s": pltpu.SMEM, "v": pltpu.VMEM, "h": pl.ANY}[space])
        for space in "".join(spaces)
    ]


def weight_scratch():
    return [pltpu.VMEM(shape, jnp.bfloat16) for shape in WEIGHTS] + [
        pltpu.SemaphoreType.DMA((11,))
    ]


def block_cost(patches, factor):
    area = sum(rows * columns for rows, columns in WEIGHTS)
    return pl.CostEstimate(
        flops=2 * patches * area + factor * patches * patches * D,
        bytes_accessed=2 * area + 64 * patches * D,
        transcendentals=patches * (FF + HEADS * patches),
    )


def image_forward(meta, arrived, bias, qkv_bias, ada, tokens, weights, buffers):
    patches, given, count = (arrived.shape[0], len(buffers), len(KEPT))
    sizes = [item + (patches,) for item in KEPT]
    images = ada.shape[0]
    outs = pl.pallas_call(
        functools.partial(forward_kernel, patches, given),
        out_shape=[jax.ShapeDtypeStruct((patches, D), jnp.bfloat16)]
        + [jax.ShapeDtypeStruct((images,) + kept_shape(*item), item[2]) for item in sizes],
        in_specs=specs("svvvv", "h" * (5 + given)),
        out_specs=specs("v", "h" * count),
        scratch_shapes=[pltpu.VMEM(kept_shape(*item), item[2]) for item in sizes]
        + [pltpu.VMEM((D, patches), jnp.bfloat16)]
        + weight_scratch()
        + [pltpu.SemaphoreType.DMA, pltpu.SemaphoreType.DMA((count,))],
        input_output_aliases={10 + i: 1 + i for i in range(given)},
        compiler_params=pltpu.CompilerParams(vmem_limit_bytes=60 << 20),
        cost_estimate=block_cost(patches, 4),
        name="image_forward",
    )(meta, arrived, bias, qkv_bias, ada, tokens, *weights, *buffers)
    return (outs[0], outs[1:])


def image_backward(meta, arrived, ada, head_grad, weights, sources, buffers):
    patches, given, images = (arrived.shape[0], len(buffers), ada.shape[0])
    reads, made = (len(READ), len(MADE))
    kinds = {name: (width, kind) for name, width, kind in KEPT}
    outs = pl.pallas_call(
        functools.partial(backward_kernel, patches, given),
        out_shape=[jax.ShapeDtypeStruct((patches, D), jnp.bfloat16)]
        + [jax.ShapeDtypeStruct((images, patches, width), kind) for unused, width, kind in MADE]
        + [jax.ShapeDtypeStruct((images, 8, D), jnp.float32)],
        in_specs=specs("svv", "h" * (5 + reads + given)),
        out_specs=specs("v", "h" * (made + 1)),
        scratch_shapes=[
            pltpu.VMEM(kept_shape(name, *kinds[name], patches), kinds[name][1]) for name in READ
        ]
        + [pltpu.VMEM((patches, width), kind) for unused, width, kind in MADE]
        + [
            pltpu.VMEM((patches, D), jnp.float32),
            pltpu.VMEM((patches, D), jnp.float32),
            pltpu.VMEM((D, patches), jnp.bfloat16),
            pltpu.VMEM((3 * D, patches), jnp.bfloat16),
            pltpu.VMEM((8, D), jnp.float32),
        ]
        + weight_scratch()
        + [
            pltpu.SemaphoreType.DMA((reads,)),
            pltpu.SemaphoreType.DMA,
            pltpu.SemaphoreType.DMA((made,)),
        ],
        input_output_aliases={8 + reads + i: 1 + i for i in range(given)},
        compiler_params=pltpu.CompilerParams(vmem_limit_bytes=60 << 20),
        cost_estimate=block_cost(patches, 10),
        name="image_backward",
    )(meta, arrived, ada, head_grad, *weights, *sources, *buffers)
    return (outs[0], outs[1:])


def head_step(residual, film, noise_part, mask_part, inv_count, w_out, b_out):
    shifting, scaling = (film[:, :D], film[:, D:])
    normed, invstd = normalize(residual)
    mixed = (normed * (1.0 + scaling[:, None]) + shifting[:, None]).astype(jnp.bfloat16)
    output = (
        jnp.einsum("bpd,dj->bpj", mixed, w_out, preferred_element_type=jnp.float32) + b_out
    )
    mismatch = output - noise_part
    mask_float = mask_part.astype(jnp.float32)[:, :, None]
    squared = jnp.sum(mask_float * mismatch * mismatch)
    d_output = (2.0 * inv_count * mask_float * mismatch).astype(jnp.bfloat16)
    g_output = jnp.einsum("bpd,bpj->dj", mixed, d_output, preferred_element_type=jnp.float32)
    d_mixed = jnp.einsum("bpj,dj->bpd", d_output, w_out, preferred_element_type=jnp.float32)
    d_film = jnp.concatenate(
        [jnp.sum(d_mixed, axis=1), jnp.sum(d_mixed * normed, axis=1)], axis=1
    ).astype(jnp.bfloat16)
    d_residual = norm_back(d_mixed * (1.0 + scaling[:, None]), normed, invstd)
    g_bias = jnp.sum(d_output.astype(jnp.float32), axis=(0, 1))
    return (squared, d_residual, d_film, g_output, g_bias)


def adam_update(weight, gradient, first_moment, second_moment, scaling):
    gradient = gradient * scaling
    first_new = BETA_ONE * first_moment + (1.0 - BETA_ONE) * gradient
    second_new = BETA_TWO * second_moment + (1.0 - BETA_TWO) * gradient * gradient
    ratio = (
        first_new
        / (1.0 - BETA_ONE**STEP_POWER)
        / (jnp.sqrt(second_new / (1.0 - BETA_TWO**STEP_POWER)) + ADAM_EPS)
    )
    return (weight - RATE * (ratio + DECAY * weight), first_new, second_new)


def body(
    latents,
    noise,
    timesteps,
    labels,
    patch_mask,
    w_in,
    w_down,
    b_blk,
    small_mats,
    small_bias,
    m_in,
    m_down,
    m_bias,
    m_small,
    m_sbias,
    v_in,
    v_down,
    v_bias,
    v_small,
    v_sbias,
):
    section_index = lax.axis_index("section")
    dp_index = lax.axis_index("dp")
    sections = lax.axis_size("section")
    is_first = section_index == 0
    is_last = section_index == sections - 1
    low = jnp.bfloat16
    images, patches = patch_mask.shape
    rows = w_in.shape[1]
    row_at = dp_index * rows
    ada_at = 4 * D + FF
    o_label = PATCH_IN + FREQ
    o_second = o_label + CLASSES
    o_film = o_second + D
    o_out = o_film + 2 * D

    def gathered(value, axis="dp", dim=0):
        return lax.all_gather(value, axis, axis=dim, tiled=True)

    in_low = w_in[0].astype(low)
    w_ada = in_low[:, ada_at:]
    w_qkv = gathered(in_low[:, : 3 * D])
    w_proj = gathered(in_low[:, 3 * D : 4 * D])
    w_hidden = gathered(in_low[:, 4 * D : ada_at])
    w_second = gathered(w_down[0].astype(low))

    small_low = small_mats.astype(low)
    edge_own = jnp.where(is_first, small_mats[:, :PATCH_IN], small_mats[:, -PATCH_IN:])
    bias_width = b_blk.shape[1]
    pieces = [
        b_blk[0],
        edge_own.reshape(-1),
        timesteps.astype(jnp.float32),
        labels.astype(jnp.float32),
        jnp.sum(patch_mask).astype(jnp.float32)[None],
    ]
    block = jnp.concatenate(pieces)[None]
    blocks = spread(block, "dp", 1)[:, 0]
    ends = [0]
    for piece in pieces:
        ends.append(ends[-1] + piece.shape[0])
    bias_full = rounded(blocks[:, : ends[1]].reshape(-1))
    w_edge = blocks[:, ends[1] : ends[2]].reshape(D, PATCH_IN).astype(low)
    times_all = blocks[:, ends[2] : ends[3]].reshape(-1).astype(jnp.int32)
    labels_all = blocks[:, ends[3] : ends[4]].reshape(-1).astype(jnp.int32)
    valid_total = jnp.sum(blocks[:, ends[4]])
    inv_count = 1.0 / (valid_total * PATCH_IN)
    weights = (w_qkv, w_proj, w_hidden, w_second)

    small_width = small_mats.shape[1]
    sbias_width = small_bias.shape[0]
    extra = -(-sbias_width // small_width)
    sbias_rows = jnp.pad(small_bias, (0, extra * small_width - sbias_width)).astype(low)
    small_block = jnp.concatenate([small_low, sbias_rows.reshape(extra, small_width)], axis=0)
    small_blocks = spread(small_block, "section", 2)
    small_rows = jnp.concatenate([small_blocks[i, :rows] for i in range(sections)], axis=1)
    small_used = (
        small_blocks[:, rows:].reshape(sections, -1)[:, :sbias_width].reshape(-1)
    ).astype(jnp.float32)

    shards = lax.axis_size("dp")
    time_low = time_features(times_all).astype(low)
    one_hot = label_table(labels_all)
    time_hidden = matmul_nt(time_low, small_rows[:, PATCH_IN:o_label]) + lax.dynamic_slice_in_dim(
        small_used, D + row_at, rows, 0
    )
    time_act = jax.nn.silu(time_hidden).astype(low)
    cond_part = matmul(time_act, small_rows[:, o_second:o_film])
    label_part = matmul_nt(one_hot, small_rows[:, o_label:o_second])
    cond_part = jnp.concatenate([cond_part, label_part], axis=1).reshape(shards, images, D + rows)
    cond_got = exchange(cond_part, "dp", 3)
    cond_own = (
        jnp.sum(cond_got[:, :, :D], axis=0)
        + small_used[2 * D : 3 * D]
        + jnp.swapaxes(cond_got[:, :, D:], 0, 1).reshape(images, D)
    )
    cond_cols = exchange(jnp.swapaxes(cond_own.reshape(images, shards, rows), 0, 1), "dp", 4)
    cond_first = cond_cols.reshape(shards * images, rows)
    cond_later = rounded(cond_first)
    cond_here = jnp.where(is_first, cond_first, cond_later)
    act_here = jax.nn.silu(cond_here).astype(low)
    act_later = jax.nn.silu(cond_later).astype(low)
    ada_part = jnp.concatenate(
        [matmul(act_here, w_ada), matmul(act_later, small_rows[:, o_film:o_out])], axis=1
    )
    ada_got = exchange(ada_part.reshape(shards, images * 8 * D // 128, 128), "dp", 5)
    ada_own = jnp.sum(ada_got, axis=0).reshape(images, 8 * D)
    film = ada_own[:, 6 * D :] + small_used[3 * D : 5 * D]
    ada = (ada_own[:, : 6 * D] + bias_full[ada_at:]).reshape(images, 6, D)
    qkv_bias = jnp.concatenate(
        [bias_full[:D], jnp.zeros((D,), jnp.float32), bias_full[D : 2 * D]]
    )[:, None]
    bias_row = bias_full[None, 2 * D : ada_at]

    fade = alpha_bar(timesteps)[:, None, None]
    noisy_low = (jnp.sqrt(fade) * latents + jnp.sqrt(1.0 - fade) * noise).astype(low)
    tokens = jnp.einsum(
        "bpi,di->bpd", noisy_low, w_edge, preferred_element_type=jnp.float32
    )
    tokens = tokens + small_used[:D] + positions(patches)[None]

    def meta_of(raw, edge, tick):
        inside = (raw >= 0) & (raw < images)
        items = [jnp.clip(raw, 0, images - 1), min(tick, images - 1), edge, inside]
        return jnp.stack([jnp.asarray(item, jnp.int32) for item in items])

    ticks = images + sections - 1
    kept_all = []
    arrived = jnp.zeros((patches, D), low)
    for tick in range(ticks):
        meta = meta_of(tick - section_index, is_first, tick)
        output, kept_all = image_forward(
            meta, arrived, bias_row, qkv_bias, ada, tokens, weights, kept_all
        )
        if tick < ticks - 1:
            arrived = passed_along(output, "section", 1)
    kept_of = {item[0]: whole for item, whole in zip(KEPT, kept_all)}

    squared, head_grad, d_film, g_output, g_out_bias = head_step(
        kept_of["output"],
        film,
        noise,
        patch_mask,
        inv_count,
        w_edge,
        small_used[5 * D :],
    )
    loss_part = jnp.where(is_last, squared * inv_count, 0.0)
    made_all = []
    arrived = jnp.zeros((patches, D), low)
    for tick in range(ticks):
        meta = meta_of(tick - (sections - 1 - section_index), is_last, tick)
        d_low, made_all = image_backward(
            meta, arrived, ada, head_grad, weights, [kept_of[name] for name in READ], made_all
        )
        if tick < ticks - 1:
            arrived = passed_along(d_low, "section", -1)
        if tick == 1:
            film_all = lax.optimization_barrier((d_film, d_low))[0]
            film_all = spread(film_all, "dp", 6).reshape(shards * images, 2 * D)
        elif tick == 2:
            film_all = lax.optimization_barrier((film_all, d_low))[0]
            film_all = spread(film_all, "section", 7)[sections - 1]
        if tick in (1, 2):
            arrived, film_all = lax.optimization_barrier((arrived, film_all))

    def flat(whole):
        return whole.reshape(images * patches, whole.shape[2])

    d_second, d_pre, d_branch, d_qkv, d_tokens = [flat(whole) for whole in made_all[:5]]
    d_ada = made_all[5][:, :6].astype(low).reshape(images, 6 * D)

    token_sums = column_sum(d_tokens)
    g_edge = jnp.where(
        is_first,
        matmul_tn(d_tokens, noisy_low.reshape(images * patches, PATCH_IN)),
        g_output,
    )
    shard_wide, shard_down, right_sums, late, (token_sums, g_edge), d_ada_all = row_sums(
        [flat(kept_of[name]) for name in ("mixed_one", "att", "mixed_two", "act")],
        [d_qkv, d_branch, d_pre, d_second],
        (token_sums, g_edge),
        d_ada,
    )
    d_ada, d_ada_all, unused = lax.optimization_barrier((d_ada, d_ada_all, late))
    d_ada_all = d_ada_all.reshape(shards * images, 6 * D)

    cond_piece = matmul_nt(d_ada_all, w_ada) * silu_grad(cond_here)
    cond_pieces = spread(cond_piece, "section", 9)
    d_cond = matmul_nt(film_all, small_rows[:, o_film:o_out]) * silu_grad(cond_later)
    for layer in reversed(range(sections)):
        d_cond = rounded(d_cond + cond_pieces[layer])
    d_cond_rows = d_cond.astype(low)
    d_cond_all = jnp.swapaxes(spread(d_cond_rows, "dp", 10), 0, 1).reshape(shards * images, D)
    d_time = (
        matmul_nt(d_cond_all, small_rows[:, o_second:o_film]) * silu_grad(time_hidden)
    ).astype(low)
    bias_sums = jnp.concatenate(
        [
            right_sums[0][:D],
            right_sums[0][2 * D :],
            right_sums[1],
            right_sums[2],
            right_sums[3],
            column_sum(d_ada),
        ]
    )
    sums = jnp.concatenate(
        [
            bias_sums.reshape(shards, -1),
            g_edge.reshape(shards, -1),
            jnp.broadcast_to(token_sums, (shards, D)),
            jnp.broadcast_to(g_out_bias, (shards, PATCH_IN)),
            jnp.broadcast_to(column_sum(d_time), (shards, rows)),
        ],
        axis=1,
    )
    sums = exchange(sums[:, None], "dp", 11)[:, 0]
    (
        sums,
        d_ada_all,
        d_cond_all,
        d_cond_rows,
        d_time,
        film_all,
        shard_wide,
        shard_down,
    ) = lax.optimization_barrier(
        (sums, d_ada_all, d_cond_all, d_cond_rows, d_time, film_all, shard_wide, shard_down)
    )
    shard_ada = matmul_tn(act_here, d_ada_all)
    shard_in = jnp.concatenate([shard_wide, shard_ada], axis=1)
    edge_end = bias_width + rows * PATCH_IN
    shard_bias = jnp.sum(sums[:, :bias_width], axis=0)
    edge_rows = jnp.sum(sums[:, bias_width:edge_end], axis=0).reshape(rows, PATCH_IN)
    token_sums = jnp.sum(sums[:, edge_end : edge_end + D], axis=0)
    out_sums = jnp.sum(sums[:, edge_end + D : edge_end + D + PATCH_IN], axis=0)
    time_sums = sums[:, edge_end + D + PATCH_IN :].reshape(-1)
    small_grad = jnp.concatenate(
        [
            edge_rows,
            matmul_tn(d_time, time_low),
            matmul_tn(d_cond_rows, one_hot),
            matmul_tn(time_act, d_cond_all),
            matmul_tn(act_later, film_all),
            edge_rows,
        ],
        axis=1,
    )
    small_shard = lax.dynamic_slice_in_dim(small_grad, section_index * small_width, small_width, 1)
    sbias_grad = jnp.concatenate(
        [token_sums, time_sums, column_sum(d_cond_all), column_sum(film_all), out_sums]
    )
    sbias_shard = lax.dynamic_slice_in_dim(
        sbias_grad, section_index * sbias_width, sbias_width, 0
    )

    dp_zero = (dp_index == 0).astype(jnp.float32)
    squares = (
        jnp.sum(shard_in * shard_in)
        + jnp.sum(shard_down * shard_down)
        + jnp.sum(shard_bias * shard_bias)
        + jnp.sum(small_shard * small_shard)
        + dp_zero * jnp.sum(sbias_shard * sbias_shard)
    )
    pair = jnp.broadcast_to(jnp.stack([squares, loss_part])[:, None], (2, 128))
    pair = jnp.sum(spread(pair, "dp", 14), axis=0)
    pair = jnp.sum(spread(pair, "section", 15), axis=0)
    norm_square, loss = (pair[0, 0], pair[1, 0])
    grad_norm = jnp.sqrt(norm_square)
    scaling = jnp.minimum(1.0, CLIP / grad_norm)
    new_in, first_in, second_in = adam_update(w_in, shard_in[None], m_in, v_in, scaling)
    new_down, first_down, second_down = adam_update(
        w_down, shard_down[None], m_down, v_down, scaling
    )
    new_bias, first_bias, second_bias = adam_update(
        b_blk, shard_bias[None], m_bias, v_bias, scaling
    )
    new_small, first_small, second_small = adam_update(
        small_mats, small_shard, m_small, v_small, scaling
    )
    new_sbias, first_sbias, second_sbias = adam_update(
        small_bias, sbias_shard, m_sbias, v_sbias, scaling
    )
    return (
        loss,
        grad_norm,
        new_in,
        first_in,
        second_in,
        new_down,
        first_down,
        second_down,
        new_bias,
        first_bias,
        second_bias,
        new_small,
        first_small,
        second_small,
        new_sbias,
        first_sbias,
        second_sbias,
    )


def solution(mesh):
    in_specs = (
        P("dp", None, None),
        P("dp", None, None),
        P("dp"),
        P("dp"),
        P("dp", None),
        P("section", "dp", None),
        P("section", "dp", None),
        P("section", "dp"),
        P("dp", "section"),
        P("section"),
        P("section", "dp", None),
        P("section", "dp", None),
        P("section", "dp"),
        P("dp", "section"),
        P("section"),
        P("section", "dp", None),
        P("section", "dp", None),
        P("section", "dp"),
        P("dp", "section"),
        P("section"),
    )
    out_specs = (
        P(),
        P(),
        P("section", "dp", None),
        P("section", "dp", None),
        P("section", "dp", None),
        P("section", "dp", None),
        P("section", "dp", None),
        P("section", "dp", None),
        P("section", "dp"),
        P("section", "dp"),
        P("section", "dp"),
        P("dp", "section"),
        P("dp", "section"),
        P("dp", "section"),
        P("section"),
        P("section"),
        P("section"),
    )
    return jax.shard_map(body, mesh=mesh, in_specs=in_specs, out_specs=out_specs, check_vma=False)
```

```python
import functools
import math

import jax
import jax.numpy as jnp
from jax import lax
from jax.experimental import pallas as pl
from jax.experimental.pallas import tpu as pltpu
from jax.sharding import PartitionSpec as P

D = 1152
HEADS = 16
HEAD_DIM = 72
FF = 4608
CLASSES = 1000
FREQ = 256
PATCH_IN = 16
GRID = 16


EPS_NORM = 1e-06
CLIP = 0.001
RATE = 0.005
BETA_ONE = 0.9
BETA_TWO = 0.999
ADAM_EPS = 1e-08
DECAY = 0.01
STEP_POWER = 10.0


def passed_along(value, axis, steps):
    count = lax.axis_size(axis)
    first, last = (max(0, -steps), min(count, count - steps))
    return lax.ppermute(value, axis, [(source, source + steps) for source in range(first, last)])


def matmul(left_side, right_side):
    return jnp.dot(left_side, right_side, preferred_element_type=jnp.float32)


def matmul_tn(left_side, right_side):
    return lax.dot_general(
        left_side, right_side, (((0,), (0,)), ((), ())), preferred_element_type=jnp.float32
    )


def matmul_nt(left_side, right_side):
    return lax.dot_general(
        left_side, right_side, (((1,), (1,)), ((), ())), preferred_element_type=jnp.float32
    )


def column_sum(values):
    return jnp.sum(values.astype(jnp.float32), axis=0)


def normalize(values):
    center = values - jnp.mean(values, axis=-1, keepdims=True)
    invstd = lax.rsqrt(jnp.mean(center * center, axis=-1, keepdims=True) + EPS_NORM)
    return (center * invstd, invstd)


def norm_back(grad_normed, normed, invstd):
    return invstd * (
        grad_normed
        - jnp.mean(grad_normed, axis=-1, keepdims=True)
        - normed * jnp.mean(grad_normed * normed, axis=-1, keepdims=True)
    )


def gelu_tanh(values):
    return (
        0.5
        * values
        * (1.0 + jnp.tanh(0.7978845608028654 * (values + 0.044715 * values * values * values)))
    )


def gelu_grad(values):
    inner = jnp.tanh(0.7978845608028654 * (values + 0.044715 * values * values * values))
    return 0.5 * (1.0 + inner) + 0.5 * values * (1.0 - inner * inner) * 0.7978845608028654 * (
        1.0 + 0.134145 * values * values
    )


def silu_grad(values):
    sigma = jax.nn.sigmoid(values)
    return sigma * (1.0 + values * (1.0 - sigma))


def positions(patches):
    quarter = D // 4
    omega = jnp.exp(-math.log(10000.0) * jnp.arange(quarter, dtype=jnp.float32) / quarter)
    spot = jnp.arange(patches, dtype=jnp.int32)
    row_angle = (spot // GRID).astype(jnp.float32)[:, None] * omega[None, :]
    col_angle = (spot % GRID).astype(jnp.float32)[:, None] * omega[None, :]
    return jnp.concatenate(
        [jnp.sin(row_angle), jnp.cos(row_angle), jnp.sin(col_angle), jnp.cos(col_angle)], axis=1
    )


def time_features(time_steps):
    half = FREQ // 2
    freqs = jnp.exp(-math.log(10000.0) * jnp.arange(half, dtype=jnp.float32) / half)
    angles = time_steps.astype(jnp.float32)[:, None] * freqs[None, :]
    return jnp.concatenate([jnp.cos(angles), jnp.sin(angles)], axis=1)


def alpha_bar(time_steps):
    return jnp.cos((time_steps.astype(jnp.float32) / 1000.0 + 0.008) / 1.008 * (math.pi / 2)) ** 2


def label_table(label_part):
    return (label_part[:, None] == jnp.arange(CLASSES, dtype=jnp.int32)[None, :]).astype(
        jnp.bfloat16
    )


MESH = pl.DeviceIdType.MESH
DIRECT = 8


def rounded(values):
    return lax.reduce_precision(values, 8, 7)


def meet(axis, count, here):
    barrier = pltpu.get_barrier_semaphore()
    for step in range(1, count):
        pl.semaphore_signal(
            barrier, inc=1, device_id={axis: lax.rem(here + step, count)}, device_id_type=MESH
        )
    pl.semaphore_wait(barrier, count - 1)


def share_kernel(axis, count, personal, in_ref, out_ref, send_sem, recv_sem):
    here = lax.axis_index(axis)
    meet(axis, count, here)
    copies = []
    for step in range(1, count):
        target = lax.rem(here + step, count)
        copy = pltpu.make_async_remote_copy(
            src_ref=in_ref.at[target] if personal else in_ref,
            dst_ref=out_ref.at[here],
            send_sem=send_sem.at[step - 1],
            recv_sem=recv_sem.at[step - 1],
            device_id={axis: target},
            device_id_type=MESH,
        )
        copy.start()
        copies.append(copy)
    out_ref[here] = in_ref[here] if personal else in_ref[...]
    for copy in copies:
        copy.wait()


def share(value, axis, personal, ident):
    count = lax.axis_size(axis)
    shape = value.shape if personal else (count,) + value.shape
    return pl.pallas_call(
        functools.partial(share_kernel, axis, count, personal),
        out_shape=jax.ShapeDtypeStruct(shape, value.dtype),
        in_specs=[pl.BlockSpec(memory_space=pltpu.VMEM)],
        out_specs=pl.BlockSpec(memory_space=pltpu.VMEM),
        scratch_shapes=[
            pltpu.SemaphoreType.DMA((count - 1,)),
            pltpu.SemaphoreType.DMA((count - 1,)),
        ],
        compiler_params=pltpu.CompilerParams(collective_id=ident, has_side_effects=True),
        name="share",
    )(value)


def spread(value, axis, ident):
    if lax.axis_size(axis) > DIRECT:
        return lax.all_gather(value, axis)
    return share(value, axis, False, ident)


def exchange(value, axis, ident):
    if lax.axis_size(axis) > DIRECT:
        return lax.all_to_all(value, axis, 0, 0)
    return share(value, axis, True, ident)


def products_kernel(units, rows, extra, *refs):
    lefts, rights, given = (refs[:4], refs[4:8], refs[8 : 8 + extra])
    refs = refs[8 + extra :]
    own_out, block_outs, bias_out, spread_out = (refs[0], refs[1:4], refs[4], refs[5 : 5 + extra])
    refs = refs[5 + extra :]
    (
        left_v,
        right_v,
        product,
        got,
        own_v,
        low_v,
        left_sem,
        right_sem,
        send_sem,
        recv_sem,
        own_sem,
        low_sem,
    ) = refs[:12]
    here = lax.axis_index("dp")
    core, chip = (lax.rem(here, 2), here // 2)
    chips = 4
    partner = {"dp": here + 1 - 2 * core}
    spreading = []
    if extra:
        count = 2 * chips
        meet("dp", count, here)
        for step in range(1, count):
            copy = pltpu.make_async_remote_copy(
                src_ref=given[0],
                dst_ref=spread_out[0].at[here],
                send_sem=refs[12].at[step - 1],
                recv_sem=refs[13].at[step - 1],
                device_id={"dp": lax.rem(here + step, count)},
                device_id_type=MESH,
            )
            copy.start()
            spreading.append(copy)
        spread_out[0][here] = given[0][...]
    else:
        barrier = pltpu.get_barrier_semaphore()
        pl.semaphore_signal(barrier, inc=1, device_id=partner, device_id_type=MESH)
        pl.semaphore_wait(barrier, 1)
    tall = chips * rows
    plan, last = ([], [None, None])
    slots = [1, 1]
    for left, left_at, right, right_at, gathers in units:
        fresh = []
        for side, key in enumerate(((left, left_at), (right, right_at))):
            fresh.append(last[side] != key)
            if fresh[-1]:
                slots[side] = 1 - slots[side]
                last[side] = key
        plan.append((tuple(slots), tuple(fresh)))

    def loads_of(index):
        left, left_at, right, right_at, gathers = units[index]
        (left_slot, right_slot), (left_fresh, right_fresh) = plan[index]
        copies = []
        if left_fresh:
            copies.append(
                pltpu.make_async_copy(
                    lefts[left].at[:, pl.ds(left_at, D)], left_v.at[left_slot], left_sem.at[left_slot]
                )
            )
        if right_fresh:
            copies.append(
                pltpu.make_async_copy(
                    rights[right].at[:, pl.ds(right_at, D)],
                    right_v.at[right_slot],
                    right_sem.at[right_slot],
                )
            )
        return copies

    def to_partner(source, target, sems):
        copy = pltpu.make_async_remote_copy(
            src_ref=source,
            dst_ref=target,
            send_sem=send_sem.at[sems],
            recv_sem=recv_sem.at[sems],
            device_id=partner,
            device_id_type=MESH,
        )
        copy.start()
        return copy

    pending, crossing, leaving = ({}, {}, {})

    def load(index):
        pending[index] = loads_of(index)
        for copy in pending[index]:
            copy.start()

    def multiply(index):
        gathers = units[index][4]
        left_slot, right_slot = plan[index][0]
        for copy in pending[index]:
            copy.wait()
        if index + 1 < len(units):
            load(index + 1)
        if index >= 2:
            for copy in crossing[index - 2]:
                copy.wait_send()
        slot, place = (index % 2, index % 4)
        product[slot] = lax.dot_general(
            left_v[left_slot],
            right_v[right_slot],
            (((0,), (0,)), ((), ())),
            preferred_element_type=jnp.float32,
        )
        if plan[index][1][1]:
            ones = jnp.ones((8, right_v.shape[1]), jnp.bfloat16)
            bias_out[index] = matmul(ones, right_v[right_slot])
        if gathers is None:
            crossing[index] = [
                to_partner(
                    product.at[slot, pl.ds(pl.multiple_of((2 * i + 1 - core) * rows, 8), rows)],
                    got.at[place, pl.ds(i * rows, rows)],
                    place * chips + i,
                )
                for i in range(chips)
            ]
        else:
            crossing[index] = [
                to_partner(
                    product.at[slot, pl.ds(pl.multiple_of((1 - core) * tall, 8), tall)],
                    got.at[place],
                    place * chips,
                )
            ]

    def combine(index):
        gathers = units[index][4]
        slot, place, side = (index % 2, index % 4, index % 2)
        for copy in crossing[index]:
            copy.wait_recv()
        if index >= 2:
            finish(index - 2)
        at_slot = slot_of[index]
        if gathers is None:
            for step in range(chips):
                other = lax.rem(chip + step, chips)
                value = (
                    product[slot, pl.ds(pl.multiple_of((2 * other + core) * rows, 8), rows)]
                    + got[place, pl.ds(pl.multiple_of(other * rows, 8), rows)]
                )
                if step == 0:
                    own_v[side, 0:rows] = value
                else:
                    low_v[side, (step - 1) * rows : step * rows] = value.astype(jnp.bfloat16)
            copies = [
                pltpu.make_async_copy(
                    own_v.at[side, pl.ds(0, rows)], own_out.at[at_slot], own_sem.at[side]
                )
            ]
            for step in range(1, chips):
                copies.append(
                    pltpu.make_async_copy(
                        low_v.at[side, pl.ds((step - 1) * rows, rows)],
                        block_outs[step - 1].at[at_slot],
                        low_sem.at[side, step - 1],
                    )
                )
            for copy in copies:
                copy.start()
            leaving[index] = [(None, copies)]
        else:
            step_here = lax.rem(gathers + chips - chip, chips)
            cases = []
            for step in range(chips):
                held = own_v if step == 0 else low_v
                out = own_out if step == 0 else block_outs[step - 1]
                sem = own_sem.at[side] if step == 0 else low_sem.at[side, step - 1]
                copies = [
                    pltpu.make_async_copy(
                        held.at[side, pl.ds(i * rows, rows)],
                        out.at[at_slot + i],
                        sem if i == 0 else more_sem(step, side, i),
                    )
                    for i in range(chips)
                ]
                cases.append((step_here == step, copies))

                @pl.when(step_here == step)
                def put(held=held, copies=copies):
                    value = product[slot, pl.ds(pl.multiple_of(core * tall, 8), tall)] + got[place]
                    held[side] = value.astype(held.dtype)
                    for copy in copies:
                        copy.start()

            leaving[index] = cases

    def more_sem(step, side, i):
        return own_sem.at[2 + side * 3 + i - 1] if step == 0 else low_sem.at[side, 3 * i + step - 1]

    def finish(index):
        for condition, copies in leaving[index]:
            if condition is None:
                for copy in copies:
                    copy.wait()
            else:

                @pl.when(condition)
                def settle(copies=copies):
                    for copy in copies:
                        copy.wait()

    slot_of, used = ({}, 0)
    for index, unit in enumerate(units):
        slot_of[index] = used
        if unit[4] is None:
            used += 1
    load(0)
    multiply(0)
    for index in range(len(units)):
        if index + 1 < len(units):
            multiply(index + 1)
        combine(index)
    for index in range(max(0, len(units) - 2), len(units)):
        finish(index)
        for copy in crossing[index]:
            copy.wait_send()
    for copy in spreading:
        copy.wait()


def chip_products(units, lefts, rights, rows, ident, given=()):
    tokens = lefts[0].shape[0]
    places = sum(unit[4] is None for unit in units) + 4 * any(unit[4] is not None for unit in units)
    outs = pl.pallas_call(
        functools.partial(products_kernel, units, rows, len(given)),
        out_shape=[jax.ShapeDtypeStruct((places, rows, D), jnp.float32)]
        + [jax.ShapeDtypeStruct((places, rows, D), jnp.bfloat16) for unused in range(3)]
        + [jax.ShapeDtypeStruct((len(units), 8, D), jnp.float32)]
        + [jax.ShapeDtypeStruct((DIRECT,) + one.shape, one.dtype) for one in given],
        in_specs=specs("h" * 8, "v" * len(given)),
        out_specs=specs("h" * 4, "v", "v" * len(given)),
        scratch_shapes=[
            pltpu.VMEM((2, tokens, D), jnp.bfloat16),
            pltpu.VMEM((2, tokens, D), jnp.bfloat16),
            pltpu.VMEM((2, 8 * rows, D), jnp.float32),
            pltpu.VMEM((4, 4 * rows, D), jnp.float32),
            pltpu.VMEM((2, 4 * rows, D), jnp.float32),
            pltpu.VMEM((2, 4 * rows, D), jnp.bfloat16),
            pltpu.SemaphoreType.DMA((2,)),
            pltpu.SemaphoreType.DMA((2,)),
            pltpu.SemaphoreType.DMA((16,)),
            pltpu.SemaphoreType.DMA((16,)),
            pltpu.SemaphoreType.DMA((8,)),
            pltpu.SemaphoreType.DMA((2, 12)),
        ]
        + [pltpu.SemaphoreType.DMA((DIRECT - 1,))] * (2 * len(given)),
        compiler_params=pltpu.CompilerParams(
            collective_id=ident, has_side_effects=True, vmem_limit_bytes=60 << 20
        ),
        cost_estimate=pl.CostEstimate(
            flops=2 * tokens * D * D * len(units),
            bytes_accessed=len(units) * tokens * D * 4,
            transcendentals=0,
        ),
        name="chip_products",
    )(*lefts, *rights, *given)
    return (outs[0], outs[1:4], outs[4][:, 0], outs[5:])


def row_sums(lefts, rights, early, given):
    count = lax.axis_size("dp")
    if count != DIRECT:
        products = [matmul_tn(one, other) for one, other in zip(lefts, rights)]
        sums = [lax.psum_scatter(one, "dp", scatter_dimension=0, tiled=True) for one in products]
        wide = jnp.concatenate([sums[0], sums[1], sums[2]], axis=1)
        given = lax.all_gather(given, "dp")
        biases = [column_sum(one) for one in rights]
        return (wide, sums[3], biases, products[3], early, given)
    rows = D // count
    chips = count // 2
    parts = FF // D
    first = [(0, 0, 0, i * D, None) for i in range(3)] + [(1, 0, 1, 0, None)]
    rest = [(2, 0, 2, i * D, None) for i in range(parts)] + [
        (3, i * D, 3, 0, i) for i in range(parts)
    ]
    totals, biases, tied, given_all = ([], [], None, None)
    for ident, units in ((12, first), (13, rest)):
        if tied is not None:
            lefts, rights, tied, early = lax.optimization_barrier((lefts, rights, tied, early))
        total, blocks, bias, shared = chip_products(
            tuple(units), lefts, rights, rows, ident, (given,) if tied is None else ()
        )
        given_all = shared[0] if tied is None else given_all
        for step in range(1, chips):
            arrived = lax.ppermute(
                blocks[step - 1], "dp", [(i, (i + 2 * step) % count) for i in range(count)]
            )
            total = total + arrived.astype(jnp.float32)
        tied = blocks
        totals.append(total)
        biases.append(bias)
    wide = [totals[0][i] for i in range(4)] + [totals[1][i] for i in range(parts)]
    sums = [biases[0][:3].reshape(-1), biases[0][3], biases[1][:parts].reshape(-1), biases[1][parts]]
    late = (tied, totals[0])
    down = totals[1][parts:].reshape(-1, D)
    return (jnp.concatenate(wide, axis=1), down, sums, late, early, given_all)


GROUP = 4


def contract(left_side, right_side, left_axis, right_axis):
    return lax.dot_general(
        left_side,
        right_side,
        (((left_axis,), (right_axis,)), ((), ())),
        preferred_element_type=jnp.float32,
    )


def heads_of(ref, at, group):
    return [
        ref[at + head * HEAD_DIM : at + (head + 1) * HEAD_DIM] for head in group
    ]


def softmax_down(scores):
    weights = jnp.exp(scores - jnp.max(scores, axis=0, keepdims=True))
    return weights * (1.0 / jnp.sum(weights, axis=0, keepdims=True))


def stacked(values):
    return jnp.concatenate([value.astype(jnp.bfloat16) for value in values], axis=0)


def attend_kernel(qkv_ref, out_ref):
    scaling = HEAD_DIM ** (-0.5)
    for first in range(0, HEADS, GROUP):
        group = range(first, first + GROUP)
        rows = slice(first * HEAD_DIM, (first + GROUP) * HEAD_DIM)
        queries, keys = (heads_of(qkv_ref, 0, group), heads_of(qkv_ref, D, group))
        values = heads_of(qkv_ref, 2 * D, group)
        scores = [contract(key, query, 0, 0) * scaling for key, query in zip(keys, queries)]
        probs = [softmax_down(score).astype(jnp.bfloat16) for score in scores]
        out_ref[rows] = stacked([contract(v, p, 1, 0) for v, p in zip(values, probs)])


def attend_back_kernel(qkv_ref, grad_ref, out_ref):
    scaling = HEAD_DIM ** (-0.5)
    for first in range(0, HEADS, GROUP):
        group = range(first, first + GROUP)
        at, to = (first * HEAD_DIM, (first + GROUP) * HEAD_DIM)
        queries, keys = (heads_of(qkv_ref, 0, group), heads_of(qkv_ref, D, group))
        values, grads = (heads_of(qkv_ref, 2 * D, group), heads_of(grad_ref, 0, group))
        scores = [contract(key, query, 0, 0) * scaling for key, query in zip(keys, queries)]
        d_probs = [contract(value, grad, 0, 0) for value, grad in zip(values, grads)]
        probs = [softmax_down(score) for score in scores]
        d_scores = [
            (p * (d - jnp.sum(p * d, axis=0, keepdims=True))).astype(jnp.bfloat16)
            for p, d in zip(probs, d_probs)
        ]
        lows = [p.astype(jnp.bfloat16) for p in probs]
        out_ref[at:to] = stacked([contract(k, d, 1, 0) * scaling for k, d in zip(keys, d_scores)])
        out_ref[D + at : D + to] = stacked(
            [contract(q, d, 1, 1) * scaling for q, d in zip(queries, d_scores)]
        )
        out_ref[2 * D + at : 2 * D + to] = stacked(
            [contract(g, p, 1, 1) for g, p in zip(grads, lows)]
        )


ROW_BLOCK = 64
HOPS = 3
RESIDUAL, MIXED_ONE, QKV, ATT, BRANCH, MIDDLE = range(6)
MIXED_TWO, PRE, ACT, SECOND, OUTPUT = range(6, 11)
D_SECOND, D_PRE, D_BRANCH, D_QKV, D_RESIDUAL = range(5)
WIDE, LOW = (jnp.float32, jnp.bfloat16)
KEPT = (
    (D, WIDE),
    (D, LOW),
    (3 * D, LOW),
    (D, LOW),
    (D, WIDE),
    (D, WIDE),
    (D, LOW),
    (FF, WIDE),
    (FF, LOW),
    (D, WIDE),
    (D, WIDE),
)
READ = (RESIDUAL, QKV, BRANCH, MIDDLE, PRE, SECOND)
MADE = ((D, LOW), (FF, LOW), (D, LOW), (3 * D, LOW), (D, LOW))
WEIGHTS = ((D, 3 * D), (D, D), (D, FF), (FF, D))


def kept_shape(name, width, patches):
    return (width, patches) if name == QKV else (patches, width)


def by_rows(patches, step):
    @pl.loop(0, patches // ROW_BLOCK)
    def run(index):
        step(pl.ds(pl.multiple_of(index * ROW_BLOCK, ROW_BLOCK), ROW_BLOCK))


def started(source, target, sem):
    copy = pltpu.make_async_copy(source, target, sem)
    copy.start()
    return copy


def parts_of(whole, parts):
    width = whole // parts
    return [slice(part * width, part * width + width) for part in range(parts)]


def wait_first(image, loads):
    @pl.when(image == 0)
    def wait():
        for load in loads:
            load.wait()


def hop_of(send, received, send_sem, recv_sem, target):
    def hop(image, part):
        cols = pl.ds(part * (D // HOPS), D // HOPS)
        return pltpu.make_async_remote_copy(
            src_ref=send.at[image, :, cols],
            dst_ref=received.at[image, :, cols],
            send_sem=send_sem.at[image, part],
            recv_sem=recv_sem.at[image, part],
            device_id={"section": target},
            device_id_type=MESH,
        )

    return hop


def forward_kernel(sections, images, bias, qkv_bias, ada, tokens, wq, wp, wh, ws, *refs):
    count, patches = (len(KEPT), tokens.shape[1])
    outs, scratch = (refs[:count], refs[count:])
    kept = scratch[:count]
    (
        att_down,
        send,
        received,
        wq_v,
        wp_v,
        wh_v,
        ws_v,
        w_sem,
        x_sem,
        out_sem,
        send_sem,
        recv_sem,
    ) = scratch[count:]
    section = lax.axis_index("section")
    loads = [
        started(wq.at[:, cols], wq_v.at[:, cols], w_sem.at[i])
        for i, cols in enumerate(parts_of(3 * D, 3))
    ]
    loads.append(started(wp, wp_v, w_sem.at[3]))
    loads.append(started(wh, wh_v, w_sem.at[4]))
    loads.append(started(ws, ws_v, w_sem.at[5]))
    meet("section", sections, section)
    hop = hop_of(send, received, send_sem, recv_sem, lax.rem(section + 1, sections))
    residual = kept[RESIDUAL]

    @pl.loop(0, images)
    def run(image):
        saves = []

        def save(name):
            saves.append(started(kept[name], outs[name].at[image], out_sem.at[name]))

        @pl.when(section == 0)
        def take_tokens():
            started(tokens.at[image], residual, x_sem).wait()

        @pl.when(section > 0)
        def take_received():
            for part in range(HOPS):
                hop(image, part).wait_recv()
            residual[...] = received[image].astype(jnp.float32)

        save(RESIDUAL)
        modulation = ada[image]

        def mix_one(at):
            normed, unused = normalize(residual[at])
            kept[MIXED_ONE][at] = (normed * (1.0 + modulation[1:2]) + modulation[0:1]).astype(
                jnp.bfloat16
            )

        by_rows(patches, mix_one)
        save(MIXED_ONE)
        wait_first(image, loads[:3])
        for cols in parts_of(3 * D, 3):
            kept[QKV][cols] = (
                contract(wq_v[:, cols], kept[MIXED_ONE][...], 0, 1) + qkv_bias[cols]
            ).astype(jnp.bfloat16)
        save(QKV)
        attend_kernel(kept[QKV], att_down)
        wait_first(image, loads[3:4])
        kept[BRANCH][...] = contract(att_down[...], wp_v[...], 0, 0) + bias[:, :D]
        kept[ATT][...] = att_down[...].T
        save(BRANCH)
        save(ATT)

        def mix_two(at):
            middle = residual[at] + modulation[2:3] * kept[BRANCH][at]
            kept[MIDDLE][at] = middle
            normed, unused = normalize(middle)
            kept[MIXED_TWO][at] = (normed * (1.0 + modulation[4:5]) + modulation[3:4]).astype(
                jnp.bfloat16
            )

        by_rows(patches, mix_two)
        save(MIDDLE)
        save(MIXED_TWO)
        wait_first(image, loads[4:5])
        for part, cols in enumerate(parts_of(FF, FF // D)):
            pre = (
                matmul(kept[MIXED_TWO][...], wh_v[:, cols])
                + bias[:, D + part * D : 2 * D + part * D]
            )
            kept[PRE][:, cols] = pre
            kept[ACT][:, cols] = gelu_tanh(pre).astype(jnp.bfloat16)
        save(PRE)
        save(ACT)
        wait_first(image, loads[5:])
        for part, cols in enumerate(parts_of(D, HOPS)):
            second = (
                matmul(kept[ACT][...], ws_v[:, cols])
                + bias[:, D + FF + cols.start : D + FF + cols.stop]
            )
            kept[SECOND][:, cols] = second
            output = kept[MIDDLE][:, cols] + modulation[5:6, cols] * second
            kept[OUTPUT][:, cols] = output
            send[image, :, cols] = output.astype(jnp.bfloat16)

            @pl.when(section < sections - 1)
            def pass_on(part=part):
                hop(image, part).start()

        save(SECOND)
        save(OUTPUT)
        for copy in saves:
            copy.wait()

    @pl.when(section < sections - 1)
    def finish():
        for image in range(images):
            for part in range(HOPS):
                hop(image, part).wait_send()


def backward_kernel(sections, images, direct, ada, head_grad, wq, wp, wh, ws, *refs):
    reads, made, patches = (len(READ), len(MADE), head_grad.shape[1])
    sources, refs = (refs[:reads], refs[reads:])
    if direct:
        film, refs = (refs[0], refs[1:])
    outs, ada_out, refs = (refs[:made], refs[made], refs[made + 1 :])
    if direct:
        film_rows, film_out, refs = (refs[0], refs[1], refs[2:])
    kept = {name: refs[i] for i, name in enumerate(READ)}
    grads = refs[reads : reads + made - 1]
    (
        flow,
        mixed,
        att_grad,
        qkv_grad,
        sums,
        send,
        received,
        wq_v,
        wp_v,
        wh_v,
        ws_v,
        w_sem,
        in_sem,
        x_sem,
        out_sem,
        send_sem,
        recv_sem,
        film_send,
        film_recv,
    ) = refs[reads + made - 1 :]
    section = lax.axis_index("section")
    here = lax.axis_index("dp")

    def fetching(name, image):
        index = READ.index(name)
        return pltpu.make_async_copy(sources[index].at[image], kept[name], in_sem.at[index])

    fetching(SECOND, 0).start()
    loads = [started(ws, ws_v, w_sem.at[0])]
    for name in READ:
        if name != SECOND:
            fetching(name, 0).start()
    loads.append(started(wh, wh_v, w_sem.at[1]))
    loads.append(started(wp, wp_v, w_sem.at[2]))
    loads.append(started(wq, wq_v, w_sem.at[3]))
    spreading, passing = ([], [])
    if direct:
        barrier = pltpu.get_barrier_semaphore()
        for axis, me, size in (("section", section, sections), ("dp", here, DIRECT)):
            for step in range(1, size):
                pl.semaphore_signal(
                    barrier, inc=1, device_id={axis: lax.rem(me + step, size)}, device_id_type=MESH
                )
        pl.semaphore_wait(barrier, sections + DIRECT - 2)
        for step in range(1, DIRECT):
            copy = pltpu.make_async_remote_copy(
                src_ref=film,
                dst_ref=film_rows.at[here],
                send_sem=film_send.at[step - 1],
                recv_sem=film_recv.at[step - 1],
                device_id={"dp": lax.rem(here + step, DIRECT)},
                device_id_type=MESH,
            )
            copy.start()
            spreading.append(copy)
        film_rows[here] = film[...]
        for step in range(1, sections):
            passing.append(
                pltpu.make_async_remote_copy(
                    src_ref=film_rows,
                    dst_ref=film_out,
                    send_sem=film_send.at[DIRECT - 2 + step],
                    recv_sem=film_recv.at[DIRECT - 2 + step],
                    device_id={"section": lax.rem(section + step, sections)},
                    device_id_type=MESH,
                )
            )
    else:
        meet("section", sections, section)
    hop = hop_of(send, received, send_sem, recv_sem, lax.rem(section + sections - 1, sections))

    @pl.loop(0, images)
    def run(image):
        saves = []

        def save(name, value=None):
            source = grads[name] if value is None else value
            saves.append(started(source, outs[name].at[image], out_sem.at[name]))

        def fetch_next(*names):
            @pl.when(image + 1 < images)
            def start():
                for name in names:
                    fetching(name, image + 1).start()

        @pl.when(section == sections - 1)
        def take_head():
            started(head_grad.at[image], flow, x_sem).wait()

        @pl.when(section < sections - 1)
        def take_received():
            for part in range(HOPS):
                hop(image, part).wait_recv()
            flow[...] = received[image].astype(jnp.float32)

        modulation = ada[image]
        sums[...] = jnp.zeros_like(sums)

        def add_sum(row, values):
            sums[row : row + 1] += jnp.sum(values, axis=0, keepdims=True)

        fetching(SECOND, image).wait()

        def open_second(at):
            grad = flow[at]
            grads[D_SECOND][at] = (grad * modulation[5:6]).astype(jnp.bfloat16)
            add_sum(5, grad * kept[SECOND][at])

        by_rows(patches, open_second)
        fetch_next(SECOND)
        save(D_SECOND)
        fetching(PRE, image).wait()
        wait_first(image, loads[:1])
        for cols in parts_of(FF, FF // D):
            grads[D_PRE][:, cols] = (
                matmul_nt(grads[D_SECOND][...], ws_v[cols]) * gelu_grad(kept[PRE][:, cols])
            ).astype(jnp.bfloat16)
        fetch_next(PRE)
        save(D_PRE)
        wait_first(image, loads[1:2])
        for cols in parts_of(D, 3):
            mixed[:, cols] = matmul_nt(grads[D_PRE][...], wh_v[cols])
        fetching(MIDDLE, image).wait()
        fetching(BRANCH, image).wait()

        def through_two(at):
            normed, invstd = normalize(kept[MIDDLE][at])
            grad = mixed[at]
            add_sum(3, grad)
            add_sum(4, grad * normed)
            total = flow[at] + norm_back(grad * (1.0 + modulation[4:5]), normed, invstd)
            flow[at] = total
            add_sum(2, total * kept[BRANCH][at])
            grads[D_BRANCH][at] = (total * modulation[2:3]).astype(jnp.bfloat16)

        by_rows(patches, through_two)
        fetch_next(MIDDLE, BRANCH)
        save(D_BRANCH)
        wait_first(image, loads[2:3])
        att_grad[...] = contract(wp_v[...], grads[D_BRANCH][...], 1, 1).astype(jnp.bfloat16)
        fetching(QKV, image).wait()
        attend_back_kernel(kept[QKV], att_grad, qkv_grad)
        fetch_next(QKV)
        wait_first(image, loads[3:])
        for cols in parts_of(D, 3):
            mixed[:, cols] = contract(qkv_grad[...], wq_v[cols], 0, 1)
        fetching(RESIDUAL, image).wait()

        def through_one(at):
            normed, invstd = normalize(kept[RESIDUAL][at])
            grad = mixed[at]
            add_sum(0, grad)
            add_sum(1, grad * normed)
            total = flow[at] + norm_back(grad * (1.0 + modulation[1:2]), normed, invstd)
            send[image, at] = total.astype(jnp.bfloat16)

        by_rows(patches, through_one)

        @pl.when(section > 0)
        def pass_on():
            for part in range(HOPS):
                hop(image, part).start()

        fetch_next(RESIDUAL)
        save(D_RESIDUAL, send.at[image])
        grads[D_QKV][...] = qkv_grad[...].T
        save(D_QKV)
        saves.append(started(sums, ada_out.at[image], x_sem))
        if direct:

            @pl.when(image == 0)
            def pass_film():
                for copy in spreading:
                    copy.wait()

                @pl.when(section == sections - 1)
                def send_film():
                    for copy in passing:
                        copy.start()

        for copy in saves:
            copy.wait()

    @pl.when(section > 0)
    def finish():
        for image in range(images):
            for part in range(HOPS):
                hop(image, part).wait_send()

    if direct:

        @pl.when(section == sections - 1)
        def own_film():
            film_out[...] = film_rows[...]
            for copy in passing:
                copy.wait_send()

        for step in range(1, sections):

            @pl.when(section == step - 1)
            def wait_film(step=step):
                passing[step - 1].wait_recv()


def specs(*spaces):
    return [
        pl.BlockSpec(memory_space={"v": pltpu.VMEM, "h": pl.ANY}[space])
        for space in "".join(spaces)
    ]


def weight_scratch():
    return [pltpu.VMEM(shape, jnp.bfloat16) for shape in WEIGHTS] + [
        pltpu.SemaphoreType.DMA((6,))
    ]


def block_cost(images, patches, factor):
    area = sum(rows * columns for rows, columns in WEIGHTS)
    return pl.CostEstimate(
        flops=images * (2 * patches * area + factor * patches * patches * D),
        bytes_accessed=2 * area + images * 64 * patches * D,
        transcendentals=images * patches * (FF + HEADS * patches),
    )


def pipeline_forward(bias, qkv_bias, ada, tokens, weights):
    images, patches, unused = tokens.shape
    sections = lax.axis_size("section")
    sizes = [(kept_shape(i, item[0], patches), item[1]) for i, item in enumerate(KEPT)]
    return pl.pallas_call(
        functools.partial(forward_kernel, sections, images),
        out_shape=[
            jax.ShapeDtypeStruct((images,) + shape, kind) for shape, kind in sizes
        ],
        in_specs=specs("vvv", "h" * 5),
        out_specs=specs("h" * len(KEPT)),
        scratch_shapes=[pltpu.VMEM(shape, kind) for shape, kind in sizes]
        + [pltpu.VMEM((D, patches), jnp.bfloat16)]
        + [pltpu.VMEM((images, patches, D), jnp.bfloat16)] * 2
        + weight_scratch()
        + [pltpu.SemaphoreType.DMA, pltpu.SemaphoreType.DMA((len(KEPT),))]
        + [pltpu.SemaphoreType.DMA((images, HOPS))] * 2,
        compiler_params=pltpu.CompilerParams(
            vmem_limit_bytes=62 << 20, collective_id=16, has_side_effects=True
        ),
        cost_estimate=block_cost(images, patches, 4),
        name="pipeline_forward",
    )(bias, qkv_bias, ada, tokens, *weights)


def pipeline_backward(ada, head_grad, weights, sources, film):
    images, patches, unused = head_grad.shape
    sections, direct = (lax.axis_size("section"), lax.axis_size("dp") == DIRECT)
    films = [jax.ShapeDtypeStruct((DIRECT,) + film.shape, film.dtype)] * (2 * direct)
    outs = pl.pallas_call(
        functools.partial(backward_kernel, sections, images, direct),
        out_shape=[
            jax.ShapeDtypeStruct((images, patches, width), kind) for width, kind in MADE
        ]
        + [jax.ShapeDtypeStruct((images, 8, D), jnp.float32)]
        + films,
        in_specs=specs("v", "h" * (5 + len(READ)), "v" * direct),
        out_specs=specs("h" * (len(MADE) + 1), "v" * len(films)),
        scratch_shapes=[
            pltpu.VMEM(kept_shape(name, KEPT[name][0], patches), KEPT[name][1]) for name in READ
        ]
        + [pltpu.VMEM((patches, width), kind) for width, kind in MADE[:-1]]
        + [
            pltpu.VMEM((patches, D), jnp.float32),
            pltpu.VMEM((patches, D), jnp.float32),
            pltpu.VMEM((D, patches), jnp.bfloat16),
            pltpu.VMEM((3 * D, patches), jnp.bfloat16),
            pltpu.VMEM((8, D), jnp.float32),
        ]
        + [pltpu.VMEM((images, patches, D), jnp.bfloat16)] * 2
        + weight_scratch()
        + [
            pltpu.SemaphoreType.DMA((len(READ),)),
            pltpu.SemaphoreType.DMA,
            pltpu.SemaphoreType.DMA((len(MADE),)),
        ]
        + [pltpu.SemaphoreType.DMA((images, HOPS))] * 2
        + [pltpu.SemaphoreType.DMA((DIRECT + sections,))] * 2,
        compiler_params=pltpu.CompilerParams(
            vmem_limit_bytes=62 << 20, collective_id=17, has_side_effects=True
        ),
        cost_estimate=block_cost(images, patches, 10),
        name="pipeline_backward",
    )(ada, head_grad, *weights, *sources, *([film] * direct))
    if direct:
        film_all = outs[-1].reshape(-1, film.shape[1])
    else:
        film_all = lax.all_gather(film, ("section", "dp"), tiled=True)
        film_all = film_all[-images * lax.axis_size("dp") :]
    return (outs[: len(MADE) + 1], film_all)


def head_step(residual, film, noise_part, mask_part, inv_count, w_out, b_out):
    shifting, scaling = (film[:, :D], film[:, D:])
    normed, invstd = normalize(residual)
    mixed = (normed * (1.0 + scaling[:, None]) + shifting[:, None]).astype(jnp.bfloat16)
    output = (
        jnp.einsum("bpd,dj->bpj", mixed, w_out, preferred_element_type=jnp.float32) + b_out
    )
    mismatch = output - noise_part
    mask_float = mask_part.astype(jnp.float32)[:, :, None]
    squared = jnp.sum(mask_float * mismatch * mismatch)
    d_output = (2.0 * inv_count * mask_float * mismatch).astype(jnp.bfloat16)
    g_output = jnp.einsum("bpd,bpj->dj", mixed, d_output, preferred_element_type=jnp.float32)
    d_mixed = jnp.einsum("bpj,dj->bpd", d_output, w_out, preferred_element_type=jnp.float32)
    d_film = jnp.concatenate(
        [jnp.sum(d_mixed, axis=1), jnp.sum(d_mixed * normed, axis=1)], axis=1
    ).astype(jnp.bfloat16)
    d_residual = norm_back(d_mixed * (1.0 + scaling[:, None]), normed, invstd)
    g_bias = jnp.sum(d_output.astype(jnp.float32), axis=(0, 1))
    return (squared, d_residual, d_film, g_output, g_bias)


def adam_update(weight, gradient, first_moment, second_moment, scaling):
    gradient = gradient * scaling
    first_new = BETA_ONE * first_moment + (1.0 - BETA_ONE) * gradient
    second_new = BETA_TWO * second_moment + (1.0 - BETA_TWO) * gradient * gradient
    ratio = (
        first_new
        / (1.0 - BETA_ONE**STEP_POWER)
        / (jnp.sqrt(second_new / (1.0 - BETA_TWO**STEP_POWER)) + ADAM_EPS)
    )
    return (weight - RATE * (ratio + DECAY * weight), first_new, second_new)


def body(
    latents,
    noise,
    timesteps,
    labels,
    patch_mask,
    w_in,
    w_down,
    b_blk,
    small_mats,
    small_bias,
    m_in,
    m_down,
    m_bias,
    m_small,
    m_sbias,
    v_in,
    v_down,
    v_bias,
    v_small,
    v_sbias,
):
    section_index = lax.axis_index("section")
    dp_index = lax.axis_index("dp")
    sections = lax.axis_size("section")
    is_first = section_index == 0
    is_last = section_index == sections - 1
    low = jnp.bfloat16
    images, patches = patch_mask.shape
    rows = w_in.shape[1]
    row_at = dp_index * rows
    ada_at = 4 * D + FF
    o_label = PATCH_IN + FREQ
    o_second = o_label + CLASSES
    o_film = o_second + D
    o_out = o_film + 2 * D

    def gathered(value, axis="dp", dim=0):
        return lax.all_gather(value, axis, axis=dim, tiled=True)

    in_low = w_in[0].astype(low)
    w_ada = in_low[:, ada_at:]
    w_qkv = gathered(in_low[:, : 3 * D])
    w_proj = gathered(in_low[:, 3 * D : 4 * D])
    w_hidden = gathered(in_low[:, 4 * D : ada_at])
    w_second = gathered(w_down[0].astype(low))

    small_low = small_mats.astype(low)
    edge_own = jnp.where(is_first, small_mats[:, :PATCH_IN], small_mats[:, -PATCH_IN:])
    bias_width = b_blk.shape[1]
    pieces = [
        b_blk[0],
        edge_own.reshape(-1),
        timesteps.astype(jnp.float32),
        labels.astype(jnp.float32),
        jnp.sum(patch_mask).astype(jnp.float32)[None],
    ]
    block = jnp.concatenate(pieces)[None]
    blocks = spread(block, "dp", 1)[:, 0]
    ends = [0]
    for piece in pieces:
        ends.append(ends[-1] + piece.shape[0])
    bias_full = rounded(blocks[:, : ends[1]].reshape(-1))
    w_edge = blocks[:, ends[1] : ends[2]].reshape(D, PATCH_IN).astype(low)
    times_all = blocks[:, ends[2] : ends[3]].reshape(-1).astype(jnp.int32)
    labels_all = blocks[:, ends[3] : ends[4]].reshape(-1).astype(jnp.int32)
    valid_total = jnp.sum(blocks[:, ends[4]])
    inv_count = 1.0 / (valid_total * PATCH_IN)
    weights = (w_qkv, w_proj, w_hidden, w_second)

    small_width = small_mats.shape[1]
    sbias_width = small_bias.shape[0]
    extra = -(-sbias_width // small_width)
    sbias_rows = jnp.pad(small_bias, (0, extra * small_width - sbias_width)).astype(low)
    small_block = jnp.concatenate([small_low, sbias_rows.reshape(extra, small_width)], axis=0)
    small_blocks = spread(small_block, "section", 2)
    small_rows = jnp.concatenate([small_blocks[i, :rows] for i in range(sections)], axis=1)
    small_used = (
        small_blocks[:, rows:].reshape(sections, -1)[:, :sbias_width].reshape(-1)
    ).astype(jnp.float32)

    shards = lax.axis_size("dp")
    time_low = time_features(times_all).astype(low)
    one_hot = label_table(labels_all)
    time_hidden = matmul_nt(time_low, small_rows[:, PATCH_IN:o_label]) + lax.dynamic_slice_in_dim(
        small_used, D + row_at, rows, 0
    )
    time_act = jax.nn.silu(time_hidden).astype(low)
    cond_part = matmul(time_act, small_rows[:, o_second:o_film])
    label_part = matmul_nt(one_hot, small_rows[:, o_label:o_second])
    cond_part = jnp.concatenate([cond_part, label_part], axis=1).reshape(shards, images, D + rows)
    cond_got = exchange(cond_part, "dp", 3)
    cond_own = (
        jnp.sum(cond_got[:, :, :D], axis=0)
        + small_used[2 * D : 3 * D]
        + jnp.swapaxes(cond_got[:, :, D:], 0, 1).reshape(images, D)
    )
    cond_cols = exchange(jnp.swapaxes(cond_own.reshape(images, shards, rows), 0, 1), "dp", 4)
    cond_first = cond_cols.reshape(shards * images, rows)
    cond_later = rounded(cond_first)
    cond_here = jnp.where(is_first, cond_first, cond_later)
    act_here = jax.nn.silu(cond_here).astype(low)
    act_later = jax.nn.silu(cond_later).astype(low)
    ada_part = jnp.concatenate(
        [matmul(act_here, w_ada), matmul(act_later, small_rows[:, o_film:o_out])], axis=1
    )
    ada_got = exchange(ada_part.reshape(shards, images * 8 * D // 128, 128), "dp", 5)
    ada_own = jnp.sum(ada_got, axis=0).reshape(images, 8 * D)
    film = ada_own[:, 6 * D :] + small_used[3 * D : 5 * D]
    ada = (ada_own[:, : 6 * D] + bias_full[ada_at:]).reshape(images, 6, D)
    qkv_bias = jnp.concatenate(
        [bias_full[:D], jnp.zeros((D,), jnp.float32), bias_full[D : 2 * D]]
    )[:, None]
    bias_row = bias_full[None, 2 * D : ada_at]

    fade = alpha_bar(timesteps)[:, None, None]
    noisy_low = (jnp.sqrt(fade) * latents + jnp.sqrt(1.0 - fade) * noise).astype(low)
    tokens = jnp.einsum(
        "bpi,di->bpd", noisy_low, w_edge, preferred_element_type=jnp.float32
    )
    tokens = tokens + small_used[:D] + positions(patches)[None]

    kept_all = pipeline_forward(bias_row, qkv_bias, ada, tokens, weights)

    squared, head_grad, d_film, g_output, g_out_bias = head_step(
        kept_all[OUTPUT],
        film,
        noise,
        patch_mask,
        inv_count,
        w_edge,
        small_used[5 * D :],
    )
    loss_part = jnp.where(is_last, squared * inv_count, 0.0)
    made_all, film_all = pipeline_backward(
        ada, head_grad, weights, [kept_all[name] for name in READ], d_film
    )

    def flat(whole):
        return whole.reshape(images * patches, whole.shape[2])

    d_second, d_pre, d_branch, d_qkv, d_tokens = [flat(whole) for whole in made_all[:5]]
    d_ada = made_all[5][:, :6].astype(low).reshape(images, 6 * D)

    token_sums = column_sum(d_tokens)
    g_edge = jnp.where(
        is_first,
        matmul_tn(d_tokens, noisy_low.reshape(images * patches, PATCH_IN)),
        g_output,
    )
    shard_wide, shard_down, right_sums, late, (token_sums, g_edge), d_ada_all = row_sums(
        [flat(kept_all[name]) for name in (MIXED_ONE, ATT, MIXED_TWO, ACT)],
        [d_qkv, d_branch, d_pre, d_second],
        (token_sums, g_edge),
        d_ada,
    )
    d_ada, d_ada_all, unused = lax.optimization_barrier((d_ada, d_ada_all, late))
    d_ada_all = d_ada_all.reshape(shards * images, 6 * D)

    cond_piece = matmul_nt(d_ada_all, w_ada) * silu_grad(cond_here)
    cond_pieces = spread(cond_piece, "section", 9)
    d_cond = matmul_nt(film_all, small_rows[:, o_film:o_out]) * silu_grad(cond_later)
    for layer in reversed(range(sections)):
        d_cond = rounded(d_cond + cond_pieces[layer])
    d_cond_rows = d_cond.astype(low)
    d_cond_all = jnp.swapaxes(spread(d_cond_rows, "dp", 10), 0, 1).reshape(shards * images, D)
    d_time = (
        matmul_nt(d_cond_all, small_rows[:, o_second:o_film]) * silu_grad(time_hidden)
    ).astype(low)
    bias_sums = jnp.concatenate(
        [
            right_sums[0][:D],
            right_sums[0][2 * D :],
            right_sums[1],
            right_sums[2],
            right_sums[3],
            column_sum(d_ada),
        ]
    )
    sums = jnp.concatenate(
        [
            bias_sums.reshape(shards, -1),
            g_edge.reshape(shards, -1),
            jnp.broadcast_to(token_sums, (shards, D)),
            jnp.broadcast_to(g_out_bias, (shards, PATCH_IN)),
            jnp.broadcast_to(column_sum(d_time), (shards, rows)),
        ],
        axis=1,
    )
    sums = exchange(sums[:, None], "dp", 11)[:, 0]
    (
        sums,
        d_ada_all,
        d_cond_all,
        d_cond_rows,
        d_time,
        film_all,
        shard_wide,
        shard_down,
    ) = lax.optimization_barrier(
        (sums, d_ada_all, d_cond_all, d_cond_rows, d_time, film_all, shard_wide, shard_down)
    )
    shard_ada = matmul_tn(act_here, d_ada_all)
    shard_in = jnp.concatenate([shard_wide, shard_ada], axis=1)
    edge_end = bias_width + rows * PATCH_IN
    shard_bias = jnp.sum(sums[:, :bias_width], axis=0)
    edge_rows = jnp.sum(sums[:, bias_width:edge_end], axis=0).reshape(rows, PATCH_IN)
    token_sums = jnp.sum(sums[:, edge_end : edge_end + D], axis=0)
    out_sums = jnp.sum(sums[:, edge_end + D : edge_end + D + PATCH_IN], axis=0)
    time_sums = sums[:, edge_end + D + PATCH_IN :].reshape(-1)
    small_grad = jnp.concatenate(
        [
            edge_rows,
            matmul_tn(d_time, time_low),
            matmul_tn(d_cond_rows, one_hot),
            matmul_tn(time_act, d_cond_all),
            matmul_tn(act_later, film_all),
            edge_rows,
        ],
        axis=1,
    )
    small_shard = lax.dynamic_slice_in_dim(small_grad, section_index * small_width, small_width, 1)
    sbias_grad = jnp.concatenate(
        [token_sums, time_sums, column_sum(d_cond_all), column_sum(film_all), out_sums]
    )
    sbias_shard = lax.dynamic_slice_in_dim(
        sbias_grad, section_index * sbias_width, sbias_width, 0
    )

    dp_zero = (dp_index == 0).astype(jnp.float32)
    squares = (
        jnp.sum(shard_in * shard_in)
        + jnp.sum(shard_down * shard_down)
        + jnp.sum(shard_bias * shard_bias)
        + jnp.sum(small_shard * small_shard)
        + dp_zero * jnp.sum(sbias_shard * sbias_shard)
    )
    pair = jnp.broadcast_to(jnp.stack([squares, loss_part])[:, None], (2, 128))
    pair = jnp.sum(spread(pair, "dp", 14), axis=0)
    pair = jnp.sum(spread(pair, "section", 15), axis=0)
    norm_square, loss = (pair[0, 0], pair[1, 0])
    grad_norm = jnp.sqrt(norm_square)
    scaling = jnp.minimum(1.0, CLIP / grad_norm)
    new_in, first_in, second_in = adam_update(w_in, shard_in[None], m_in, v_in, scaling)
    new_down, first_down, second_down = adam_update(
        w_down, shard_down[None], m_down, v_down, scaling
    )
    new_bias, first_bias, second_bias = adam_update(
        b_blk, shard_bias[None], m_bias, v_bias, scaling
    )
    new_small, first_small, second_small = adam_update(
        small_mats, small_shard, m_small, v_small, scaling
    )
    new_sbias, first_sbias, second_sbias = adam_update(
        small_bias, sbias_shard, m_sbias, v_sbias, scaling
    )
    return (
        loss,
        grad_norm,
        new_in,
        first_in,
        second_in,
        new_down,
        first_down,
        second_down,
        new_bias,
        first_bias,
        second_bias,
        new_small,
        first_small,
        second_small,
        new_sbias,
        first_sbias,
        second_sbias,
    )


def solution(mesh):
    in_specs = (
        P("dp", None, None),
        P("dp", None, None),
        P("dp"),
        P("dp"),
        P("dp", None),
        P("section", "dp", None),
        P("section", "dp", None),
        P("section", "dp"),
        P("dp", "section"),
        P("section"),
        P("section", "dp", None),
        P("section", "dp", None),
        P("section", "dp"),
        P("dp", "section"),
        P("section"),
        P("section", "dp", None),
        P("section", "dp", None),
        P("section", "dp"),
        P("dp", "section"),
        P("section"),
    )
    out_specs = (
        P(),
        P(),
        P("section", "dp", None),
        P("section", "dp", None),
        P("section", "dp", None),
        P("section", "dp", None),
        P("section", "dp", None),
        P("section", "dp", None),
        P("section", "dp"),
        P("section", "dp"),
        P("section", "dp"),
        P("dp", "section"),
        P("dp", "section"),
        P("dp", "section"),
        P("section"),
        P("section"),
        P("section"),
    )
    return jax.shard_map(body, mesh=mesh, in_specs=in_specs, out_specs=out_specs, check_vma=False)
```

```python
import functools
import math

import jax
import jax.numpy as jnp
from jax import lax
from jax.experimental import pallas as pl
from jax.experimental.pallas import tpu as pltpu
from jax.sharding import PartitionSpec as P

D = 1152
HEADS = 16
HEAD_DIM = 72
FF = 4608
CLASSES = 1000
FREQ = 256
PATCH_IN = 16
GRID = 16


EPS_NORM = 1e-06
CLIP = 0.001
RATE = 0.005
BETA_ONE = 0.9
BETA_TWO = 0.999
ADAM_EPS = 1e-08
DECAY = 0.01
STEP_POWER = 10.0


def passed_along(value, axis, steps):
    count = lax.axis_size(axis)
    first, last = (max(0, -steps), min(count, count - steps))
    return lax.ppermute(value, axis, [(source, source + steps) for source in range(first, last)])


def matmul(left_side, right_side):
    return jnp.dot(left_side, right_side, preferred_element_type=jnp.float32)


def matmul_tn(left_side, right_side):
    return lax.dot_general(
        left_side, right_side, (((0,), (0,)), ((), ())), preferred_element_type=jnp.float32
    )


def matmul_nt(left_side, right_side):
    return lax.dot_general(
        left_side, right_side, (((1,), (1,)), ((), ())), preferred_element_type=jnp.float32
    )


def column_sum(values):
    return jnp.sum(values.astype(jnp.float32), axis=0)


def normalize(values):
    center = values - jnp.mean(values, axis=-1, keepdims=True)
    invstd = lax.rsqrt(jnp.mean(center * center, axis=-1, keepdims=True) + EPS_NORM)
    return (center * invstd, invstd)


def norm_back(grad_normed, normed, invstd):
    return invstd * (
        grad_normed
        - jnp.mean(grad_normed, axis=-1, keepdims=True)
        - normed * jnp.mean(grad_normed * normed, axis=-1, keepdims=True)
    )


def gelu_tanh(values):
    return (
        0.5
        * values
        * (1.0 + jnp.tanh(0.7978845608028654 * (values + 0.044715 * values * values * values)))
    )


def gelu_grad(values):
    inner = jnp.tanh(0.7978845608028654 * (values + 0.044715 * values * values * values))
    return 0.5 * (1.0 + inner) + 0.5 * values * (1.0 - inner * inner) * 0.7978845608028654 * (
        1.0 + 0.134145 * values * values
    )


def silu_grad(values):
    sigma = jax.nn.sigmoid(values)
    return sigma * (1.0 + values * (1.0 - sigma))


def positions(patches):
    quarter = D // 4
    omega = jnp.exp(-math.log(10000.0) * jnp.arange(quarter, dtype=jnp.float32) / quarter)
    spot = jnp.arange(patches, dtype=jnp.int32)
    row_angle = (spot // GRID).astype(jnp.float32)[:, None] * omega[None, :]
    col_angle = (spot % GRID).astype(jnp.float32)[:, None] * omega[None, :]
    return jnp.concatenate(
        [jnp.sin(row_angle), jnp.cos(row_angle), jnp.sin(col_angle), jnp.cos(col_angle)], axis=1
    )


def time_features(time_steps):
    half = FREQ // 2
    freqs = jnp.exp(-math.log(10000.0) * jnp.arange(half, dtype=jnp.float32) / half)
    angles = time_steps.astype(jnp.float32)[:, None] * freqs[None, :]
    return jnp.concatenate([jnp.cos(angles), jnp.sin(angles)], axis=1)


def alpha_bar(time_steps):
    return jnp.cos((time_steps.astype(jnp.float32) / 1000.0 + 0.008) / 1.008 * (math.pi / 2)) ** 2


def label_table(label_part):
    return (label_part[:, None] == jnp.arange(CLASSES, dtype=jnp.int32)[None, :]).astype(
        jnp.bfloat16
    )


MESH = pl.DeviceIdType.MESH
DIRECT = 8


def rounded(values):
    return lax.reduce_precision(values, 8, 7)


def meet(axis, count, here):
    barrier = pltpu.get_barrier_semaphore()
    for step in range(1, count):
        pl.semaphore_signal(
            barrier, inc=1, device_id={axis: lax.rem(here + step, count)}, device_id_type=MESH
        )
    pl.semaphore_wait(barrier, count - 1)


def share_kernel(axis, count, personal, in_ref, out_ref, send_sem, recv_sem):
    here = lax.axis_index(axis)
    meet(axis, count, here)
    copies = []
    for step in range(1, count):
        target = lax.rem(here + step, count)
        copy = pltpu.make_async_remote_copy(
            src_ref=in_ref.at[target] if personal else in_ref,
            dst_ref=out_ref.at[here],
            send_sem=send_sem.at[step - 1],
            recv_sem=recv_sem.at[step - 1],
            device_id={axis: target},
            device_id_type=MESH,
        )
        copy.start()
        copies.append(copy)
    out_ref[here] = in_ref[here] if personal else in_ref[...]
    for copy in copies:
        copy.wait()


def share(value, axis, personal, ident):
    count = lax.axis_size(axis)
    shape = value.shape if personal else (count,) + value.shape
    return pl.pallas_call(
        functools.partial(share_kernel, axis, count, personal),
        out_shape=jax.ShapeDtypeStruct(shape, value.dtype),
        in_specs=[pl.BlockSpec(memory_space=pltpu.VMEM)],
        out_specs=pl.BlockSpec(memory_space=pltpu.VMEM),
        scratch_shapes=[
            pltpu.SemaphoreType.DMA((count - 1,)),
            pltpu.SemaphoreType.DMA((count - 1,)),
        ],
        compiler_params=pltpu.CompilerParams(collective_id=ident, has_side_effects=True),
        name="share",
    )(value)


def spread(value, axis, ident):
    if lax.axis_size(axis) > DIRECT:
        return lax.all_gather(value, axis)
    return share(value, axis, False, ident)


def exchange(value, axis, ident):
    if lax.axis_size(axis) > DIRECT:
        return lax.all_to_all(value, axis, 0, 0)
    return share(value, axis, True, ident)


FINAL, LATER, NEAR, FAR, PASS = range(5)
STEPS = 16
CHIPS = 4


def sums_kernel(units, rows, *refs):
    lefts, rights, given = (refs[:4], refs[4:8], refs[8])
    own_out, final_out, later_out, bias_out, spread_out = refs[9:14]
    (
        left_v,
        right_v,
        product,
        got,
        own_v,
        stage,
        near,
        far,
        passed,
        left_sem,
        right_sem,
        send_sem,
        recv_sem,
        own_sem,
        stage_sem,
        block_sem,
        pass_sem,
        given_send,
        given_recv,
    ) = refs[14:]
    here = lax.axis_index("dp")
    core, chip = (lax.rem(here, 2), here // 2)
    partner = {"dp": here + 1 - 2 * core}
    tall = CHIPS * rows
    meet("dp", DIRECT, here)
    spreading = []
    for step in range(1, DIRECT):
        copy = pltpu.make_async_remote_copy(
            src_ref=given,
            dst_ref=spread_out.at[here],
            send_sem=given_send.at[step - 1],
            recv_sem=given_recv.at[step - 1],
            device_id={"dp": lax.rem(here + step, DIRECT)},
            device_id_type=MESH,
        )
        copy.start()
        spreading.append(copy)
    spread_out[here] = given[...]
    places = {FINAL: final_out, LATER: later_out, NEAR: near, FAR: far, PASS: passed}
    plan, last, slots = ([], [None, None], [1, 1])
    for left, left_at, right, right_at, gathers in units:
        fresh = []
        for side, key in enumerate(((left, left_at), (right, right_at))):
            fresh.append(last[side] != key)
            if fresh[-1]:
                slots[side] = 1 - slots[side]
                last[side] = key
        plan.append((tuple(slots), tuple(fresh)))
    slot_of, used = ({}, 0)
    for index, unit in enumerate(units):
        slot_of[index] = used
        used += unit[4] is None

    def loads_of(index):
        left, left_at, right, right_at, gathers = units[index]
        (left_slot, right_slot), (left_fresh, right_fresh) = plan[index]
        copies = []
        if left_fresh:
            source = lefts[left].at[:, pl.ds(left_at, D)]
            copies.append(
                pltpu.make_async_copy(source, left_v.at[left_slot], left_sem.at[left_slot])
            )
        if right_fresh:
            source = rights[right].at[:, pl.ds(right_at, D)]
            copies.append(
                pltpu.make_async_copy(source, right_v.at[right_slot], right_sem.at[right_slot])
            )
        return copies

    pending, crossing, leaving, keeping = ({}, {}, {}, {})

    def load(index):
        pending[index] = loads_of(index)
        for copy in pending[index]:
            copy.start()

    def to_partner(source, target, sems):
        copy = pltpu.make_async_remote_copy(
            src_ref=source,
            dst_ref=target,
            send_sem=send_sem.at[sems],
            recv_sem=recv_sem.at[sems],
            device_id=partner,
            device_id_type=MESH,
        )
        copy.start()
        return copy

    def multiply(index):
        gathers = units[index][4]
        left_slot, right_slot = plan[index][0]
        for copy in pending[index]:
            copy.wait()
        if index + 1 < len(units):
            load(index + 1)
        if index >= 2:
            for copy in crossing[index - 2]:
                copy.wait_send()
        slot, place = (index % 2, index % 4)
        product[slot] = contract(left_v[left_slot], right_v[right_slot], 0, 0)
        if plan[index][1][1]:
            ones = jnp.ones((8, right_v.shape[1]), jnp.bfloat16)
            bias_out[index] = matmul(ones, right_v[right_slot])
        if gathers is None:
            crossing[index] = [
                to_partner(
                    product.at[slot, pl.ds(pl.multiple_of((2 * i + 1 - core) * rows, 8), rows)],
                    got.at[place, pl.ds(i * rows, rows)],
                    place * CHIPS + i,
                )
                for i in range(CHIPS)
            ]
        else:
            crossing[index] = [
                to_partner(
                    product.at[slot, pl.ds(pl.multiple_of((1 - core) * tall, 8), tall)],
                    got.at[place],
                    place * CHIPS,
                )
            ]

    def crossed(source, kind, slot, to, sem):
        return pltpu.make_async_remote_copy(
            src_ref=source,
            dst_ref=places[kind].at[slot],
            send_sem=sem,
            recv_sem=block_sem.at[kind, slot],
            device_id={"dp": 2 * to + core},
            device_id_type=MESH,
        )

    def landed(kind, slot):
        crossed(stage.at[0, 0], kind, slot, chip, stage_sem.at[0, 0]).wait_recv()

    def filled(target, index, block, gathers, added=None):
        slot, place = (index % 2, index % 4)
        base = (2 * block + core) * rows if gathers is None else core * tall + block * rows

        @pl.loop(0, rows // STEPS)
        def run(step):
            at = step * STEPS
            value = (
                product[slot, pl.ds(pl.multiple_of(base + at, STEPS), STEPS)]
                + got[place, pl.ds(pl.multiple_of(block * rows + at, STEPS), STEPS)]
            )
            to = pl.ds(pl.multiple_of(at, STEPS), STEPS)
            if added is not None:
                value = value + added[to].astype(jnp.float32)
            target[to] = value.astype(target.dtype)

    def route(index, block, owner, slot, gathers):
        side = index % 3

        def case(at, kind, to, added=None):
            copy = crossed(
                stage.at[side, block], kind, slot, to, stage_sem.at[side, block]
            )

            @pl.when(chip == at)
            def act():
                if added is not None:
                    landed(added, slot)
                filled(
                    stage.at[side, block],
                    index,
                    block,
                    gathers,
                    None if added is None else places[added].at[slot],
                )
                copy.start()

            leaving[index].append((chip == at, copy.wait_send))

        keep = pltpu.make_async_copy(
            own_v.at[side, block], own_out.at[slot], own_sem.at[side, block]
        )

        @pl.when(chip == owner)
        def hold():
            filled(own_v.at[side, block], index, block, gathers)
            keep.start()

        leaving[index].append((chip == owner, keep.wait))
        flip = (lambda at: at) if owner < 2 else (lambda at: CHIPS - 1 - at)
        if owner in (0, CHIPS - 1):
            case(flip(3), FAR, flip(2))
            case(flip(1), FINAL, flip(0))
            case(flip(2), PASS, flip(1), FAR)
        else:
            case(flip(3), NEAR, flip(2))
            case(flip(0), FINAL, flip(1))
            case(flip(2), LATER, flip(1), NEAR)

    def blocks_of(index):
        gathers = units[index][4]
        if gathers is None:
            return [(owner, owner, slot_of[index]) for owner in (0, 3, 1, 2)]
        return [(block, gathers, slot_of[index] + block) for block in range(CHIPS)]

    def combine(index):
        for copy in crossing[index]:
            copy.wait_recv()
        if index >= 3:
            finish(index - 3)
        leaving[index] = []
        for block, owner, slot in blocks_of(index):
            route(index, block, owner, slot, units[index][4])

    def finish(index):
        for condition, wait in leaving[index]:

            @pl.when(condition)
            def settle(wait=wait):
                wait()

    def pass_on(index):
        for block, owner, slot in blocks_of(index):
            if owner not in (0, CHIPS - 1):
                continue
            middle = 1 if owner == 0 else CHIPS - 2

            @pl.when(chip == middle)
            def forward(slot=slot, owner=owner):
                landed(PASS, slot)
                crossed(passed.at[slot], LATER, slot, owner, pass_sem.at[slot]).start()

    total = len(units)
    load(0)
    multiply(0)
    for index in range(total):
        if index + 1 < total:
            multiply(index + 1)
        combine(index)
        if index >= 1:
            pass_on(index - 1)
    pass_on(total - 1)
    for index in range(max(0, total - 3), total):
        finish(index)
    for index in range(max(0, total - 2), total):
        for copy in crossing[index]:
            copy.wait_send()
    for index in range(total):
        for block, owner, slot in blocks_of(index):

            @pl.when(chip == owner)
            def received(slot=slot):
                landed(FINAL, slot)
                landed(LATER, slot)

            if owner in (0, CHIPS - 1):

                @pl.when(chip == (1 if owner == 0 else CHIPS - 2))
                def sent(slot=slot, owner=owner):
                    crossed(passed.at[slot], LATER, slot, owner, pass_sem.at[slot]).wait_send()

    for copy in spreading:
        copy.wait()


def line_sums(units, lefts, rights, rows, ident, given):
    tokens = lefts[0].shape[0]
    places = sum(unit[4] is None for unit in units) + 4
    block = (rows, D)
    outs = pl.pallas_call(
        functools.partial(sums_kernel, units, rows),
        out_shape=[
            jax.ShapeDtypeStruct((places,) + block, jnp.float32),
            jax.ShapeDtypeStruct((places,) + block, jnp.bfloat16),
            jax.ShapeDtypeStruct((places,) + block, jnp.bfloat16),
            jax.ShapeDtypeStruct((len(units), 8, D), jnp.float32),
            jax.ShapeDtypeStruct((DIRECT,) + given.shape, given.dtype),
        ],
        in_specs=specs("h" * 8, "v"),
        out_specs=specs("hhhvv"),
        scratch_shapes=[
            pltpu.VMEM((2, tokens, D), jnp.bfloat16),
            pltpu.VMEM((2, tokens, D), jnp.bfloat16),
            pltpu.VMEM((2, 8 * rows, D), jnp.float32),
            pltpu.VMEM((4, 4 * rows, D), jnp.float32),
            pltpu.VMEM((3, 4) + block, jnp.float32),
            pltpu.VMEM((3, 4) + block, jnp.bfloat16),
            pltpu.VMEM((places,) + block, jnp.bfloat16),
            pltpu.VMEM((places,) + block, jnp.bfloat16),
            pltpu.VMEM((places,) + block, jnp.bfloat16),
            pltpu.SemaphoreType.DMA((2,)),
            pltpu.SemaphoreType.DMA((2,)),
            pltpu.SemaphoreType.DMA((16,)),
            pltpu.SemaphoreType.DMA((16,)),
            pltpu.SemaphoreType.DMA((3, 4)),
            pltpu.SemaphoreType.DMA((3, 4)),
            pltpu.SemaphoreType.DMA((5, places)),
            pltpu.SemaphoreType.DMA((places,)),
            pltpu.SemaphoreType.DMA((DIRECT - 1,)),
            pltpu.SemaphoreType.DMA((DIRECT - 1,)),
        ],
        compiler_params=pltpu.CompilerParams(
            collective_id=ident, has_side_effects=True, vmem_limit_bytes=62 << 20
        ),
        cost_estimate=pl.CostEstimate(
            flops=2 * tokens * D * D * len(units),
            bytes_accessed=len(units) * tokens * D * 4,
            transcendentals=0,
        ),
        name="line_sums",
    )(*lefts, *rights, given)
    total = outs[0] + outs[1].astype(jnp.float32) + outs[2].astype(jnp.float32)
    return (total, outs[3][:, 0], outs[4])


def row_sums(lefts, rights, given):
    count = lax.axis_size("dp")
    if count != DIRECT:
        products = [matmul_tn(one, other) for one, other in zip(lefts, rights)]
        sums = [lax.psum_scatter(one, "dp", scatter_dimension=0, tiled=True) for one in products]
        wide = jnp.concatenate([sums[0], sums[1], sums[2]], axis=1)
        given = lax.all_gather(given, "dp")
        return (wide, sums[3], [column_sum(one) for one in rights], given)
    rows = D // count
    parts = FF // D
    units = (
        [(0, 0, 0, i * D, None) for i in range(3)]
        + [(1, 0, 1, 0, None)]
        + [(2, 0, 2, i * D, None) for i in range(parts)]
        + [(3, i * D, 3, 0, i) for i in range(parts)]
    )
    total, bias, given_all = line_sums(tuple(units), lefts, rights, rows, 12, given)
    wide = jnp.concatenate([total[i] for i in range(4 + parts)], axis=1)
    sums = [bias[:3].reshape(-1), bias[3], bias[4 : 4 + parts].reshape(-1), bias[4 + parts]]
    return (wide, total[4 + parts :].reshape(-1, D), sums, given_all)


GROUP = 4


def contract(left_side, right_side, left_axis, right_axis):
    return lax.dot_general(
        left_side,
        right_side,
        (((left_axis,), (right_axis,)), ((), ())),
        preferred_element_type=jnp.float32,
    )


def heads_of(ref, at, group):
    return [
        ref[at + head * HEAD_DIM : at + (head + 1) * HEAD_DIM] for head in group
    ]


def softmax_down(scores):
    weights = jnp.exp(scores - jnp.max(scores, axis=0, keepdims=True))
    return weights * (1.0 / jnp.sum(weights, axis=0, keepdims=True))


def stacked(values):
    return jnp.concatenate([value.astype(jnp.bfloat16) for value in values], axis=0)


def attend_kernel(qkv_ref, out_ref):
    scaling = HEAD_DIM ** (-0.5)
    for first in range(0, HEADS, GROUP):
        group = range(first, first + GROUP)
        rows = slice(first * HEAD_DIM, (first + GROUP) * HEAD_DIM)
        queries, keys = (heads_of(qkv_ref, 0, group), heads_of(qkv_ref, D, group))
        values = heads_of(qkv_ref, 2 * D, group)
        scores = [contract(key, query, 0, 0) * scaling for key, query in zip(keys, queries)]
        probs = [softmax_down(score).astype(jnp.bfloat16) for score in scores]
        out_ref[rows] = stacked([contract(v, p, 1, 0) for v, p in zip(values, probs)])


def attend_back_kernel(qkv_ref, grad_ref, out_ref):
    scaling = HEAD_DIM ** (-0.5)
    for first in range(0, HEADS, GROUP):
        group = range(first, first + GROUP)
        at, to = (first * HEAD_DIM, (first + GROUP) * HEAD_DIM)
        queries, keys = (heads_of(qkv_ref, 0, group), heads_of(qkv_ref, D, group))
        values, grads = (heads_of(qkv_ref, 2 * D, group), heads_of(grad_ref, 0, group))
        scores = [contract(key, query, 0, 0) * scaling for key, query in zip(keys, queries)]
        d_probs = [contract(value, grad, 0, 0) for value, grad in zip(values, grads)]
        probs = [softmax_down(score) for score in scores]
        d_scores = [
            (p * (d - jnp.sum(p * d, axis=0, keepdims=True))).astype(jnp.bfloat16)
            for p, d in zip(probs, d_probs)
        ]
        lows = [p.astype(jnp.bfloat16) for p in probs]
        out_ref[at:to] = stacked([contract(k, d, 1, 0) * scaling for k, d in zip(keys, d_scores)])
        out_ref[D + at : D + to] = stacked(
            [contract(q, d, 1, 1) * scaling for q, d in zip(queries, d_scores)]
        )
        out_ref[2 * D + at : 2 * D + to] = stacked(
            [contract(g, p, 1, 1) for g, p in zip(grads, lows)]
        )


ROW_BLOCK = 64
HOPS = 3
RESIDUAL, MIXED_ONE, QKV, ATT, BRANCH, MIDDLE = range(6)
MIXED_TWO, PRE, ACT, SECOND, OUTPUT = range(6, 11)
D_SECOND, D_PRE, D_BRANCH, D_QKV, D_RESIDUAL = range(5)
WIDE, LOW = (jnp.float32, jnp.bfloat16)
KEPT = (
    (D, WIDE),
    (D, LOW),
    (3 * D, LOW),
    (D, LOW),
    (D, WIDE),
    (D, WIDE),
    (D, LOW),
    (FF, WIDE),
    (FF, LOW),
    (D, WIDE),
    (D, WIDE),
)
READ = (RESIDUAL, QKV, BRANCH, MIDDLE, PRE, SECOND)
MADE = ((D, LOW), (FF, LOW), (D, LOW), (3 * D, LOW), (D, LOW))
WEIGHTS = ((D, 3 * D), (D, D), (D, FF), (FF, D))


def kept_shape(name, width, patches):
    return (width, patches) if name == QKV else (patches, width)


def by_rows(patches, step):
    @pl.loop(0, patches // ROW_BLOCK)
    def run(index):
        step(pl.ds(pl.multiple_of(index * ROW_BLOCK, ROW_BLOCK), ROW_BLOCK))


def started(source, target, sem):
    copy = pltpu.make_async_copy(source, target, sem)
    copy.start()
    return copy


def parts_of(whole, parts):
    width = whole // parts
    return [slice(part * width, part * width + width) for part in range(parts)]


def wait_first(image, loads):
    @pl.when(image == 0)
    def wait():
        for load in loads:
            load.wait()


def hop_of(send, received, send_sem, recv_sem, target):
    def hop(image, part):
        cols = pl.ds(part * (D // HOPS), D // HOPS)
        return pltpu.make_async_remote_copy(
            src_ref=send.at[image, :, cols],
            dst_ref=received.at[image, :, cols],
            send_sem=send_sem.at[image, part],
            recv_sem=recv_sem.at[image, part],
            device_id={"section": target},
            device_id_type=MESH,
        )

    return hop


def forward_kernel(sections, images, bias, qkv_bias, ada, tokens, wq, wp, wh, ws, *refs):
    count, patches = (len(KEPT), tokens.shape[1])
    outs, scratch = (refs[:count], refs[count:])
    kept = scratch[:count]
    (
        att_down,
        send,
        received,
        wq_v,
        wp_v,
        wh_v,
        ws_v,
        w_sem,
        x_sem,
        out_sem,
        send_sem,
        recv_sem,
    ) = scratch[count:]
    section = lax.axis_index("section")
    loads = [
        started(wq.at[:, cols], wq_v.at[:, cols], w_sem.at[i])
        for i, cols in enumerate(parts_of(3 * D, 3))
    ]
    loads.append(started(wp, wp_v, w_sem.at[3]))
    loads.append(started(wh, wh_v, w_sem.at[4]))
    loads.append(started(ws, ws_v, w_sem.at[5]))
    meet("section", sections, section)
    hop = hop_of(send, received, send_sem, recv_sem, lax.rem(section + 1, sections))
    residual = kept[RESIDUAL]

    @pl.loop(0, images)
    def run(image):
        saves = []

        def save(name):
            saves.append(started(kept[name], outs[name].at[image], out_sem.at[name]))

        @pl.when(section == 0)
        def take_tokens():
            started(tokens.at[image], residual, x_sem).wait()

        @pl.when(section > 0)
        def take_received():
            for part in range(HOPS):
                hop(image, part).wait_recv()
            residual[...] = received[image].astype(jnp.float32)

        save(RESIDUAL)
        modulation = ada[image]

        def mix_one(at):
            normed, unused = normalize(residual[at])
            kept[MIXED_ONE][at] = (normed * (1.0 + modulation[1:2]) + modulation[0:1]).astype(
                jnp.bfloat16
            )

        by_rows(patches, mix_one)
        save(MIXED_ONE)
        wait_first(image, loads[:3])
        for cols in parts_of(3 * D, 3):
            kept[QKV][cols] = (
                contract(wq_v[:, cols], kept[MIXED_ONE][...], 0, 1) + qkv_bias[cols]
            ).astype(jnp.bfloat16)
        save(QKV)
        attend_kernel(kept[QKV], att_down)
        wait_first(image, loads[3:4])
        kept[BRANCH][...] = contract(att_down[...], wp_v[...], 0, 0) + bias[:, :D]
        kept[ATT][...] = att_down[...].T
        save(BRANCH)
        save(ATT)

        def mix_two(at):
            middle = residual[at] + modulation[2:3] * kept[BRANCH][at]
            kept[MIDDLE][at] = middle
            normed, unused = normalize(middle)
            kept[MIXED_TWO][at] = (normed * (1.0 + modulation[4:5]) + modulation[3:4]).astype(
                jnp.bfloat16
            )

        by_rows(patches, mix_two)
        save(MIDDLE)
        save(MIXED_TWO)
        wait_first(image, loads[4:5])
        for part, cols in enumerate(parts_of(FF, FF // D)):
            pre = (
                matmul(kept[MIXED_TWO][...], wh_v[:, cols])
                + bias[:, D + part * D : 2 * D + part * D]
            )
            kept[PRE][:, cols] = pre
            kept[ACT][:, cols] = gelu_tanh(pre).astype(jnp.bfloat16)
        save(PRE)
        save(ACT)
        wait_first(image, loads[5:])
        for part, cols in enumerate(parts_of(D, HOPS)):
            second = (
                matmul(kept[ACT][...], ws_v[:, cols])
                + bias[:, D + FF + cols.start : D + FF + cols.stop]
            )
            kept[SECOND][:, cols] = second
            output = kept[MIDDLE][:, cols] + modulation[5:6, cols] * second
            kept[OUTPUT][:, cols] = output
            send[image, :, cols] = output.astype(jnp.bfloat16)

            @pl.when(section < sections - 1)
            def pass_on(part=part):
                hop(image, part).start()

        save(SECOND)
        save(OUTPUT)
        for copy in saves:
            copy.wait()

    @pl.when(section < sections - 1)
    def finish():
        for image in range(images):
            for part in range(HOPS):
                hop(image, part).wait_send()


def backward_kernel(sections, images, direct, ada, head_grad, wq, wp, wh, ws, *refs):
    reads, made, patches = (len(READ), len(MADE), head_grad.shape[1])
    sources, refs = (refs[:reads], refs[reads:])
    if direct:
        film, refs = (refs[0], refs[1:])
    outs, ada_out, refs = (refs[:made], refs[made], refs[made + 1 :])
    if direct:
        film_rows, film_out, refs = (refs[0], refs[1], refs[2:])
    kept = {name: refs[i] for i, name in enumerate(READ)}
    grads = refs[reads : reads + made - 1]
    (
        flow,
        mixed,
        att_grad,
        qkv_grad,
        sums,
        send,
        received,
        wq_v,
        wp_v,
        wh_v,
        ws_v,
        w_sem,
        in_sem,
        x_sem,
        out_sem,
        send_sem,
        recv_sem,
        film_send,
        film_recv,
    ) = refs[reads + made - 1 :]
    section = lax.axis_index("section")
    here = lax.axis_index("dp")

    def fetching(name, image):
        index = READ.index(name)
        return pltpu.make_async_copy(sources[index].at[image], kept[name], in_sem.at[index])

    fetching(SECOND, 0).start()
    loads = [started(ws, ws_v, w_sem.at[0])]
    for name in READ:
        if name != SECOND:
            fetching(name, 0).start()
    loads.append(started(wh, wh_v, w_sem.at[1]))
    loads.append(started(wp, wp_v, w_sem.at[2]))
    loads.append(started(wq, wq_v, w_sem.at[3]))
    spreading, passing = ([], [])
    if direct:
        barrier = pltpu.get_barrier_semaphore()
        for axis, me, size in (("section", section, sections), ("dp", here, DIRECT)):
            for step in range(1, size):
                pl.semaphore_signal(
                    barrier, inc=1, device_id={axis: lax.rem(me + step, size)}, device_id_type=MESH
                )
        pl.semaphore_wait(barrier, sections + DIRECT - 2)
        for step in range(1, DIRECT):
            copy = pltpu.make_async_remote_copy(
                src_ref=film,
                dst_ref=film_rows.at[here],
                send_sem=film_send.at[step - 1],
                recv_sem=film_recv.at[step - 1],
                device_id={"dp": lax.rem(here + step, DIRECT)},
                device_id_type=MESH,
            )
            copy.start()
            spreading.append(copy)
        film_rows[here] = film[...]
        for step in range(1, sections):
            passing.append(
                pltpu.make_async_remote_copy(
                    src_ref=film_rows,
                    dst_ref=film_out,
                    send_sem=film_send.at[DIRECT - 2 + step],
                    recv_sem=film_recv.at[DIRECT - 2 + step],
                    device_id={"section": lax.rem(section + step, sections)},
                    device_id_type=MESH,
                )
            )
    else:
        meet("section", sections, section)
    hop = hop_of(send, received, send_sem, recv_sem, lax.rem(section + sections - 1, sections))

    @pl.loop(0, images)
    def run(image):
        saves = []

        def save(name, value=None):
            source = grads[name] if value is None else value
            saves.append(started(source, outs[name].at[image], out_sem.at[name]))

        def fetch_next(*names):
            @pl.when(image + 1 < images)
            def start():
                for name in names:
                    fetching(name, image + 1).start()

        @pl.when(section == sections - 1)
        def take_head():
            started(head_grad.at[image], flow, x_sem).wait()

        @pl.when(section < sections - 1)
        def take_received():
            for part in range(HOPS):
                hop(image, part).wait_recv()
            flow[...] = received[image].astype(jnp.float32)

        modulation = ada[image]
        sums[...] = jnp.zeros_like(sums)

        def add_sum(row, values):
            sums[row : row + 1] += jnp.sum(values, axis=0, keepdims=True)

        fetching(SECOND, image).wait()

        def open_second(at):
            grad = flow[at]
            grads[D_SECOND][at] = (grad * modulation[5:6]).astype(jnp.bfloat16)
            add_sum(5, grad * kept[SECOND][at])

        by_rows(patches, open_second)
        fetch_next(SECOND)
        save(D_SECOND)
        fetching(PRE, image).wait()
        wait_first(image, loads[:1])
        for cols in parts_of(FF, FF // D):
            grads[D_PRE][:, cols] = (
                matmul_nt(grads[D_SECOND][...], ws_v[cols]) * gelu_grad(kept[PRE][:, cols])
            ).astype(jnp.bfloat16)
        fetch_next(PRE)
        save(D_PRE)
        wait_first(image, loads[1:2])
        for cols in parts_of(D, 3):
            mixed[:, cols] = matmul_nt(grads[D_PRE][...], wh_v[cols])
        fetching(MIDDLE, image).wait()
        fetching(BRANCH, image).wait()

        def through_two(at):
            normed, invstd = normalize(kept[MIDDLE][at])
            grad = mixed[at]
            add_sum(3, grad)
            add_sum(4, grad * normed)
            total = flow[at] + norm_back(grad * (1.0 + modulation[4:5]), normed, invstd)
            flow[at] = total
            add_sum(2, total * kept[BRANCH][at])
            grads[D_BRANCH][at] = (total * modulation[2:3]).astype(jnp.bfloat16)

        by_rows(patches, through_two)
        fetch_next(MIDDLE, BRANCH)
        save(D_BRANCH)
        wait_first(image, loads[2:3])
        att_grad[...] = contract(wp_v[...], grads[D_BRANCH][...], 1, 1).astype(jnp.bfloat16)
        fetching(QKV, image).wait()
        attend_back_kernel(kept[QKV], att_grad, qkv_grad)
        fetch_next(QKV)
        wait_first(image, loads[3:])
        for cols in parts_of(D, 3):
            mixed[:, cols] = contract(qkv_grad[...], wq_v[cols], 0, 1)
        fetching(RESIDUAL, image).wait()

        def through_one(at):
            normed, invstd = normalize(kept[RESIDUAL][at])
            grad = mixed[at]
            add_sum(0, grad)
            add_sum(1, grad * normed)
            total = flow[at] + norm_back(grad * (1.0 + modulation[1:2]), normed, invstd)
            send[image, at] = total.astype(jnp.bfloat16)

        by_rows(patches, through_one)

        @pl.when(section > 0)
        def pass_on():
            for part in range(HOPS):
                hop(image, part).start()

        fetch_next(RESIDUAL)
        save(D_RESIDUAL, send.at[image])
        grads[D_QKV][...] = qkv_grad[...].T
        save(D_QKV)
        saves.append(started(sums, ada_out.at[image], x_sem))
        if direct:

            @pl.when(image == 0)
            def pass_film():
                for copy in spreading:
                    copy.wait()

                @pl.when(section == sections - 1)
                def send_film():
                    for copy in passing:
                        copy.start()

        for copy in saves:
            copy.wait()

    @pl.when(section > 0)
    def finish():
        for image in range(images):
            for part in range(HOPS):
                hop(image, part).wait_send()

    if direct:

        @pl.when(section == sections - 1)
        def own_film():
            film_out[...] = film_rows[...]
            for copy in passing:
                copy.wait_send()

        for step in range(1, sections):

            @pl.when(section == step - 1)
            def wait_film(step=step):
                passing[step - 1].wait_recv()


def specs(*spaces):
    return [
        pl.BlockSpec(memory_space={"v": pltpu.VMEM, "h": pl.ANY}[space])
        for space in "".join(spaces)
    ]


def weight_scratch():
    return [pltpu.VMEM(shape, jnp.bfloat16) for shape in WEIGHTS] + [
        pltpu.SemaphoreType.DMA((6,))
    ]


def block_cost(images, patches, factor):
    area = sum(rows * columns for rows, columns in WEIGHTS)
    return pl.CostEstimate(
        flops=images * (2 * patches * area + factor * patches * patches * D),
        bytes_accessed=2 * area + images * 64 * patches * D,
        transcendentals=images * patches * (FF + HEADS * patches),
    )


def pipeline_forward(bias, qkv_bias, ada, tokens, weights):
    images, patches, unused = tokens.shape
    sections = lax.axis_size("section")
    sizes = [(kept_shape(i, item[0], patches), item[1]) for i, item in enumerate(KEPT)]
    return pl.pallas_call(
        functools.partial(forward_kernel, sections, images),
        out_shape=[
            jax.ShapeDtypeStruct((images,) + shape, kind) for shape, kind in sizes
        ],
        in_specs=specs("vvv", "h" * 5),
        out_specs=specs("h" * len(KEPT)),
        scratch_shapes=[pltpu.VMEM(shape, kind) for shape, kind in sizes]
        + [pltpu.VMEM((D, patches), jnp.bfloat16)]
        + [pltpu.VMEM((images, patches, D), jnp.bfloat16)] * 2
        + weight_scratch()
        + [pltpu.SemaphoreType.DMA, pltpu.SemaphoreType.DMA((len(KEPT),))]
        + [pltpu.SemaphoreType.DMA((images, HOPS))] * 2,
        compiler_params=pltpu.CompilerParams(
            vmem_limit_bytes=62 << 20, collective_id=16, has_side_effects=True
        ),
        cost_estimate=block_cost(images, patches, 4),
        name="pipeline_forward",
    )(bias, qkv_bias, ada, tokens, *weights)


def pipeline_backward(ada, head_grad, weights, sources, film):
    images, patches, unused = head_grad.shape
    sections, direct = (lax.axis_size("section"), lax.axis_size("dp") == DIRECT)
    films = [jax.ShapeDtypeStruct((DIRECT,) + film.shape, film.dtype)] * (2 * direct)
    outs = pl.pallas_call(
        functools.partial(backward_kernel, sections, images, direct),
        out_shape=[
            jax.ShapeDtypeStruct((images, patches, width), kind) for width, kind in MADE
        ]
        + [jax.ShapeDtypeStruct((images, 8, D), jnp.float32)]
        + films,
        in_specs=specs("v", "h" * (5 + len(READ)), "v" * direct),
        out_specs=specs("h" * (len(MADE) + 1), "v" * len(films)),
        scratch_shapes=[
            pltpu.VMEM(kept_shape(name, KEPT[name][0], patches), KEPT[name][1]) for name in READ
        ]
        + [pltpu.VMEM((patches, width), kind) for width, kind in MADE[:-1]]
        + [
            pltpu.VMEM((patches, D), jnp.float32),
            pltpu.VMEM((patches, D), jnp.float32),
            pltpu.VMEM((D, patches), jnp.bfloat16),
            pltpu.VMEM((3 * D, patches), jnp.bfloat16),
            pltpu.VMEM((8, D), jnp.float32),
        ]
        + [pltpu.VMEM((images, patches, D), jnp.bfloat16)] * 2
        + weight_scratch()
        + [
            pltpu.SemaphoreType.DMA((len(READ),)),
            pltpu.SemaphoreType.DMA,
            pltpu.SemaphoreType.DMA((len(MADE),)),
        ]
        + [pltpu.SemaphoreType.DMA((images, HOPS))] * 2
        + [pltpu.SemaphoreType.DMA((DIRECT + sections,))] * 2,
        compiler_params=pltpu.CompilerParams(
            vmem_limit_bytes=62 << 20, collective_id=17, has_side_effects=True
        ),
        cost_estimate=block_cost(images, patches, 10),
        name="pipeline_backward",
    )(ada, head_grad, *weights, *sources, *([film] * direct))
    if direct:
        film_all = outs[-1].reshape(-1, film.shape[1])
    else:
        film_all = lax.all_gather(film, ("section", "dp"), tiled=True)
        film_all = film_all[-images * lax.axis_size("dp") :]
    return (outs[: len(MADE) + 1], film_all)


def head_step(residual, film, noise_part, mask_part, inv_count, w_out, b_out):
    shifting, scaling = (film[:, :D], film[:, D:])
    normed, invstd = normalize(residual)
    mixed = (normed * (1.0 + scaling[:, None]) + shifting[:, None]).astype(jnp.bfloat16)
    output = (
        jnp.einsum("bpd,dj->bpj", mixed, w_out, preferred_element_type=jnp.float32) + b_out
    )
    mismatch = output - noise_part
    mask_float = mask_part.astype(jnp.float32)[:, :, None]
    squared = jnp.sum(mask_float * mismatch * mismatch)
    d_output = (2.0 * inv_count * mask_float * mismatch).astype(jnp.bfloat16)
    g_output = jnp.einsum("bpd,bpj->dj", mixed, d_output, preferred_element_type=jnp.float32)
    d_mixed = jnp.einsum("bpj,dj->bpd", d_output, w_out, preferred_element_type=jnp.float32)
    d_film = jnp.concatenate(
        [jnp.sum(d_mixed, axis=1), jnp.sum(d_mixed * normed, axis=1)], axis=1
    ).astype(jnp.bfloat16)
    d_residual = norm_back(d_mixed * (1.0 + scaling[:, None]), normed, invstd)
    g_bias = jnp.sum(d_output.astype(jnp.float32), axis=(0, 1))
    return (squared, d_residual, d_film, g_output, g_bias)


def adam_update(weight, gradient, first_moment, second_moment, scaling):
    gradient = gradient * scaling
    first_new = BETA_ONE * first_moment + (1.0 - BETA_ONE) * gradient
    second_new = BETA_TWO * second_moment + (1.0 - BETA_TWO) * gradient * gradient
    ratio = (
        first_new
        / (1.0 - BETA_ONE**STEP_POWER)
        / (jnp.sqrt(second_new / (1.0 - BETA_TWO**STEP_POWER)) + ADAM_EPS)
    )
    return (weight - RATE * (ratio + DECAY * weight), first_new, second_new)


def body(
    latents,
    noise,
    timesteps,
    labels,
    patch_mask,
    w_in,
    w_down,
    b_blk,
    small_mats,
    small_bias,
    m_in,
    m_down,
    m_bias,
    m_small,
    m_sbias,
    v_in,
    v_down,
    v_bias,
    v_small,
    v_sbias,
):
    section_index = lax.axis_index("section")
    dp_index = lax.axis_index("dp")
    sections = lax.axis_size("section")
    is_first = section_index == 0
    is_last = section_index == sections - 1
    low = jnp.bfloat16
    images, patches = patch_mask.shape
    rows = w_in.shape[1]
    row_at = dp_index * rows
    ada_at = 4 * D + FF
    o_label = PATCH_IN + FREQ
    o_second = o_label + CLASSES
    o_film = o_second + D
    o_out = o_film + 2 * D

    def gathered(value, axis="dp", dim=0):
        return lax.all_gather(value, axis, axis=dim, tiled=True)

    in_low = w_in[0].astype(low)
    w_ada = in_low[:, ada_at:]
    w_qkv = gathered(in_low[:, : 3 * D])
    w_proj = gathered(in_low[:, 3 * D : 4 * D])
    w_hidden = gathered(in_low[:, 4 * D : ada_at])
    w_second = gathered(w_down[0].astype(low))

    small_low = small_mats.astype(low)
    edge_own = jnp.where(is_first, small_mats[:, :PATCH_IN], small_mats[:, -PATCH_IN:])
    bias_width = b_blk.shape[1]
    pieces = [
        b_blk[0],
        edge_own.reshape(-1),
        timesteps.astype(jnp.float32),
        labels.astype(jnp.float32),
        jnp.sum(patch_mask).astype(jnp.float32)[None],
    ]
    block = jnp.concatenate(pieces)[None]
    blocks = spread(block, "dp", 1)[:, 0]
    ends = [0]
    for piece in pieces:
        ends.append(ends[-1] + piece.shape[0])
    bias_full = rounded(blocks[:, : ends[1]].reshape(-1))
    w_edge = blocks[:, ends[1] : ends[2]].reshape(D, PATCH_IN).astype(low)
    times_all = blocks[:, ends[2] : ends[3]].reshape(-1).astype(jnp.int32)
    labels_all = blocks[:, ends[3] : ends[4]].reshape(-1).astype(jnp.int32)
    valid_total = jnp.sum(blocks[:, ends[4]])
    inv_count = 1.0 / (valid_total * PATCH_IN)
    weights = (w_qkv, w_proj, w_hidden, w_second)

    small_width = small_mats.shape[1]
    sbias_width = small_bias.shape[0]
    extra = -(-sbias_width // small_width)
    sbias_rows = jnp.pad(small_bias, (0, extra * small_width - sbias_width)).astype(low)
    small_block = jnp.concatenate([small_low, sbias_rows.reshape(extra, small_width)], axis=0)
    small_blocks = spread(small_block, "section", 2)
    small_rows = jnp.concatenate([small_blocks[i, :rows] for i in range(sections)], axis=1)
    small_used = (
        small_blocks[:, rows:].reshape(sections, -1)[:, :sbias_width].reshape(-1)
    ).astype(jnp.float32)

    shards = lax.axis_size("dp")
    time_low = time_features(times_all).astype(low)
    one_hot = label_table(labels_all)
    time_hidden = matmul_nt(time_low, small_rows[:, PATCH_IN:o_label]) + lax.dynamic_slice_in_dim(
        small_used, D + row_at, rows, 0
    )
    time_act = jax.nn.silu(time_hidden).astype(low)
    cond_part = matmul(time_act, small_rows[:, o_second:o_film])
    label_part = matmul_nt(one_hot, small_rows[:, o_label:o_second])
    cond_part = jnp.concatenate([cond_part, label_part], axis=1).reshape(shards, images, D + rows)
    cond_got = exchange(cond_part, "dp", 3)
    cond_own = (
        jnp.sum(cond_got[:, :, :D], axis=0)
        + small_used[2 * D : 3 * D]
        + jnp.swapaxes(cond_got[:, :, D:], 0, 1).reshape(images, D)
    )
    cond_cols = exchange(jnp.swapaxes(cond_own.reshape(images, shards, rows), 0, 1), "dp", 4)
    cond_first = cond_cols.reshape(shards * images, rows)
    cond_later = rounded(cond_first)
    cond_here = jnp.where(is_first, cond_first, cond_later)
    act_here = jax.nn.silu(cond_here).astype(low)
    act_later = jax.nn.silu(cond_later).astype(low)
    ada_part = jnp.concatenate(
        [matmul(act_here, w_ada), matmul(act_later, small_rows[:, o_film:o_out])], axis=1
    )
    ada_got = exchange(ada_part.reshape(shards, images * 8 * D // 128, 128), "dp", 5)
    ada_own = jnp.sum(ada_got, axis=0).reshape(images, 8 * D)
    film = ada_own[:, 6 * D :] + small_used[3 * D : 5 * D]
    ada = (ada_own[:, : 6 * D] + bias_full[ada_at:]).reshape(images, 6, D)
    qkv_bias = jnp.concatenate(
        [bias_full[:D], jnp.zeros((D,), jnp.float32), bias_full[D : 2 * D]]
    )[:, None]
    bias_row = bias_full[None, 2 * D : ada_at]

    fade = alpha_bar(timesteps)[:, None, None]
    noisy_low = (jnp.sqrt(fade) * latents + jnp.sqrt(1.0 - fade) * noise).astype(low)
    tokens = jnp.einsum(
        "bpi,di->bpd", noisy_low, w_edge, preferred_element_type=jnp.float32
    )
    tokens = tokens + small_used[:D] + positions(patches)[None]

    kept_all = pipeline_forward(bias_row, qkv_bias, ada, tokens, weights)

    squared, head_grad, d_film, g_output, g_out_bias = head_step(
        kept_all[OUTPUT],
        film,
        noise,
        patch_mask,
        inv_count,
        w_edge,
        small_used[5 * D :],
    )
    loss_part = jnp.where(is_last, squared * inv_count, 0.0)
    made_all, film_all = pipeline_backward(
        ada, head_grad, weights, [kept_all[name] for name in READ], d_film
    )

    def flat(whole):
        return whole.reshape(images * patches, whole.shape[2])

    d_second, d_pre, d_branch, d_qkv, d_tokens = [flat(whole) for whole in made_all[:5]]
    d_ada = made_all[5][:, :6].astype(low).reshape(images, 6 * D)

    token_sums = column_sum(d_tokens)
    g_edge = jnp.where(
        is_first,
        matmul_tn(d_tokens, noisy_low.reshape(images * patches, PATCH_IN)),
        g_output,
    )
    shard_wide, shard_down, right_sums, d_ada_all = row_sums(
        [flat(kept_all[name]) for name in (MIXED_ONE, ATT, MIXED_TWO, ACT)],
        [d_qkv, d_branch, d_pre, d_second],
        d_ada,
    )
    d_ada_all = d_ada_all.reshape(shards * images, 6 * D)

    cond_piece = matmul_nt(d_ada_all, w_ada) * silu_grad(cond_here)
    cond_pieces = spread(cond_piece, "section", 9)
    d_cond = matmul_nt(film_all, small_rows[:, o_film:o_out]) * silu_grad(cond_later)
    for layer in reversed(range(sections)):
        d_cond = rounded(d_cond + cond_pieces[layer])
    d_cond_rows = d_cond.astype(low)
    d_cond_all = jnp.swapaxes(spread(d_cond_rows, "dp", 10), 0, 1).reshape(shards * images, D)
    d_time = (
        matmul_nt(d_cond_all, small_rows[:, o_second:o_film]) * silu_grad(time_hidden)
    ).astype(low)
    bias_sums = jnp.concatenate(
        [
            right_sums[0][:D],
            right_sums[0][2 * D :],
            right_sums[1],
            right_sums[2],
            right_sums[3],
            column_sum(d_ada),
        ]
    )
    sums = jnp.concatenate(
        [
            bias_sums.reshape(shards, -1),
            g_edge.reshape(shards, -1),
            jnp.broadcast_to(token_sums, (shards, D)),
            jnp.broadcast_to(g_out_bias, (shards, PATCH_IN)),
            jnp.broadcast_to(column_sum(d_time), (shards, rows)),
        ],
        axis=1,
    )
    sums = exchange(sums[:, None], "dp", 11)[:, 0]
    shard_ada = matmul_tn(act_here, d_ada_all)
    shard_in = jnp.concatenate([shard_wide, shard_ada], axis=1)
    edge_end = bias_width + rows * PATCH_IN
    shard_bias = jnp.sum(sums[:, :bias_width], axis=0)
    edge_rows = jnp.sum(sums[:, bias_width:edge_end], axis=0).reshape(rows, PATCH_IN)
    token_sums = jnp.sum(sums[:, edge_end : edge_end + D], axis=0)
    out_sums = jnp.sum(sums[:, edge_end + D : edge_end + D + PATCH_IN], axis=0)
    time_sums = sums[:, edge_end + D + PATCH_IN :].reshape(-1)
    small_grad = jnp.concatenate(
        [
            edge_rows,
            matmul_tn(d_time, time_low),
            matmul_tn(d_cond_rows, one_hot),
            matmul_tn(time_act, d_cond_all),
            matmul_tn(act_later, film_all),
            edge_rows,
        ],
        axis=1,
    )
    small_shard = lax.dynamic_slice_in_dim(small_grad, section_index * small_width, small_width, 1)
    sbias_grad = jnp.concatenate(
        [token_sums, time_sums, column_sum(d_cond_all), column_sum(film_all), out_sums]
    )
    sbias_shard = lax.dynamic_slice_in_dim(
        sbias_grad, section_index * sbias_width, sbias_width, 0
    )

    dp_zero = (dp_index == 0).astype(jnp.float32)
    squares = (
        jnp.sum(shard_in * shard_in)
        + jnp.sum(shard_down * shard_down)
        + jnp.sum(shard_bias * shard_bias)
        + jnp.sum(small_shard * small_shard)
        + dp_zero * jnp.sum(sbias_shard * sbias_shard)
    )
    pair = jnp.broadcast_to(jnp.stack([squares, loss_part])[:, None], (2, 128))
    pair = jnp.sum(spread(pair, "dp", 14), axis=0)
    pair = jnp.sum(spread(pair, "section", 15), axis=0)
    norm_square, loss = (pair[0, 0], pair[1, 0])
    grad_norm = jnp.sqrt(norm_square)
    scaling = jnp.minimum(1.0, CLIP / grad_norm)
    new_in, first_in, second_in = adam_update(w_in, shard_in[None], m_in, v_in, scaling)
    new_down, first_down, second_down = adam_update(
        w_down, shard_down[None], m_down, v_down, scaling
    )
    new_bias, first_bias, second_bias = adam_update(
        b_blk, shard_bias[None], m_bias, v_bias, scaling
    )
    new_small, first_small, second_small = adam_update(
        small_mats, small_shard, m_small, v_small, scaling
    )
    new_sbias, first_sbias, second_sbias = adam_update(
        small_bias, sbias_shard, m_sbias, v_sbias, scaling
    )
    return (
        loss,
        grad_norm,
        new_in,
        first_in,
        second_in,
        new_down,
        first_down,
        second_down,
        new_bias,
        first_bias,
        second_bias,
        new_small,
        first_small,
        second_small,
        new_sbias,
        first_sbias,
        second_sbias,
    )


def solution(mesh):
    in_specs = (
        P("dp", None, None),
        P("dp", None, None),
        P("dp"),
        P("dp"),
        P("dp", None),
        P("section", "dp", None),
        P("section", "dp", None),
        P("section", "dp"),
        P("dp", "section"),
        P("section"),
        P("section", "dp", None),
        P("section", "dp", None),
        P("section", "dp"),
        P("dp", "section"),
        P("section"),
        P("section", "dp", None),
        P("section", "dp", None),
        P("section", "dp"),
        P("dp", "section"),
        P("section"),
    )
    out_specs = (
        P(),
        P(),
        P("section", "dp", None),
        P("section", "dp", None),
        P("section", "dp", None),
        P("section", "dp", None),
        P("section", "dp", None),
        P("section", "dp", None),
        P("section", "dp"),
        P("section", "dp"),
        P("section", "dp"),
        P("dp", "section"),
        P("dp", "section"),
        P("dp", "section"),
        P("section"),
        P("section"),
        P("section"),
    )
    return jax.shard_map(body, mesh=mesh, in_specs=in_specs, out_specs=out_specs, check_vma=False)
```

```python
import functools
import math

import jax
import jax.numpy as jnp
from jax import lax
from jax.experimental import pallas as pl
from jax.experimental.pallas import tpu as pltpu
from jax.sharding import PartitionSpec as P

D = 1152
HEADS = 16
HEAD_DIM = 72
FF = 4608
CLASSES = 1000
FREQ = 256
PATCH_IN = 16
GRID = 16


EPS_NORM = 1e-06
CLIP = 0.001
RATE = 0.005
BETA_ONE = 0.9
BETA_TWO = 0.999
ADAM_EPS = 1e-08
DECAY = 0.01
STEP_POWER = 10.0


def passed_along(value, axis, steps):
    count = lax.axis_size(axis)
    first, last = (max(0, -steps), min(count, count - steps))
    return lax.ppermute(value, axis, [(source, source + steps) for source in range(first, last)])


def matmul(left_side, right_side):
    return jnp.dot(left_side, right_side, preferred_element_type=jnp.float32)


def matmul_tn(left_side, right_side):
    return lax.dot_general(
        left_side, right_side, (((0,), (0,)), ((), ())), preferred_element_type=jnp.float32
    )


def matmul_nt(left_side, right_side):
    return lax.dot_general(
        left_side, right_side, (((1,), (1,)), ((), ())), preferred_element_type=jnp.float32
    )


def column_sum(values):
    return jnp.sum(values.astype(jnp.float32), axis=0)


def normalize(values):
    center = values - jnp.mean(values, axis=-1, keepdims=True)
    invstd = lax.rsqrt(jnp.mean(center * center, axis=-1, keepdims=True) + EPS_NORM)
    return (center * invstd, invstd)


def norm_back(grad_normed, normed, invstd):
    return invstd * (
        grad_normed
        - jnp.mean(grad_normed, axis=-1, keepdims=True)
        - normed * jnp.mean(grad_normed * normed, axis=-1, keepdims=True)
    )


def gelu_tanh(values):
    return (
        0.5
        * values
        * (1.0 + jnp.tanh(0.7978845608028654 * (values + 0.044715 * values * values * values)))
    )


def gelu_grad(values):
    inner = jnp.tanh(0.7978845608028654 * (values + 0.044715 * values * values * values))
    return 0.5 * (1.0 + inner) + 0.5 * values * (1.0 - inner * inner) * 0.7978845608028654 * (
        1.0 + 0.134145 * values * values
    )


def silu_grad(values):
    sigma = jax.nn.sigmoid(values)
    return sigma * (1.0 + values * (1.0 - sigma))


def positions(patches):
    quarter = D // 4
    omega = jnp.exp(-math.log(10000.0) * jnp.arange(quarter, dtype=jnp.float32) / quarter)
    spot = jnp.arange(patches, dtype=jnp.int32)
    row_angle = (spot // GRID).astype(jnp.float32)[:, None] * omega[None, :]
    col_angle = (spot % GRID).astype(jnp.float32)[:, None] * omega[None, :]
    return jnp.concatenate(
        [jnp.sin(row_angle), jnp.cos(row_angle), jnp.sin(col_angle), jnp.cos(col_angle)], axis=1
    )


def time_features(time_steps):
    half = FREQ // 2
    freqs = jnp.exp(-math.log(10000.0) * jnp.arange(half, dtype=jnp.float32) / half)
    angles = time_steps.astype(jnp.float32)[:, None] * freqs[None, :]
    return jnp.concatenate([jnp.cos(angles), jnp.sin(angles)], axis=1)


def alpha_bar(time_steps):
    return jnp.cos((time_steps.astype(jnp.float32) / 1000.0 + 0.008) / 1.008 * (math.pi / 2)) ** 2


def label_table(label_part):
    return (label_part[:, None] == jnp.arange(CLASSES, dtype=jnp.int32)[None, :]).astype(
        jnp.bfloat16
    )


MESH = pl.DeviceIdType.MESH
DIRECT = 8


def rounded(values):
    return lax.reduce_precision(values, 8, 7)


def meet(axis, count, here):
    barrier = pltpu.get_barrier_semaphore()
    for step in range(1, count):
        pl.semaphore_signal(
            barrier, inc=1, device_id={axis: lax.rem(here + step, count)}, device_id_type=MESH
        )
    pl.semaphore_wait(barrier, count - 1)


def share_kernel(axis, count, personal, in_ref, out_ref, send_sem, recv_sem):
    here = lax.axis_index(axis)
    meet(axis, count, here)
    copies = []
    for step in range(1, count):
        target = lax.rem(here + step, count)
        copy = pltpu.make_async_remote_copy(
            src_ref=in_ref.at[target] if personal else in_ref,
            dst_ref=out_ref.at[here],
            send_sem=send_sem.at[step - 1],
            recv_sem=recv_sem.at[step - 1],
            device_id={axis: target},
            device_id_type=MESH,
        )
        copy.start()
        copies.append(copy)
    out_ref[here] = in_ref[here] if personal else in_ref[...]
    for copy in copies:
        copy.wait()


def share(value, axis, personal, ident):
    count = lax.axis_size(axis)
    shape = value.shape if personal else (count,) + value.shape
    return pl.pallas_call(
        functools.partial(share_kernel, axis, count, personal),
        out_shape=jax.ShapeDtypeStruct(shape, value.dtype),
        in_specs=[pl.BlockSpec(memory_space=pltpu.VMEM)],
        out_specs=pl.BlockSpec(memory_space=pltpu.VMEM),
        scratch_shapes=[
            pltpu.SemaphoreType.DMA((count - 1,)),
            pltpu.SemaphoreType.DMA((count - 1,)),
        ],
        compiler_params=pltpu.CompilerParams(collective_id=ident, has_side_effects=True),
        name="share",
    )(value)


def spread(value, axis, ident):
    if lax.axis_size(axis) > DIRECT:
        return lax.all_gather(value, axis)
    return share(value, axis, False, ident)


def exchange(value, axis, ident):
    if lax.axis_size(axis) > DIRECT:
        return lax.all_to_all(value, axis, 0, 0)
    return share(value, axis, True, ident)


FINAL, LATER, NEAR, FAR, PASS = range(5)
STEPS = 16
CHIPS = 4


def sums_kernel(units, rows, *refs):
    lefts, rights, given = (refs[:4], refs[4:8], refs[8])
    owns, finals, laters = (refs[9:11], refs[11:13], refs[13:15])
    bias_out, spread_out, refs = (refs[15], refs[16], refs[17:])
    (
        left_v,
        right_v,
        product,
        got,
        own_v,
        stage,
        near,
        far,
        passed,
        left_sem,
        right_sem,
        send_sem,
        recv_sem,
        own_sem,
        stage_sem,
        block_sem,
        pass_sem,
        given_send,
        given_recv,
    ) = refs
    here = lax.axis_index("dp")
    core, chip = (lax.rem(here, 2), here // 2)
    partner = {"dp": here + 1 - 2 * core}
    tall = CHIPS * rows
    meet("dp", DIRECT, here)
    spreading = []
    for step in range(1, DIRECT):
        copy = pltpu.make_async_remote_copy(
            src_ref=given,
            dst_ref=spread_out.at[here],
            send_sem=given_send.at[step - 1],
            recv_sem=given_recv.at[step - 1],
            device_id={"dp": lax.rem(here + step, DIRECT)},
            device_id_type=MESH,
        )
        copy.start()
        spreading.append(copy)
    spread_out[here] = given[...]
    places = {NEAR: near, FAR: far, PASS: passed}

    def placed(pair, slot):
        wide, down = pair
        side_by_side = wide.shape[1] // D
        if slot < side_by_side:
            return wide.at[:, pl.ds(slot * D, D)]
        return down.at[pl.ds((slot - side_by_side) * rows, rows)]

    plan, last, slots = ([], [None, None], [1, 1])
    for left, left_at, right, right_at, gathers, slot in units:
        fresh = []
        for side, key in enumerate(((left, left_at), (right, right_at))):
            fresh.append(last[side] != key)
            if fresh[-1]:
                slots[side] = 1 - slots[side]
                last[side] = key
        plan.append((tuple(slots), tuple(fresh)))
    def loads_of(index):
        left, left_at, right, right_at, gathers, slot = units[index]
        (left_slot, right_slot), (left_fresh, right_fresh) = plan[index]
        copies = []
        if left_fresh:
            source = lefts[left].at[:, pl.ds(left_at, D)]
            copies.append(
                pltpu.make_async_copy(source, left_v.at[left_slot], left_sem.at[left_slot])
            )
        if right_fresh:
            source = rights[right].at[:, pl.ds(right_at, D)]
            copies.append(
                pltpu.make_async_copy(source, right_v.at[right_slot], right_sem.at[right_slot])
            )
        return copies

    pending, crossing, leaving, keeping = ({}, {}, {}, {})

    def load(index):
        pending[index] = loads_of(index)
        for copy in pending[index]:
            copy.start()

    def to_partner(source, target, sems):
        copy = pltpu.make_async_remote_copy(
            src_ref=source,
            dst_ref=target,
            send_sem=send_sem.at[sems],
            recv_sem=recv_sem.at[sems],
            device_id=partner,
            device_id_type=MESH,
        )
        copy.start()
        return copy

    def multiply(index):
        gathers = units[index][4]
        left_slot, right_slot = plan[index][0]
        for copy in pending[index]:
            copy.wait()
        if index + 1 < len(units):
            load(index + 1)
        if index >= 2:
            for copy in crossing[index - 2]:
                copy.wait_send()
        slot, place = (index % 2, index % 4)
        product[slot] = contract(left_v[left_slot], right_v[right_slot], 0, 0)
        if gathers is None or gathers == 0:
            ones = jnp.ones((8, right_v.shape[1]), jnp.bfloat16)
            bias_out[units[index][5]] = matmul(ones, right_v[right_slot])
        if gathers is None:
            crossing[index] = [
                to_partner(
                    product.at[slot, pl.ds(pl.multiple_of((2 * i + 1 - core) * rows, 8), rows)],
                    got.at[place, pl.ds(i * rows, rows)],
                    place * CHIPS + i,
                )
                for i in range(CHIPS)
            ]
        else:
            crossing[index] = [
                to_partner(
                    product.at[slot, pl.ds(pl.multiple_of((1 - core) * tall, 8), tall)],
                    got.at[place],
                    place * CHIPS,
                )
            ]

    def crossed(source, kind, slot, to, sem):
        pair = {FINAL: finals, LATER: laters}.get(kind)
        return pltpu.make_async_remote_copy(
            src_ref=source,
            dst_ref=places[kind].at[slot] if pair is None else placed(pair, slot),
            send_sem=sem,
            recv_sem=block_sem.at[kind, slot],
            device_id={"dp": 2 * to + core},
            device_id_type=MESH,
        )

    def landed(kind, slot):
        crossed(stage.at[0, 0], kind, slot, chip, stage_sem.at[0, 0]).wait_recv()

    def filled(target, index, block, gathers, added=None):
        slot, place = (index % 2, index % 4)
        base = (2 * block + core) * rows if gathers is None else core * tall + block * rows

        @pl.loop(0, rows // STEPS)
        def run(step):
            at = step * STEPS
            value = (
                product[slot, pl.ds(pl.multiple_of(base + at, STEPS), STEPS)]
                + got[place, pl.ds(pl.multiple_of(block * rows + at, STEPS), STEPS)]
            )
            to = pl.ds(pl.multiple_of(at, STEPS), STEPS)
            if added is not None:
                value = value + added[to].astype(jnp.float32)
            target[to] = value.astype(target.dtype)

    def route(index, block, owner, slot, gathers):
        side = index % 3

        def case(at, kind, to, added=None):
            copy = crossed(
                stage.at[side, block], kind, slot, to, stage_sem.at[side, block]
            )

            @pl.when(chip == at)
            def act():
                if added is not None:
                    landed(added, slot)
                filled(
                    stage.at[side, block],
                    index,
                    block,
                    gathers,
                    None if added is None else places[added].at[slot],
                )
                copy.start()

            leaving[index].append((chip == at, copy.wait_send))

        keep = pltpu.make_async_copy(
            own_v.at[side, block], placed(owns, slot), own_sem.at[side, block]
        )

        @pl.when(chip == owner)
        def hold():
            filled(own_v.at[side, block], index, block, gathers)
            keep.start()

        leaving[index].append((chip == owner, keep.wait))
        flip = (lambda at: at) if owner < 2 else (lambda at: CHIPS - 1 - at)
        if owner in (0, CHIPS - 1):
            case(flip(3), FAR, flip(2))
            case(flip(1), FINAL, flip(0))
            case(flip(2), PASS, flip(1), FAR)
        else:
            case(flip(3), NEAR, flip(2))
            case(flip(0), FINAL, flip(1))
            case(flip(2), LATER, flip(1), NEAR)

    def blocks_of(index):
        gathers = units[index][4]
        if gathers is None:
            return [(owner, owner, units[index][5]) for owner in (0, 3, 1, 2)]
        return [(block, gathers, units[index][5] + block) for block in range(CHIPS)]

    def combine(index):
        for copy in crossing[index]:
            copy.wait_recv()
        if index >= 3:
            finish(index - 3)
        leaving[index] = []
        for block, owner, slot in blocks_of(index):
            route(index, block, owner, slot, units[index][4])

    def finish(index):
        for condition, wait in leaving[index]:

            @pl.when(condition)
            def settle(wait=wait):
                wait()

    def pass_on(index):
        for block, owner, slot in blocks_of(index):
            if owner not in (0, CHIPS - 1):
                continue
            middle = 1 if owner == 0 else CHIPS - 2

            @pl.when(chip == middle)
            def forward(slot=slot, owner=owner):
                landed(PASS, slot)
                crossed(passed.at[slot], LATER, slot, owner, pass_sem.at[slot]).start()

    total = len(units)
    load(0)
    multiply(0)
    for index in range(total):
        if index + 1 < total:
            multiply(index + 1)
        combine(index)
        if index >= 1:
            pass_on(index - 1)
    pass_on(total - 1)
    for index in range(max(0, total - 3), total):
        finish(index)
    for index in range(max(0, total - 2), total):
        for copy in crossing[index]:
            copy.wait_send()
    for index in range(total):
        for block, owner, slot in blocks_of(index):

            @pl.when(chip == owner)
            def received(slot=slot):
                landed(FINAL, slot)
                landed(LATER, slot)

            if owner in (0, CHIPS - 1):

                @pl.when(chip == (1 if owner == 0 else CHIPS - 2))
                def sent(slot=slot, owner=owner):
                    crossed(passed.at[slot], LATER, slot, owner, pass_sem.at[slot]).wait_send()

    for copy in spreading:
        copy.wait()


def line_sums(units, lefts, rights, rows, ident, given):
    tokens = lefts[0].shape[0]
    places = sum(unit[4] is None for unit in units) + 4
    block = (rows, D)
    outs = pl.pallas_call(
        functools.partial(sums_kernel, units, rows),
        out_shape=[
            jax.ShapeDtypeStruct(shape, kind)
            for kind in (jnp.float32, jnp.bfloat16, jnp.bfloat16)
            for shape in ((rows, (places - CHIPS) * D), (CHIPS * rows, D))
        ]
        + [
            jax.ShapeDtypeStruct((places - CHIPS + 1, 8, D), jnp.float32),
            jax.ShapeDtypeStruct((DIRECT,) + given.shape, given.dtype),
        ],
        in_specs=specs("h" * 8, "v"),
        out_specs=specs("h" * 6, "vv"),
        scratch_shapes=[
            pltpu.VMEM((2, tokens, D), jnp.bfloat16),
            pltpu.VMEM((2, tokens, D), jnp.bfloat16),
            pltpu.VMEM((2, 8 * rows, D), jnp.float32),
            pltpu.VMEM((4, 4 * rows, D), jnp.float32),
            pltpu.VMEM((3, 4) + block, jnp.float32),
            pltpu.VMEM((3, 4) + block, jnp.bfloat16),
            pltpu.VMEM((places,) + block, jnp.bfloat16),
            pltpu.VMEM((places,) + block, jnp.bfloat16),
            pltpu.VMEM((places,) + block, jnp.bfloat16),
            pltpu.SemaphoreType.DMA((2,)),
            pltpu.SemaphoreType.DMA((2,)),
            pltpu.SemaphoreType.DMA((16,)),
            pltpu.SemaphoreType.DMA((16,)),
            pltpu.SemaphoreType.DMA((3, 4)),
            pltpu.SemaphoreType.DMA((3, 4)),
            pltpu.SemaphoreType.DMA((5, places)),
            pltpu.SemaphoreType.DMA((places,)),
            pltpu.SemaphoreType.DMA((DIRECT - 1,)),
            pltpu.SemaphoreType.DMA((DIRECT - 1,)),
        ],
        compiler_params=pltpu.CompilerParams(
            collective_id=ident, has_side_effects=True, vmem_limit_bytes=62 << 20
        ),
        cost_estimate=pl.CostEstimate(
            flops=2 * tokens * D * D * len(units),
            bytes_accessed=len(units) * tokens * D * 4,
            transcendentals=0,
        ),
        name="line_sums",
    )(*lefts, *rights, given)
    wide, down = [
        outs[i] + outs[2 + i].astype(jnp.float32) + outs[4 + i].astype(jnp.float32)
        for i in range(2)
    ]
    return (wide, down, outs[6][:, 0], outs[7])


def row_sums(lefts, rights, given):
    count = lax.axis_size("dp")
    if count != DIRECT:
        products = [matmul_tn(one, other) for one, other in zip(lefts, rights)]
        sums = [lax.psum_scatter(one, "dp", scatter_dimension=0, tiled=True) for one in products]
        wide = jnp.concatenate([sums[0], sums[1], sums[2]], axis=1)
        given = lax.all_gather(given, "dp")
        return (wide, sums[3], [column_sum(one) for one in rights], given)
    rows = D // count
    parts = FF // D
    attention = [(0, 0, 0, i * D, None, i) for i in range(3)] + [(1, 0, 1, 0, None, 3)]
    hidden = [(2, 0, 2, i * D, None, 4 + i) for i in range(parts)]
    second = [(3, i * D, 3, 0, i, 4 + parts) for i in (0, 3, 1, 2)]
    units = hidden[:1] + second[:2] + hidden[1:2] + second[2:] + hidden[2:] + attention
    wide, down, bias, given_all = line_sums(tuple(units), lefts, rights, rows, 12, given)
    sums = [bias[:3].reshape(-1), bias[3], bias[4 : 4 + parts].reshape(-1), bias[4 + parts]]
    return (wide, down, sums, given_all)


GROUP = 4


def contract(left_side, right_side, left_axis, right_axis):
    return lax.dot_general(
        left_side,
        right_side,
        (((left_axis,), (right_axis,)), ((), ())),
        preferred_element_type=jnp.float32,
    )


def heads_of(ref, at, group):
    return [
        ref[at + head * HEAD_DIM : at + (head + 1) * HEAD_DIM] for head in group
    ]


def softmax_down(scores):
    weights = jnp.exp(scores - jnp.max(scores, axis=0, keepdims=True))
    return weights * (1.0 / jnp.sum(weights, axis=0, keepdims=True))


def stacked(values):
    return jnp.concatenate([value.astype(jnp.bfloat16) for value in values], axis=0)


def attend_kernel(qkv_ref, out_ref):
    scaling = HEAD_DIM ** (-0.5)
    for first in range(0, HEADS, GROUP):
        group = range(first, first + GROUP)
        rows = slice(first * HEAD_DIM, (first + GROUP) * HEAD_DIM)
        queries, keys = (heads_of(qkv_ref, 0, group), heads_of(qkv_ref, D, group))
        values = heads_of(qkv_ref, 2 * D, group)
        scores = [contract(key, query, 0, 0) * scaling for key, query in zip(keys, queries)]
        probs = [softmax_down(score).astype(jnp.bfloat16) for score in scores]
        out_ref[rows] = stacked([contract(v, p, 1, 0) for v, p in zip(values, probs)])


def attend_back_kernel(qkv_ref, grad_ref, out_ref):
    scaling = HEAD_DIM ** (-0.5)
    for first in range(0, HEADS, GROUP):
        group = range(first, first + GROUP)
        at, to = (first * HEAD_DIM, (first + GROUP) * HEAD_DIM)
        queries, keys = (heads_of(qkv_ref, 0, group), heads_of(qkv_ref, D, group))
        values, grads = (heads_of(qkv_ref, 2 * D, group), heads_of(grad_ref, 0, group))
        scores = [contract(key, query, 0, 0) * scaling for key, query in zip(keys, queries)]
        d_probs = [contract(value, grad, 0, 0) for value, grad in zip(values, grads)]
        probs = [softmax_down(score) for score in scores]
        d_scores = [
            (p * (d - jnp.sum(p * d, axis=0, keepdims=True))).astype(jnp.bfloat16)
            for p, d in zip(probs, d_probs)
        ]
        lows = [p.astype(jnp.bfloat16) for p in probs]
        out_ref[at:to] = stacked([contract(k, d, 1, 0) * scaling for k, d in zip(keys, d_scores)])
        out_ref[D + at : D + to] = stacked(
            [contract(q, d, 1, 1) * scaling for q, d in zip(queries, d_scores)]
        )
        out_ref[2 * D + at : 2 * D + to] = stacked(
            [contract(g, p, 1, 1) for g, p in zip(grads, lows)]
        )


ROW_BLOCK = 64
HOPS = 3
RESIDUAL, MIXED_ONE, QKV, ATT, BRANCH, MIDDLE = range(6)
MIXED_TWO, PRE, ACT, SECOND, OUTPUT = range(6, 11)
D_SECOND, D_PRE, D_BRANCH, D_QKV, D_RESIDUAL = range(5)
WIDE, LOW = (jnp.float32, jnp.bfloat16)
KEPT = (
    (D, WIDE),
    (D, LOW),
    (3 * D, LOW),
    (D, LOW),
    (D, WIDE),
    (D, WIDE),
    (D, LOW),
    (FF, WIDE),
    (FF, LOW),
    (D, WIDE),
    (D, WIDE),
)
READ = (RESIDUAL, QKV, BRANCH, MIDDLE, PRE, SECOND)
MADE = ((D, LOW), (FF, LOW), (D, LOW), (3 * D, LOW), (D, LOW))
WEIGHTS = ((D, 3 * D), (D, D), (D, FF), (FF, D))


def kept_shape(name, width, patches):
    return (width, patches) if name == QKV else (patches, width)


def by_rows(patches, step):
    @pl.loop(0, patches // ROW_BLOCK)
    def run(index):
        step(pl.ds(pl.multiple_of(index * ROW_BLOCK, ROW_BLOCK), ROW_BLOCK))


def started(source, target, sem):
    copy = pltpu.make_async_copy(source, target, sem)
    copy.start()
    return copy


def parts_of(whole, parts):
    width = whole // parts
    return [slice(part * width, part * width + width) for part in range(parts)]


def wait_first(image, loads):
    @pl.when(image == 0)
    def wait():
        for load in loads:
            load.wait()


def hop_of(send, received, send_sem, recv_sem, target):
    def hop(image, part):
        cols = pl.ds(part * (D // HOPS), D // HOPS)
        return pltpu.make_async_remote_copy(
            src_ref=send.at[image, :, cols],
            dst_ref=received.at[image, :, cols],
            send_sem=send_sem.at[image, part],
            recv_sem=recv_sem.at[image, part],
            device_id={"section": target},
            device_id_type=MESH,
        )

    return hop


def forward_kernel(sections, images, bias, qkv_bias, ada, tokens, wx, ws, *refs):
    count, patches = (len(KEPT), tokens.shape[1])
    outs, scratch = (refs[:count], refs[count:])
    kept = scratch[:count]
    (
        att_down,
        send,
        received,
        wq_v,
        wp_v,
        wh_v,
        ws_v,
        w_sem,
        x_sem,
        out_sem,
        send_sem,
        recv_sem,
    ) = scratch[count:]
    section = lax.axis_index("section")
    loads = [
        started(wx.at[:, cols], wq_v.at[:, cols], w_sem.at[i])
        for i, cols in enumerate(parts_of(3 * D, 3))
    ]
    loads.append(started(wx.at[:, pl.ds(3 * D, D)], wp_v, w_sem.at[3]))
    loads.append(started(wx.at[:, pl.ds(4 * D, FF)], wh_v, w_sem.at[4]))
    loads.append(started(ws, ws_v, w_sem.at[5]))
    meet("section", sections, section)
    hop = hop_of(send, received, send_sem, recv_sem, lax.rem(section + 1, sections))
    residual = kept[RESIDUAL]

    @pl.loop(0, images)
    def run(image):
        saves = []

        def save(name):
            saves.append(started(kept[name], outs[name].at[image], out_sem.at[name]))

        @pl.when(section == 0)
        def take_tokens():
            started(tokens.at[image], residual, x_sem).wait()

        @pl.when(section > 0)
        def take_received():
            for part in range(HOPS):
                hop(image, part).wait_recv()
            residual[...] = received[image].astype(jnp.float32)

        save(RESIDUAL)
        modulation = ada[image]

        def mix_one(at):
            normed, unused = normalize(residual[at])
            kept[MIXED_ONE][at] = (normed * (1.0 + modulation[1:2]) + modulation[0:1]).astype(
                jnp.bfloat16
            )

        by_rows(patches, mix_one)
        save(MIXED_ONE)
        wait_first(image, loads[:3])
        for cols in parts_of(3 * D, 3):
            kept[QKV][cols] = (
                contract(wq_v[:, cols], kept[MIXED_ONE][...], 0, 1) + qkv_bias[cols]
            ).astype(jnp.bfloat16)
        save(QKV)
        attend_kernel(kept[QKV], att_down)
        wait_first(image, loads[3:4])
        kept[BRANCH][...] = contract(att_down[...], wp_v[...], 0, 0) + bias[:, :D]
        kept[ATT][...] = att_down[...].T
        save(BRANCH)
        save(ATT)

        def mix_two(at):
            middle = residual[at] + modulation[2:3] * kept[BRANCH][at]
            kept[MIDDLE][at] = middle
            normed, unused = normalize(middle)
            kept[MIXED_TWO][at] = (normed * (1.0 + modulation[4:5]) + modulation[3:4]).astype(
                jnp.bfloat16
            )

        by_rows(patches, mix_two)
        save(MIDDLE)
        save(MIXED_TWO)
        wait_first(image, loads[4:5])
        for part, cols in enumerate(parts_of(FF, FF // D)):
            pre = (
                matmul(kept[MIXED_TWO][...], wh_v[:, cols])
                + bias[:, D + part * D : 2 * D + part * D]
            )
            kept[PRE][:, cols] = pre
            kept[ACT][:, cols] = gelu_tanh(pre).astype(jnp.bfloat16)
        save(PRE)
        save(ACT)
        wait_first(image, loads[5:])
        for part, cols in enumerate(parts_of(D, HOPS)):
            second = (
                matmul(kept[ACT][...], ws_v[:, cols])
                + bias[:, D + FF + cols.start : D + FF + cols.stop]
            )
            kept[SECOND][:, cols] = second
            output = kept[MIDDLE][:, cols] + modulation[5:6, cols] * second
            kept[OUTPUT][:, cols] = output
            send[image, :, cols] = output.astype(jnp.bfloat16)

            @pl.when(section < sections - 1)
            def pass_on(part=part):
                hop(image, part).start()

        save(SECOND)
        save(OUTPUT)
        for copy in saves:
            copy.wait()

    @pl.when(section < sections - 1)
    def finish():
        for image in range(images):
            for part in range(HOPS):
                hop(image, part).wait_send()


def backward_kernel(sections, images, direct, ada, head_grad, wx, ws, *refs):
    reads, made, patches = (len(READ), len(MADE), head_grad.shape[1])
    sources, refs = (refs[:reads], refs[reads:])
    if direct:
        film, refs = (refs[0], refs[1:])
    outs, ada_out, refs = (refs[:made], refs[made], refs[made + 1 :])
    if direct:
        film_rows, film_out, refs = (refs[0], refs[1], refs[2:])
    kept = {name: refs[i] for i, name in enumerate(READ)}
    grads = refs[reads : reads + made - 1]
    (
        flow,
        mixed,
        att_grad,
        qkv_grad,
        sums,
        send,
        received,
        wq_v,
        wp_v,
        wh_v,
        ws_v,
        w_sem,
        in_sem,
        x_sem,
        out_sem,
        send_sem,
        recv_sem,
        film_send,
        film_recv,
    ) = refs[reads + made - 1 :]
    section = lax.axis_index("section")
    here = lax.axis_index("dp")

    def fetching(name, image):
        index = READ.index(name)
        return pltpu.make_async_copy(sources[index].at[image], kept[name], in_sem.at[index])

    fetching(SECOND, 0).start()
    loads = [started(ws, ws_v, w_sem.at[0])]
    for name in READ:
        if name != SECOND:
            fetching(name, 0).start()
    loads.append(started(wx.at[:, pl.ds(4 * D, FF)], wh_v, w_sem.at[1]))
    loads.append(started(wx.at[:, pl.ds(3 * D, D)], wp_v, w_sem.at[2]))
    loads.append(started(wx.at[:, pl.ds(0, 3 * D)], wq_v, w_sem.at[3]))
    spreading, passing = ([], [])
    if direct:
        barrier = pltpu.get_barrier_semaphore()
        for axis, me, size in (("section", section, sections), ("dp", here, DIRECT)):
            for step in range(1, size):
                pl.semaphore_signal(
                    barrier, inc=1, device_id={axis: lax.rem(me + step, size)}, device_id_type=MESH
                )
        pl.semaphore_wait(barrier, sections + DIRECT - 2)
        for step in range(1, DIRECT):
            copy = pltpu.make_async_remote_copy(
                src_ref=film,
                dst_ref=film_rows.at[here],
                send_sem=film_send.at[step - 1],
                recv_sem=film_recv.at[step - 1],
                device_id={"dp": lax.rem(here + step, DIRECT)},
                device_id_type=MESH,
            )
            copy.start()
            spreading.append(copy)
        film_rows[here] = film[...]
        for step in range(1, sections):
            passing.append(
                pltpu.make_async_remote_copy(
                    src_ref=film_rows,
                    dst_ref=film_out,
                    send_sem=film_send.at[DIRECT - 2 + step],
                    recv_sem=film_recv.at[DIRECT - 2 + step],
                    device_id={"section": lax.rem(section + step, sections)},
                    device_id_type=MESH,
                )
            )
    else:
        meet("section", sections, section)
    hop = hop_of(send, received, send_sem, recv_sem, lax.rem(section + sections - 1, sections))

    @pl.loop(0, images)
    def run(image):
        saves = []

        def save(name, value=None):
            source = grads[name] if value is None else value
            saves.append(started(source, outs[name].at[image], out_sem.at[name]))

        def fetch_next(*names):
            @pl.when(image + 1 < images)
            def start():
                for name in names:
                    fetching(name, image + 1).start()

        @pl.when(section == sections - 1)
        def take_head():
            started(head_grad.at[image], flow, x_sem).wait()

        @pl.when(section < sections - 1)
        def take_received():
            for part in range(HOPS):
                hop(image, part).wait_recv()
            flow[...] = received[image].astype(jnp.float32)

        modulation = ada[image]
        sums[...] = jnp.zeros_like(sums)

        def add_sum(row, values):
            sums[row : row + 1] += jnp.sum(values, axis=0, keepdims=True)

        fetching(SECOND, image).wait()

        def open_second(at):
            grad = flow[at]
            grads[D_SECOND][at] = (grad * modulation[5:6]).astype(jnp.bfloat16)
            add_sum(5, grad * kept[SECOND][at])

        by_rows(patches, open_second)
        fetch_next(SECOND)
        save(D_SECOND)
        fetching(PRE, image).wait()
        wait_first(image, loads[:1])
        for cols in parts_of(FF, FF // D):
            grads[D_PRE][:, cols] = (
                matmul_nt(grads[D_SECOND][...], ws_v[cols]) * gelu_grad(kept[PRE][:, cols])
            ).astype(jnp.bfloat16)
        fetch_next(PRE)
        save(D_PRE)
        wait_first(image, loads[1:2])
        for cols in parts_of(D, 3):
            mixed[:, cols] = matmul_nt(grads[D_PRE][...], wh_v[cols])
        fetching(MIDDLE, image).wait()
        fetching(BRANCH, image).wait()

        def through_two(at):
            normed, invstd = normalize(kept[MIDDLE][at])
            grad = mixed[at]
            add_sum(3, grad)
            add_sum(4, grad * normed)
            total = flow[at] + norm_back(grad * (1.0 + modulation[4:5]), normed, invstd)
            flow[at] = total
            add_sum(2, total * kept[BRANCH][at])
            grads[D_BRANCH][at] = (total * modulation[2:3]).astype(jnp.bfloat16)

        by_rows(patches, through_two)
        fetch_next(MIDDLE, BRANCH)
        save(D_BRANCH)
        wait_first(image, loads[2:3])
        att_grad[...] = contract(wp_v[...], grads[D_BRANCH][...], 1, 1).astype(jnp.bfloat16)
        fetching(QKV, image).wait()
        attend_back_kernel(kept[QKV], att_grad, qkv_grad)
        fetch_next(QKV)
        wait_first(image, loads[3:])
        for cols in parts_of(D, 3):
            mixed[:, cols] = contract(qkv_grad[...], wq_v[cols], 0, 1)
        fetching(RESIDUAL, image).wait()

        def through_one(at):
            normed, invstd = normalize(kept[RESIDUAL][at])
            grad = mixed[at]
            add_sum(0, grad)
            add_sum(1, grad * normed)
            total = flow[at] + norm_back(grad * (1.0 + modulation[1:2]), normed, invstd)
            send[image, at] = total.astype(jnp.bfloat16)

        by_rows(patches, through_one)

        @pl.when(section > 0)
        def pass_on():
            for part in range(HOPS):
                hop(image, part).start()

        fetch_next(RESIDUAL)
        save(D_RESIDUAL, send.at[image])
        grads[D_QKV][...] = qkv_grad[...].T
        save(D_QKV)
        saves.append(started(sums, ada_out.at[image], x_sem))
        if direct:

            @pl.when(image == 0)
            def pass_film():
                for copy in spreading:
                    copy.wait()

                @pl.when(section == sections - 1)
                def send_film():
                    for copy in passing:
                        copy.start()

        for copy in saves:
            copy.wait()

    @pl.when(section > 0)
    def finish():
        for image in range(images):
            for part in range(HOPS):
                hop(image, part).wait_send()

    if direct:

        @pl.when(section == sections - 1)
        def own_film():
            film_out[...] = film_rows[...]
            for copy in passing:
                copy.wait_send()

        for step in range(1, sections):

            @pl.when(section == step - 1)
            def wait_film(step=step):
                passing[step - 1].wait_recv()


def specs(*spaces):
    return [
        pl.BlockSpec(memory_space={"v": pltpu.VMEM, "h": pl.ANY}[space])
        for space in "".join(spaces)
    ]


def weight_scratch():
    return [pltpu.VMEM(shape, jnp.bfloat16) for shape in WEIGHTS] + [
        pltpu.SemaphoreType.DMA((6,))
    ]


def block_cost(images, patches, factor):
    area = sum(rows * columns for rows, columns in WEIGHTS)
    return pl.CostEstimate(
        flops=images * (2 * patches * area + factor * patches * patches * D),
        bytes_accessed=2 * area + images * 64 * patches * D,
        transcendentals=images * patches * (FF + HEADS * patches),
    )


def pipeline_forward(bias, qkv_bias, ada, tokens, weights):
    images, patches, unused = tokens.shape
    sections = lax.axis_size("section")
    sizes = [(kept_shape(i, item[0], patches), item[1]) for i, item in enumerate(KEPT)]
    return pl.pallas_call(
        functools.partial(forward_kernel, sections, images),
        out_shape=[
            jax.ShapeDtypeStruct((images,) + shape, kind) for shape, kind in sizes
        ],
        in_specs=specs("vvv", "h" * 3),
        out_specs=specs("h" * len(KEPT)),
        scratch_shapes=[pltpu.VMEM(shape, kind) for shape, kind in sizes]
        + [pltpu.VMEM((D, patches), jnp.bfloat16)]
        + [pltpu.VMEM((images, patches, D), jnp.bfloat16)] * 2
        + weight_scratch()
        + [pltpu.SemaphoreType.DMA, pltpu.SemaphoreType.DMA((len(KEPT),))]
        + [pltpu.SemaphoreType.DMA((images, HOPS))] * 2,
        compiler_params=pltpu.CompilerParams(
            vmem_limit_bytes=62 << 20, collective_id=16, has_side_effects=True
        ),
        cost_estimate=block_cost(images, patches, 4),
        name="pipeline_forward",
    )(bias, qkv_bias, ada, tokens, *weights)


def pipeline_backward(ada, head_grad, weights, sources, film):
    images, patches, unused = head_grad.shape
    sections, direct = (lax.axis_size("section"), lax.axis_size("dp") == DIRECT)
    films = [jax.ShapeDtypeStruct((DIRECT,) + film.shape, film.dtype)] * (2 * direct)
    outs = pl.pallas_call(
        functools.partial(backward_kernel, sections, images, direct),
        out_shape=[
            jax.ShapeDtypeStruct((images, patches, width), kind) for width, kind in MADE
        ]
        + [jax.ShapeDtypeStruct((images, 8, D), jnp.float32)]
        + films,
        in_specs=specs("v", "h" * (3 + len(READ)), "v" * direct),
        out_specs=specs("h" * (len(MADE) + 1), "v" * len(films)),
        scratch_shapes=[
            pltpu.VMEM(kept_shape(name, KEPT[name][0], patches), KEPT[name][1]) for name in READ
        ]
        + [pltpu.VMEM((patches, width), kind) for width, kind in MADE[:-1]]
        + [
            pltpu.VMEM((patches, D), jnp.float32),
            pltpu.VMEM((patches, D), jnp.float32),
            pltpu.VMEM((D, patches), jnp.bfloat16),
            pltpu.VMEM((3 * D, patches), jnp.bfloat16),
            pltpu.VMEM((8, D), jnp.float32),
        ]
        + [pltpu.VMEM((images, patches, D), jnp.bfloat16)] * 2
        + weight_scratch()
        + [
            pltpu.SemaphoreType.DMA((len(READ),)),
            pltpu.SemaphoreType.DMA,
            pltpu.SemaphoreType.DMA((len(MADE),)),
        ]
        + [pltpu.SemaphoreType.DMA((images, HOPS))] * 2
        + [pltpu.SemaphoreType.DMA((DIRECT + sections,))] * 2,
        compiler_params=pltpu.CompilerParams(
            vmem_limit_bytes=62 << 20, collective_id=17, has_side_effects=True
        ),
        cost_estimate=block_cost(images, patches, 10),
        name="pipeline_backward",
    )(ada, head_grad, *weights, *sources, *([film] * direct))
    if direct:
        film_all = outs[-1].reshape(-1, film.shape[1])
    else:
        film_all = lax.all_gather(film, ("section", "dp"), tiled=True)
        film_all = film_all[-images * lax.axis_size("dp") :]
    return (outs[: len(MADE) + 1], film_all)


def head_step(residual, film, noise_part, mask_part, inv_count, w_out, b_out):
    shifting, scaling = (film[:, :D], film[:, D:])
    normed, invstd = normalize(residual)
    mixed = (normed * (1.0 + scaling[:, None]) + shifting[:, None]).astype(jnp.bfloat16)
    output = (
        jnp.einsum("bpd,dj->bpj", mixed, w_out, preferred_element_type=jnp.float32) + b_out
    )
    mismatch = output - noise_part
    mask_float = mask_part.astype(jnp.float32)[:, :, None]
    squared = jnp.sum(mask_float * mismatch * mismatch)
    d_output = (2.0 * inv_count * mask_float * mismatch).astype(jnp.bfloat16)
    g_output = jnp.einsum("bpd,bpj->dj", mixed, d_output, preferred_element_type=jnp.float32)
    d_mixed = jnp.einsum("bpj,dj->bpd", d_output, w_out, preferred_element_type=jnp.float32)
    d_film = jnp.concatenate(
        [jnp.sum(d_mixed, axis=1), jnp.sum(d_mixed * normed, axis=1)], axis=1
    ).astype(jnp.bfloat16)
    d_residual = norm_back(d_mixed * (1.0 + scaling[:, None]), normed, invstd)
    g_bias = jnp.sum(d_output.astype(jnp.float32), axis=(0, 1))
    return (squared, d_residual, d_film, g_output, g_bias)


def adam_update(weight, gradient, first_moment, second_moment, scaling):
    gradient = gradient * scaling
    first_new = BETA_ONE * first_moment + (1.0 - BETA_ONE) * gradient
    second_new = BETA_TWO * second_moment + (1.0 - BETA_TWO) * gradient * gradient
    ratio = (
        first_new
        / (1.0 - BETA_ONE**STEP_POWER)
        / (jnp.sqrt(second_new / (1.0 - BETA_TWO**STEP_POWER)) + ADAM_EPS)
    )
    return (weight - RATE * (ratio + DECAY * weight), first_new, second_new)


def body(
    latents,
    noise,
    timesteps,
    labels,
    patch_mask,
    w_in,
    w_down,
    b_blk,
    small_mats,
    small_bias,
    m_in,
    m_down,
    m_bias,
    m_small,
    m_sbias,
    v_in,
    v_down,
    v_bias,
    v_small,
    v_sbias,
):
    section_index = lax.axis_index("section")
    dp_index = lax.axis_index("dp")
    sections = lax.axis_size("section")
    is_first = section_index == 0
    is_last = section_index == sections - 1
    low = jnp.bfloat16
    images, patches = patch_mask.shape
    rows = w_in.shape[1]
    row_at = dp_index * rows
    ada_at = 4 * D + FF
    o_label = PATCH_IN + FREQ
    o_second = o_label + CLASSES
    o_film = o_second + D
    o_out = o_film + 2 * D

    def gathered(value, axis="dp", dim=0):
        return lax.all_gather(value, axis, axis=dim, tiled=True)

    in_low = w_in[0].astype(low)
    w_ada = in_low[:, ada_at:]
    w_tokens = gathered(in_low[:, :ada_at])
    w_second = gathered(w_down[0].astype(low))

    small_low = small_mats.astype(low)
    edge_own = jnp.where(is_first, small_mats[:, :PATCH_IN], small_mats[:, -PATCH_IN:])
    bias_width = b_blk.shape[1]
    pieces = [
        b_blk[0],
        edge_own.reshape(-1),
        timesteps.astype(jnp.float32),
        labels.astype(jnp.float32),
        jnp.sum(patch_mask).astype(jnp.float32)[None],
    ]
    block = jnp.concatenate(pieces)[None]
    blocks = spread(block, "dp", 1)[:, 0]
    ends = [0]
    for piece in pieces:
        ends.append(ends[-1] + piece.shape[0])
    bias_full = rounded(blocks[:, : ends[1]].reshape(-1))
    w_edge = blocks[:, ends[1] : ends[2]].reshape(D, PATCH_IN).astype(low)
    times_all = blocks[:, ends[2] : ends[3]].reshape(-1).astype(jnp.int32)
    labels_all = blocks[:, ends[3] : ends[4]].reshape(-1).astype(jnp.int32)
    valid_total = jnp.sum(blocks[:, ends[4]])
    inv_count = 1.0 / (valid_total * PATCH_IN)
    weights = (w_tokens, w_second)

    small_width = small_mats.shape[1]
    sbias_width = small_bias.shape[0]
    extra = -(-sbias_width // small_width)
    sbias_rows = jnp.pad(small_bias, (0, extra * small_width - sbias_width)).astype(low)
    small_block = jnp.concatenate([small_low, sbias_rows.reshape(extra, small_width)], axis=0)
    small_blocks = spread(small_block, "section", 2)
    small_rows = jnp.concatenate([small_blocks[i, :rows] for i in range(sections)], axis=1)
    small_used = (
        small_blocks[:, rows:].reshape(sections, -1)[:, :sbias_width].reshape(-1)
    ).astype(jnp.float32)

    shards = lax.axis_size("dp")
    time_low = time_features(times_all).astype(low)
    one_hot = label_table(labels_all)
    time_hidden = matmul_nt(time_low, small_rows[:, PATCH_IN:o_label]) + lax.dynamic_slice_in_dim(
        small_used, D + row_at, rows, 0
    )
    time_act = jax.nn.silu(time_hidden).astype(low)
    cond_part = matmul(time_act, small_rows[:, o_second:o_film])
    label_part = matmul_nt(one_hot, small_rows[:, o_label:o_second])
    cond_part = jnp.concatenate([cond_part, label_part], axis=1).reshape(shards, images, D + rows)
    cond_got = exchange(cond_part, "dp", 3)
    cond_own = (
        jnp.sum(cond_got[:, :, :D], axis=0)
        + small_used[2 * D : 3 * D]
        + jnp.swapaxes(cond_got[:, :, D:], 0, 1).reshape(images, D)
    )
    cond_cols = exchange(jnp.swapaxes(cond_own.reshape(images, shards, rows), 0, 1), "dp", 4)
    cond_first = cond_cols.reshape(shards * images, rows)
    cond_later = rounded(cond_first)
    cond_here = jnp.where(is_first, cond_first, cond_later)
    act_here = jax.nn.silu(cond_here).astype(low)
    act_later = jax.nn.silu(cond_later).astype(low)
    ada_part = jnp.concatenate(
        [matmul(act_here, w_ada), matmul(act_later, small_rows[:, o_film:o_out])], axis=1
    )
    ada_got = exchange(ada_part.reshape(shards, images * 8 * D // 128, 128), "dp", 5)
    ada_own = jnp.sum(ada_got, axis=0).reshape(images, 8 * D)
    film = ada_own[:, 6 * D :] + small_used[3 * D : 5 * D]
    ada = (ada_own[:, : 6 * D] + bias_full[ada_at:]).reshape(images, 6, D)
    qkv_bias = jnp.concatenate(
        [bias_full[:D], jnp.zeros((D,), jnp.float32), bias_full[D : 2 * D]]
    )[:, None]
    bias_row = bias_full[None, 2 * D : ada_at]

    fade = alpha_bar(timesteps)[:, None, None]
    noisy_low = (jnp.sqrt(fade) * latents + jnp.sqrt(1.0 - fade) * noise).astype(low)
    tokens = jnp.einsum(
        "bpi,di->bpd", noisy_low, w_edge, preferred_element_type=jnp.float32
    )
    tokens = tokens + small_used[:D] + positions(patches)[None]

    kept_all = pipeline_forward(bias_row, qkv_bias, ada, tokens, weights)

    squared, head_grad, d_film, g_output, g_out_bias = head_step(
        kept_all[OUTPUT],
        film,
        noise,
        patch_mask,
        inv_count,
        w_edge,
        small_used[5 * D :],
    )
    loss_part = jnp.where(is_last, squared * inv_count, 0.0)
    made_all, film_all = pipeline_backward(
        ada, head_grad, weights, [kept_all[name] for name in READ], d_film
    )

    def flat(whole):
        return whole.reshape(images * patches, whole.shape[2])

    d_second, d_pre, d_branch, d_qkv, d_tokens = [flat(whole) for whole in made_all[:5]]
    d_ada = made_all[5][:, :6].astype(low).reshape(images, 6 * D)

    token_sums = column_sum(d_tokens)
    g_edge = jnp.where(
        is_first,
        matmul_tn(d_tokens, noisy_low.reshape(images * patches, PATCH_IN)),
        g_output,
    )
    shard_wide, shard_down, right_sums, d_ada_all = row_sums(
        [flat(kept_all[name]) for name in (MIXED_ONE, ATT, MIXED_TWO, ACT)],
        [d_qkv, d_branch, d_pre, d_second],
        d_ada,
    )
    d_ada_all = d_ada_all.reshape(shards * images, 6 * D)

    cond_piece = matmul_nt(d_ada_all, w_ada) * silu_grad(cond_here)
    cond_pieces = spread(cond_piece, "section", 9)
    d_cond = matmul_nt(film_all, small_rows[:, o_film:o_out]) * silu_grad(cond_later)
    for layer in reversed(range(sections)):
        d_cond = rounded(d_cond + cond_pieces[layer])
    d_cond_rows = d_cond.astype(low)
    d_cond_all = jnp.swapaxes(spread(d_cond_rows, "dp", 10), 0, 1).reshape(shards * images, D)
    d_time = (
        matmul_nt(d_cond_all, small_rows[:, o_second:o_film]) * silu_grad(time_hidden)
    ).astype(low)
    bias_sums = jnp.concatenate(
        [
            right_sums[0][:D],
            right_sums[0][2 * D :],
            right_sums[1],
            right_sums[2],
            right_sums[3],
            column_sum(d_ada),
        ]
    )
    sums = jnp.concatenate(
        [
            bias_sums.reshape(shards, -1),
            g_edge.reshape(shards, -1),
            jnp.broadcast_to(token_sums, (shards, D)),
            jnp.broadcast_to(g_out_bias, (shards, PATCH_IN)),
            jnp.broadcast_to(column_sum(d_time), (shards, rows)),
        ],
        axis=1,
    )
    sums = exchange(sums[:, None], "dp", 11)[:, 0]
    shard_ada = matmul_tn(act_here, d_ada_all)
    shard_in = jnp.concatenate([shard_wide, shard_ada], axis=1)
    edge_end = bias_width + rows * PATCH_IN
    shard_bias = jnp.sum(sums[:, :bias_width], axis=0)
    edge_rows = jnp.sum(sums[:, bias_width:edge_end], axis=0).reshape(rows, PATCH_IN)
    token_sums = jnp.sum(sums[:, edge_end : edge_end + D], axis=0)
    out_sums = jnp.sum(sums[:, edge_end + D : edge_end + D + PATCH_IN], axis=0)
    time_sums = sums[:, edge_end + D + PATCH_IN :].reshape(-1)
    small_grad = jnp.concatenate(
        [
            edge_rows,
            matmul_tn(d_time, time_low),
            matmul_tn(d_cond_rows, one_hot),
            matmul_tn(time_act, d_cond_all),
            matmul_tn(act_later, film_all),
            edge_rows,
        ],
        axis=1,
    )
    small_shard = lax.dynamic_slice_in_dim(small_grad, section_index * small_width, small_width, 1)
    sbias_grad = jnp.concatenate(
        [token_sums, time_sums, column_sum(d_cond_all), column_sum(film_all), out_sums]
    )
    sbias_shard = lax.dynamic_slice_in_dim(
        sbias_grad, section_index * sbias_width, sbias_width, 0
    )

    shard_in, shard_down, small_shard, sbias_shard, shard_bias = lax.optimization_barrier(
        (shard_in, shard_down, small_shard, sbias_shard, shard_bias)
    )
    dp_zero = (dp_index == 0).astype(jnp.float32)
    squares = (
        jnp.sum(shard_in * shard_in)
        + jnp.sum(shard_down * shard_down)
        + jnp.sum(shard_bias * shard_bias)
        + jnp.sum(small_shard * small_shard)
        + dp_zero * jnp.sum(sbias_shard * sbias_shard)
    )
    pair = jnp.broadcast_to(jnp.stack([squares, loss_part])[:, None], (2, 128))
    pair = jnp.sum(spread(pair, "dp", 14), axis=0)
    pair = jnp.sum(spread(pair, "section", 15), axis=0)
    norm_square, loss = (pair[0, 0], pair[1, 0])
    grad_norm = jnp.sqrt(norm_square)
    scaling = jnp.minimum(1.0, CLIP / grad_norm)
    new_in, first_in, second_in = adam_update(w_in, shard_in[None], m_in, v_in, scaling)
    new_down, first_down, second_down = adam_update(
        w_down, shard_down[None], m_down, v_down, scaling
    )
    new_bias, first_bias, second_bias = adam_update(
        b_blk, shard_bias[None], m_bias, v_bias, scaling
    )
    new_small, first_small, second_small = adam_update(
        small_mats, small_shard, m_small, v_small, scaling
    )
    new_sbias, first_sbias, second_sbias = adam_update(
        small_bias, sbias_shard, m_sbias, v_sbias, scaling
    )
    return (
        loss,
        grad_norm,
        new_in,
        first_in,
        second_in,
        new_down,
        first_down,
        second_down,
        new_bias,
        first_bias,
        second_bias,
        new_small,
        first_small,
        second_small,
        new_sbias,
        first_sbias,
        second_sbias,
    )


def solution(mesh):
    in_specs = (
        P("dp", None, None),
        P("dp", None, None),
        P("dp"),
        P("dp"),
        P("dp", None),
        P("section", "dp", None),
        P("section", "dp", None),
        P("section", "dp"),
        P("dp", "section"),
        P("section"),
        P("section", "dp", None),
        P("section", "dp", None),
        P("section", "dp"),
        P("dp", "section"),
        P("section"),
        P("section", "dp", None),
        P("section", "dp", None),
        P("section", "dp"),
        P("dp", "section"),
        P("section"),
    )
    out_specs = (
        P(),
        P(),
        P("section", "dp", None),
        P("section", "dp", None),
        P("section", "dp", None),
        P("section", "dp", None),
        P("section", "dp", None),
        P("section", "dp", None),
        P("section", "dp"),
        P("section", "dp"),
        P("section", "dp"),
        P("dp", "section"),
        P("dp", "section"),
        P("dp", "section"),
        P("section"),
        P("section"),
        P("section"),
    )
    return jax.shard_map(body, mesh=mesh, in_specs=in_specs, out_specs=out_specs, check_vma=False)
```

```python
import functools
import math

import jax
import jax.numpy as jnp
from jax import lax
from jax.experimental import pallas as pl
from jax.experimental.pallas import tpu as pltpu
from jax.sharding import PartitionSpec as P

D = 1152
HEADS = 16
HEAD_DIM = 72
FF = 4608
CLASSES = 1000
FREQ = 256
PATCH_IN = 16
GRID = 16


EPS_NORM = 1e-06
CLIP = 0.001
RATE = 0.005
BETA_ONE = 0.9
BETA_TWO = 0.999
ADAM_EPS = 1e-08
DECAY = 0.01
STEP_POWER = 10.0


def passed_along(value, axis, steps):
    count = lax.axis_size(axis)
    first, last = (max(0, -steps), min(count, count - steps))
    return lax.ppermute(value, axis, [(source, source + steps) for source in range(first, last)])


def matmul(left_side, right_side):
    return jnp.dot(left_side, right_side, preferred_element_type=jnp.float32)


def matmul_tn(left_side, right_side):
    return lax.dot_general(
        left_side, right_side, (((0,), (0,)), ((), ())), preferred_element_type=jnp.float32
    )


def matmul_nt(left_side, right_side):
    return lax.dot_general(
        left_side, right_side, (((1,), (1,)), ((), ())), preferred_element_type=jnp.float32
    )


def column_sum(values):
    return jnp.sum(values.astype(jnp.float32), axis=0)


def normalize(values):
    center = values - jnp.mean(values, axis=-1, keepdims=True)
    invstd = lax.rsqrt(jnp.mean(center * center, axis=-1, keepdims=True) + EPS_NORM)
    return (center * invstd, invstd)


def norm_back(grad_normed, normed, invstd):
    return invstd * (
        grad_normed
        - jnp.mean(grad_normed, axis=-1, keepdims=True)
        - normed * jnp.mean(grad_normed * normed, axis=-1, keepdims=True)
    )


def gelu_tanh(values):
    return (
        0.5
        * values
        * (1.0 + jnp.tanh(0.7978845608028654 * (values + 0.044715 * values * values * values)))
    )


def gelu_grad(values):
    inner = jnp.tanh(0.7978845608028654 * (values + 0.044715 * values * values * values))
    return 0.5 * (1.0 + inner) + 0.5 * values * (1.0 - inner * inner) * 0.7978845608028654 * (
        1.0 + 0.134145 * values * values
    )


def silu_grad(values):
    sigma = jax.nn.sigmoid(values)
    return sigma * (1.0 + values * (1.0 - sigma))


def positions(patches):
    quarter = D // 4
    omega = jnp.exp(-math.log(10000.0) * jnp.arange(quarter, dtype=jnp.float32) / quarter)
    spot = jnp.arange(patches, dtype=jnp.int32)
    row_angle = (spot // GRID).astype(jnp.float32)[:, None] * omega[None, :]
    col_angle = (spot % GRID).astype(jnp.float32)[:, None] * omega[None, :]
    return jnp.concatenate(
        [jnp.sin(row_angle), jnp.cos(row_angle), jnp.sin(col_angle), jnp.cos(col_angle)], axis=1
    )


def time_features(time_steps):
    half = FREQ // 2
    freqs = jnp.exp(-math.log(10000.0) * jnp.arange(half, dtype=jnp.float32) / half)
    angles = time_steps.astype(jnp.float32)[:, None] * freqs[None, :]
    return jnp.concatenate([jnp.cos(angles), jnp.sin(angles)], axis=1)


def alpha_bar(time_steps):
    return jnp.cos((time_steps.astype(jnp.float32) / 1000.0 + 0.008) / 1.008 * (math.pi / 2)) ** 2


def label_table(label_part):
    return (label_part[:, None] == jnp.arange(CLASSES, dtype=jnp.int32)[None, :]).astype(
        jnp.bfloat16
    )


MESH = pl.DeviceIdType.MESH
DIRECT = 8


def rounded(values):
    return lax.reduce_precision(values, 8, 7)


def meet(axis, count, here, stride=1):
    barrier = pltpu.get_barrier_semaphore()
    for step in range(1, count):
        pl.semaphore_signal(
            barrier,
            inc=1,
            device_id={axis: lax.rem(here + step * stride, count * stride)},
            device_id_type=MESH,
        )
    pl.semaphore_wait(barrier, count - 1)


def meet_both(sections, section, here):
    barrier = pltpu.get_barrier_semaphore()
    for axis, me, size in (("section", section, sections), ("dp", here, DIRECT)):
        for step in range(1, size):
            pl.semaphore_signal(
                barrier, inc=1, device_id={axis: lax.rem(me + step, size)}, device_id_type=MESH
            )
    pl.semaphore_wait(barrier, sections + DIRECT - 2)


def share_kernel(axis, count, stride, personal, in_ref, out_ref, send_sem, recv_sem):
    here = lax.axis_index(axis)
    meet(axis, count, here, stride)
    place = here // stride
    copies = []
    for step in range(1, count):
        copy = pltpu.make_async_remote_copy(
            src_ref=in_ref.at[lax.rem(place + step, count)] if personal else in_ref,
            dst_ref=out_ref.at[place],
            send_sem=send_sem.at[step - 1],
            recv_sem=recv_sem.at[step - 1],
            device_id={axis: lax.rem(here + step * stride, count * stride)},
            device_id_type=MESH,
        )
        copy.start()
        copies.append(copy)
    out_ref[place] = in_ref[place] if personal else in_ref[...]
    for copy in copies:
        copy.wait()


def share(value, axis, personal, ident, stride=1):
    count = lax.axis_size(axis) // stride
    shape = value.shape if personal else (count,) + value.shape
    return pl.pallas_call(
        functools.partial(share_kernel, axis, count, stride, personal),
        out_shape=jax.ShapeDtypeStruct(shape, value.dtype),
        in_specs=[pl.BlockSpec(memory_space=pltpu.VMEM)],
        out_specs=pl.BlockSpec(memory_space=pltpu.VMEM),
        scratch_shapes=[
            pltpu.SemaphoreType.DMA((count - 1,)),
            pltpu.SemaphoreType.DMA((count - 1,)),
        ],
        compiler_params=pltpu.CompilerParams(collective_id=ident, has_side_effects=True),
        name="share",
    )(value)


def spread(value, axis, ident):
    if lax.axis_size(axis) > DIRECT:
        return lax.all_gather(value, axis)
    return share(value, axis, False, ident)


def exchanged_sum(value, ident):
    count = lax.axis_size("dp")
    if count != DIRECT:
        return jnp.sum(exchange(value, "dp", ident), axis=0)
    core = lax.axis_index("dp") % 2
    parted = value.reshape((count // 2, 2) + value.shape[1:])
    other = lax.dynamic_index_in_dim(parted, 1 - core, 1, keepdims=False)
    same = lax.dynamic_index_in_dim(parted, core, 1, keepdims=False)
    both = same + lax.ppermute(other, "dp", [(i, i ^ 1) for i in range(count)])
    return jnp.sum(share(both, "dp", True, ident, 2), axis=0)


def exchange(value, axis, ident):
    if lax.axis_size(axis) > DIRECT:
        return lax.all_to_all(value, axis, 0, 0)
    return share(value, axis, True, ident)


FINAL, LATER, NEAR, FAR, PASS = range(5)
STEPS = 16
CHIPS = 4


def sums_kernel(units, rows, sections, *refs):
    lefts, rights = (refs[:4], refs[4:8])
    given, w_ada, slope, head_part, refs = (refs[8], refs[9], refs[10], refs[11], refs[12:])
    owns, finals, laters = (refs[0:2], refs[2:4], refs[4:6])
    bias_out, spread_out, cond_out, refs = (refs[6], refs[7], refs[8], refs[9:])
    (
        left_v,
        right_v,
        product,
        got,
        own_v,
        stage,
        near,
        far,
        passed,
        left_sem,
        right_sem,
        send_sem,
        recv_sem,
        own_sem,
        stage_sem,
        block_sem,
        pass_sem,
        given_send,
        given_recv,
        cond_pieces,
        cond_low,
        cond_send,
        cond_recv,
    ) = refs
    here = lax.axis_index("dp")
    core, chip = (lax.rem(here, 2), here // 2)
    partner = {"dp": here + 1 - 2 * core}
    tall = CHIPS * rows
    section = lax.axis_index("section")
    meet_both(sections, section, here)
    spreading = []
    for step in range(1, DIRECT):
        copy = pltpu.make_async_remote_copy(
            src_ref=given,
            dst_ref=spread_out.at[here],
            send_sem=given_send.at[step - 1],
            recv_sem=given_recv.at[step - 1],
            device_id={"dp": lax.rem(here + step, DIRECT)},
            device_id_type=MESH,
        )
        copy.start()
        spreading.append(copy)
    spread_out[here] = given[...]
    places = {NEAR: near, FAR: far, PASS: passed}
    shared = []

    def share_pieces():
        for copy in spreading:
            copy.wait()
        each = given.shape[0]
        for i in range(DIRECT):
            at = slice(i * each, (i + 1) * each)
            cond_pieces[section, at] = contract(spread_out[i], w_ada[...], 1, 1) * slope[at]
        for step in range(1, sections):
            copy = pltpu.make_async_remote_copy(
                src_ref=cond_pieces.at[section],
                dst_ref=cond_pieces.at[section],
                send_sem=cond_send.at[step - 1],
                recv_sem=cond_recv.at[step - 1],
                device_id={"section": lax.rem(section + step, sections)},
                device_id_type=MESH,
            )
            copy.start()
            shared.append(copy)

    def share_rows():
        for copy in shared:
            copy.wait()
        value = head_part[...]
        for layer in reversed(range(sections)):
            value = (value + cond_pieces[layer]).astype(jnp.bfloat16).astype(jnp.float32)
        cond_low[...] = value.astype(jnp.bfloat16)
        cond_out[here] = value.astype(jnp.bfloat16)
        shared.clear()
        for step in range(1, DIRECT):
            copy = pltpu.make_async_remote_copy(
                src_ref=cond_low,
                dst_ref=cond_out.at[here],
                send_sem=cond_send.at[sections + step],
                recv_sem=cond_recv.at[sections + step],
                device_id={"dp": lax.rem(here + step, DIRECT)},
                device_id_type=MESH,
            )
            copy.start()
            shared.append(copy)


    def placed(pair, slot):
        wide, down = pair
        side_by_side = wide.shape[1] // D
        if slot < side_by_side:
            return wide.at[:, pl.ds(slot * D, D)]
        return down.at[pl.ds((slot - side_by_side) * rows, rows)]

    plan, last, slots = ([], [None, None], [1, 1])
    for left, left_at, right, right_at, gathers, slot in units:
        fresh = []
        for side, key in enumerate(((left, left_at), (right, right_at))):
            fresh.append(last[side] != key)
            if fresh[-1]:
                slots[side] = 1 - slots[side]
                last[side] = key
        plan.append((tuple(slots), tuple(fresh)))
    def loads_of(index):
        left, left_at, right, right_at, gathers, slot = units[index]
        (left_slot, right_slot), (left_fresh, right_fresh) = plan[index]
        copies = []
        if left_fresh:
            source = lefts[left].at[:, pl.ds(left_at, D)]
            copies.append(
                pltpu.make_async_copy(source, left_v.at[left_slot], left_sem.at[left_slot])
            )
        if right_fresh:
            source = rights[right].at[:, pl.ds(right_at, D)]
            copies.append(
                pltpu.make_async_copy(source, right_v.at[right_slot], right_sem.at[right_slot])
            )
        return copies

    pending, crossing, leaving, keeping = ({}, {}, {}, {})

    def load(index):
        pending[index] = loads_of(index)
        for copy in pending[index]:
            copy.start()

    def to_partner(source, target, sems):
        copy = pltpu.make_async_remote_copy(
            src_ref=source,
            dst_ref=target,
            send_sem=send_sem.at[sems],
            recv_sem=recv_sem.at[sems],
            device_id=partner,
            device_id_type=MESH,
        )
        copy.start()
        return copy

    def multiply(index):
        gathers = units[index][4]
        left_slot, right_slot = plan[index][0]
        for copy in pending[index]:
            copy.wait()
        if index + 1 < len(units):
            load(index + 1)
        if index >= 2:
            for copy in crossing[index - 2]:
                copy.wait_send()
        slot, place = (index % 2, index % 4)

        @pl.loop(0, 3)
        def tile(step):
            at = pl.ds(pl.multiple_of(step * (D // 3), 128), D // 3)
            product[slot, at] = contract(left_v[left_slot, :, at], right_v[right_slot], 0, 0)

        if gathers is None or gathers == 0:
            ones = jnp.ones((8, right_v.shape[1]), jnp.bfloat16)
            bias_out[units[index][5]] = matmul(ones, right_v[right_slot])
        if gathers is None:
            crossing[index] = [
                to_partner(
                    product.at[slot, pl.ds(pl.multiple_of((2 * i + 1 - core) * rows, 8), rows)],
                    got.at[place, pl.ds(i * rows, rows)],
                    place * CHIPS + i,
                )
                for i in range(CHIPS)
            ]
        else:
            crossing[index] = [
                to_partner(
                    product.at[slot, pl.ds(pl.multiple_of((1 - core) * tall, 8), tall)],
                    got.at[place],
                    place * CHIPS,
                )
            ]

    def crossed(source, kind, slot, to, sem):
        pair = {FINAL: finals, LATER: laters}.get(kind)
        return pltpu.make_async_remote_copy(
            src_ref=source,
            dst_ref=places[kind].at[slot] if pair is None else placed(pair, slot),
            send_sem=sem,
            recv_sem=block_sem.at[kind, slot],
            device_id={"dp": 2 * to + core},
            device_id_type=MESH,
        )

    def landed(kind, slot):
        crossed(stage.at[0, 0], kind, slot, chip, stage_sem.at[0, 0]).wait_recv()

    def filled(target, index, block, gathers, added=None):
        slot, place = (index % 2, index % 4)
        base = (2 * block + core) * rows if gathers is None else core * tall + block * rows

        @pl.loop(0, rows // STEPS)
        def run(step):
            at = step * STEPS
            value = (
                product[slot, pl.ds(pl.multiple_of(base + at, STEPS), STEPS)]
                + got[place, pl.ds(pl.multiple_of(block * rows + at, STEPS), STEPS)]
            )
            to = pl.ds(pl.multiple_of(at, STEPS), STEPS)
            if added is not None:
                value = value + added[to].astype(jnp.float32)
            target[to] = value.astype(target.dtype)

    def route(index, block, owner, slot, gathers):
        side = index % 3

        def case(at, kind, to, added=None):
            copy = crossed(
                stage.at[side, block], kind, slot, to, stage_sem.at[side, block]
            )

            @pl.when(chip == at)
            def act():
                if added is not None:
                    landed(added, slot)
                filled(
                    stage.at[side, block],
                    index,
                    block,
                    gathers,
                    None if added is None else places[added].at[slot],
                )
                copy.start()

            leaving[index].append((chip == at, copy.wait_send))

        keep = pltpu.make_async_copy(
            own_v.at[side, block], placed(owns, slot), own_sem.at[side, block]
        )

        @pl.when(chip == owner)
        def hold():
            filled(own_v.at[side, block], index, block, gathers)
            keep.start()

        leaving[index].append((chip == owner, keep.wait))
        flip = (lambda at: at) if owner < 2 else (lambda at: CHIPS - 1 - at)
        if owner in (0, CHIPS - 1):
            case(flip(3), FAR, flip(2))
            case(flip(1), FINAL, flip(0))
            case(flip(2), PASS, flip(1), FAR)
        else:
            case(flip(3), NEAR, flip(2))
            case(flip(0), FINAL, flip(1))
            case(flip(2), LATER, flip(1), NEAR)

    def blocks_of(index):
        gathers = units[index][4]
        if gathers is None:
            return [(owner, owner, units[index][5]) for owner in (0, 3, 1, 2)]
        return [(block, gathers, units[index][5] + block) for block in range(CHIPS)]

    def combine(index):
        for copy in crossing[index]:
            copy.wait_recv()
        if index >= 3:
            finish(index - 3)
        leaving[index] = []
        for block, owner, slot in blocks_of(index):
            route(index, block, owner, slot, units[index][4])

    def finish(index):
        for condition, wait in leaving[index]:

            @pl.when(condition)
            def settle(wait=wait):
                wait()

    def pass_on(index):
        for block, owner, slot in blocks_of(index):
            if owner not in (0, CHIPS - 1):
                continue
            middle = 1 if owner == 0 else CHIPS - 2

            @pl.when(chip == middle)
            def forward(slot=slot, owner=owner):
                landed(PASS, slot)
                crossed(passed.at[slot], LATER, slot, owner, pass_sem.at[slot]).start()

    total = len(units)
    load(0)
    multiply(0)
    for index in range(total):
        if index + 1 < total:
            multiply(index + 1)
        combine(index)
        if index >= 1:
            pass_on(index - 1)
        if index == 2:
            share_pieces()
        elif index == 5:
            share_rows()
    pass_on(total - 1)
    for index in range(max(0, total - 3), total):
        finish(index)
    for index in range(max(0, total - 2), total):
        for copy in crossing[index]:
            copy.wait_send()
    for index in range(total):
        for block, owner, slot in blocks_of(index):

            @pl.when(chip == owner)
            def received(slot=slot):
                landed(FINAL, slot)
                landed(LATER, slot)

            if owner in (0, CHIPS - 1):

                @pl.when(chip == (1 if owner == 0 else CHIPS - 2))
                def sent(slot=slot, owner=owner):
                    crossed(passed.at[slot], LATER, slot, owner, pass_sem.at[slot]).wait_send()

    for copy in shared:
        copy.wait()


def line_sums(units, lefts, rights, rows, ident, given, w_ada, slope, head_part):
    sections = lax.axis_size("section")
    tokens = lefts[0].shape[0]
    places = sum(unit[4] is None for unit in units) + 4
    block = (rows, D)
    outs = pl.pallas_call(
        functools.partial(sums_kernel, units, rows, sections),
        out_shape=[
            jax.ShapeDtypeStruct(shape, kind)
            for kind in (jnp.float32, jnp.bfloat16, jnp.bfloat16)
            for shape in ((rows, (places - CHIPS) * D), (CHIPS * rows, D))
        ]
        + [
            jax.ShapeDtypeStruct((places - CHIPS + 1, 8, D), jnp.float32),
            jax.ShapeDtypeStruct((DIRECT,) + given.shape, given.dtype),
            jax.ShapeDtypeStruct((DIRECT,) + slope.shape, jnp.bfloat16),
        ],
        in_specs=specs("h" * 8, "vvvv"),
        out_specs=specs("h" * 6, "vvv"),
        scratch_shapes=[
            pltpu.VMEM((2, tokens, D), jnp.bfloat16),
            pltpu.VMEM((2, tokens, D), jnp.bfloat16),
            pltpu.VMEM((2, 8 * rows, D), jnp.float32),
            pltpu.VMEM((4, 4 * rows, D), jnp.float32),
            pltpu.VMEM((3, 4) + block, jnp.float32),
            pltpu.VMEM((3, 4) + block, jnp.bfloat16),
            pltpu.VMEM((places,) + block, jnp.bfloat16),
            pltpu.VMEM((places,) + block, jnp.bfloat16),
            pltpu.VMEM((places,) + block, jnp.bfloat16),
            pltpu.SemaphoreType.DMA((2,)),
            pltpu.SemaphoreType.DMA((2,)),
            pltpu.SemaphoreType.DMA((16,)),
            pltpu.SemaphoreType.DMA((16,)),
            pltpu.SemaphoreType.DMA((3, 4)),
            pltpu.SemaphoreType.DMA((3, 4)),
            pltpu.SemaphoreType.DMA((5, places)),
            pltpu.SemaphoreType.DMA((places,)),
            pltpu.SemaphoreType.DMA((DIRECT - 1,)),
            pltpu.SemaphoreType.DMA((DIRECT - 1,)),
            pltpu.VMEM((sections,) + slope.shape, jnp.float32),
            pltpu.VMEM(slope.shape, jnp.bfloat16),
            pltpu.SemaphoreType.DMA((sections + DIRECT,)),
            pltpu.SemaphoreType.DMA((sections + DIRECT,)),
        ],
        compiler_params=pltpu.CompilerParams(
            collective_id=ident, has_side_effects=True, vmem_limit_bytes=62 << 20
        ),
        cost_estimate=pl.CostEstimate(
            flops=2 * tokens * D * D * len(units),
            bytes_accessed=len(units) * tokens * D * 4,
            transcendentals=0,
        ),
        name="line_sums",
    )(*lefts, *rights, given, w_ada, slope, head_part)
    wide, down = [
        outs[i] + outs[2 + i].astype(jnp.float32) + outs[4 + i].astype(jnp.float32)
        for i in range(2)
    ]
    return (wide, down, outs[6][:, 0], outs[7], outs[8])


def row_sums(lefts, rights, given, w_ada, slope, head_part):
    count = lax.axis_size("dp")
    if count != DIRECT:
        products = [matmul_tn(one, other) for one, other in zip(lefts, rights)]
        sums = [lax.psum_scatter(one, "dp", scatter_dimension=0, tiled=True) for one in products]
        wide = jnp.concatenate([sums[0], sums[1], sums[2]], axis=1)
        given = lax.all_gather(given, "dp")
        pieces = matmul_nt(given.reshape(-1, given.shape[2]), w_ada) * slope
        pieces = lax.all_gather(pieces, "section")
        for layer in reversed(range(lax.axis_size("section"))):
            head_part = rounded(head_part + pieces[layer])
        conds = lax.all_gather(head_part.astype(jnp.bfloat16), "dp")
        return (wide, sums[3], [column_sum(one) for one in rights], given, conds)
    rows = D // count
    parts = FF // D
    attention = [(0, 0, 0, i * D, None, i) for i in range(3)] + [(1, 0, 1, 0, None, 3)]
    hidden = [(2, 0, 2, i * D, None, 4 + i) for i in range(parts)]
    second = [(3, i * D, 3, 0, i, 4 + parts) for i in (0, 3, 1, 2)]
    units = hidden[:1] + second[:2] + hidden[1:2] + second[2:] + hidden[2:] + attention
    wide, down, bias, given_all, conds = line_sums(
        tuple(units), lefts, rights, rows, 12, given, w_ada, slope, head_part
    )
    sums = [bias[:3].reshape(-1), bias[3], bias[4 : 4 + parts].reshape(-1), bias[4 + parts]]
    return (wide, down, sums, given_all, conds)


GROUP = 4


def contract(left_side, right_side, left_axis, right_axis):
    return lax.dot_general(
        left_side,
        right_side,
        (((left_axis,), (right_axis,)), ((), ())),
        preferred_element_type=jnp.float32,
    )


def heads_of(ref, at, group):
    return [
        ref[at + head * HEAD_DIM : at + (head + 1) * HEAD_DIM] for head in group
    ]


def softmax_down(scores):
    weights = jnp.exp(scores - jnp.max(scores, axis=0, keepdims=True))
    return weights * (1.0 / jnp.sum(weights, axis=0, keepdims=True))


def stacked(values):
    return jnp.concatenate([value.astype(jnp.bfloat16) for value in values], axis=0)


def attend_kernel(qkv_ref, out_ref):
    scaling = HEAD_DIM ** (-0.5)
    for first in range(0, HEADS, GROUP):
        group = range(first, first + GROUP)
        rows = slice(first * HEAD_DIM, (first + GROUP) * HEAD_DIM)
        queries, keys = (heads_of(qkv_ref, 0, group), heads_of(qkv_ref, D, group))
        values = heads_of(qkv_ref, 2 * D, group)
        scores = [contract(key, query, 0, 0) * scaling for key, query in zip(keys, queries)]
        probs = [softmax_down(score).astype(jnp.bfloat16) for score in scores]
        out_ref[rows] = stacked([contract(v, p, 1, 0) for v, p in zip(values, probs)])


def attend_back_kernel(qkv_ref, grad_ref, out_ref):
    scaling = HEAD_DIM ** (-0.5)
    for first in range(0, HEADS, GROUP):
        group = range(first, first + GROUP)
        at, to = (first * HEAD_DIM, (first + GROUP) * HEAD_DIM)
        queries, keys = (heads_of(qkv_ref, 0, group), heads_of(qkv_ref, D, group))
        values, grads = (heads_of(qkv_ref, 2 * D, group), heads_of(grad_ref, 0, group))
        scores = [contract(key, query, 0, 0) * scaling for key, query in zip(keys, queries)]
        d_probs = [contract(value, grad, 0, 0) for value, grad in zip(values, grads)]
        probs = [softmax_down(score) for score in scores]
        d_scores = [
            (p * (d - jnp.sum(p * d, axis=0, keepdims=True))).astype(jnp.bfloat16)
            for p, d in zip(probs, d_probs)
        ]
        lows = [p.astype(jnp.bfloat16) for p in probs]
        out_ref[at:to] = stacked([contract(k, d, 1, 0) * scaling for k, d in zip(keys, d_scores)])
        out_ref[D + at : D + to] = stacked(
            [contract(q, d, 1, 1) * scaling for q, d in zip(queries, d_scores)]
        )
        out_ref[2 * D + at : 2 * D + to] = stacked(
            [contract(g, p, 1, 1) for g, p in zip(grads, lows)]
        )


ROW_BLOCK = 64
HOPS = 3
RESIDUAL, MIXED_ONE, QKV, ATT, BRANCH, MIDDLE = range(6)
MIXED_TWO, PRE, ACT, SECOND, OUTPUT = range(6, 11)
D_SECOND, D_PRE, D_BRANCH, D_QKV, D_RESIDUAL = range(5)
WIDE, LOW = (jnp.float32, jnp.bfloat16)
KEPT = (
    (D, WIDE),
    (D, LOW),
    (3 * D, LOW),
    (D, LOW),
    (D, WIDE),
    (D, WIDE),
    (D, LOW),
    (FF, WIDE),
    (FF, LOW),
    (D, WIDE),
    (D, WIDE),
)
READ = (RESIDUAL, QKV, BRANCH, MIDDLE, PRE, SECOND)
MADE = ((D, LOW), (FF, LOW), (D, LOW), (3 * D, LOW), (D, LOW))
WEIGHTS = ((D, 3 * D), (D, D), (D, FF), (FF, D))


def kept_shape(name, width, patches):
    return (width, patches) if name == QKV else (patches, width)


def by_rows(patches, step):
    @pl.loop(0, patches // ROW_BLOCK)
    def run(index):
        step(pl.ds(pl.multiple_of(index * ROW_BLOCK, ROW_BLOCK), ROW_BLOCK))


def started(source, target, sem):
    copy = pltpu.make_async_copy(source, target, sem)
    copy.start()
    return copy


def parts_of(whole, parts):
    width = whole // parts
    return [slice(part * width, part * width + width) for part in range(parts)]


def wait_first(image, loads):
    @pl.when(image == 0)
    def wait():
        for load in loads:
            load.wait()


def hop_of(send, received, send_sem, recv_sem, target):
    def hop(image, part):
        cols = pl.ds(part * (D // HOPS), D // HOPS)
        return pltpu.make_async_remote_copy(
            src_ref=send.at[image, :, cols],
            dst_ref=received.at[image, :, cols],
            send_sem=send_sem.at[image, part],
            recv_sem=recv_sem.at[image, part],
            device_id={"section": target},
            device_id_type=MESH,
        )

    return hop


def forward_kernel(sections, images, bias, qkv_bias, ada, tokens, wx, ws, *refs):
    count, patches = (len(KEPT), tokens.shape[1])
    outs, scratch = (refs[:count], refs[count:])
    kept = scratch[:count]
    (
        att_down,
        send,
        received,
        wq_v,
        wp_v,
        wh_v,
        ws_v,
        w_sem,
        x_sem,
        out_sem,
        send_sem,
        recv_sem,
    ) = scratch[count:]
    section = lax.axis_index("section")
    loads = [
        started(wx.at[:, cols], wq_v.at[:, cols], w_sem.at[i])
        for i, cols in enumerate(parts_of(3 * D, 3))
    ]
    loads.append(started(wx.at[:, pl.ds(3 * D, D)], wp_v, w_sem.at[3]))
    loads.append(started(wx.at[:, pl.ds(4 * D, FF)], wh_v, w_sem.at[4]))
    loads.append(started(ws, ws_v, w_sem.at[5]))
    meet("section", sections, section)
    hop = hop_of(send, received, send_sem, recv_sem, lax.rem(section + 1, sections))
    residual = kept[RESIDUAL]

    @pl.loop(0, images)
    def run(image):
        saves = []

        def save(name):
            saves.append(started(kept[name], outs[name].at[image], out_sem.at[name]))

        @pl.when(section == 0)
        def take_tokens():
            started(tokens.at[image], residual, x_sem).wait()

        @pl.when(section > 0)
        def take_received():
            for part in range(HOPS):
                hop(image, part).wait_recv()
            residual[...] = received[image].astype(jnp.float32)

        save(RESIDUAL)
        modulation = ada[image]

        def mix_one(at):
            normed, unused = normalize(residual[at])
            kept[MIXED_ONE][at] = (normed * (1.0 + modulation[1:2]) + modulation[0:1]).astype(
                jnp.bfloat16
            )

        by_rows(patches, mix_one)
        save(MIXED_ONE)
        wait_first(image, loads[:3])
        for cols in parts_of(3 * D, 3):
            kept[QKV][cols] = (
                contract(wq_v[:, cols], kept[MIXED_ONE][...], 0, 1) + qkv_bias[cols]
            ).astype(jnp.bfloat16)
        save(QKV)
        attend_kernel(kept[QKV], att_down)
        wait_first(image, loads[3:4])
        kept[BRANCH][...] = contract(att_down[...], wp_v[...], 0, 0) + bias[:, :D]
        kept[ATT][...] = att_down[...].T
        save(BRANCH)
        save(ATT)

        def mix_two(at):
            middle = residual[at] + modulation[2:3] * kept[BRANCH][at]
            kept[MIDDLE][at] = middle
            normed, unused = normalize(middle)
            kept[MIXED_TWO][at] = (normed * (1.0 + modulation[4:5]) + modulation[3:4]).astype(
                jnp.bfloat16
            )

        by_rows(patches, mix_two)
        save(MIDDLE)
        save(MIXED_TWO)
        wait_first(image, loads[4:5])
        for part, cols in enumerate(parts_of(FF, FF // D)):
            pre = (
                matmul(kept[MIXED_TWO][...], wh_v[:, cols])
                + bias[:, D + part * D : 2 * D + part * D]
            )
            kept[PRE][:, cols] = pre
            kept[ACT][:, cols] = gelu_tanh(pre).astype(jnp.bfloat16)
        save(PRE)
        save(ACT)
        wait_first(image, loads[5:])
        for part, cols in enumerate(parts_of(D, HOPS)):
            second = (
                matmul(kept[ACT][...], ws_v[:, cols])
                + bias[:, D + FF + cols.start : D + FF + cols.stop]
            )
            kept[SECOND][:, cols] = second
            output = kept[MIDDLE][:, cols] + modulation[5:6, cols] * second
            kept[OUTPUT][:, cols] = output
            send[image, :, cols] = output.astype(jnp.bfloat16)

            @pl.when(section < sections - 1)
            def pass_on(part=part):
                hop(image, part).start()

        save(SECOND)
        save(OUTPUT)
        for copy in saves:
            copy.wait()

    @pl.when(section < sections - 1)
    def finish():
        for image in range(images):
            for part in range(HOPS):
                hop(image, part).wait_send()


def backward_kernel(sections, images, direct, ada, head_grad, wx, ws, *refs):
    reads, made, patches = (len(READ), len(MADE), head_grad.shape[1])
    sources, refs = (refs[:reads], refs[reads:])
    if direct:
        film, refs = (refs[0], refs[1:])
    outs, ada_out, refs = (refs[:made], refs[made], refs[made + 1 :])
    if direct:
        film_rows, film_out, refs = (refs[0], refs[1], refs[2:])
    kept = {name: refs[i] for i, name in enumerate(READ)}
    grads = refs[reads : reads + made - 1]
    (
        flow,
        mixed,
        att_grad,
        qkv_grad,
        sums,
        send,
        received,
        wq_v,
        wp_v,
        wh_v,
        ws_v,
        w_sem,
        in_sem,
        x_sem,
        out_sem,
        send_sem,
        recv_sem,
        film_send,
        film_recv,
    ) = refs[reads + made - 1 :]
    section = lax.axis_index("section")
    here = lax.axis_index("dp")

    def fetching(name, image):
        index = READ.index(name)
        return pltpu.make_async_copy(sources[index].at[image], kept[name], in_sem.at[index])

    fetching(SECOND, 0).start()
    loads = [started(ws, ws_v, w_sem.at[0])]
    for name in READ:
        if name != SECOND:
            fetching(name, 0).start()
    loads.append(started(wx.at[:, pl.ds(4 * D, FF)], wh_v, w_sem.at[1]))
    loads.append(started(wx.at[:, pl.ds(3 * D, D)], wp_v, w_sem.at[2]))
    loads.append(started(wx.at[:, pl.ds(0, 3 * D)], wq_v, w_sem.at[3]))
    spreading, passing = ([], [])
    if direct:
        meet_both(sections, section, here)
        for step in range(1, DIRECT):
            copy = pltpu.make_async_remote_copy(
                src_ref=film,
                dst_ref=film_rows.at[here],
                send_sem=film_send.at[step - 1],
                recv_sem=film_recv.at[step - 1],
                device_id={"dp": lax.rem(here + step, DIRECT)},
                device_id_type=MESH,
            )
            copy.start()
            spreading.append(copy)
        film_rows[here] = film[...]
        for step in range(1, sections):
            passing.append(
                pltpu.make_async_remote_copy(
                    src_ref=film_rows,
                    dst_ref=film_out,
                    send_sem=film_send.at[DIRECT - 2 + step],
                    recv_sem=film_recv.at[DIRECT - 2 + step],
                    device_id={"section": lax.rem(section + step, sections)},
                    device_id_type=MESH,
                )
            )
    else:
        meet("section", sections, section)
    hop = hop_of(send, received, send_sem, recv_sem, lax.rem(section + sections - 1, sections))

    @pl.loop(0, images)
    def run(image):
        saves = []

        def save(name, value=None):
            source = grads[name] if value is None else value
            saves.append(started(source, outs[name].at[image], out_sem.at[name]))

        def fetch_next(*names):
            @pl.when(image + 1 < images)
            def start():
                for name in names:
                    fetching(name, image + 1).start()

        @pl.when(section == sections - 1)
        def take_head():
            started(head_grad.at[image], flow, x_sem).wait()

        @pl.when(section < sections - 1)
        def take_received():
            for part in range(HOPS):
                hop(image, part).wait_recv()
            flow[...] = received[image].astype(jnp.float32)

        modulation = ada[image]
        sums[...] = jnp.zeros_like(sums)

        def add_sum(row, values):
            sums[row : row + 1] += jnp.sum(values, axis=0, keepdims=True)

        fetching(SECOND, image).wait()

        def open_second(at):
            grad = flow[at]
            grads[D_SECOND][at] = (grad * modulation[5:6]).astype(jnp.bfloat16)
            add_sum(5, grad * kept[SECOND][at])

        by_rows(patches, open_second)
        fetch_next(SECOND)
        save(D_SECOND)
        fetching(PRE, image).wait()
        wait_first(image, loads[:1])
        for cols in parts_of(FF, FF // D):
            grads[D_PRE][:, cols] = (
                matmul_nt(grads[D_SECOND][...], ws_v[cols]) * gelu_grad(kept[PRE][:, cols])
            ).astype(jnp.bfloat16)
        fetch_next(PRE)
        save(D_PRE)
        wait_first(image, loads[1:2])
        for cols in parts_of(D, 3):
            mixed[:, cols] = matmul_nt(grads[D_PRE][...], wh_v[cols])
        fetching(MIDDLE, image).wait()
        fetching(BRANCH, image).wait()

        def through_two(at):
            normed, invstd = normalize(kept[MIDDLE][at])
            grad = mixed[at]
            add_sum(3, grad)
            add_sum(4, grad * normed)
            total = flow[at] + norm_back(grad * (1.0 + modulation[4:5]), normed, invstd)
            flow[at] = total
            add_sum(2, total * kept[BRANCH][at])
            grads[D_BRANCH][at] = (total * modulation[2:3]).astype(jnp.bfloat16)

        by_rows(patches, through_two)
        fetch_next(MIDDLE, BRANCH)
        save(D_BRANCH)
        wait_first(image, loads[2:3])
        att_grad[...] = contract(wp_v[...], grads[D_BRANCH][...], 1, 1).astype(jnp.bfloat16)
        fetching(QKV, image).wait()
        attend_back_kernel(kept[QKV], att_grad, qkv_grad)
        fetch_next(QKV)
        wait_first(image, loads[3:])
        for cols in parts_of(D, 3):
            mixed[:, cols] = contract(qkv_grad[...], wq_v[cols], 0, 1)
        fetching(RESIDUAL, image).wait()

        def through_one(at):
            normed, invstd = normalize(kept[RESIDUAL][at])
            grad = mixed[at]
            add_sum(0, grad)
            add_sum(1, grad * normed)
            total = flow[at] + norm_back(grad * (1.0 + modulation[1:2]), normed, invstd)
            send[image, at] = total.astype(jnp.bfloat16)

        by_rows(patches, through_one)

        @pl.when(section > 0)
        def pass_on():
            for part in range(HOPS):
                hop(image, part).start()

        fetch_next(RESIDUAL)
        save(D_RESIDUAL, send.at[image])
        grads[D_QKV][...] = qkv_grad[...].T
        save(D_QKV)
        saves.append(started(sums, ada_out.at[image], x_sem))
        if direct:

            @pl.when(image == 0)
            def pass_film():
                for copy in spreading:
                    copy.wait()

                @pl.when(section == sections - 1)
                def send_film():
                    for copy in passing:
                        copy.start()

        for copy in saves:
            copy.wait()

    @pl.when(section > 0)
    def finish():
        for image in range(images):
            for part in range(HOPS):
                hop(image, part).wait_send()

    if direct:

        @pl.when(section == sections - 1)
        def own_film():
            film_out[...] = film_rows[...]
            for copy in passing:
                copy.wait_send()

        for step in range(1, sections):

            @pl.when(section == step - 1)
            def wait_film(step=step):
                passing[step - 1].wait_recv()


def specs(*spaces):
    return [
        pl.BlockSpec(memory_space={"v": pltpu.VMEM, "h": pl.ANY}[space])
        for space in "".join(spaces)
    ]


def weight_scratch():
    return [pltpu.VMEM(shape, jnp.bfloat16) for shape in WEIGHTS] + [
        pltpu.SemaphoreType.DMA((6,))
    ]


def block_cost(images, patches, factor):
    area = sum(rows * columns for rows, columns in WEIGHTS)
    return pl.CostEstimate(
        flops=images * (2 * patches * area + factor * patches * patches * D),
        bytes_accessed=2 * area + images * 64 * patches * D,
        transcendentals=images * patches * (FF + HEADS * patches),
    )


def pipeline_forward(bias, qkv_bias, ada, tokens, weights):
    images, patches, unused = tokens.shape
    sections = lax.axis_size("section")
    sizes = [(kept_shape(i, item[0], patches), item[1]) for i, item in enumerate(KEPT)]
    return pl.pallas_call(
        functools.partial(forward_kernel, sections, images),
        out_shape=[
            jax.ShapeDtypeStruct((images,) + shape, kind) for shape, kind in sizes
        ],
        in_specs=specs("vvv", "h" * 3),
        out_specs=specs("h" * len(KEPT)),
        scratch_shapes=[pltpu.VMEM(shape, kind) for shape, kind in sizes]
        + [pltpu.VMEM((D, patches), jnp.bfloat16)]
        + [pltpu.VMEM((images, patches, D), jnp.bfloat16)] * 2
        + weight_scratch()
        + [pltpu.SemaphoreType.DMA, pltpu.SemaphoreType.DMA((len(KEPT),))]
        + [pltpu.SemaphoreType.DMA((images, HOPS))] * 2,
        compiler_params=pltpu.CompilerParams(
            vmem_limit_bytes=62 << 20, collective_id=16, has_side_effects=True
        ),
        cost_estimate=block_cost(images, patches, 4),
        name="pipeline_forward",
    )(bias, qkv_bias, ada, tokens, *weights)


def pipeline_backward(ada, head_grad, weights, sources, film):
    images, patches, unused = head_grad.shape
    sections, direct = (lax.axis_size("section"), lax.axis_size("dp") == DIRECT)
    films = [jax.ShapeDtypeStruct((DIRECT,) + film.shape, film.dtype)] * (2 * direct)
    outs = pl.pallas_call(
        functools.partial(backward_kernel, sections, images, direct),
        out_shape=[
            jax.ShapeDtypeStruct((images, patches, width), kind) for width, kind in MADE
        ]
        + [jax.ShapeDtypeStruct((images, 8, D), jnp.float32)]
        + films,
        in_specs=specs("v", "h" * (3 + len(READ)), "v" * direct),
        out_specs=specs("h" * (len(MADE) + 1), "v" * len(films)),
        scratch_shapes=[
            pltpu.VMEM(kept_shape(name, KEPT[name][0], patches), KEPT[name][1]) for name in READ
        ]
        + [pltpu.VMEM((patches, width), kind) for width, kind in MADE[:-1]]
        + [
            pltpu.VMEM((patches, D), jnp.float32),
            pltpu.VMEM((patches, D), jnp.float32),
            pltpu.VMEM((D, patches), jnp.bfloat16),
            pltpu.VMEM((3 * D, patches), jnp.bfloat16),
            pltpu.VMEM((8, D), jnp.float32),
        ]
        + [pltpu.VMEM((images, patches, D), jnp.bfloat16)] * 2
        + weight_scratch()
        + [
            pltpu.SemaphoreType.DMA((len(READ),)),
            pltpu.SemaphoreType.DMA,
            pltpu.SemaphoreType.DMA((len(MADE),)),
        ]
        + [pltpu.SemaphoreType.DMA((images, HOPS))] * 2
        + [pltpu.SemaphoreType.DMA((DIRECT + sections,))] * 2,
        compiler_params=pltpu.CompilerParams(
            vmem_limit_bytes=62 << 20, collective_id=17, has_side_effects=True
        ),
        cost_estimate=block_cost(images, patches, 10),
        name="pipeline_backward",
    )(ada, head_grad, *weights, *sources, *([film] * direct))
    if direct:
        film_all = outs[-1].reshape(-1, film.shape[1])
    else:
        film_all = lax.all_gather(film, ("section", "dp"), tiled=True)
        film_all = film_all[-images * lax.axis_size("dp") :]
    return (outs[: len(MADE) + 1], film_all)


def head_step(residual, film, noise_part, mask_part, inv_count, w_out, b_out):
    shifting, scaling = (film[:, :D], film[:, D:])
    normed, invstd = normalize(residual)
    mixed = (normed * (1.0 + scaling[:, None]) + shifting[:, None]).astype(jnp.bfloat16)
    output = (
        jnp.einsum("bpd,dj->bpj", mixed, w_out, preferred_element_type=jnp.float32) + b_out
    )
    mismatch = output - noise_part
    mask_float = mask_part.astype(jnp.float32)[:, :, None]
    squared = jnp.sum(mask_float * mismatch * mismatch)
    d_output = (2.0 * inv_count * mask_float * mismatch).astype(jnp.bfloat16)
    g_output = jnp.einsum("bpd,bpj->dj", mixed, d_output, preferred_element_type=jnp.float32)
    d_mixed = jnp.einsum("bpj,dj->bpd", d_output, w_out, preferred_element_type=jnp.float32)
    d_film = jnp.concatenate(
        [jnp.sum(d_mixed, axis=1), jnp.sum(d_mixed * normed, axis=1)], axis=1
    ).astype(jnp.bfloat16)
    d_residual = norm_back(d_mixed * (1.0 + scaling[:, None]), normed, invstd)
    g_bias = jnp.sum(d_output.astype(jnp.float32), axis=(0, 1))
    return (squared, d_residual, d_film, g_output, g_bias)


def adam_update(weight, gradient, first_moment, second_moment, scaling):
    gradient = gradient * scaling
    first_new = BETA_ONE * first_moment + (1.0 - BETA_ONE) * gradient
    second_new = BETA_TWO * second_moment + (1.0 - BETA_TWO) * gradient * gradient
    ratio = (
        first_new
        / (1.0 - BETA_ONE**STEP_POWER)
        / (jnp.sqrt(second_new / (1.0 - BETA_TWO**STEP_POWER)) + ADAM_EPS)
    )
    return (weight - RATE * (ratio + DECAY * weight), first_new, second_new)


def body(
    latents,
    noise,
    timesteps,
    labels,
    patch_mask,
    w_in,
    w_down,
    b_blk,
    small_mats,
    small_bias,
    m_in,
    m_down,
    m_bias,
    m_small,
    m_sbias,
    v_in,
    v_down,
    v_bias,
    v_small,
    v_sbias,
):
    section_index = lax.axis_index("section")
    dp_index = lax.axis_index("dp")
    sections = lax.axis_size("section")
    is_first = section_index == 0
    is_last = section_index == sections - 1
    low = jnp.bfloat16
    images, patches = patch_mask.shape
    rows = w_in.shape[1]
    row_at = dp_index * rows
    ada_at = 4 * D + FF
    o_label = PATCH_IN + FREQ
    o_second = o_label + CLASSES
    o_film = o_second + D
    o_out = o_film + 2 * D

    def gathered(value, axis="dp", dim=0):
        return lax.all_gather(value, axis, axis=dim, tiled=True)

    in_low = w_in[0].astype(low)
    w_ada = in_low[:, ada_at:]
    w_tokens = gathered(in_low[:, :ada_at])
    w_second = gathered(w_down[0].astype(low))

    small_low = small_mats.astype(low)
    edge_own = jnp.where(is_first, small_mats[:, :PATCH_IN], small_mats[:, -PATCH_IN:])
    bias_width = b_blk.shape[1]
    pieces = [
        b_blk[0],
        edge_own.reshape(-1),
        timesteps.astype(jnp.float32),
        labels.astype(jnp.float32),
        jnp.sum(patch_mask).astype(jnp.float32)[None],
    ]
    block = jnp.concatenate(pieces)[None]
    blocks = spread(block, "dp", 1)[:, 0]
    ends = [0]
    for piece in pieces:
        ends.append(ends[-1] + piece.shape[0])
    bias_full = rounded(blocks[:, : ends[1]].reshape(-1))
    w_edge = blocks[:, ends[1] : ends[2]].reshape(D, PATCH_IN).astype(low)
    times_all = blocks[:, ends[2] : ends[3]].reshape(-1).astype(jnp.int32)
    labels_all = blocks[:, ends[3] : ends[4]].reshape(-1).astype(jnp.int32)
    valid_total = jnp.sum(blocks[:, ends[4]])
    inv_count = 1.0 / (valid_total * PATCH_IN)
    weights = (w_tokens, w_second)

    small_width = small_mats.shape[1]
    sbias_width = small_bias.shape[0]
    extra = -(-sbias_width // small_width)
    sbias_rows = jnp.pad(small_bias, (0, extra * small_width - sbias_width)).astype(low)
    small_block = jnp.concatenate([small_low, sbias_rows.reshape(extra, small_width)], axis=0)
    small_blocks = spread(small_block, "section", 2)
    small_rows = jnp.concatenate([small_blocks[i, :rows] for i in range(sections)], axis=1)
    small_used = (
        small_blocks[:, rows:].reshape(sections, -1)[:, :sbias_width].reshape(-1)
    ).astype(jnp.float32)

    shards = lax.axis_size("dp")
    time_low = time_features(times_all).astype(low)
    one_hot = label_table(labels_all)
    time_hidden = matmul_nt(time_low, small_rows[:, PATCH_IN:o_label]) + lax.dynamic_slice_in_dim(
        small_used, D + row_at, rows, 0
    )
    time_act = jax.nn.silu(time_hidden).astype(low)
    cond_part = matmul(time_act, small_rows[:, o_second:o_film])
    label_part = matmul_nt(one_hot, small_rows[:, o_label:o_second])
    cond_part = jnp.concatenate([cond_part, label_part], axis=1).reshape(shards, images, D + rows)
    cond_got = exchange(cond_part, "dp", 3)
    cond_own = (
        jnp.sum(cond_got[:, :, :D], axis=0)
        + small_used[2 * D : 3 * D]
        + jnp.swapaxes(cond_got[:, :, D:], 0, 1).reshape(images, D)
    )
    cond_cols = exchange(jnp.swapaxes(cond_own.reshape(images, shards, rows), 0, 1), "dp", 4)
    cond_first = cond_cols.reshape(shards * images, rows)
    cond_later = rounded(cond_first)
    cond_here = jnp.where(is_first, cond_first, cond_later)
    act_here = jax.nn.silu(cond_here).astype(low)
    act_later = jax.nn.silu(cond_later).astype(low)
    ada_part = jnp.concatenate(
        [matmul(act_here, w_ada), matmul(act_later, small_rows[:, o_film:o_out])], axis=1
    )
    ada_own = exchanged_sum(ada_part.reshape(shards, images * 8 * D // 128, 128), 5)
    ada_own = ada_own.reshape(images, 8 * D)
    film = ada_own[:, 6 * D :] + small_used[3 * D : 5 * D]
    ada = (ada_own[:, : 6 * D] + bias_full[ada_at:]).reshape(images, 6, D)
    qkv_bias = jnp.concatenate(
        [bias_full[:D], jnp.zeros((D,), jnp.float32), bias_full[D : 2 * D]]
    )[:, None]
    bias_row = bias_full[None, 2 * D : ada_at]

    fade = alpha_bar(timesteps)[:, None, None]
    noisy_low = (jnp.sqrt(fade) * latents + jnp.sqrt(1.0 - fade) * noise).astype(low)
    tokens = jnp.einsum(
        "bpi,di->bpd", noisy_low, w_edge, preferred_element_type=jnp.float32
    )
    tokens = tokens + small_used[:D] + positions(patches)[None]

    kept_all = pipeline_forward(bias_row, qkv_bias, ada, tokens, weights)

    squared, head_grad, d_film, g_output, g_out_bias = head_step(
        kept_all[OUTPUT],
        film,
        noise,
        patch_mask,
        inv_count,
        w_edge,
        small_used[5 * D :],
    )
    loss_part = jnp.where(is_last, squared * inv_count, 0.0)
    made_all, film_all = pipeline_backward(
        ada, head_grad, weights, [kept_all[name] for name in READ], d_film
    )

    def flat(whole):
        return whole.reshape(images * patches, whole.shape[2])

    d_second, d_pre, d_branch, d_qkv, d_tokens = [flat(whole) for whole in made_all[:5]]
    d_ada = made_all[5][:, :6].astype(low).reshape(images, 6 * D)

    token_sums = column_sum(d_tokens)
    g_edge = jnp.where(
        is_first,
        matmul_tn(d_tokens, noisy_low.reshape(images * patches, PATCH_IN)),
        g_output,
    )
    d_cond = matmul_nt(film_all, small_rows[:, o_film:o_out]) * silu_grad(cond_later)
    shard_wide, shard_down, right_sums, d_ada_all, conds = row_sums(
        [flat(kept_all[name]) for name in (MIXED_ONE, ATT, MIXED_TWO, ACT)],
        [d_qkv, d_branch, d_pre, d_second],
        d_ada,
        w_ada,
        silu_grad(cond_here),
        d_cond,
    )
    d_ada_all = d_ada_all.reshape(shards * images, 6 * D)

    d_cond_rows = lax.dynamic_index_in_dim(conds, dp_index, 0, keepdims=False)
    d_cond_all = jnp.swapaxes(conds, 0, 1).reshape(shards * images, D)
    d_time = (
        matmul_nt(d_cond_all, small_rows[:, o_second:o_film]) * silu_grad(time_hidden)
    ).astype(low)
    bias_sums = jnp.concatenate(
        [
            right_sums[0][:D],
            right_sums[0][2 * D :],
            right_sums[1],
            right_sums[2],
            right_sums[3],
            column_sum(d_ada),
        ]
    )
    sums = jnp.concatenate(
        [
            bias_sums.reshape(shards, -1),
            g_edge.reshape(shards, -1),
            jnp.broadcast_to(token_sums, (shards, D)),
            jnp.broadcast_to(g_out_bias, (shards, PATCH_IN)),
            jnp.broadcast_to(column_sum(d_time), (shards, rows)),
        ],
        axis=1,
    )
    sums = exchange(sums[:, None], "dp", 11)[:, 0]
    shard_ada = matmul_tn(act_here, d_ada_all)
    shard_in = jnp.concatenate([shard_wide, shard_ada], axis=1)
    edge_end = bias_width + rows * PATCH_IN
    shard_bias = jnp.sum(sums[:, :bias_width], axis=0)
    edge_rows = jnp.sum(sums[:, bias_width:edge_end], axis=0).reshape(rows, PATCH_IN)
    token_sums = jnp.sum(sums[:, edge_end : edge_end + D], axis=0)
    out_sums = jnp.sum(sums[:, edge_end + D : edge_end + D + PATCH_IN], axis=0)
    time_sums = sums[:, edge_end + D + PATCH_IN :].reshape(-1)
    small_grad = jnp.concatenate(
        [
            edge_rows,
            matmul_tn(d_time, time_low),
            matmul_tn(d_cond_rows, one_hot),
            matmul_tn(time_act, d_cond_all),
            matmul_tn(act_later, film_all),
            edge_rows,
        ],
        axis=1,
    )
    small_shard = lax.dynamic_slice_in_dim(small_grad, section_index * small_width, small_width, 1)
    sbias_grad = jnp.concatenate(
        [token_sums, time_sums, column_sum(d_cond_all), column_sum(film_all), out_sums]
    )
    sbias_shard = lax.dynamic_slice_in_dim(
        sbias_grad, section_index * sbias_width, sbias_width, 0
    )

    shard_in, shard_down, small_shard, sbias_shard, shard_bias = lax.optimization_barrier(
        (shard_in, shard_down, small_shard, sbias_shard, shard_bias)
    )
    dp_zero = (dp_index == 0).astype(jnp.float32)
    squares = (
        jnp.sum(shard_in * shard_in)
        + jnp.sum(shard_down * shard_down)
        + jnp.sum(shard_bias * shard_bias)
        + jnp.sum(small_shard * small_shard)
        + dp_zero * jnp.sum(sbias_shard * sbias_shard)
    )
    pair = jnp.broadcast_to(jnp.stack([squares, loss_part])[:, None], (2, 128))
    pair = jnp.sum(spread(pair, "dp", 14), axis=0)
    pair = jnp.sum(spread(pair, "section", 15), axis=0)
    norm_square, loss = (pair[0, 0], pair[1, 0])
    grad_norm = jnp.sqrt(norm_square)
    scaling = jnp.minimum(1.0, CLIP / grad_norm)
    new_in, first_in, second_in = adam_update(w_in, shard_in[None], m_in, v_in, scaling)
    new_down, first_down, second_down = adam_update(
        w_down, shard_down[None], m_down, v_down, scaling
    )
    new_bias, first_bias, second_bias = adam_update(
        b_blk, shard_bias[None], m_bias, v_bias, scaling
    )
    new_small, first_small, second_small = adam_update(
        small_mats, small_shard, m_small, v_small, scaling
    )
    new_sbias, first_sbias, second_sbias = adam_update(
        small_bias, sbias_shard, m_sbias, v_sbias, scaling
    )
    return (
        loss,
        grad_norm,
        new_in,
        first_in,
        second_in,
        new_down,
        first_down,
        second_down,
        new_bias,
        first_bias,
        second_bias,
        new_small,
        first_small,
        second_small,
        new_sbias,
        first_sbias,
        second_sbias,
    )


def solution(mesh):
    in_specs = (
        P("dp", None, None),
        P("dp", None, None),
        P("dp"),
        P("dp"),
        P("dp", None),
        P("section", "dp", None),
        P("section", "dp", None),
        P("section", "dp"),
        P("dp", "section"),
        P("section"),
        P("section", "dp", None),
        P("section", "dp", None),
        P("section", "dp"),
        P("dp", "section"),
        P("section"),
        P("section", "dp", None),
        P("section", "dp", None),
        P("section", "dp"),
        P("dp", "section"),
        P("section"),
    )
    out_specs = (
        P(),
        P(),
        P("section", "dp", None),
        P("section", "dp", None),
        P("section", "dp", None),
        P("section", "dp", None),
        P("section", "dp", None),
        P("section", "dp", None),
        P("section", "dp"),
        P("section", "dp"),
        P("section", "dp"),
        P("dp", "section"),
        P("dp", "section"),
        P("dp", "section"),
        P("section"),
        P("section"),
        P("section"),
    )
    return jax.shard_map(body, mesh=mesh, in_specs=in_specs, out_specs=out_specs, check_vma=False)
```

```python
import functools
import math

import jax
import jax.numpy as jnp
from jax import lax
from jax.experimental import pallas as pl
from jax.experimental.pallas import tpu as pltpu
from jax.sharding import PartitionSpec as P

D = 1152
HEADS = 16
HEAD_DIM = 72
FF = 4608
CLASSES = 1000
FREQ = 256
PATCH_IN = 16
GRID = 16


EPS_NORM = 1e-06
CLIP = 0.001
RATE = 0.005
BETA_ONE = 0.9
BETA_TWO = 0.999
ADAM_EPS = 1e-08
DECAY = 0.01
STEP_POWER = 10.0


def passed_along(value, axis, steps):
    count = lax.axis_size(axis)
    first, last = (max(0, -steps), min(count, count - steps))
    return lax.ppermute(value, axis, [(source, source + steps) for source in range(first, last)])


def matmul(left_side, right_side):
    return jnp.dot(left_side, right_side, preferred_element_type=jnp.float32)


def matmul_tn(left_side, right_side):
    return lax.dot_general(
        left_side, right_side, (((0,), (0,)), ((), ())), preferred_element_type=jnp.float32
    )


def matmul_nt(left_side, right_side):
    return lax.dot_general(
        left_side, right_side, (((1,), (1,)), ((), ())), preferred_element_type=jnp.float32
    )


def column_sum(values):
    return jnp.sum(values.astype(jnp.float32), axis=0)


def normalize(values):
    center = values - jnp.mean(values, axis=-1, keepdims=True)
    invstd = lax.rsqrt(jnp.mean(center * center, axis=-1, keepdims=True) + EPS_NORM)
    return (center * invstd, invstd)


def norm_back(grad_normed, normed, invstd):
    return invstd * (
        grad_normed
        - jnp.mean(grad_normed, axis=-1, keepdims=True)
        - normed * jnp.mean(grad_normed * normed, axis=-1, keepdims=True)
    )


def gelu_tanh(values):
    return (
        0.5
        * values
        * (1.0 + jnp.tanh(0.7978845608028654 * (values + 0.044715 * values * values * values)))
    )


def gelu_grad(values):
    inner = jnp.tanh(0.7978845608028654 * (values + 0.044715 * values * values * values))
    return 0.5 * (1.0 + inner) + 0.5 * values * (1.0 - inner * inner) * 0.7978845608028654 * (
        1.0 + 0.134145 * values * values
    )


def silu_grad(values):
    sigma = jax.nn.sigmoid(values)
    return sigma * (1.0 + values * (1.0 - sigma))


def positions(patches):
    quarter = D // 4
    omega = jnp.exp(-math.log(10000.0) * jnp.arange(quarter, dtype=jnp.float32) / quarter)
    spot = jnp.arange(patches, dtype=jnp.int32)
    row_angle = (spot // GRID).astype(jnp.float32)[:, None] * omega[None, :]
    col_angle = (spot % GRID).astype(jnp.float32)[:, None] * omega[None, :]
    return jnp.concatenate(
        [jnp.sin(row_angle), jnp.cos(row_angle), jnp.sin(col_angle), jnp.cos(col_angle)], axis=1
    )


def time_features(time_steps):
    half = FREQ // 2
    freqs = jnp.exp(-math.log(10000.0) * jnp.arange(half, dtype=jnp.float32) / half)
    angles = time_steps.astype(jnp.float32)[:, None] * freqs[None, :]
    return jnp.concatenate([jnp.cos(angles), jnp.sin(angles)], axis=1)


def alpha_bar(time_steps):
    return jnp.cos((time_steps.astype(jnp.float32) / 1000.0 + 0.008) / 1.008 * (math.pi / 2)) ** 2


def label_table(label_part):
    return (label_part[:, None] == jnp.arange(CLASSES, dtype=jnp.int32)[None, :]).astype(
        jnp.bfloat16
    )


MESH = pl.DeviceIdType.MESH
DIRECT = 8


def rounded(values):
    return lax.reduce_precision(values, 8, 7)


def meet(axis, count, here, stride=1):
    barrier = pltpu.get_barrier_semaphore()
    for step in range(1, count):
        pl.semaphore_signal(
            barrier,
            inc=1,
            device_id={axis: lax.rem(here + step * stride, count * stride)},
            device_id_type=MESH,
        )
    pl.semaphore_wait(barrier, count - 1)


def meet_both(sections, section, here):
    barrier = pltpu.get_barrier_semaphore()
    for axis, me, size in (("section", section, sections), ("dp", here, DIRECT)):
        for step in range(1, size):
            pl.semaphore_signal(
                barrier, inc=1, device_id={axis: lax.rem(me + step, size)}, device_id_type=MESH
            )
    pl.semaphore_wait(barrier, sections + DIRECT - 2)


def share_kernel(axis, count, stride, personal, in_ref, out_ref, send_sem, recv_sem):
    here = lax.axis_index(axis)
    meet(axis, count, here, stride)
    place = here // stride
    copies = []
    for step in range(1, count):
        copy = pltpu.make_async_remote_copy(
            src_ref=in_ref.at[lax.rem(place + step, count)] if personal else in_ref,
            dst_ref=out_ref.at[place],
            send_sem=send_sem.at[step - 1],
            recv_sem=recv_sem.at[step - 1],
            device_id={axis: lax.rem(here + step * stride, count * stride)},
            device_id_type=MESH,
        )
        copy.start()
        copies.append(copy)
    out_ref[place] = in_ref[place] if personal else in_ref[...]
    for copy in copies:
        copy.wait()


def share(value, axis, personal, ident, stride=1):
    count = lax.axis_size(axis) // stride
    shape = value.shape if personal else (count,) + value.shape
    return pl.pallas_call(
        functools.partial(share_kernel, axis, count, stride, personal),
        out_shape=jax.ShapeDtypeStruct(shape, value.dtype),
        in_specs=[pl.BlockSpec(memory_space=pltpu.VMEM)],
        out_specs=pl.BlockSpec(memory_space=pltpu.VMEM),
        scratch_shapes=[
            pltpu.SemaphoreType.DMA((count - 1,)),
            pltpu.SemaphoreType.DMA((count - 1,)),
        ],
        compiler_params=pltpu.CompilerParams(collective_id=ident, has_side_effects=True),
        name="share",
    )(value)


def spread(value, axis, ident):
    if lax.axis_size(axis) > DIRECT:
        return lax.all_gather(value, axis)
    return share(value, axis, False, ident)


def exchanged_sum(value, ident):
    count = lax.axis_size("dp")
    if count != DIRECT:
        return jnp.sum(exchange(value, "dp", ident), axis=0)
    core = lax.axis_index("dp") % 2
    parted = value.reshape((count // 2, 2) + value.shape[1:])
    other = lax.dynamic_index_in_dim(parted, 1 - core, 1, keepdims=False)
    same = lax.dynamic_index_in_dim(parted, core, 1, keepdims=False)
    both = same + lax.ppermute(other, "dp", [(i, i ^ 1) for i in range(count)])
    return jnp.sum(share(both, "dp", True, ident, 2), axis=0)


def exchange(value, axis, ident):
    if lax.axis_size(axis) > DIRECT:
        return lax.all_to_all(value, axis, 0, 0)
    return share(value, axis, True, ident)


FINAL, LATER, NEAR, FAR, PASS = range(5)
STEPS = 16
CHIPS = 4


def sums_kernel(units, rows, sections, *refs):
    lefts, rights = (refs[:4], refs[4:8])
    given, w_ada, slope, head_part, refs = (refs[8], refs[9], refs[10], refs[11], refs[12:])
    owns, finals, laters = (refs[0:2], refs[2:4], refs[4:6])
    bias_out, spread_out, cond_out, refs = (refs[6], refs[7], refs[8], refs[9:])
    (
        left_v,
        right_v,
        product,
        got,
        own_v,
        stage,
        near,
        far,
        passed,
        left_sem,
        right_sem,
        send_sem,
        recv_sem,
        own_sem,
        stage_sem,
        block_sem,
        pass_sem,
        given_send,
        given_recv,
        cond_pieces,
        cond_low,
        cond_send,
        cond_recv,
    ) = refs
    here = lax.axis_index("dp")
    core, chip = (lax.rem(here, 2), here // 2)
    partner = {"dp": here + 1 - 2 * core}
    tall = CHIPS * rows
    section = lax.axis_index("section")
    meet_both(sections, section, here)
    spreading = []
    for step in range(1, DIRECT):
        copy = pltpu.make_async_remote_copy(
            src_ref=given,
            dst_ref=spread_out.at[here],
            send_sem=given_send.at[step - 1],
            recv_sem=given_recv.at[step - 1],
            device_id={"dp": lax.rem(here + step, DIRECT)},
            device_id_type=MESH,
        )
        copy.start()
        spreading.append(copy)
    spread_out[here] = given[...]
    places = {NEAR: near, FAR: far, PASS: passed}
    shared = []

    def share_pieces():
        for copy in spreading:
            copy.wait()
        each = given.shape[0]
        for i in range(DIRECT):
            at = slice(i * each, (i + 1) * each)
            cond_pieces[section, at] = contract(spread_out[i], w_ada[...], 1, 1) * slope[at]
        for step in range(1, sections):
            copy = pltpu.make_async_remote_copy(
                src_ref=cond_pieces.at[section],
                dst_ref=cond_pieces.at[section],
                send_sem=cond_send.at[step - 1],
                recv_sem=cond_recv.at[step - 1],
                device_id={"section": lax.rem(section + step, sections)},
                device_id_type=MESH,
            )
            copy.start()
            shared.append(copy)

    def share_rows():
        for copy in shared:
            copy.wait()
        value = head_part[...]
        for layer in reversed(range(sections)):
            value = (value + cond_pieces[layer]).astype(jnp.bfloat16).astype(jnp.float32)
        cond_low[...] = value.astype(jnp.bfloat16)
        cond_out[here] = value.astype(jnp.bfloat16)
        shared.clear()
        for step in range(1, DIRECT):
            copy = pltpu.make_async_remote_copy(
                src_ref=cond_low,
                dst_ref=cond_out.at[here],
                send_sem=cond_send.at[sections + step],
                recv_sem=cond_recv.at[sections + step],
                device_id={"dp": lax.rem(here + step, DIRECT)},
                device_id_type=MESH,
            )
            copy.start()
            shared.append(copy)


    def placed(pair, slot):
        wide, down = pair
        side_by_side = wide.shape[1] // D
        if slot < side_by_side:
            return wide.at[:, pl.ds(slot * D, D)]
        return down.at[pl.ds((slot - side_by_side) * rows, rows)]

    plan, last, slots = ([], [None, None], [1, 1])
    for left, left_at, right, right_at, gathers, slot in units:
        fresh = []
        for side, key in enumerate(((left, left_at), (right, right_at))):
            fresh.append(last[side] != key)
            if fresh[-1]:
                slots[side] = 1 - slots[side]
                last[side] = key
        plan.append((tuple(slots), tuple(fresh)))
    def loads_of(index):
        left, left_at, right, right_at, gathers, slot = units[index]
        (left_slot, right_slot), (left_fresh, right_fresh) = plan[index]
        copies = []
        if left_fresh:
            source = lefts[left].at[:, pl.ds(left_at, D)]
            copies.append(
                pltpu.make_async_copy(source, left_v.at[left_slot], left_sem.at[left_slot])
            )
        if right_fresh:
            source = rights[right].at[:, pl.ds(right_at, D)]
            copies.append(
                pltpu.make_async_copy(source, right_v.at[right_slot], right_sem.at[right_slot])
            )
        return copies

    pending, crossing, leaving, keeping = ({}, {}, {}, {})

    def load(index):
        pending[index] = loads_of(index)
        for copy in pending[index]:
            copy.start()

    def to_partner(source, target, sems):
        copy = pltpu.make_async_remote_copy(
            src_ref=source,
            dst_ref=target,
            send_sem=send_sem.at[sems],
            recv_sem=recv_sem.at[sems],
            device_id=partner,
            device_id_type=MESH,
        )
        copy.start()
        return copy

    def multiply(index):
        gathers = units[index][4]
        left_slot, right_slot = plan[index][0]
        for copy in pending[index]:
            copy.wait()
        if index + 1 < len(units):
            load(index + 1)
        if index >= 2:
            for copy in crossing[index - 2]:
                copy.wait_send()
        slot, place = (index % 2, index % 4)

        @pl.loop(0, 3)
        def tile(step):
            at = pl.ds(pl.multiple_of(step * (D // 3), 128), D // 3)
            product[slot, at] = contract(left_v[left_slot, :, at], right_v[right_slot], 0, 0)

        if gathers is None or gathers == 0:
            ones = jnp.ones((8, right_v.shape[1]), jnp.bfloat16)
            bias_out[units[index][5]] = matmul(ones, right_v[right_slot])
        if gathers is None:
            crossing[index] = [
                to_partner(
                    product.at[slot, pl.ds(pl.multiple_of((2 * i + 1 - core) * rows, 8), rows)],
                    got.at[place, pl.ds(i * rows, rows)],
                    place * CHIPS + i,
                )
                for i in range(CHIPS)
            ]
        else:
            crossing[index] = [
                to_partner(
                    product.at[slot, pl.ds(pl.multiple_of((1 - core) * tall, 8), tall)],
                    got.at[place],
                    place * CHIPS,
                )
            ]

    def crossed(source, kind, slot, to, sem):
        pair = {FINAL: finals, LATER: laters}.get(kind)
        return pltpu.make_async_remote_copy(
            src_ref=source,
            dst_ref=places[kind].at[slot] if pair is None else placed(pair, slot),
            send_sem=sem,
            recv_sem=block_sem.at[kind, slot],
            device_id={"dp": 2 * to + core},
            device_id_type=MESH,
        )

    def landed(kind, slot):
        crossed(stage.at[0, 0], kind, slot, chip, stage_sem.at[0, 0]).wait_recv()

    def filled(target, index, block, gathers, added=None):
        slot, place = (index % 2, index % 4)
        base = (2 * block + core) * rows if gathers is None else core * tall + block * rows

        @pl.loop(0, rows // STEPS)
        def run(step):
            at = step * STEPS
            value = (
                product[slot, pl.ds(pl.multiple_of(base + at, STEPS), STEPS)]
                + got[place, pl.ds(pl.multiple_of(block * rows + at, STEPS), STEPS)]
            )
            to = pl.ds(pl.multiple_of(at, STEPS), STEPS)
            if added is not None:
                value = value + added[to].astype(jnp.float32)
            target[to] = value.astype(target.dtype)

    def route(index, block, owner, slot, gathers):
        side = index % 3

        def case(at, kind, to, added=None):
            copy = crossed(
                stage.at[side, block], kind, slot, to, stage_sem.at[side, block]
            )

            @pl.when(chip == at)
            def act():
                if added is not None:
                    landed(added, slot)
                filled(
                    stage.at[side, block],
                    index,
                    block,
                    gathers,
                    None if added is None else places[added].at[slot],
                )
                copy.start()

            leaving[index].append((chip == at, copy.wait_send))

        keep = pltpu.make_async_copy(
            own_v.at[side, block], placed(owns, slot), own_sem.at[side, block]
        )

        @pl.when(chip == owner)
        def hold():
            filled(own_v.at[side, block], index, block, gathers)
            keep.start()

        leaving[index].append((chip == owner, keep.wait))
        flip = (lambda at: at) if owner < 2 else (lambda at: CHIPS - 1 - at)
        if owner in (0, CHIPS - 1):
            case(flip(3), FAR, flip(2))
            case(flip(1), FINAL, flip(0))
            case(flip(2), PASS, flip(1), FAR)
        else:
            case(flip(3), NEAR, flip(2))
            case(flip(0), FINAL, flip(1))
            case(flip(2), LATER, flip(1), NEAR)

    def blocks_of(index):
        gathers = units[index][4]
        if gathers is None:
            return [(owner, owner, units[index][5]) for owner in (0, 3, 1, 2)]
        return [(block, gathers, units[index][5] + block) for block in range(CHIPS)]

    def combine(index):
        for copy in crossing[index]:
            copy.wait_recv()
        if index >= 3:
            finish(index - 3)
        leaving[index] = []
        for block, owner, slot in blocks_of(index):
            route(index, block, owner, slot, units[index][4])

    def finish(index):
        for condition, wait in leaving[index]:

            @pl.when(condition)
            def settle(wait=wait):
                wait()

    def pass_on(index):
        for block, owner, slot in blocks_of(index):
            if owner not in (0, CHIPS - 1):
                continue
            middle = 1 if owner == 0 else CHIPS - 2

            @pl.when(chip == middle)
            def forward(slot=slot, owner=owner):
                landed(PASS, slot)
                crossed(passed.at[slot], LATER, slot, owner, pass_sem.at[slot]).start()

    total = len(units)
    load(0)
    multiply(0)
    for index in range(total):
        if index + 1 < total:
            multiply(index + 1)
        combine(index)
        if index >= 1:
            pass_on(index - 1)
        if index == 2:
            share_pieces()
        elif index == 5:
            share_rows()
    pass_on(total - 1)
    for index in range(max(0, total - 3), total):
        finish(index)
    for index in range(max(0, total - 2), total):
        for copy in crossing[index]:
            copy.wait_send()
    for index in range(total):
        for block, owner, slot in blocks_of(index):

            @pl.when(chip == owner)
            def received(slot=slot):
                landed(FINAL, slot)
                landed(LATER, slot)

            if owner in (0, CHIPS - 1):

                @pl.when(chip == (1 if owner == 0 else CHIPS - 2))
                def sent(slot=slot, owner=owner):
                    crossed(passed.at[slot], LATER, slot, owner, pass_sem.at[slot]).wait_send()

    for copy in shared:
        copy.wait()


def line_sums(units, lefts, rights, rows, ident, given, w_ada, slope, head_part):
    sections = lax.axis_size("section")
    tokens = lefts[0].shape[0]
    places = sum(unit[4] is None for unit in units) + 4
    block = (rows, D)
    outs = pl.pallas_call(
        functools.partial(sums_kernel, units, rows, sections),
        out_shape=[
            jax.ShapeDtypeStruct(shape, kind)
            for kind in (jnp.float32, jnp.bfloat16, jnp.bfloat16)
            for shape in ((rows, (places - CHIPS) * D), (CHIPS * rows, D))
        ]
        + [
            jax.ShapeDtypeStruct((places - CHIPS + 1, 8, D), jnp.float32),
            jax.ShapeDtypeStruct((DIRECT,) + given.shape, given.dtype),
            jax.ShapeDtypeStruct((DIRECT,) + slope.shape, jnp.bfloat16),
        ],
        in_specs=specs("h" * 8, "vvvv"),
        out_specs=specs("h" * 6, "vvv"),
        scratch_shapes=[
            pltpu.VMEM((2, tokens, D), jnp.bfloat16),
            pltpu.VMEM((2, tokens, D), jnp.bfloat16),
            pltpu.VMEM((2, 8 * rows, D), jnp.float32),
            pltpu.VMEM((4, 4 * rows, D), jnp.float32),
            pltpu.VMEM((3, 4) + block, jnp.float32),
            pltpu.VMEM((3, 4) + block, jnp.bfloat16),
            pltpu.VMEM((places,) + block, jnp.bfloat16),
            pltpu.VMEM((places,) + block, jnp.bfloat16),
            pltpu.VMEM((places,) + block, jnp.bfloat16),
            pltpu.SemaphoreType.DMA((2,)),
            pltpu.SemaphoreType.DMA((2,)),
            pltpu.SemaphoreType.DMA((16,)),
            pltpu.SemaphoreType.DMA((16,)),
            pltpu.SemaphoreType.DMA((3, 4)),
            pltpu.SemaphoreType.DMA((3, 4)),
            pltpu.SemaphoreType.DMA((5, places)),
            pltpu.SemaphoreType.DMA((places,)),
            pltpu.SemaphoreType.DMA((DIRECT - 1,)),
            pltpu.SemaphoreType.DMA((DIRECT - 1,)),
            pltpu.VMEM((sections,) + slope.shape, jnp.float32),
            pltpu.VMEM(slope.shape, jnp.bfloat16),
            pltpu.SemaphoreType.DMA((sections + DIRECT,)),
            pltpu.SemaphoreType.DMA((sections + DIRECT,)),
        ],
        compiler_params=pltpu.CompilerParams(
            collective_id=ident, has_side_effects=True, vmem_limit_bytes=62 << 20
        ),
        cost_estimate=pl.CostEstimate(
            flops=2 * tokens * D * D * len(units),
            bytes_accessed=len(units) * tokens * D * 4,
            transcendentals=0,
        ),
        name="line_sums",
    )(*lefts, *rights, given, w_ada, slope, head_part)
    wide, down = [
        outs[i] + outs[2 + i].astype(jnp.float32) + outs[4 + i].astype(jnp.float32)
        for i in range(2)
    ]
    return (wide, down, outs[6][:, 0], outs[7], outs[8])


def row_sums(lefts, rights, given, w_ada, slope, head_part):
    count = lax.axis_size("dp")
    if count != DIRECT:
        products = [matmul_tn(one, other) for one, other in zip(lefts, rights)]
        sums = [lax.psum_scatter(one, "dp", scatter_dimension=0, tiled=True) for one in products]
        wide = jnp.concatenate([sums[0], sums[1], sums[2]], axis=1)
        given = lax.all_gather(given, "dp")
        pieces = matmul_nt(given.reshape(-1, given.shape[2]), w_ada) * slope
        pieces = lax.all_gather(pieces, "section")
        for layer in reversed(range(lax.axis_size("section"))):
            head_part = rounded(head_part + pieces[layer])
        conds = lax.all_gather(head_part.astype(jnp.bfloat16), "dp")
        return (wide, sums[3], [column_sum(one) for one in rights], given, conds)
    rows = D // count
    parts = FF // D
    attention = [(0, 0, 0, i * D, None, i) for i in range(3)] + [(1, 0, 1, 0, None, 3)]
    hidden = [(2, 0, 2, i * D, None, 4 + i) for i in range(parts)]
    second = [(3, i * D, 3, 0, i, 4 + parts) for i in (0, 3, 1, 2)]
    units = hidden[:1] + second[:2] + hidden[1:2] + second[2:] + hidden[2:] + attention
    wide, down, bias, given_all, conds = line_sums(
        tuple(units), lefts, rights, rows, 12, given, w_ada, slope, head_part
    )
    sums = [bias[:3].reshape(-1), bias[3], bias[4 : 4 + parts].reshape(-1), bias[4 + parts]]
    return (wide, down, sums, given_all, conds)


GROUP = 4


def contract(left_side, right_side, left_axis, right_axis):
    return lax.dot_general(
        left_side,
        right_side,
        (((left_axis,), (right_axis,)), ((), ())),
        preferred_element_type=jnp.float32,
    )


def heads_of(ref, at, group):
    return [
        ref[at + head * HEAD_DIM : at + (head + 1) * HEAD_DIM] for head in group
    ]


def softmax_down(scores):
    weights = jnp.exp(scores - jnp.max(scores, axis=0, keepdims=True))
    return weights * (1.0 / jnp.sum(weights, axis=0, keepdims=True))


def stacked(values):
    return jnp.concatenate([value.astype(jnp.bfloat16) for value in values], axis=0)


def attend_kernel(qkv_ref, out_ref):
    scaling = HEAD_DIM ** (-0.5)
    for first in range(0, HEADS, GROUP):
        group = range(first, first + GROUP)
        rows = slice(first * HEAD_DIM, (first + GROUP) * HEAD_DIM)
        queries, keys = (heads_of(qkv_ref, 0, group), heads_of(qkv_ref, D, group))
        values = heads_of(qkv_ref, 2 * D, group)
        scores = [contract(key, query, 0, 0) * scaling for key, query in zip(keys, queries)]
        probs = [softmax_down(score).astype(jnp.bfloat16) for score in scores]
        out_ref[rows] = stacked([contract(v, p, 1, 0) for v, p in zip(values, probs)])


def attend_back_kernel(qkv_ref, grad_ref, out_ref):
    scaling = HEAD_DIM ** (-0.5)
    for first in range(0, HEADS, GROUP):
        group = range(first, first + GROUP)
        at, to = (first * HEAD_DIM, (first + GROUP) * HEAD_DIM)
        queries, keys = (heads_of(qkv_ref, 0, group), heads_of(qkv_ref, D, group))
        values, grads = (heads_of(qkv_ref, 2 * D, group), heads_of(grad_ref, 0, group))
        scores = [contract(key, query, 0, 0) * scaling for key, query in zip(keys, queries)]
        d_probs = [contract(value, grad, 0, 0) for value, grad in zip(values, grads)]
        probs = [softmax_down(score) for score in scores]
        d_scores = [
            (p * (d - jnp.sum(p * d, axis=0, keepdims=True))).astype(jnp.bfloat16)
            for p, d in zip(probs, d_probs)
        ]
        lows = [p.astype(jnp.bfloat16) for p in probs]
        out_ref[at:to] = stacked([contract(k, d, 1, 0) * scaling for k, d in zip(keys, d_scores)])
        out_ref[D + at : D + to] = stacked(
            [contract(q, d, 1, 1) * scaling for q, d in zip(queries, d_scores)]
        )
        out_ref[2 * D + at : 2 * D + to] = stacked(
            [contract(g, p, 1, 1) for g, p in zip(grads, lows)]
        )


ROW_BLOCK = 64
HOPS = 3
RESIDUAL, MIXED_ONE, QKV, ATT, BRANCH, MIDDLE = range(6)
MIXED_TWO, PRE, ACT, SECOND, OUTPUT = range(6, 11)
D_SECOND, D_PRE, D_BRANCH, D_QKV, D_RESIDUAL = range(5)
WIDE, LOW = (jnp.float32, jnp.bfloat16)
KEPT = (
    (D, WIDE),
    (D, LOW),
    (3 * D, LOW),
    (D, LOW),
    (D, WIDE),
    (D, WIDE),
    (D, LOW),
    (FF, WIDE),
    (FF, LOW),
    (D, WIDE),
    (D, WIDE),
)
READ = (RESIDUAL, QKV, BRANCH, MIDDLE, PRE, SECOND)
MADE = ((D, LOW), (FF, LOW), (D, LOW), (3 * D, LOW), (D, LOW))
WEIGHTS = ((D, 3 * D), (D, D), (D, FF), (FF, D))


def kept_shape(name, width, patches):
    return (width, patches) if name == QKV else (patches, width)


def by_rows(patches, step):
    @pl.loop(0, patches // ROW_BLOCK)
    def run(index):
        step(pl.ds(pl.multiple_of(index * ROW_BLOCK, ROW_BLOCK), ROW_BLOCK))


def started(source, target, sem):
    copy = pltpu.make_async_copy(source, target, sem)
    copy.start()
    return copy


def parts_of(whole, parts):
    width = whole // parts
    return [slice(part * width, part * width + width) for part in range(parts)]


def wait_first(image, loads):
    @pl.when(image == 0)
    def wait():
        for load in loads:
            load.wait()


def hop_of(send, received, send_sem, recv_sem, target):
    def hop(image, part):
        cols = pl.ds(part * (D // HOPS), D // HOPS)
        return pltpu.make_async_remote_copy(
            src_ref=send.at[image, :, cols],
            dst_ref=received.at[image, :, cols],
            send_sem=send_sem.at[image, part],
            recv_sem=recv_sem.at[image, part],
            device_id={"section": target},
            device_id_type=MESH,
        )

    return hop


def forward_kernel(sections, images, bias, qkv_bias, ada, tokens, wx, ws, *refs):
    count, patches = (len(KEPT), tokens.shape[1])
    outs, scratch = (refs[:count], refs[count:])
    kept = scratch[:count]
    (
        att_down,
        send,
        received,
        wq_v,
        wp_v,
        wh_v,
        ws_v,
        w_sem,
        x_sem,
        out_sem,
        send_sem,
        recv_sem,
    ) = scratch[count:]
    section = lax.axis_index("section")
    loads = [
        started(wx.at[:, cols], wq_v.at[:, cols], w_sem.at[i])
        for i, cols in enumerate(parts_of(3 * D, 3))
    ]
    loads.append(started(wx.at[:, pl.ds(3 * D, D)], wp_v, w_sem.at[3]))
    loads.append(started(wx.at[:, pl.ds(4 * D, FF)], wh_v, w_sem.at[4]))
    loads.append(started(ws, ws_v, w_sem.at[5]))
    meet("section", sections, section)
    hop = hop_of(send, received, send_sem, recv_sem, lax.rem(section + 1, sections))
    residual = kept[RESIDUAL]
    late = (PRE, ACT, SECOND, OUTPUT)

    def saving(name, image):
        return pltpu.make_async_copy(kept[name], outs[name].at[image], out_sem.at[name])

    @pl.loop(0, images)
    def run(image):
        saves = []

        def save(name):
            copy = saving(name, image)
            copy.start()
            if name not in late:
                saves.append(copy)

        def settle(*names):
            @pl.when(image > 0)
            def wait():
                for name in names:
                    saving(name, image - 1).wait()

        @pl.when(section == 0)
        def take_tokens():
            started(tokens.at[image], residual, x_sem).wait()

        @pl.when(section > 0)
        def take_received():
            for part in range(HOPS):
                hop(image, part).wait_recv()
            residual[...] = received[image].astype(jnp.float32)

        save(RESIDUAL)
        modulation = ada[image]

        def mix_one(at):
            normed, unused = normalize(residual[at])
            kept[MIXED_ONE][at] = (normed * (1.0 + modulation[1:2]) + modulation[0:1]).astype(
                jnp.bfloat16
            )

        by_rows(patches, mix_one)
        save(MIXED_ONE)
        wait_first(image, loads[:3])
        for cols in parts_of(3 * D, 3):
            kept[QKV][cols] = (
                contract(wq_v[:, cols], kept[MIXED_ONE][...], 0, 1) + qkv_bias[cols]
            ).astype(jnp.bfloat16)
        save(QKV)
        attend_kernel(kept[QKV], att_down)
        wait_first(image, loads[3:4])
        kept[BRANCH][...] = contract(att_down[...], wp_v[...], 0, 0) + bias[:, :D]
        kept[ATT][...] = att_down[...].T
        save(BRANCH)
        save(ATT)

        def mix_two(at):
            middle = residual[at] + modulation[2:3] * kept[BRANCH][at]
            kept[MIDDLE][at] = middle
            normed, unused = normalize(middle)
            kept[MIXED_TWO][at] = (normed * (1.0 + modulation[4:5]) + modulation[3:4]).astype(
                jnp.bfloat16
            )

        by_rows(patches, mix_two)
        save(MIDDLE)
        save(MIXED_TWO)
        wait_first(image, loads[4:5])
        settle(PRE, ACT)
        for part, cols in enumerate(parts_of(FF, FF // D)):
            pre = (
                matmul(kept[MIXED_TWO][...], wh_v[:, cols])
                + bias[:, D + part * D : 2 * D + part * D]
            )
            kept[PRE][:, cols] = pre
            kept[ACT][:, cols] = gelu_tanh(pre).astype(jnp.bfloat16)
        save(PRE)
        save(ACT)
        wait_first(image, loads[5:])
        settle(SECOND, OUTPUT)
        for part, cols in enumerate(parts_of(D, HOPS)):
            second = (
                matmul(kept[ACT][...], ws_v[:, cols])
                + bias[:, D + FF + cols.start : D + FF + cols.stop]
            )
            kept[SECOND][:, cols] = second
            output = kept[MIDDLE][:, cols] + modulation[5:6, cols] * second
            kept[OUTPUT][:, cols] = output
            send[image, :, cols] = output.astype(jnp.bfloat16)

            @pl.when(section < sections - 1)
            def pass_on(part=part):
                hop(image, part).start()

        save(SECOND)
        save(OUTPUT)
        for copy in saves:
            copy.wait()

    for name in late:
        saving(name, images - 1).wait()

    @pl.when(section < sections - 1)
    def finish():
        for image in range(images):
            for part in range(HOPS):
                hop(image, part).wait_send()


def backward_kernel(sections, images, direct, ada, head_grad, wx, ws, *refs):
    reads, made, patches = (len(READ), len(MADE), head_grad.shape[1])
    sources, refs = (refs[:reads], refs[reads:])
    if direct:
        film, refs = (refs[0], refs[1:])
    outs, ada_out, refs = (refs[:made], refs[made], refs[made + 1 :])
    if direct:
        film_rows, film_out, refs = (refs[0], refs[1], refs[2:])
    kept = {name: refs[i] for i, name in enumerate(READ)}
    grads = refs[reads : reads + made - 1]
    (
        flow,
        mixed,
        att_grad,
        qkv_grad,
        sums,
        send,
        received,
        wq_v,
        wp_v,
        wh_v,
        ws_v,
        w_sem,
        in_sem,
        x_sem,
        out_sem,
        send_sem,
        recv_sem,
        film_send,
        film_recv,
    ) = refs[reads + made - 1 :]
    section = lax.axis_index("section")
    here = lax.axis_index("dp")

    def fetching(name, image):
        index = READ.index(name)
        return pltpu.make_async_copy(sources[index].at[image], kept[name], in_sem.at[index])

    fetching(SECOND, 0).start()
    loads = [started(ws, ws_v, w_sem.at[0])]
    for name in READ:
        if name != SECOND:
            fetching(name, 0).start()
    loads.append(started(wx.at[:, pl.ds(4 * D, FF)], wh_v, w_sem.at[1]))
    loads.append(started(wx.at[:, pl.ds(3 * D, D)], wp_v, w_sem.at[2]))
    loads.append(started(wx.at[:, pl.ds(0, 3 * D)], wq_v, w_sem.at[3]))
    spreading, passing = ([], [])
    if direct:
        meet_both(sections, section, here)
        for step in range(1, DIRECT):
            copy = pltpu.make_async_remote_copy(
                src_ref=film,
                dst_ref=film_rows.at[here],
                send_sem=film_send.at[step - 1],
                recv_sem=film_recv.at[step - 1],
                device_id={"dp": lax.rem(here + step, DIRECT)},
                device_id_type=MESH,
            )
            copy.start()
            spreading.append(copy)
        film_rows[here] = film[...]
        for step in range(1, sections):
            passing.append(
                pltpu.make_async_remote_copy(
                    src_ref=film_rows,
                    dst_ref=film_out,
                    send_sem=film_send.at[DIRECT - 2 + step],
                    recv_sem=film_recv.at[DIRECT - 2 + step],
                    device_id={"section": lax.rem(section + step, sections)},
                    device_id_type=MESH,
                )
            )
    else:
        meet("section", sections, section)
    hop = hop_of(send, received, send_sem, recv_sem, lax.rem(section + sections - 1, sections))

    late = (D_QKV, D_RESIDUAL)
    sums[...] = jnp.zeros_like(sums)

    def saving(name, image):
        source = send.at[image] if name == D_RESIDUAL else grads[name]
        return pltpu.make_async_copy(source, outs[name].at[image], out_sem.at[name])

    @pl.loop(0, images)
    def run(image):
        saves = []

        def save(name):
            copy = saving(name, image)
            copy.start()
            if name not in late:
                saves.append(copy)

        def settle(name):
            @pl.when(image > 0)
            def wait():
                saving(name, image - 1).wait()

        def fetch_next(*names):
            @pl.when(image + 1 < images)
            def start():
                for name in names:
                    fetching(name, image + 1).start()

        @pl.when(section == sections - 1)
        def take_head():
            started(head_grad.at[image], flow, x_sem).wait()

        @pl.when(section < sections - 1)
        def take_received():
            for part in range(HOPS):
                hop(image, part).wait_recv()
            flow[...] = received[image].astype(jnp.float32)

        modulation = ada[image]

        def add_sum(row, values):
            sums[image, row : row + 1] += jnp.sum(values, axis=0, keepdims=True)

        fetching(SECOND, image).wait()

        def open_second(at):
            grad = flow[at]
            grads[D_SECOND][at] = (grad * modulation[5:6]).astype(jnp.bfloat16)
            add_sum(5, grad * kept[SECOND][at])

        by_rows(patches, open_second)
        fetch_next(SECOND)
        save(D_SECOND)
        fetching(PRE, image).wait()
        wait_first(image, loads[:1])
        for cols in parts_of(FF, FF // D):
            grads[D_PRE][:, cols] = (
                matmul_nt(grads[D_SECOND][...], ws_v[cols]) * gelu_grad(kept[PRE][:, cols])
            ).astype(jnp.bfloat16)
        fetch_next(PRE)
        save(D_PRE)
        wait_first(image, loads[1:2])
        for cols in parts_of(D, 3):
            mixed[:, cols] = matmul_nt(grads[D_PRE][...], wh_v[cols])
        fetching(MIDDLE, image).wait()
        fetching(BRANCH, image).wait()

        def through_two(at):
            normed, invstd = normalize(kept[MIDDLE][at])
            grad = mixed[at]
            add_sum(3, grad)
            add_sum(4, grad * normed)
            total = flow[at] + norm_back(grad * (1.0 + modulation[4:5]), normed, invstd)
            flow[at] = total
            add_sum(2, total * kept[BRANCH][at])
            grads[D_BRANCH][at] = (total * modulation[2:3]).astype(jnp.bfloat16)

        by_rows(patches, through_two)
        fetch_next(MIDDLE, BRANCH)
        save(D_BRANCH)
        wait_first(image, loads[2:3])
        att_grad[...] = contract(wp_v[...], grads[D_BRANCH][...], 1, 1).astype(jnp.bfloat16)
        fetching(QKV, image).wait()
        attend_back_kernel(kept[QKV], att_grad, qkv_grad)
        fetch_next(QKV)
        wait_first(image, loads[3:])
        for cols in parts_of(D, 3):
            mixed[:, cols] = contract(qkv_grad[...], wq_v[cols], 0, 1)
        fetching(RESIDUAL, image).wait()

        def through_one(at):
            normed, invstd = normalize(kept[RESIDUAL][at])
            grad = mixed[at]
            add_sum(0, grad)
            add_sum(1, grad * normed)
            total = flow[at] + norm_back(grad * (1.0 + modulation[1:2]), normed, invstd)
            send[image, at] = total.astype(jnp.bfloat16)

        by_rows(patches, through_one)

        @pl.when(section > 0)
        def pass_on():
            for part in range(HOPS):
                hop(image, part).start()

        fetch_next(RESIDUAL)
        settle(D_RESIDUAL)
        save(D_RESIDUAL)
        settle(D_QKV)
        grads[D_QKV][...] = qkv_grad[...].T
        save(D_QKV)
        if direct:

            @pl.when(image == 0)
            def pass_film():
                for copy in spreading:
                    copy.wait()

                @pl.when(section == sections - 1)
                def send_film():
                    for copy in passing:
                        copy.start()

        for copy in saves:
            copy.wait()

    started(sums, ada_out, x_sem).wait()
    for name in late:
        saving(name, images - 1).wait()

    @pl.when(section > 0)
    def finish():
        for image in range(images):
            for part in range(HOPS):
                hop(image, part).wait_send()

    if direct:

        @pl.when(section == sections - 1)
        def own_film():
            film_out[...] = film_rows[...]
            for copy in passing:
                copy.wait_send()

        for step in range(1, sections):

            @pl.when(section == step - 1)
            def wait_film(step=step):
                passing[step - 1].wait_recv()


def specs(*spaces):
    return [
        pl.BlockSpec(memory_space={"v": pltpu.VMEM, "h": pl.ANY}[space])
        for space in "".join(spaces)
    ]


def weight_scratch():
    return [pltpu.VMEM(shape, jnp.bfloat16) for shape in WEIGHTS] + [
        pltpu.SemaphoreType.DMA((6,))
    ]


def block_cost(images, patches, factor):
    area = sum(rows * columns for rows, columns in WEIGHTS)
    return pl.CostEstimate(
        flops=images * (2 * patches * area + factor * patches * patches * D),
        bytes_accessed=2 * area + images * 64 * patches * D,
        transcendentals=images * patches * (FF + HEADS * patches),
    )


def pipeline_forward(bias, qkv_bias, ada, tokens, weights):
    images, patches, unused = tokens.shape
    sections = lax.axis_size("section")
    sizes = [(kept_shape(i, item[0], patches), item[1]) for i, item in enumerate(KEPT)]
    return pl.pallas_call(
        functools.partial(forward_kernel, sections, images),
        out_shape=[
            jax.ShapeDtypeStruct((images,) + shape, kind) for shape, kind in sizes
        ],
        in_specs=specs("vvv", "h" * 3),
        out_specs=specs("h" * len(KEPT)),
        scratch_shapes=[pltpu.VMEM(shape, kind) for shape, kind in sizes]
        + [pltpu.VMEM((D, patches), jnp.bfloat16)]
        + [pltpu.VMEM((images, patches, D), jnp.bfloat16)] * 2
        + weight_scratch()
        + [pltpu.SemaphoreType.DMA, pltpu.SemaphoreType.DMA((len(KEPT),))]
        + [pltpu.SemaphoreType.DMA((images, HOPS))] * 2,
        compiler_params=pltpu.CompilerParams(
            vmem_limit_bytes=62 << 20, collective_id=16, has_side_effects=True
        ),
        cost_estimate=block_cost(images, patches, 4),
        name="pipeline_forward",
    )(bias, qkv_bias, ada, tokens, *weights)


def pipeline_backward(ada, head_grad, weights, sources, film):
    images, patches, unused = head_grad.shape
    sections, direct = (lax.axis_size("section"), lax.axis_size("dp") == DIRECT)
    films = [jax.ShapeDtypeStruct((DIRECT,) + film.shape, film.dtype)] * (2 * direct)
    outs = pl.pallas_call(
        functools.partial(backward_kernel, sections, images, direct),
        out_shape=[
            jax.ShapeDtypeStruct((images, patches, width), kind) for width, kind in MADE
        ]
        + [jax.ShapeDtypeStruct((images, 8, D), jnp.float32)]
        + films,
        in_specs=specs("v", "h" * (3 + len(READ)), "v" * direct),
        out_specs=specs("h" * (len(MADE) + 1), "v" * len(films)),
        scratch_shapes=[
            pltpu.VMEM(kept_shape(name, KEPT[name][0], patches), KEPT[name][1]) for name in READ
        ]
        + [pltpu.VMEM((patches, width), kind) for width, kind in MADE[:-1]]
        + [
            pltpu.VMEM((patches, D), jnp.float32),
            pltpu.VMEM((patches, D), jnp.float32),
            pltpu.VMEM((D, patches), jnp.bfloat16),
            pltpu.VMEM((3 * D, patches), jnp.bfloat16),
            pltpu.VMEM((images, 8, D), jnp.float32),
        ]
        + [pltpu.VMEM((images, patches, D), jnp.bfloat16)] * 2
        + weight_scratch()
        + [
            pltpu.SemaphoreType.DMA((len(READ),)),
            pltpu.SemaphoreType.DMA,
            pltpu.SemaphoreType.DMA((len(MADE),)),
        ]
        + [pltpu.SemaphoreType.DMA((images, HOPS))] * 2
        + [pltpu.SemaphoreType.DMA((DIRECT + sections,))] * 2,
        compiler_params=pltpu.CompilerParams(
            vmem_limit_bytes=62 << 20, collective_id=17, has_side_effects=True
        ),
        cost_estimate=block_cost(images, patches, 10),
        name="pipeline_backward",
    )(ada, head_grad, *weights, *sources, *([film] * direct))
    if direct:
        film_all = outs[-1].reshape(-1, film.shape[1])
    else:
        film_all = lax.all_gather(film, ("section", "dp"), tiled=True)
        film_all = film_all[-images * lax.axis_size("dp") :]
    return (outs[: len(MADE) + 1], film_all)


def head_step(residual, film, noise_part, mask_part, inv_count, w_out, b_out):
    shifting, scaling = (film[:, :D], film[:, D:])
    normed, invstd = normalize(residual)
    mixed = (normed * (1.0 + scaling[:, None]) + shifting[:, None]).astype(jnp.bfloat16)
    output = (
        jnp.einsum("bpd,dj->bpj", mixed, w_out, preferred_element_type=jnp.float32) + b_out
    )
    mismatch = output - noise_part
    mask_float = mask_part.astype(jnp.float32)[:, :, None]
    squared = jnp.sum(mask_float * mismatch * mismatch)
    d_output = (2.0 * inv_count * mask_float * mismatch).astype(jnp.bfloat16)
    g_output = jnp.einsum("bpd,bpj->dj", mixed, d_output, preferred_element_type=jnp.float32)
    d_mixed = jnp.einsum("bpj,dj->bpd", d_output, w_out, preferred_element_type=jnp.float32)
    d_film = jnp.concatenate(
        [jnp.sum(d_mixed, axis=1), jnp.sum(d_mixed * normed, axis=1)], axis=1
    ).astype(jnp.bfloat16)
    d_residual = norm_back(d_mixed * (1.0 + scaling[:, None]), normed, invstd)
    g_bias = jnp.sum(d_output.astype(jnp.float32), axis=(0, 1))
    return (squared, d_residual, d_film, g_output, g_bias)


def adam_update(weight, gradient, first_moment, second_moment, scaling):
    gradient = gradient * scaling
    first_new = BETA_ONE * first_moment + (1.0 - BETA_ONE) * gradient
    second_new = BETA_TWO * second_moment + (1.0 - BETA_TWO) * gradient * gradient
    ratio = (
        first_new
        / (1.0 - BETA_ONE**STEP_POWER)
        / (jnp.sqrt(second_new / (1.0 - BETA_TWO**STEP_POWER)) + ADAM_EPS)
    )
    return (weight - RATE * (ratio + DECAY * weight), first_new, second_new)


def body(
    latents,
    noise,
    timesteps,
    labels,
    patch_mask,
    w_in,
    w_down,
    b_blk,
    small_mats,
    small_bias,
    m_in,
    m_down,
    m_bias,
    m_small,
    m_sbias,
    v_in,
    v_down,
    v_bias,
    v_small,
    v_sbias,
):
    section_index = lax.axis_index("section")
    dp_index = lax.axis_index("dp")
    sections = lax.axis_size("section")
    is_first = section_index == 0
    is_last = section_index == sections - 1
    low = jnp.bfloat16
    images, patches = patch_mask.shape
    rows = w_in.shape[1]
    row_at = dp_index * rows
    ada_at = 4 * D + FF
    o_label = PATCH_IN + FREQ
    o_second = o_label + CLASSES
    o_film = o_second + D
    o_out = o_film + 2 * D

    def gathered(value, axis="dp", dim=0):
        return lax.all_gather(value, axis, axis=dim, tiled=True)

    in_low = w_in[0].astype(low)
    w_ada = in_low[:, ada_at:]
    w_tokens = gathered(in_low[:, :ada_at])
    w_second = gathered(w_down[0].astype(low))

    small_low = small_mats.astype(low)
    edge_own = jnp.where(is_first, small_mats[:, :PATCH_IN], small_mats[:, -PATCH_IN:])
    bias_width = b_blk.shape[1]
    pieces = [
        b_blk[0],
        edge_own.reshape(-1),
        timesteps.astype(jnp.float32),
        labels.astype(jnp.float32),
        jnp.sum(patch_mask).astype(jnp.float32)[None],
    ]
    block = jnp.concatenate(pieces)[None]
    blocks = spread(block, "dp", 1)[:, 0]
    ends = [0]
    for piece in pieces:
        ends.append(ends[-1] + piece.shape[0])
    bias_full = rounded(blocks[:, : ends[1]].reshape(-1))
    w_edge = blocks[:, ends[1] : ends[2]].reshape(D, PATCH_IN).astype(low)
    times_all = blocks[:, ends[2] : ends[3]].reshape(-1).astype(jnp.int32)
    labels_all = blocks[:, ends[3] : ends[4]].reshape(-1).astype(jnp.int32)
    valid_total = jnp.sum(blocks[:, ends[4]])
    inv_count = 1.0 / (valid_total * PATCH_IN)
    weights = (w_tokens, w_second)

    small_width = small_mats.shape[1]
    sbias_width = small_bias.shape[0]
    extra = -(-sbias_width // small_width)
    sbias_rows = jnp.pad(small_bias, (0, extra * small_width - sbias_width)).astype(low)
    small_block = jnp.concatenate([small_low, sbias_rows.reshape(extra, small_width)], axis=0)
    small_blocks = spread(small_block, "section", 2)
    small_rows = jnp.concatenate([small_blocks[i, :rows] for i in range(sections)], axis=1)
    small_used = (
        small_blocks[:, rows:].reshape(sections, -1)[:, :sbias_width].reshape(-1)
    ).astype(jnp.float32)

    shards = lax.axis_size("dp")
    time_low = time_features(times_all).astype(low)
    one_hot = label_table(labels_all)
    time_hidden = matmul_nt(time_low, small_rows[:, PATCH_IN:o_label]) + lax.dynamic_slice_in_dim(
        small_used, D + row_at, rows, 0
    )
    time_act = jax.nn.silu(time_hidden).astype(low)
    cond_part = matmul(time_act, small_rows[:, o_second:o_film])
    label_part = matmul_nt(one_hot, small_rows[:, o_label:o_second])
    cond_part = jnp.concatenate([cond_part, label_part], axis=1).reshape(shards, images, D + rows)
    cond_got = exchange(cond_part, "dp", 3)
    cond_own = (
        jnp.sum(cond_got[:, :, :D], axis=0)
        + small_used[2 * D : 3 * D]
        + jnp.swapaxes(cond_got[:, :, D:], 0, 1).reshape(images, D)
    )
    cond_cols = exchange(jnp.swapaxes(cond_own.reshape(images, shards, rows), 0, 1), "dp", 4)
    cond_first = cond_cols.reshape(shards * images, rows)
    cond_later = rounded(cond_first)
    cond_here = jnp.where(is_first, cond_first, cond_later)
    act_here = jax.nn.silu(cond_here).astype(low)
    act_later = jax.nn.silu(cond_later).astype(low)
    ada_part = jnp.concatenate(
        [matmul(act_here, w_ada), matmul(act_later, small_rows[:, o_film:o_out])], axis=1
    )
    ada_own = exchanged_sum(ada_part.reshape(shards, images * 8 * D // 128, 128), 5)
    ada_own = ada_own.reshape(images, 8 * D)
    film = ada_own[:, 6 * D :] + small_used[3 * D : 5 * D]
    ada = (ada_own[:, : 6 * D] + bias_full[ada_at:]).reshape(images, 6, D)
    qkv_bias = jnp.concatenate(
        [bias_full[:D], jnp.zeros((D,), jnp.float32), bias_full[D : 2 * D]]
    )[:, None]
    bias_row = bias_full[None, 2 * D : ada_at]

    fade = alpha_bar(timesteps)[:, None, None]
    noisy_low = (jnp.sqrt(fade) * latents + jnp.sqrt(1.0 - fade) * noise).astype(low)
    tokens = jnp.einsum(
        "bpi,di->bpd", noisy_low, w_edge, preferred_element_type=jnp.float32
    )
    tokens = tokens + small_used[:D] + positions(patches)[None]

    kept_all = pipeline_forward(bias_row, qkv_bias, ada, tokens, weights)

    squared, head_grad, d_film, g_output, g_out_bias = head_step(
        kept_all[OUTPUT],
        film,
        noise,
        patch_mask,
        inv_count,
        w_edge,
        small_used[5 * D :],
    )
    loss_part = jnp.where(is_last, squared * inv_count, 0.0)
    made_all, film_all = pipeline_backward(
        ada, head_grad, weights, [kept_all[name] for name in READ], d_film
    )

    def flat(whole):
        return whole.reshape(images * patches, whole.shape[2])

    d_second, d_pre, d_branch, d_qkv, d_tokens = [flat(whole) for whole in made_all[:5]]
    d_ada = made_all[5][:, :6].astype(low).reshape(images, 6 * D)

    token_sums = column_sum(d_tokens)
    g_edge = jnp.where(
        is_first,
        matmul_tn(d_tokens, noisy_low.reshape(images * patches, PATCH_IN)),
        g_output,
    )
    d_cond = matmul_nt(film_all, small_rows[:, o_film:o_out]) * silu_grad(cond_later)
    shard_wide, shard_down, right_sums, d_ada_all, conds = row_sums(
        [flat(kept_all[name]) for name in (MIXED_ONE, ATT, MIXED_TWO, ACT)],
        [d_qkv, d_branch, d_pre, d_second],
        d_ada,
        w_ada,
        silu_grad(cond_here),
        d_cond,
    )
    d_ada_all = d_ada_all.reshape(shards * images, 6 * D)

    d_cond_rows = lax.dynamic_index_in_dim(conds, dp_index, 0, keepdims=False)
    d_cond_all = jnp.swapaxes(conds, 0, 1).reshape(shards * images, D)
    d_time = (
        matmul_nt(d_cond_all, small_rows[:, o_second:o_film]) * silu_grad(time_hidden)
    ).astype(low)
    bias_sums = jnp.concatenate(
        [
            right_sums[0][:D],
            right_sums[0][2 * D :],
            right_sums[1],
            right_sums[2],
            right_sums[3],
            column_sum(d_ada),
        ]
    )
    sums = jnp.concatenate(
        [
            bias_sums.reshape(shards, -1),
            g_edge.reshape(shards, -1),
            jnp.broadcast_to(token_sums, (shards, D)),
            jnp.broadcast_to(g_out_bias, (shards, PATCH_IN)),
            jnp.broadcast_to(column_sum(d_time), (shards, rows)),
        ],
        axis=1,
    )
    sums = exchange(sums[:, None], "dp", 11)[:, 0]
    shard_ada = matmul_tn(act_here, d_ada_all)
    shard_in = jnp.concatenate([shard_wide, shard_ada], axis=1)
    edge_end = bias_width + rows * PATCH_IN
    shard_bias = jnp.sum(sums[:, :bias_width], axis=0)
    edge_rows = jnp.sum(sums[:, bias_width:edge_end], axis=0).reshape(rows, PATCH_IN)
    token_sums = jnp.sum(sums[:, edge_end : edge_end + D], axis=0)
    out_sums = jnp.sum(sums[:, edge_end + D : edge_end + D + PATCH_IN], axis=0)
    time_sums = sums[:, edge_end + D + PATCH_IN :].reshape(-1)
    small_grad = jnp.concatenate(
        [
            edge_rows,
            matmul_tn(d_time, time_low),
            matmul_tn(d_cond_rows, one_hot),
            matmul_tn(time_act, d_cond_all),
            matmul_tn(act_later, film_all),
            edge_rows,
        ],
        axis=1,
    )
    small_shard = lax.dynamic_slice_in_dim(small_grad, section_index * small_width, small_width, 1)
    sbias_grad = jnp.concatenate(
        [token_sums, time_sums, column_sum(d_cond_all), column_sum(film_all), out_sums]
    )
    sbias_shard = lax.dynamic_slice_in_dim(
        sbias_grad, section_index * sbias_width, sbias_width, 0
    )

    shard_in, shard_down, small_shard, sbias_shard, shard_bias = lax.optimization_barrier(
        (shard_in, shard_down, small_shard, sbias_shard, shard_bias)
    )
    dp_zero = (dp_index == 0).astype(jnp.float32)
    squares = (
        jnp.sum(shard_in * shard_in)
        + jnp.sum(shard_down * shard_down)
        + jnp.sum(shard_bias * shard_bias)
        + jnp.sum(small_shard * small_shard)
        + dp_zero * jnp.sum(sbias_shard * sbias_shard)
    )
    pair = jnp.broadcast_to(jnp.stack([squares, loss_part])[:, None], (2, 128))
    pair = jnp.sum(spread(pair, "dp", 14), axis=0)
    pair = jnp.sum(spread(pair, "section", 15), axis=0)
    norm_square, loss = (pair[0, 0], pair[1, 0])
    grad_norm = jnp.sqrt(norm_square)
    scaling = jnp.minimum(1.0, CLIP / grad_norm)
    new_in, first_in, second_in = adam_update(w_in, shard_in[None], m_in, v_in, scaling)
    new_down, first_down, second_down = adam_update(
        w_down, shard_down[None], m_down, v_down, scaling
    )
    new_bias, first_bias, second_bias = adam_update(
        b_blk, shard_bias[None], m_bias, v_bias, scaling
    )
    new_small, first_small, second_small = adam_update(
        small_mats, small_shard, m_small, v_small, scaling
    )
    new_sbias, first_sbias, second_sbias = adam_update(
        small_bias, sbias_shard, m_sbias, v_sbias, scaling
    )
    return (
        loss,
        grad_norm,
        new_in,
        first_in,
        second_in,
        new_down,
        first_down,
        second_down,
        new_bias,
        first_bias,
        second_bias,
        new_small,
        first_small,
        second_small,
        new_sbias,
        first_sbias,
        second_sbias,
    )


def solution(mesh):
    in_specs = (
        P("dp", None, None),
        P("dp", None, None),
        P("dp"),
        P("dp"),
        P("dp", None),
        P("section", "dp", None),
        P("section", "dp", None),
        P("section", "dp"),
        P("dp", "section"),
        P("section"),
        P("section", "dp", None),
        P("section", "dp", None),
        P("section", "dp"),
        P("dp", "section"),
        P("section"),
        P("section", "dp", None),
        P("section", "dp", None),
        P("section", "dp"),
        P("dp", "section"),
        P("section"),
    )
    out_specs = (
        P(),
        P(),
        P("section", "dp", None),
        P("section", "dp", None),
        P("section", "dp", None),
        P("section", "dp", None),
        P("section", "dp", None),
        P("section", "dp", None),
        P("section", "dp"),
        P("section", "dp"),
        P("section", "dp"),
        P("dp", "section"),
        P("dp", "section"),
        P("dp", "section"),
        P("section"),
        P("section"),
        P("section"),
    )
    return jax.shard_map(body, mesh=mesh, in_specs=in_specs, out_specs=out_specs, check_vma=False)
```

```python
import functools
import math

import jax
import jax.numpy as jnp
from jax import lax
from jax.experimental import pallas as pl
from jax.experimental.pallas import tpu as pltpu
from jax.sharding import PartitionSpec as P

D = 1152
HEADS = 16
HEAD_DIM = 72
FF = 4608
CLASSES = 1000
FREQ = 256
PATCH_IN = 16
GRID = 16


EPS_NORM = 1e-06
CLIP = 0.001
RATE = 0.005
BETA_ONE = 0.9
BETA_TWO = 0.999
ADAM_EPS = 1e-08
DECAY = 0.01
STEP_POWER = 10.0


def passed_along(value, axis, steps):
    count = lax.axis_size(axis)
    first, last = (max(0, -steps), min(count, count - steps))
    return lax.ppermute(value, axis, [(source, source + steps) for source in range(first, last)])


def matmul(left_side, right_side):
    return jnp.dot(left_side, right_side, preferred_element_type=jnp.float32)


def matmul_tn(left_side, right_side):
    return lax.dot_general(
        left_side, right_side, (((0,), (0,)), ((), ())), preferred_element_type=jnp.float32
    )


def matmul_nt(left_side, right_side):
    return lax.dot_general(
        left_side, right_side, (((1,), (1,)), ((), ())), preferred_element_type=jnp.float32
    )


def column_sum(values):
    return jnp.sum(values.astype(jnp.float32), axis=0)


def normalize(values):
    center = values - jnp.mean(values, axis=-1, keepdims=True)
    invstd = lax.rsqrt(jnp.mean(center * center, axis=-1, keepdims=True) + EPS_NORM)
    return (center * invstd, invstd)


def norm_back(grad_normed, normed, invstd):
    return invstd * (
        grad_normed
        - jnp.mean(grad_normed, axis=-1, keepdims=True)
        - normed * jnp.mean(grad_normed * normed, axis=-1, keepdims=True)
    )


def gelu_tanh(values):
    return (
        0.5
        * values
        * (1.0 + jnp.tanh(0.7978845608028654 * (values + 0.044715 * values * values * values)))
    )


def gelu_grad(values):
    inner = jnp.tanh(0.7978845608028654 * (values + 0.044715 * values * values * values))
    return 0.5 * (1.0 + inner) + 0.5 * values * (1.0 - inner * inner) * 0.7978845608028654 * (
        1.0 + 0.134145 * values * values
    )


def silu_grad(values):
    sigma = jax.nn.sigmoid(values)
    return sigma * (1.0 + values * (1.0 - sigma))


def positions(patches):
    quarter = D // 4
    omega = jnp.exp(-math.log(10000.0) * jnp.arange(quarter, dtype=jnp.float32) / quarter)
    spot = jnp.arange(patches, dtype=jnp.int32)
    row_angle = (spot // GRID).astype(jnp.float32)[:, None] * omega[None, :]
    col_angle = (spot % GRID).astype(jnp.float32)[:, None] * omega[None, :]
    return jnp.concatenate(
        [jnp.sin(row_angle), jnp.cos(row_angle), jnp.sin(col_angle), jnp.cos(col_angle)], axis=1
    )


def time_features(time_steps):
    half = FREQ // 2
    freqs = jnp.exp(-math.log(10000.0) * jnp.arange(half, dtype=jnp.float32) / half)
    angles = time_steps.astype(jnp.float32)[:, None] * freqs[None, :]
    return jnp.concatenate([jnp.cos(angles), jnp.sin(angles)], axis=1)


def alpha_bar(time_steps):
    return jnp.cos((time_steps.astype(jnp.float32) / 1000.0 + 0.008) / 1.008 * (math.pi / 2)) ** 2


def label_table(label_part):
    return (label_part[:, None] == jnp.arange(CLASSES, dtype=jnp.int32)[None, :]).astype(
        jnp.bfloat16
    )


MESH = pl.DeviceIdType.MESH
DIRECT = 8


def rounded(values):
    return lax.reduce_precision(values, 8, 7)


def meet(axis, count, here, stride=1):
    barrier = pltpu.get_barrier_semaphore()
    for step in range(1, count):
        pl.semaphore_signal(
            barrier,
            inc=1,
            device_id={axis: lax.rem(here + step * stride, count * stride)},
            device_id_type=MESH,
        )
    pl.semaphore_wait(barrier, count - 1)


def meet_both(sections, section, here):
    barrier = pltpu.get_barrier_semaphore()
    for axis, me, size in (("section", section, sections), ("dp", here, DIRECT)):
        for step in range(1, size):
            pl.semaphore_signal(
                barrier, inc=1, device_id={axis: lax.rem(me + step, size)}, device_id_type=MESH
            )
    pl.semaphore_wait(barrier, sections + DIRECT - 2)


def share_kernel(axis, count, stride, personal, in_ref, out_ref, send_sem, recv_sem):
    here = lax.axis_index(axis)
    meet(axis, count, here, stride)
    place = here // stride
    copies = []
    for step in range(1, count):
        copy = pltpu.make_async_remote_copy(
            src_ref=in_ref.at[lax.rem(place + step, count)] if personal else in_ref,
            dst_ref=out_ref.at[place],
            send_sem=send_sem.at[step - 1],
            recv_sem=recv_sem.at[step - 1],
            device_id={axis: lax.rem(here + step * stride, count * stride)},
            device_id_type=MESH,
        )
        copy.start()
        copies.append(copy)
    out_ref[place] = in_ref[place] if personal else in_ref[...]
    for copy in copies:
        copy.wait()


def share(value, axis, personal, ident, stride=1):
    count = lax.axis_size(axis) // stride
    shape = value.shape if personal else (count,) + value.shape
    return pl.pallas_call(
        functools.partial(share_kernel, axis, count, stride, personal),
        out_shape=jax.ShapeDtypeStruct(shape, value.dtype),
        in_specs=[pl.BlockSpec(memory_space=pltpu.VMEM)],
        out_specs=pl.BlockSpec(memory_space=pltpu.VMEM),
        scratch_shapes=[
            pltpu.SemaphoreType.DMA((count - 1,)),
            pltpu.SemaphoreType.DMA((count - 1,)),
        ],
        compiler_params=pltpu.CompilerParams(collective_id=ident, has_side_effects=True),
        name="share",
    )(value)


def spread(value, axis, ident):
    if lax.axis_size(axis) > DIRECT:
        return lax.all_gather(value, axis)
    return share(value, axis, False, ident)


def share_all_kernel(sections, count, in_ref, out_ref, send_sem, recv_sem):
    section, here = (lax.axis_index("section"), lax.axis_index("dp"))
    targets = [
        {"section": lax.rem(section + i // count, sections), "dp": lax.rem(here + i % count, count)}
        for i in range(1, sections * count)
    ]
    barrier = pltpu.get_barrier_semaphore()
    for target in targets:
        pl.semaphore_signal(barrier, inc=1, device_id=target, device_id_type=MESH)
    pl.semaphore_wait(barrier, len(targets))
    copies = []
    for i, target in enumerate(targets):
        copy = pltpu.make_async_remote_copy(
            src_ref=in_ref,
            dst_ref=out_ref.at[section, here],
            send_sem=send_sem.at[i],
            recv_sem=recv_sem.at[i],
            device_id=target,
            device_id_type=MESH,
        )
        copy.start()
        copies.append(copy)
    out_ref[section, here] = in_ref[...]
    for copy in copies:
        copy.wait()


def sum_all(value, ident):
    sections, count = (lax.axis_size("section"), lax.axis_size("dp"))
    if count != DIRECT:
        return lax.psum(value, ("section", "dp"))
    shared = pl.pallas_call(
        functools.partial(share_all_kernel, sections, count),
        out_shape=jax.ShapeDtypeStruct((sections, count) + value.shape, value.dtype),
        in_specs=[pl.BlockSpec(memory_space=pltpu.VMEM)],
        out_specs=pl.BlockSpec(memory_space=pltpu.VMEM),
        scratch_shapes=[pltpu.SemaphoreType.DMA((sections * count - 1,))] * 2,
        compiler_params=pltpu.CompilerParams(collective_id=ident, has_side_effects=True),
        name="share_all",
    )(value)
    return jnp.sum(shared, axis=(0, 1))


def exchanged_sum(value, ident):
    count = lax.axis_size("dp")
    if count != DIRECT:
        return jnp.sum(exchange(value, "dp", ident), axis=0)
    core = lax.axis_index("dp") % 2
    parted = value.reshape((count // 2, 2) + value.shape[1:])
    other = lax.dynamic_index_in_dim(parted, 1 - core, 1, keepdims=False)
    same = lax.dynamic_index_in_dim(parted, core, 1, keepdims=False)
    both = same + lax.ppermute(other, "dp", [(i, i ^ 1) for i in range(count)])
    return jnp.sum(share(both, "dp", True, ident, 2), axis=0)


def exchange(value, axis, ident):
    if lax.axis_size(axis) > DIRECT:
        return lax.all_to_all(value, axis, 0, 0)
    return share(value, axis, True, ident)


FINAL, LATER, NEAR, FAR, PASS = range(5)
STEPS = 16
CHIPS = 4


def sums_kernel(units, rows, sections, *refs):
    lefts, rights = (refs[:4], refs[4:8])
    given, w_ada, slope, head_part, refs = (refs[8], refs[9], refs[10], refs[11], refs[12:])
    owns, finals, laters = (refs[0:2], refs[2:4], refs[4:6])
    bias_out, spread_out, cond_out, refs = (refs[6], refs[7], refs[8], refs[9:])
    (
        left_v,
        right_v,
        product,
        got,
        own_v,
        stage,
        near,
        far,
        passed,
        left_sem,
        right_sem,
        send_sem,
        recv_sem,
        own_sem,
        stage_sem,
        block_sem,
        pass_sem,
        given_send,
        given_recv,
        cond_pieces,
        cond_low,
        cond_send,
        cond_recv,
    ) = refs
    here = lax.axis_index("dp")
    core, chip = (lax.rem(here, 2), here // 2)
    partner = {"dp": here + 1 - 2 * core}
    tall = CHIPS * rows
    section = lax.axis_index("section")
    meet_both(sections, section, here)
    spreading = []
    for step in range(1, DIRECT):
        copy = pltpu.make_async_remote_copy(
            src_ref=given,
            dst_ref=spread_out.at[here],
            send_sem=given_send.at[step - 1],
            recv_sem=given_recv.at[step - 1],
            device_id={"dp": lax.rem(here + step, DIRECT)},
            device_id_type=MESH,
        )
        copy.start()
        spreading.append(copy)
    spread_out[here] = given[...]
    places = {NEAR: near, FAR: far, PASS: passed}
    shared = []

    def share_pieces():
        for copy in spreading:
            copy.wait()
        each = given.shape[0]
        for i in range(DIRECT):
            at = slice(i * each, (i + 1) * each)
            cond_pieces[section, at] = contract(spread_out[i], w_ada[...], 1, 1) * slope[at]
        for step in range(1, sections):
            copy = pltpu.make_async_remote_copy(
                src_ref=cond_pieces.at[section],
                dst_ref=cond_pieces.at[section],
                send_sem=cond_send.at[step - 1],
                recv_sem=cond_recv.at[step - 1],
                device_id={"section": lax.rem(section + step, sections)},
                device_id_type=MESH,
            )
            copy.start()
            shared.append(copy)

    def share_rows():
        for copy in shared:
            copy.wait()
        value = head_part[...]
        for layer in reversed(range(sections)):
            value = (value + cond_pieces[layer]).astype(jnp.bfloat16).astype(jnp.float32)
        cond_low[...] = value.astype(jnp.bfloat16)
        cond_out[here] = value.astype(jnp.bfloat16)
        shared.clear()
        for step in range(1, DIRECT):
            copy = pltpu.make_async_remote_copy(
                src_ref=cond_low,
                dst_ref=cond_out.at[here],
                send_sem=cond_send.at[sections + step],
                recv_sem=cond_recv.at[sections + step],
                device_id={"dp": lax.rem(here + step, DIRECT)},
                device_id_type=MESH,
            )
            copy.start()
            shared.append(copy)


    def placed(pair, slot):
        wide, down = pair
        side_by_side = wide.shape[1] // D
        if slot < side_by_side:
            return wide.at[:, pl.ds(slot * D, D)]
        return down.at[pl.ds((slot - side_by_side) * rows, rows)]

    plan, last, slots = ([], [None, None], [1, 1])
    for left, left_at, right, right_at, gathers, slot in units:
        fresh = []
        for side, key in enumerate(((left, left_at), (right, right_at))):
            fresh.append(last[side] != key)
            if fresh[-1]:
                slots[side] = 1 - slots[side]
                last[side] = key
        plan.append((tuple(slots), tuple(fresh)))
    def loads_of(index):
        left, left_at, right, right_at, gathers, slot = units[index]
        (left_slot, right_slot), (left_fresh, right_fresh) = plan[index]
        copies = []
        if left_fresh:
            source = lefts[left].at[:, pl.ds(left_at, D)]
            copies.append(
                pltpu.make_async_copy(source, left_v.at[left_slot], left_sem.at[left_slot])
            )
        if right_fresh:
            source = rights[right].at[:, pl.ds(right_at, D)]
            copies.append(
                pltpu.make_async_copy(source, right_v.at[right_slot], right_sem.at[right_slot])
            )
        return copies

    pending, crossing, leaving, keeping = ({}, {}, {}, {})

    def load(index):
        pending[index] = loads_of(index)
        for copy in pending[index]:
            copy.start()

    def to_partner(source, target, sems):
        copy = pltpu.make_async_remote_copy(
            src_ref=source,
            dst_ref=target,
            send_sem=send_sem.at[sems],
            recv_sem=recv_sem.at[sems],
            device_id=partner,
            device_id_type=MESH,
        )
        copy.start()
        return copy

    def multiply(index):
        gathers = units[index][4]
        left_slot, right_slot = plan[index][0]
        for copy in pending[index]:
            copy.wait()
        if index + 1 < len(units):
            load(index + 1)
        if index >= 2:
            for copy in crossing[index - 2]:
                copy.wait_send()
        slot, place = (index % 2, index % 4)

        @pl.loop(0, 3)
        def tile(step):
            at = pl.ds(pl.multiple_of(step * (D // 3), 128), D // 3)
            product[slot, at] = contract(left_v[left_slot, :, at], right_v[right_slot], 0, 0)

        if gathers is None or gathers == 0:
            ones = jnp.ones((8, right_v.shape[1]), jnp.bfloat16)
            bias_out[units[index][5]] = matmul(ones, right_v[right_slot])
        if gathers is None:
            crossing[index] = [
                to_partner(
                    product.at[slot, pl.ds(pl.multiple_of((2 * i + 1 - core) * rows, 8), rows)],
                    got.at[place, pl.ds(i * rows, rows)],
                    place * CHIPS + i,
                )
                for i in range(CHIPS)
            ]
        else:
            crossing[index] = [
                to_partner(
                    product.at[slot, pl.ds(pl.multiple_of((1 - core) * tall, 8), tall)],
                    got.at[place],
                    place * CHIPS,
                )
            ]

    def crossed(source, kind, slot, to, sem):
        pair = {FINAL: finals, LATER: laters}.get(kind)
        return pltpu.make_async_remote_copy(
            src_ref=source,
            dst_ref=places[kind].at[slot] if pair is None else placed(pair, slot),
            send_sem=sem,
            recv_sem=block_sem.at[kind, slot],
            device_id={"dp": 2 * to + core},
            device_id_type=MESH,
        )

    def landed(kind, slot):
        crossed(stage.at[0, 0], kind, slot, chip, stage_sem.at[0, 0]).wait_recv()

    def filled(target, index, block, gathers, added=None):
        slot, place = (index % 2, index % 4)
        base = (2 * block + core) * rows if gathers is None else core * tall + block * rows

        @pl.loop(0, rows // STEPS)
        def run(step):
            at = step * STEPS
            value = (
                product[slot, pl.ds(pl.multiple_of(base + at, STEPS), STEPS)]
                + got[place, pl.ds(pl.multiple_of(block * rows + at, STEPS), STEPS)]
            )
            to = pl.ds(pl.multiple_of(at, STEPS), STEPS)
            if added is not None:
                value = value + added[to].astype(jnp.float32)
            target[to] = value.astype(target.dtype)

    def route(index, block, owner, slot, gathers):
        side = index % 3

        def case(at, kind, to, added=None):
            copy = crossed(
                stage.at[side, block], kind, slot, to, stage_sem.at[side, block]
            )

            @pl.when(chip == at)
            def act():
                if added is not None:
                    landed(added, slot)
                filled(
                    stage.at[side, block],
                    index,
                    block,
                    gathers,
                    None if added is None else places[added].at[slot],
                )
                copy.start()

            leaving[index].append((chip == at, copy.wait_send))

        keep = pltpu.make_async_copy(
            own_v.at[side, block], placed(owns, slot), own_sem.at[side, block]
        )

        @pl.when(chip == owner)
        def hold():
            filled(own_v.at[side, block], index, block, gathers)
            keep.start()

        leaving[index].append((chip == owner, keep.wait))
        flip = (lambda at: at) if owner < 2 else (lambda at: CHIPS - 1 - at)
        if owner in (0, CHIPS - 1):
            case(flip(3), FAR, flip(2))
            case(flip(1), FINAL, flip(0))
            case(flip(2), PASS, flip(1), FAR)
        else:
            case(flip(3), NEAR, flip(2))
            case(flip(0), FINAL, flip(1))
            case(flip(2), LATER, flip(1), NEAR)

    def blocks_of(index):
        gathers = units[index][4]
        if gathers is None:
            return [(owner, owner, units[index][5]) for owner in (0, 3, 1, 2)]
        return [(block, gathers, units[index][5] + block) for block in range(CHIPS)]

    def combine(index):
        for copy in crossing[index]:
            copy.wait_recv()
        if index >= 3:
            finish(index - 3)
        leaving[index] = []
        for block, owner, slot in blocks_of(index):
            route(index, block, owner, slot, units[index][4])

    def finish(index):
        for condition, wait in leaving[index]:

            @pl.when(condition)
            def settle(wait=wait):
                wait()

    def pass_on(index):
        for block, owner, slot in blocks_of(index):
            if owner not in (0, CHIPS - 1):
                continue
            middle = 1 if owner == 0 else CHIPS - 2

            @pl.when(chip == middle)
            def forward(slot=slot, owner=owner):
                landed(PASS, slot)
                crossed(passed.at[slot], LATER, slot, owner, pass_sem.at[slot]).start()

    total = len(units)
    load(0)
    multiply(0)
    for index in range(total):
        if index + 1 < total:
            multiply(index + 1)
        combine(index)
        if index >= 1:
            pass_on(index - 1)
        if index == 2:
            share_pieces()
        elif index == 5:
            share_rows()
    pass_on(total - 1)
    for index in range(max(0, total - 3), total):
        finish(index)
    for index in range(max(0, total - 2), total):
        for copy in crossing[index]:
            copy.wait_send()
    for index in range(total):
        for block, owner, slot in blocks_of(index):

            @pl.when(chip == owner)
            def received(slot=slot):
                landed(FINAL, slot)
                landed(LATER, slot)

            if owner in (0, CHIPS - 1):

                @pl.when(chip == (1 if owner == 0 else CHIPS - 2))
                def sent(slot=slot, owner=owner):
                    crossed(passed.at[slot], LATER, slot, owner, pass_sem.at[slot]).wait_send()

    for copy in shared:
        copy.wait()


def line_sums(units, lefts, rights, rows, ident, given, w_ada, slope, head_part):
    sections = lax.axis_size("section")
    tokens = lefts[0].shape[0]
    places = sum(unit[4] is None for unit in units) + 4
    block = (rows, D)
    outs = pl.pallas_call(
        functools.partial(sums_kernel, units, rows, sections),
        out_shape=[
            jax.ShapeDtypeStruct(shape, kind)
            for kind in (jnp.float32, jnp.bfloat16, jnp.bfloat16)
            for shape in ((rows, (places - CHIPS) * D), (CHIPS * rows, D))
        ]
        + [
            jax.ShapeDtypeStruct((places - CHIPS + 1, 8, D), jnp.float32),
            jax.ShapeDtypeStruct((DIRECT,) + given.shape, given.dtype),
            jax.ShapeDtypeStruct((DIRECT,) + slope.shape, jnp.bfloat16),
        ],
        in_specs=specs("h" * 8, "vvvv"),
        out_specs=specs("h" * 6, "vvv"),
        scratch_shapes=[
            pltpu.VMEM((2, tokens, D), jnp.bfloat16),
            pltpu.VMEM((2, tokens, D), jnp.bfloat16),
            pltpu.VMEM((2, 8 * rows, D), jnp.float32),
            pltpu.VMEM((4, 4 * rows, D), jnp.float32),
            pltpu.VMEM((3, 4) + block, jnp.float32),
            pltpu.VMEM((3, 4) + block, jnp.bfloat16),
            pltpu.VMEM((places,) + block, jnp.bfloat16),
            pltpu.VMEM((places,) + block, jnp.bfloat16),
            pltpu.VMEM((places,) + block, jnp.bfloat16),
            pltpu.SemaphoreType.DMA((2,)),
            pltpu.SemaphoreType.DMA((2,)),
            pltpu.SemaphoreType.DMA((16,)),
            pltpu.SemaphoreType.DMA((16,)),
            pltpu.SemaphoreType.DMA((3, 4)),
            pltpu.SemaphoreType.DMA((3, 4)),
            pltpu.SemaphoreType.DMA((5, places)),
            pltpu.SemaphoreType.DMA((places,)),
            pltpu.SemaphoreType.DMA((DIRECT - 1,)),
            pltpu.SemaphoreType.DMA((DIRECT - 1,)),
            pltpu.VMEM((sections,) + slope.shape, jnp.float32),
            pltpu.VMEM(slope.shape, jnp.bfloat16),
            pltpu.SemaphoreType.DMA((sections + DIRECT,)),
            pltpu.SemaphoreType.DMA((sections + DIRECT,)),
        ],
        compiler_params=pltpu.CompilerParams(
            collective_id=ident, has_side_effects=True, vmem_limit_bytes=62 << 20
        ),
        cost_estimate=pl.CostEstimate(
            flops=2 * tokens * D * D * len(units),
            bytes_accessed=len(units) * tokens * D * 4,
            transcendentals=0,
        ),
        name="line_sums",
    )(*lefts, *rights, given, w_ada, slope, head_part)
    wide, down = [
        outs[i] + outs[2 + i].astype(jnp.float32) + outs[4 + i].astype(jnp.float32)
        for i in range(2)
    ]
    return (wide, down, outs[6][:, 0], outs[7], outs[8])


def row_sums(lefts, rights, given, w_ada, slope, head_part):
    count = lax.axis_size("dp")
    if count != DIRECT:
        products = [matmul_tn(one, other) for one, other in zip(lefts, rights)]
        sums = [lax.psum_scatter(one, "dp", scatter_dimension=0, tiled=True) for one in products]
        wide = jnp.concatenate([sums[0], sums[1], sums[2]], axis=1)
        given = lax.all_gather(given, "dp")
        pieces = matmul_nt(given.reshape(-1, given.shape[2]), w_ada) * slope
        pieces = lax.all_gather(pieces, "section")
        for layer in reversed(range(lax.axis_size("section"))):
            head_part = rounded(head_part + pieces[layer])
        conds = lax.all_gather(head_part.astype(jnp.bfloat16), "dp")
        return (wide, sums[3], [column_sum(one) for one in rights], given, conds)
    rows = D // count
    parts = FF // D
    attention = [(0, 0, 0, i * D, None, i) for i in range(3)] + [(1, 0, 1, 0, None, 3)]
    hidden = [(2, 0, 2, i * D, None, 4 + i) for i in range(parts)]
    second = [(3, i * D, 3, 0, i, 4 + parts) for i in (0, 3, 1, 2)]
    units = hidden[:1] + second[:2] + hidden[1:2] + second[2:] + hidden[2:] + attention
    wide, down, bias, given_all, conds = line_sums(
        tuple(units), lefts, rights, rows, 12, given, w_ada, slope, head_part
    )
    sums = [bias[:3].reshape(-1), bias[3], bias[4 : 4 + parts].reshape(-1), bias[4 + parts]]
    return (wide, down, sums, given_all, conds)


GROUP = 4


def contract(left_side, right_side, left_axis, right_axis):
    return lax.dot_general(
        left_side,
        right_side,
        (((left_axis,), (right_axis,)), ((), ())),
        preferred_element_type=jnp.float32,
    )


def heads_of(ref, at, group):
    return [
        ref[at + head * HEAD_DIM : at + (head + 1) * HEAD_DIM] for head in group
    ]


def softmax_down(scores):
    weights = jnp.exp(scores - jnp.max(scores, axis=0, keepdims=True))
    return weights * (1.0 / jnp.sum(weights, axis=0, keepdims=True))


def stacked(values):
    return jnp.concatenate([value.astype(jnp.bfloat16) for value in values], axis=0)


def attend_kernel(qkv_ref, out_ref):
    scaling = HEAD_DIM ** (-0.5)
    for first in range(0, HEADS, GROUP):
        group = range(first, first + GROUP)
        rows = slice(first * HEAD_DIM, (first + GROUP) * HEAD_DIM)
        queries, keys = (heads_of(qkv_ref, 0, group), heads_of(qkv_ref, D, group))
        values = heads_of(qkv_ref, 2 * D, group)
        scores = [contract(key, query, 0, 0) * scaling for key, query in zip(keys, queries)]
        probs = [softmax_down(score).astype(jnp.bfloat16) for score in scores]
        out_ref[rows] = stacked([contract(v, p, 1, 0) for v, p in zip(values, probs)])


def attend_back_kernel(qkv_ref, grad_ref, out_ref):
    scaling = HEAD_DIM ** (-0.5)
    for first in range(0, HEADS, GROUP):
        group = range(first, first + GROUP)
        at, to = (first * HEAD_DIM, (first + GROUP) * HEAD_DIM)
        queries, keys = (heads_of(qkv_ref, 0, group), heads_of(qkv_ref, D, group))
        values, grads = (heads_of(qkv_ref, 2 * D, group), heads_of(grad_ref, 0, group))
        scores = [contract(key, query, 0, 0) * scaling for key, query in zip(keys, queries)]
        d_probs = [contract(value, grad, 0, 0) for value, grad in zip(values, grads)]
        probs = [softmax_down(score) for score in scores]
        d_scores = [
            (p * (d - jnp.sum(p * d, axis=0, keepdims=True))).astype(jnp.bfloat16)
            for p, d in zip(probs, d_probs)
        ]
        lows = [p.astype(jnp.bfloat16) for p in probs]
        out_ref[at:to] = stacked([contract(k, d, 1, 0) * scaling for k, d in zip(keys, d_scores)])
        out_ref[D + at : D + to] = stacked(
            [contract(q, d, 1, 1) * scaling for q, d in zip(queries, d_scores)]
        )
        out_ref[2 * D + at : 2 * D + to] = stacked(
            [contract(g, p, 1, 1) for g, p in zip(grads, lows)]
        )


ROW_BLOCK = 64
HOPS = 3
RESIDUAL, MIXED_ONE, QKV, ATT, BRANCH, MIDDLE = range(6)
MIXED_TWO, PRE, ACT, SECOND, OUTPUT = range(6, 11)
D_SECOND, D_PRE, D_BRANCH, D_QKV, D_RESIDUAL = range(5)
WIDE, LOW = (jnp.float32, jnp.bfloat16)
KEPT = (
    (D, WIDE),
    (D, LOW),
    (3 * D, LOW),
    (D, LOW),
    (D, WIDE),
    (D, WIDE),
    (D, LOW),
    (FF, WIDE),
    (FF, LOW),
    (D, WIDE),
    (D, WIDE),
)
READ = (RESIDUAL, QKV, BRANCH, MIDDLE, PRE, SECOND)
MADE = ((D, LOW), (FF, LOW), (D, LOW), (3 * D, LOW), (D, LOW))
WEIGHTS = ((D, 3 * D), (D, D), (D, FF), (FF, D))


def kept_shape(name, width, patches):
    return (width, patches) if name == QKV else (patches, width)


def by_rows(patches, step):
    @pl.loop(0, patches // ROW_BLOCK)
    def run(index):
        step(pl.ds(pl.multiple_of(index * ROW_BLOCK, ROW_BLOCK), ROW_BLOCK))


def started(source, target, sem):
    copy = pltpu.make_async_copy(source, target, sem)
    copy.start()
    return copy


def parts_of(whole, parts):
    width = whole // parts
    return [slice(part * width, part * width + width) for part in range(parts)]


def wait_first(image, loads):
    @pl.when(image == 0)
    def wait():
        for load in loads:
            load.wait()


def hop_of(send, received, send_sem, recv_sem, target):
    def hop(image, part):
        cols = pl.ds(part * (D // HOPS), D // HOPS)
        return pltpu.make_async_remote_copy(
            src_ref=send.at[image, :, cols],
            dst_ref=received.at[image, :, cols],
            send_sem=send_sem.at[image, part],
            recv_sem=recv_sem.at[image, part],
            device_id={"section": target},
            device_id_type=MESH,
        )

    return hop


def forward_kernel(sections, images, bias, qkv_bias, ada, tokens, wx, ws, *refs):
    count, patches = (len(KEPT), tokens.shape[1])
    outs, scratch = (refs[:count], refs[count:])
    kept = scratch[:count]
    (
        att_down,
        send,
        received,
        wq_v,
        wp_v,
        wh_v,
        ws_v,
        w_sem,
        x_sem,
        out_sem,
        send_sem,
        recv_sem,
    ) = scratch[count:]
    section = lax.axis_index("section")
    loads = [
        started(wx.at[:, cols], wq_v.at[:, cols], w_sem.at[i])
        for i, cols in enumerate(parts_of(3 * D, 3))
    ]
    loads.append(started(wx.at[:, pl.ds(3 * D, D)], wp_v, w_sem.at[3]))
    loads.append(started(wx.at[:, pl.ds(4 * D, FF)], wh_v, w_sem.at[4]))
    loads.append(started(ws, ws_v, w_sem.at[5]))
    meet("section", sections, section)
    hop = hop_of(send, received, send_sem, recv_sem, lax.rem(section + 1, sections))
    residual = kept[RESIDUAL]

    @pl.loop(0, images)
    def run(image):
        saves = []

        def save(name):
            saves.append(started(kept[name], outs[name].at[image], out_sem.at[name]))

        @pl.when(section == 0)
        def take_tokens():
            started(tokens.at[image], residual, x_sem).wait()

        @pl.when(section > 0)
        def take_received():
            for part in range(HOPS):
                hop(image, part).wait_recv()
            residual[...] = received[image].astype(jnp.float32)

        save(RESIDUAL)
        modulation = ada[image]

        def mix_one(at):
            normed, unused = normalize(residual[at])
            kept[MIXED_ONE][at] = (normed * (1.0 + modulation[1:2]) + modulation[0:1]).astype(
                jnp.bfloat16
            )

        by_rows(patches, mix_one)
        save(MIXED_ONE)
        wait_first(image, loads[:3])
        for cols in parts_of(3 * D, 3):
            kept[QKV][cols] = (
                contract(wq_v[:, cols], kept[MIXED_ONE][...], 0, 1) + qkv_bias[cols]
            ).astype(jnp.bfloat16)
        save(QKV)
        attend_kernel(kept[QKV], att_down)
        wait_first(image, loads[3:4])
        kept[BRANCH][...] = contract(att_down[...], wp_v[...], 0, 0) + bias[:, :D]
        kept[ATT][...] = att_down[...].T
        save(BRANCH)
        save(ATT)

        def mix_two(at):
            middle = residual[at] + modulation[2:3] * kept[BRANCH][at]
            kept[MIDDLE][at] = middle
            normed, unused = normalize(middle)
            kept[MIXED_TWO][at] = (normed * (1.0 + modulation[4:5]) + modulation[3:4]).astype(
                jnp.bfloat16
            )

        by_rows(patches, mix_two)
        save(MIDDLE)
        save(MIXED_TWO)
        wait_first(image, loads[4:5])
        for part, cols in enumerate(parts_of(FF, FF // D)):
            pre = (
                matmul(kept[MIXED_TWO][...], wh_v[:, cols])
                + bias[:, D + part * D : 2 * D + part * D]
            )
            kept[PRE][:, cols] = pre
            kept[ACT][:, cols] = gelu_tanh(pre).astype(jnp.bfloat16)
        save(PRE)
        save(ACT)
        wait_first(image, loads[5:])
        for part, cols in enumerate(parts_of(D, HOPS)):
            second = (
                matmul(kept[ACT][...], ws_v[:, cols])
                + bias[:, D + FF + cols.start : D + FF + cols.stop]
            )
            kept[SECOND][:, cols] = second
            output = kept[MIDDLE][:, cols] + modulation[5:6, cols] * second
            kept[OUTPUT][:, cols] = output
            send[image, :, cols] = output.astype(jnp.bfloat16)

            @pl.when(section < sections - 1)
            def pass_on(part=part):
                hop(image, part).start()

        save(SECOND)
        save(OUTPUT)
        for copy in saves:
            copy.wait()

    @pl.when(section < sections - 1)
    def finish():
        for image in range(images):
            for part in range(HOPS):
                hop(image, part).wait_send()


def backward_kernel(sections, images, direct, ada, head_grad, wx, ws, *refs):
    reads, made, patches = (len(READ), len(MADE), head_grad.shape[1])
    sources, refs = (refs[:reads], refs[reads:])
    if direct:
        film, refs = (refs[0], refs[1:])
    outs, ada_out, refs = (refs[:made], refs[made], refs[made + 1 :])
    if direct:
        film_rows, film_out, refs = (refs[0], refs[1], refs[2:])
    kept = {name: refs[i] for i, name in enumerate(READ)}
    grads = refs[reads : reads + made - 1]
    (
        flow,
        mixed,
        att_grad,
        qkv_grad,
        sums,
        send,
        received,
        wq_v,
        wp_v,
        wh_v,
        ws_v,
        w_sem,
        in_sem,
        x_sem,
        out_sem,
        send_sem,
        recv_sem,
        film_send,
        film_recv,
    ) = refs[reads + made - 1 :]
    section = lax.axis_index("section")
    here = lax.axis_index("dp")

    def fetching(name, image):
        index = READ.index(name)
        return pltpu.make_async_copy(sources[index].at[image], kept[name], in_sem.at[index])

    fetching(SECOND, 0).start()
    loads = [started(ws, ws_v, w_sem.at[0])]
    for name in READ:
        if name != SECOND:
            fetching(name, 0).start()
    loads.append(started(wx.at[:, pl.ds(4 * D, FF)], wh_v, w_sem.at[1]))
    loads.append(started(wx.at[:, pl.ds(3 * D, D)], wp_v, w_sem.at[2]))
    loads.append(started(wx.at[:, pl.ds(0, 3 * D)], wq_v, w_sem.at[3]))
    spreading, passing = ([], [])
    if direct:
        meet_both(sections, section, here)
        for step in range(1, DIRECT):
            copy = pltpu.make_async_remote_copy(
                src_ref=film,
                dst_ref=film_rows.at[here],
                send_sem=film_send.at[step - 1],
                recv_sem=film_recv.at[step - 1],
                device_id={"dp": lax.rem(here + step, DIRECT)},
                device_id_type=MESH,
            )
            copy.start()
            spreading.append(copy)
        film_rows[here] = film[...]
        for step in range(1, sections):
            passing.append(
                pltpu.make_async_remote_copy(
                    src_ref=film_rows,
                    dst_ref=film_out,
                    send_sem=film_send.at[DIRECT - 2 + step],
                    recv_sem=film_recv.at[DIRECT - 2 + step],
                    device_id={"section": lax.rem(section + step, sections)},
                    device_id_type=MESH,
                )
            )
    else:
        meet("section", sections, section)
    hop = hop_of(send, received, send_sem, recv_sem, lax.rem(section + sections - 1, sections))

    late = (D_QKV, D_RESIDUAL)
    sums[...] = jnp.zeros_like(sums)

    def saving(name, image):
        source = send.at[image] if name == D_RESIDUAL else grads[name]
        return pltpu.make_async_copy(source, outs[name].at[image], out_sem.at[name])

    @pl.loop(0, images)
    def run(image):
        saves = []

        def save(name):
            copy = saving(name, image)
            copy.start()
            if name not in late:
                saves.append(copy)

        def settle(name):
            @pl.when(image > 0)
            def wait():
                saving(name, image - 1).wait()

        def fetch_next(*names):
            @pl.when(image + 1 < images)
            def start():
                for name in names:
                    fetching(name, image + 1).start()

        @pl.when(section == sections - 1)
        def take_head():
            started(head_grad.at[image], flow, x_sem).wait()

        @pl.when(section < sections - 1)
        def take_received():
            for part in range(HOPS):
                hop(image, part).wait_recv()
            flow[...] = received[image].astype(jnp.float32)

        modulation = ada[image]

        def add_sum(row, values):
            sums[image, row : row + 1] += jnp.sum(values, axis=0, keepdims=True)

        fetching(SECOND, image).wait()

        def open_second(at):
            grad = flow[at]
            grads[D_SECOND][at] = (grad * modulation[5:6]).astype(jnp.bfloat16)
            add_sum(5, grad * kept[SECOND][at])

        by_rows(patches, open_second)
        fetch_next(SECOND)
        save(D_SECOND)
        fetching(PRE, image).wait()
        wait_first(image, loads[:1])
        for cols in parts_of(FF, FF // D):
            grads[D_PRE][:, cols] = (
                matmul_nt(grads[D_SECOND][...], ws_v[cols]) * gelu_grad(kept[PRE][:, cols])
            ).astype(jnp.bfloat16)
        fetch_next(PRE)
        save(D_PRE)
        wait_first(image, loads[1:2])
        for cols in parts_of(D, 3):
            mixed[:, cols] = matmul_nt(grads[D_PRE][...], wh_v[cols])
        fetching(MIDDLE, image).wait()
        fetching(BRANCH, image).wait()

        def through_two(at):
            normed, invstd = normalize(kept[MIDDLE][at])
            grad = mixed[at]
            add_sum(3, grad)
            add_sum(4, grad * normed)
            total = flow[at] + norm_back(grad * (1.0 + modulation[4:5]), normed, invstd)
            flow[at] = total
            add_sum(2, total * kept[BRANCH][at])
            grads[D_BRANCH][at] = (total * modulation[2:3]).astype(jnp.bfloat16)

        by_rows(patches, through_two)
        fetch_next(MIDDLE, BRANCH)
        save(D_BRANCH)
        wait_first(image, loads[2:3])
        att_grad[...] = contract(wp_v[...], grads[D_BRANCH][...], 1, 1).astype(jnp.bfloat16)
        fetching(QKV, image).wait()
        attend_back_kernel(kept[QKV], att_grad, qkv_grad)
        fetch_next(QKV)
        wait_first(image, loads[3:])
        for cols in parts_of(D, 3):
            mixed[:, cols] = contract(qkv_grad[...], wq_v[cols], 0, 1)
        fetching(RESIDUAL, image).wait()

        def through_one(at):
            normed, invstd = normalize(kept[RESIDUAL][at])
            grad = mixed[at]
            add_sum(0, grad)
            add_sum(1, grad * normed)
            total = flow[at] + norm_back(grad * (1.0 + modulation[1:2]), normed, invstd)
            send[image, at] = total.astype(jnp.bfloat16)

        by_rows(patches, through_one)

        @pl.when(section > 0)
        def pass_on():
            for part in range(HOPS):
                hop(image, part).start()

        fetch_next(RESIDUAL)
        settle(D_RESIDUAL)
        save(D_RESIDUAL)
        settle(D_QKV)
        grads[D_QKV][...] = qkv_grad[...].T
        save(D_QKV)
        if direct:

            @pl.when(image == 0)
            def pass_film():
                for copy in spreading:
                    copy.wait()

                @pl.when(section == sections - 1)
                def send_film():
                    for copy in passing:
                        copy.start()

        for copy in saves:
            copy.wait()

    started(sums, ada_out, x_sem).wait()
    for name in late:
        saving(name, images - 1).wait()

    @pl.when(section > 0)
    def finish():
        for image in range(images):
            for part in range(HOPS):
                hop(image, part).wait_send()

    if direct:

        @pl.when(section == sections - 1)
        def own_film():
            film_out[...] = film_rows[...]
            for copy in passing:
                copy.wait_send()

        for step in range(1, sections):

            @pl.when(section == step - 1)
            def wait_film(step=step):
                passing[step - 1].wait_recv()


def specs(*spaces):
    return [
        pl.BlockSpec(memory_space={"v": pltpu.VMEM, "h": pl.ANY}[space])
        for space in "".join(spaces)
    ]


def weight_scratch():
    return [pltpu.VMEM(shape, jnp.bfloat16) for shape in WEIGHTS] + [
        pltpu.SemaphoreType.DMA((6,))
    ]


def block_cost(images, patches, factor):
    area = sum(rows * columns for rows, columns in WEIGHTS)
    return pl.CostEstimate(
        flops=images * (2 * patches * area + factor * patches * patches * D),
        bytes_accessed=2 * area + images * 64 * patches * D,
        transcendentals=images * patches * (FF + HEADS * patches),
    )


def pipeline_forward(bias, qkv_bias, ada, tokens, weights):
    images, patches, unused = tokens.shape
    sections = lax.axis_size("section")
    sizes = [(kept_shape(i, item[0], patches), item[1]) for i, item in enumerate(KEPT)]
    return pl.pallas_call(
        functools.partial(forward_kernel, sections, images),
        out_shape=[
            jax.ShapeDtypeStruct((images,) + shape, kind) for shape, kind in sizes
        ],
        in_specs=specs("vvv", "h" * 3),
        out_specs=specs("h" * len(KEPT)),
        scratch_shapes=[pltpu.VMEM(shape, kind) for shape, kind in sizes]
        + [pltpu.VMEM((D, patches), jnp.bfloat16)]
        + [pltpu.VMEM((images, patches, D), jnp.bfloat16)] * 2
        + weight_scratch()
        + [pltpu.SemaphoreType.DMA, pltpu.SemaphoreType.DMA((len(KEPT),))]
        + [pltpu.SemaphoreType.DMA((images, HOPS))] * 2,
        compiler_params=pltpu.CompilerParams(
            vmem_limit_bytes=62 << 20, collective_id=16, has_side_effects=True
        ),
        cost_estimate=block_cost(images, patches, 4),
        name="pipeline_forward",
    )(bias, qkv_bias, ada, tokens, *weights)


def pipeline_backward(ada, head_grad, weights, sources, film):
    images, patches, unused = head_grad.shape
    sections, direct = (lax.axis_size("section"), lax.axis_size("dp") == DIRECT)
    films = [jax.ShapeDtypeStruct((DIRECT,) + film.shape, film.dtype)] * (2 * direct)
    outs = pl.pallas_call(
        functools.partial(backward_kernel, sections, images, direct),
        out_shape=[
            jax.ShapeDtypeStruct((images, patches, width), kind) for width, kind in MADE
        ]
        + [jax.ShapeDtypeStruct((images, 8, D), jnp.float32)]
        + films,
        in_specs=specs("v", "h" * (3 + len(READ)), "v" * direct),
        out_specs=specs("h" * (len(MADE) + 1), "v" * len(films)),
        scratch_shapes=[
            pltpu.VMEM(kept_shape(name, KEPT[name][0], patches), KEPT[name][1]) for name in READ
        ]
        + [pltpu.VMEM((patches, width), kind) for width, kind in MADE[:-1]]
        + [
            pltpu.VMEM((patches, D), jnp.float32),
            pltpu.VMEM((patches, D), jnp.float32),
            pltpu.VMEM((D, patches), jnp.bfloat16),
            pltpu.VMEM((3 * D, patches), jnp.bfloat16),
            pltpu.VMEM((images, 8, D), jnp.float32),
        ]
        + [pltpu.VMEM((images, patches, D), jnp.bfloat16)] * 2
        + weight_scratch()
        + [
            pltpu.SemaphoreType.DMA((len(READ),)),
            pltpu.SemaphoreType.DMA,
            pltpu.SemaphoreType.DMA((len(MADE),)),
        ]
        + [pltpu.SemaphoreType.DMA((images, HOPS))] * 2
        + [pltpu.SemaphoreType.DMA((DIRECT + sections,))] * 2,
        compiler_params=pltpu.CompilerParams(
            vmem_limit_bytes=62 << 20, collective_id=17, has_side_effects=True
        ),
        cost_estimate=block_cost(images, patches, 10),
        name="pipeline_backward",
    )(ada, head_grad, *weights, *sources, *([film] * direct))
    if direct:
        film_all = outs[-1].reshape(-1, film.shape[1])
    else:
        film_all = lax.all_gather(film, ("section", "dp"), tiled=True)
        film_all = film_all[-images * lax.axis_size("dp") :]
    return (outs[: len(MADE) + 1], film_all)


def head_step(residual, film, noise_part, mask_part, inv_count, w_out, b_out):
    shifting, scaling = (film[:, :D], film[:, D:])
    normed, invstd = normalize(residual)
    mixed = (normed * (1.0 + scaling[:, None]) + shifting[:, None]).astype(jnp.bfloat16)
    output = (
        jnp.einsum("bpd,dj->bpj", mixed, w_out, preferred_element_type=jnp.float32) + b_out
    )
    mismatch = output - noise_part
    mask_float = mask_part.astype(jnp.float32)[:, :, None]
    squared = jnp.sum(mask_float * mismatch * mismatch)
    d_output = (2.0 * inv_count * mask_float * mismatch).astype(jnp.bfloat16)
    g_output = jnp.einsum("bpd,bpj->dj", mixed, d_output, preferred_element_type=jnp.float32)
    d_mixed = jnp.einsum("bpj,dj->bpd", d_output, w_out, preferred_element_type=jnp.float32)
    d_film = jnp.concatenate(
        [jnp.sum(d_mixed, axis=1), jnp.sum(d_mixed * normed, axis=1)], axis=1
    ).astype(jnp.bfloat16)
    d_residual = norm_back(d_mixed * (1.0 + scaling[:, None]), normed, invstd)
    g_bias = jnp.sum(d_output.astype(jnp.float32), axis=(0, 1))
    return (squared, d_residual, d_film, g_output, g_bias)


def adam_update(weight, gradient, first_moment, second_moment, scaling):
    gradient = gradient * scaling
    first_new = BETA_ONE * first_moment + (1.0 - BETA_ONE) * gradient
    second_new = BETA_TWO * second_moment + (1.0 - BETA_TWO) * gradient * gradient
    ratio = (
        first_new
        / (1.0 - BETA_ONE**STEP_POWER)
        / (jnp.sqrt(second_new / (1.0 - BETA_TWO**STEP_POWER)) + ADAM_EPS)
    )
    return (weight - RATE * (ratio + DECAY * weight), first_new, second_new)


def body(
    latents,
    noise,
    timesteps,
    labels,
    patch_mask,
    w_in,
    w_down,
    b_blk,
    small_mats,
    small_bias,
    m_in,
    m_down,
    m_bias,
    m_small,
    m_sbias,
    v_in,
    v_down,
    v_bias,
    v_small,
    v_sbias,
):
    section_index = lax.axis_index("section")
    dp_index = lax.axis_index("dp")
    sections = lax.axis_size("section")
    is_first = section_index == 0
    is_last = section_index == sections - 1
    low = jnp.bfloat16
    images, patches = patch_mask.shape
    rows = w_in.shape[1]
    row_at = dp_index * rows
    ada_at = 4 * D + FF
    o_label = PATCH_IN + FREQ
    o_second = o_label + CLASSES
    o_film = o_second + D
    o_out = o_film + 2 * D

    def gathered(value, axis="dp", dim=0):
        return lax.all_gather(value, axis, axis=dim, tiled=True)

    in_low = w_in[0].astype(low)
    w_ada = in_low[:, ada_at:]
    w_tokens = gathered(in_low[:, :ada_at])
    w_second = gathered(w_down[0].astype(low))

    small_low = small_mats.astype(low)
    edge_own = jnp.where(is_first, small_mats[:, :PATCH_IN], small_mats[:, -PATCH_IN:])
    bias_width = b_blk.shape[1]
    pieces = [
        b_blk[0],
        edge_own.reshape(-1),
        timesteps.astype(jnp.float32),
        labels.astype(jnp.float32),
        jnp.sum(patch_mask).astype(jnp.float32)[None],
    ]
    block = jnp.concatenate(pieces)[None]
    blocks = spread(block, "dp", 1)[:, 0]
    ends = [0]
    for piece in pieces:
        ends.append(ends[-1] + piece.shape[0])
    bias_full = rounded(blocks[:, : ends[1]].reshape(-1))
    w_edge = blocks[:, ends[1] : ends[2]].reshape(D, PATCH_IN).astype(low)
    times_all = blocks[:, ends[2] : ends[3]].reshape(-1).astype(jnp.int32)
    labels_all = blocks[:, ends[3] : ends[4]].reshape(-1).astype(jnp.int32)
    valid_total = jnp.sum(blocks[:, ends[4]])
    inv_count = 1.0 / (valid_total * PATCH_IN)
    weights = (w_tokens, w_second)

    small_width = small_mats.shape[1]
    sbias_width = small_bias.shape[0]
    extra = -(-sbias_width // small_width)
    sbias_rows = jnp.pad(small_bias, (0, extra * small_width - sbias_width)).astype(low)
    small_block = jnp.concatenate([small_low, sbias_rows.reshape(extra, small_width)], axis=0)
    small_blocks = spread(small_block, "section", 2)
    small_rows = jnp.concatenate([small_blocks[i, :rows] for i in range(sections)], axis=1)
    small_used = (
        small_blocks[:, rows:].reshape(sections, -1)[:, :sbias_width].reshape(-1)
    ).astype(jnp.float32)

    shards = lax.axis_size("dp")
    time_low = time_features(times_all).astype(low)
    one_hot = label_table(labels_all)
    time_hidden = matmul_nt(time_low, small_rows[:, PATCH_IN:o_label]) + lax.dynamic_slice_in_dim(
        small_used, D + row_at, rows, 0
    )
    time_act = jax.nn.silu(time_hidden).astype(low)
    cond_part = matmul(time_act, small_rows[:, o_second:o_film])
    label_part = matmul_nt(one_hot, small_rows[:, o_label:o_second])
    cond_part = jnp.concatenate([cond_part, label_part], axis=1).reshape(shards, images, D + rows)
    cond_got = exchange(cond_part, "dp", 3)
    cond_own = (
        jnp.sum(cond_got[:, :, :D], axis=0)
        + small_used[2 * D : 3 * D]
        + jnp.swapaxes(cond_got[:, :, D:], 0, 1).reshape(images, D)
    )
    cond_cols = exchange(jnp.swapaxes(cond_own.reshape(images, shards, rows), 0, 1), "dp", 4)
    cond_first = cond_cols.reshape(shards * images, rows)
    cond_later = rounded(cond_first)
    cond_here = jnp.where(is_first, cond_first, cond_later)
    act_here = jax.nn.silu(cond_here).astype(low)
    act_later = jax.nn.silu(cond_later).astype(low)
    ada_part = jnp.concatenate(
        [matmul(act_here, w_ada), matmul(act_later, small_rows[:, o_film:o_out])], axis=1
    )
    ada_own = exchanged_sum(ada_part.reshape(shards, images * 8 * D // 128, 128), 5)
    ada_own = ada_own.reshape(images, 8 * D)
    film = ada_own[:, 6 * D :] + small_used[3 * D : 5 * D]
    ada = (ada_own[:, : 6 * D] + bias_full[ada_at:]).reshape(images, 6, D)
    qkv_bias = jnp.concatenate(
        [bias_full[:D], jnp.zeros((D,), jnp.float32), bias_full[D : 2 * D]]
    )[:, None]
    bias_row = bias_full[None, 2 * D : ada_at]

    fade = alpha_bar(timesteps)[:, None, None]
    noisy_low = (jnp.sqrt(fade) * latents + jnp.sqrt(1.0 - fade) * noise).astype(low)
    tokens = jnp.einsum(
        "bpi,di->bpd", noisy_low, w_edge, preferred_element_type=jnp.float32
    )
    tokens = tokens + small_used[:D] + positions(patches)[None]

    kept_all = pipeline_forward(bias_row, qkv_bias, ada, tokens, weights)

    squared, head_grad, d_film, g_output, g_out_bias = head_step(
        kept_all[OUTPUT],
        film,
        noise,
        patch_mask,
        inv_count,
        w_edge,
        small_used[5 * D :],
    )
    loss_part = jnp.where(is_last, squared * inv_count, 0.0)
    made_all, film_all = pipeline_backward(
        ada, head_grad, weights, [kept_all[name] for name in READ], d_film
    )

    def flat(whole):
        return whole.reshape(images * patches, whole.shape[2])

    d_second, d_pre, d_branch, d_qkv, d_tokens = [flat(whole) for whole in made_all[:5]]
    d_ada = made_all[5][:, :6].astype(low).reshape(images, 6 * D)

    token_sums = column_sum(d_tokens)
    g_edge = jnp.where(
        is_first,
        matmul_tn(d_tokens, noisy_low.reshape(images * patches, PATCH_IN)),
        g_output,
    )
    d_cond = matmul_nt(film_all, small_rows[:, o_film:o_out]) * silu_grad(cond_later)
    shard_wide, shard_down, right_sums, d_ada_all, conds = row_sums(
        [flat(kept_all[name]) for name in (MIXED_ONE, ATT, MIXED_TWO, ACT)],
        [d_qkv, d_branch, d_pre, d_second],
        d_ada,
        w_ada,
        silu_grad(cond_here),
        d_cond,
    )
    d_ada_all = d_ada_all.reshape(shards * images, 6 * D)

    d_cond_rows = lax.dynamic_index_in_dim(conds, dp_index, 0, keepdims=False)
    d_cond_all = jnp.swapaxes(conds, 0, 1).reshape(shards * images, D)
    d_time = (
        matmul_nt(d_cond_all, small_rows[:, o_second:o_film]) * silu_grad(time_hidden)
    ).astype(low)
    bias_sums = jnp.concatenate(
        [
            right_sums[0][:D],
            right_sums[0][2 * D :],
            right_sums[1],
            right_sums[2],
            right_sums[3],
            column_sum(d_ada),
        ]
    )
    sums = jnp.concatenate(
        [
            bias_sums.reshape(shards, -1),
            g_edge.reshape(shards, -1),
            jnp.broadcast_to(token_sums, (shards, D)),
            jnp.broadcast_to(g_out_bias, (shards, PATCH_IN)),
            jnp.broadcast_to(column_sum(d_time), (shards, rows)),
        ],
        axis=1,
    )
    sums = exchange(sums[:, None], "dp", 11)[:, 0]
    shard_ada = matmul_tn(act_here, d_ada_all)
    shard_in = jnp.concatenate([shard_wide, shard_ada], axis=1)
    edge_end = bias_width + rows * PATCH_IN
    shard_bias = jnp.sum(sums[:, :bias_width], axis=0)
    edge_rows = jnp.sum(sums[:, bias_width:edge_end], axis=0).reshape(rows, PATCH_IN)
    token_sums = jnp.sum(sums[:, edge_end : edge_end + D], axis=0)
    out_sums = jnp.sum(sums[:, edge_end + D : edge_end + D + PATCH_IN], axis=0)
    time_sums = sums[:, edge_end + D + PATCH_IN :].reshape(-1)
    small_grad = jnp.concatenate(
        [
            edge_rows,
            matmul_tn(d_time, time_low),
            matmul_tn(d_cond_rows, one_hot),
            matmul_tn(time_act, d_cond_all),
            matmul_tn(act_later, film_all),
            edge_rows,
        ],
        axis=1,
    )
    small_shard = lax.dynamic_slice_in_dim(small_grad, section_index * small_width, small_width, 1)
    sbias_grad = jnp.concatenate(
        [token_sums, time_sums, column_sum(d_cond_all), column_sum(film_all), out_sums]
    )
    sbias_shard = lax.dynamic_slice_in_dim(
        sbias_grad, section_index * sbias_width, sbias_width, 0
    )

    shard_in, shard_down, small_shard, sbias_shard, shard_bias = lax.optimization_barrier(
        (shard_in, shard_down, small_shard, sbias_shard, shard_bias)
    )
    dp_zero = (dp_index == 0).astype(jnp.float32)
    squares = (
        jnp.sum(shard_in * shard_in)
        + jnp.sum(shard_down * shard_down)
        + jnp.sum(shard_bias * shard_bias)
        + jnp.sum(small_shard * small_shard)
        + dp_zero * jnp.sum(sbias_shard * sbias_shard)
    )
    pair = jnp.broadcast_to(jnp.stack([squares, loss_part])[:, None], (2, 128))
    pair = sum_all(pair, 14)
    norm_square, loss = (pair[0, 0], pair[1, 0])
    grad_norm = jnp.sqrt(norm_square)
    scaling = jnp.minimum(1.0, CLIP / grad_norm)
    new_in, first_in, second_in = adam_update(w_in, shard_in[None], m_in, v_in, scaling)
    new_down, first_down, second_down = adam_update(
        w_down, shard_down[None], m_down, v_down, scaling
    )
    new_bias, first_bias, second_bias = adam_update(
        b_blk, shard_bias[None], m_bias, v_bias, scaling
    )
    new_small, first_small, second_small = adam_update(
        small_mats, small_shard, m_small, v_small, scaling
    )
    new_sbias, first_sbias, second_sbias = adam_update(
        small_bias, sbias_shard, m_sbias, v_sbias, scaling
    )
    return (
        loss,
        grad_norm,
        new_in,
        first_in,
        second_in,
        new_down,
        first_down,
        second_down,
        new_bias,
        first_bias,
        second_bias,
        new_small,
        first_small,
        second_small,
        new_sbias,
        first_sbias,
        second_sbias,
    )


def solution(mesh):
    in_specs = (
        P("dp", None, None),
        P("dp", None, None),
        P("dp"),
        P("dp"),
        P("dp", None),
        P("section", "dp", None),
        P("section", "dp", None),
        P("section", "dp"),
        P("dp", "section"),
        P("section"),
        P("section", "dp", None),
        P("section", "dp", None),
        P("section", "dp"),
        P("dp", "section"),
        P("section"),
        P("section", "dp", None),
        P("section", "dp", None),
        P("section", "dp"),
        P("dp", "section"),
        P("section"),
    )
    out_specs = (
        P(),
        P(),
        P("section", "dp", None),
        P("section", "dp", None),
        P("section", "dp", None),
        P("section", "dp", None),
        P("section", "dp", None),
        P("section", "dp", None),
        P("section", "dp"),
        P("section", "dp"),
        P("section", "dp"),
        P("dp", "section"),
        P("dp", "section"),
        P("dp", "section"),
        P("section"),
        P("section"),
        P("section"),
    )
    return jax.shard_map(body, mesh=mesh, in_specs=in_specs, out_specs=out_specs, check_vma=False)
```
